32 devices in a mesh: width: 4 (over y, x), seq: 8 (over z, core).
Axes of the slice: x: 2, y: 2, z: 4, core: 2. Of those that a mesh axis runs over, the one named last changes fastest.
Arguments:
- hidden_in: bfloat16 [4, 2, 1024, 2048], P('width', None, 'seq'), may hold values from -6 to 6
- starts: int32 [4, 2, 4], P('width'), may hold values from 0 to 1023, as said below
- in_gain: float32 [2048], replicated, may hold values from 0.1 to 1.9
- in_weight: bfloat16 [2048, 8512], P('seq'), may hold values from -0.125 to 0.125
- conv_weight: float32 [4, 4352], replicated, may hold values from -3 to 3
- conv_bias: float32 [4352], replicated, may hold values from -3 to 3
- step_bias: float32 [64], replicated, may hold values from -5 to -2
- decay_log: float32 [64], replicated, may hold values from -9 to 1.5
- skip_gain: float32 [64], replicated, may hold values from 0.5 to 1.5
- gate_gain: float32 [4096], replicated, may hold values from 0.1 to 1.9
- out_weight: bfloat16 [4096, 2048], P('seq'), may hold values from -0.125 to 0.125
- cotangent: bfloat16 [4, 2, 1024, 2048], P('width', None, 'seq'), may hold values from -6 to 6
Outputs:
- output: bfloat16 [4, 2, 1024, 2048], P('width', None, 'seq')
- grad_hidden: bfloat16 [4, 2, 1024, 2048], P('width', None, 'seq')
- grad_in_gain: float32 [2048], replicated
- grad_in_weight: float32 [2048, 8512], P('seq', 'width')
- grad_conv_weight: float32 [4, 4352], replicated
- grad_conv_bias: float32 [4352], replicated
- grad_step_bias: float32 [64], replicated
- grad_decay_log: float32 [64], replicated
- grad_skip_gain: float32 [64], replicated
- grad_gate_gain: float32 [4096], replicated
- grad_out_weight: float32 [4096, 2048], P('width', 'seq')
The draws below stay inside these ranges and needn't reach their ends.
Inputs may be any that keep to these rules, and one draw needn't show every extreme that they name: In each group and micro-batch the 4 starts increase strictly from 0; the second lies below 128 and the third above 896, so one document runs from the first index of seq to the last.
All inputs are finite; a program needn't handle non-finite values.
Results may differ from the reference program's by a relative error of at most 0.0087.
Values may be sent and summed in bfloat16 or wider, within the bound.
A program may use at most 384 MiB of HBM per device.

```python
from functools import partial
import jax
import jax.numpy as jnp
from jax import lax

D = 2048
INNER = 4096
HEADS = 64
HEAD_DIM = 64
STATE = 128
KCONV = 4
TOK_MB = 128
MICRO = 2
WIDTHS = 4
TOKENS = 1024
CONV = 4352
PROJ = 8512
N_SEQ = 8


def draw_starts(key, part):
    keys_all = jax.random.split(key, 3)
    shape_all = (WIDTHS, MICRO)
    second = jax.random.randint(keys_all[0], shape_all, 1, TOK_MB)
    third_start = TOKENS - TOK_MB + jax.random.randint(keys_all[1], shape_all, 1, TOK_MB - 1)
    fourth = third_start + 1 + jax.random.randint(keys_all[2], shape_all, 0, TOKENS - 1 - third_start)
    return jnp.stack([jnp.zeros(shape_all, jnp.int32), second, third_start, fourth], axis=-1).astype(jnp.int32)


def with_spikes(values, key, source, target, blocks, factor):
    owner, partner = [(jnp.arange(values.shape[position]) // (values.shape[position] // blocks)).reshape([-1 if axis == position else 1 for axis in range(values.ndim)]) for position in (source, target)]
    chosen = jax.random.permutation(key, blocks)[partner]
    strong = (owner == chosen) | (owner == (partner + blocks // 2) % blocks)
    return jnp.where(strong, factor * values, values)


def shard_levels(stream_key, shape, shards, low, largest):
    gain = 1.0
    for position, parts in shards:
        steps = jax.random.uniform(jax.random.fold_in(jax.random.fold_in(stream_key, 6), position), (parts,), jnp.float32, low / len(shards), largest / len(shards))
        gain = gain * jnp.repeat(jnp.exp(steps), shape[position] // parts).reshape((-1,) + (1,) * (len(shape) - 1 - position))
    return gain


def bell_draw(rng, shape, width, reach, cuts=(), kind=jnp.bfloat16):
    drawn = width * jax.random.normal(rng, shape, jnp.float32)
    if cuts:
        drawn = drawn * shard_levels(rng, shape, cuts, -0.22, 0.18)
    return jnp.clip(drawn, -reach, reach).astype(kind)


def heavy_noise(key, dims, deviation, reach, cuts, heavy, kind=jnp.bfloat16):
    drawn = deviation * jax.random.normal(key, dims, jnp.float32)
    if cuts:
        drawn = drawn * shard_levels(key, dims, cuts, -0.22, 0.18)
    return jnp.clip(with_spikes(drawn, jax.random.fold_in(key, 3), *heavy), -reach, reach).astype(kind)


def setup_inputs(seed: int = 0) -> dict:
    key_list = jax.random.split(jax.random.key(seed), 13)
    hidden_in = heavy_noise(key_list[0], (WIDTHS, MICRO, TOKENS, D), 1.0, 6.0, ((0, 4), (2, 8)), (2, 3, 8, 2.0))
    starts = draw_starts(jax.random.fold_in(key_list[12], 71), 0)
    in_gain = jnp.clip(1.0 + 0.18 * jax.random.normal(key_list[2], (D,), jnp.float32), 0.1, 1.9)
    in_weight = bell_draw(key_list[3], (D, PROJ), D ** -0.5, 0.125, ((0, 8),))
    conv_weight = bell_draw(key_list[4], (KCONV, CONV), KCONV ** -0.5, 3.0, (), jnp.float32)
    conv_bias = bell_draw(key_list[5], (CONV,), 0.5, 3.0, (), jnp.float32)
    step_bias = jnp.clip(jax.random.uniform(key_list[6], (HEADS,), jnp.float32, -5.0, -2.0), -5.0, -2.0)
    decay_log = jnp.clip(jax.random.uniform(key_list[7], (HEADS,), jnp.float32, -9.0, 1.5), -9.0, 1.5)
    skip_gain = jnp.clip(jax.random.uniform(key_list[8], (HEADS,), jnp.float32, 0.5, 1.5), 0.5, 1.5)
    gate_gain = jnp.clip(1.0 + 0.18 * jax.random.normal(key_list[9], (INNER,), jnp.float32), 0.1, 1.9)
    out_weight = bell_draw(key_list[10], (INNER, D), (INNER // 2) ** -0.5, 0.125, ((0, 8),))
    cotangent = heavy_noise(key_list[11], (WIDTHS, MICRO, TOKENS, D), 1.0, 6.0, ((0, 4), (2, 8)), (2, 3, 8, 2.0))
    return dict(hidden_in=hidden_in, starts=starts, in_gain=in_gain, in_weight=in_weight, conv_weight=conv_weight, conv_bias=conv_bias, step_bias=step_bias, decay_log=decay_log, skip_gain=skip_gain, gate_gain=gate_gain, out_weight=out_weight, cotangent=cotangent)


EPSILON = 1e-05
PRECISION = lax.Precision.HIGHEST

@jax.custom_vjp
def low(v):
    return lax.optimization_barrier(v.astype(jnp.bfloat16)).astype(jnp.float32)

@jax.custom_vjp
def low_back(v):
    return v

def low_keep(v):
    return (low(v), None)

def low_pass(kept, grad):
    return (grad,)

def back_keep(v):
    return (v, None)

def back_low(kept, grad):
    return (low(grad),)
low.defvjp(low_keep, low_pass)
low_back.defvjp(back_keep, back_low)

def input_norm(hidden, in_gain):
    return hidden * lax.rsqrt(lax.optimization_barrier(jnp.mean(hidden * hidden, axis=1, keepdims=True)) + EPSILON) * in_gain

def doc_number(doc_starts, positions):
    return lax.optimization_barrier(jnp.sum((doc_starts[None, :] <= positions[:, None]).astype(jnp.int32), axis=1)) - 1

def doc_masks(doc_starts, positions, tap_count):
    doc_ids = doc_number(doc_starts, positions)
    columns = [(doc_ids == doc_number(doc_starts, positions - offset)).astype(jnp.float32) for offset in range(1, tap_count)]
    start_flags = lax.optimization_barrier(jnp.sum((positions[:, None] == doc_starts[None, :]).astype(jnp.int32), axis=1))
    return (jnp.stack(columns, axis=1), start_flags)

def conv_block(xbc_ext, conv_weight, conv_bias, same_doc):
    tap_count = conv_weight.shape[0]
    row_count = xbc_ext.shape[0] - tap_count + 1
    conv_sum = conv_bias + conv_weight[tap_count - 1] * xbc_ext[tap_count - 1:]
    for offset in range(1, tap_count):
        first_row = tap_count - 1 - offset
        conv_sum = conv_sum + conv_weight[first_row] * xbc_ext[first_row:first_row + row_count] * same_doc[:, offset - 1:offset]
    return conv_sum

def mixer_front(xbc_ext, step_raw, conv_weight, conv_bias, step_bias, decay_log, same_doc, start_flags):
    row_count = step_raw.shape[0]
    activated = jax.nn.silu(conv_block(xbc_ext, conv_weight, conv_bias, same_doc))
    x_heads = activated[:, :INNER].reshape(row_count, HEADS, HEAD_DIM)
    write_vecs = activated[:, INNER:INNER + STATE]
    read_vecs = activated[:, INNER + STATE:]
    step_size = jax.nn.softplus(step_raw + step_bias)
    log_cum = jnp.cumsum(-step_size * jnp.exp(decay_log), axis=0).T
    reset_count = jnp.cumsum(start_flags)
    row_index = jnp.arange(row_count)
    causal_keep = (row_index[:, None] >= row_index[None, :]) & (reset_count[:, None] == reset_count[None, :])
    keep_float = causal_keep.astype(jnp.float32)
    decays = jnp.exp(jnp.where(causal_keep[None], log_cum[:, :, None] - log_cum[:, None, :], 0.0)) * keep_float[None]
    scores = jnp.dot(read_vecs, write_vecs.T, precision=PRECISION)
    inputs = x_heads * step_size[:, :, None]
    local_out = jnp.einsum('hij,jhp->ihp', decays * scores[None], inputs, precision=PRECISION)
    carry_in = jnp.exp(log_cum.T) * (reset_count == 0).astype(jnp.float32)[:, None]
    local_state = jnp.einsum('hj,jhp,jn->hpn', decays[:, -1, :], inputs, write_vecs, precision=PRECISION)
    return (x_heads, read_vecs, carry_in, local_out, local_state, carry_in[-1])

def mixer_rear(local_out, x_heads, read_vecs, carry_in, state_in, gate_z, skip_gain, gate_gain, head_mask, active):
    row_count = local_out.shape[0]
    from_state = jnp.einsum('in,hpn->ihp', read_vecs, state_in, precision=PRECISION) * carry_in[:, :, None]
    mixed = (local_out + from_state + skip_gain[None, :, None] * x_heads) * head_mask[None, :, None]
    gated = mixed.reshape(row_count, INNER) * jax.nn.silu(gate_z)
    return gated * lax.rsqrt(lax.optimization_barrier(jnp.sum(gated * gated, axis=1, keepdims=True)) / active + EPSILON) * gate_gain

def forward(hidden, weights_all, doc_starts, head_count):
    in_gain, in_weight, conv_weight, conv_bias, step_bias, decay_log, skip_gain, gate_gain, out_weight = weights_all
    tap_count = conv_weight.shape[0]
    normed = low(input_norm(hidden, in_gain))
    projected = low_back(low(jnp.dot(normed, in_weight, precision=PRECISION)))
    gate_z = projected[:, :INNER]
    conv_in = projected[:, INNER:INNER + CONV]
    step_raw = projected[:, INNER + CONV:]
    positions = jnp.arange(TOKENS, dtype=jnp.int32)
    same_doc, start_flags = doc_masks(doc_starts, positions, tap_count)
    padded = jnp.concatenate([jnp.zeros((tap_count - 1, CONV), jnp.float32), conv_in], axis=0)
    window_rows = jnp.arange(N_SEQ, dtype=jnp.int32)[:, None] * TOK_MB + jnp.arange(TOK_MB + tap_count - 1, dtype=jnp.int32)[None, :]
    ext_blocks = padded[window_rows]
    head_mask = (jnp.arange(HEADS, dtype=jnp.int32) < head_count).astype(jnp.float32)
    active = jnp.float32(head_count * HEAD_DIM)

    def block_step(state_in, pieces):
        ext_rows, raw_steps, same_docs, flag_rows, gate_rows = pieces
        x_heads, read_vecs, carry_in, local_out, local_state, block_decay = mixer_front(ext_rows, raw_steps, conv_weight, conv_bias, step_bias, decay_log, same_docs, flag_rows)
        gated_norm = mixer_rear(local_out, x_heads, read_vecs, carry_in, state_in, gate_rows, skip_gain, gate_gain, head_mask, active)
        return (block_decay[:, None, None] * state_in + local_state, gated_norm)
    blocks = (ext_blocks, step_raw.reshape(N_SEQ, TOK_MB, HEADS), same_doc.reshape(N_SEQ, TOK_MB, tap_count - 1), start_flags.reshape(N_SEQ, TOK_MB), gate_z.reshape(N_SEQ, TOK_MB, INNER))
    initial = jnp.zeros((HEADS, HEAD_DIM, STATE), jnp.float32)
    final_state, gated_blocks = lax.scan(jax.checkpoint(block_step), initial, blocks)
    gated_norm = low(gated_blocks.reshape(TOKENS, INNER))
    return hidden + jnp.dot(gated_norm, out_weight, precision=PRECISION)

def reference(hidden_in, starts, in_gain, in_weight, conv_weight, conv_bias, step_bias, decay_log, skip_gain, gate_gain, out_weight, cotangent):
    weights_all = tuple((weight_item.astype(jnp.float32) for weight_item in (in_gain, in_weight, conv_weight, conv_bias, step_bias, decay_log, skip_gain, gate_gain, out_weight)))
    gradients = tuple((jnp.zeros_like(weight_item) for weight_item in weights_all))
    out_groups, back_groups = ([], [])
    for group_index in range(WIDTHS):
        group_heads = HEADS // 8 * 2 ** group_index
        out_list, back_list = ([], [])
        for micro_index in range(MICRO):
            hidden = hidden_in[group_index, micro_index].astype(jnp.float32)
            result, pullback = jax.vjp(partial(forward, doc_starts=starts[group_index, micro_index], head_count=group_heads), hidden, weights_all)
            grad_hidden, grad_weights = pullback(cotangent[group_index, micro_index].astype(jnp.float32))
            gradients = tuple((running + addition for running, addition in zip(gradients, grad_weights)))
            out_list.append(result.astype(jnp.bfloat16))
            back_list.append(grad_hidden.astype(jnp.bfloat16))
        out_groups.append(jnp.stack(out_list))
        back_groups.append(jnp.stack(back_list))
    return (jnp.stack(out_groups), jnp.stack(back_groups), gradients[0], gradients[1], gradients[2], gradients[3], gradients[4], gradients[5], gradients[6], gradients[7], gradients[8])
```

```python
from functools import partial

import jax
import jax.numpy as jnp
from jax import lax
from jax.experimental import pallas as pl
from jax.experimental.pallas import tpu as pltpu
from jax.sharding import PartitionSpec as P

INNER = 4096
HEADS = 64
HEAD_DIM = 64
STATE = 128
CONV = 4352
EPSILON = 1e-05
LANES = 128
TAPS = 4
NEG = -1e30
F32 = jnp.float32
BF16 = jnp.bfloat16


def mm(a, b):
    return lax.dot_general(a, b, (((1,), (0,)), ((), ())), preferred_element_type=F32)


def mm_nt(a, b):
    return lax.dot_general(a, b, (((1,), (1,)), ((), ())), preferred_element_type=F32)


def mm_tn(a, b):
    return lax.dot_general(a, b, (((0,), (0,)), ((), ())), preferred_element_type=F32)


def halves(value, axis):
    high = value.astype(BF16)
    low = (value - high.astype(F32)).astype(BF16)
    return jnp.concatenate([high, low], axis=axis)


def sigmoid(value):
    return 0.5 * jnp.tanh(0.5 * value) + 0.5


def prefix_sum(tri, value):
    high = value.astype(BF16)
    rest = value - high.astype(F32)
    middle = rest.astype(BF16)
    low = (rest - middle.astype(F32)).astype(BF16)
    parts = mm(tri, jnp.concatenate([high, middle, low], axis=1))
    width = value.shape[1]
    return parts[:, :width] + parts[:, width : 2 * width] + parts[:, 2 * width :]


def doc_number(starts_ref, micro, positions):
    count = jnp.zeros_like(positions)
    for item in range(starts_ref.shape[1]):
        count = count + (starts_ref[micro, item] <= positions).astype(jnp.int32)
    return count


class Chunk:
    def __init__(self, starts_ref, micro, chunk, rows, raw_dt, head_ref, expand, tri):
        first = chunk * rows
        column = lax.broadcasted_iota(jnp.int32, (rows, 1), 0) + first
        line = lax.broadcasted_iota(jnp.int32, (1, rows), 1) + first
        doc_col = doc_number(starts_ref, micro, column)
        doc_row = doc_number(starts_ref, micro, line)
        self.same = [
            (doc_number(starts_ref, micro, column - offset) == doc_col).astype(F32)
            for offset in range(1, TAPS)
        ]
        before = jnp.int32(0)
        last = jnp.int32(0)
        for item in range(starts_ref.shape[1]):
            before = before + (starts_ref[micro, item] <= first - 1).astype(jnp.int32)
            last = last + (starts_ref[micro, item] <= first + rows - 1).astype(jnp.int32)
        carry = (doc_col == before).astype(F32)
        same_last = (doc_col == last).astype(F32)
        self.bias = jnp.where((column >= line) & (doc_col == doc_row), 0.0, NEG)
        self.shifted_dt = raw_dt + head_ref[0:1]
        self.step = jnp.maximum(self.shifted_dt, 0.0) + jnp.log1p(
            jnp.exp(-jnp.abs(self.shifted_dt))
        )
        self.log_keep = self.step * head_ref[1:2]
        self.cum = prefix_sum(tri, self.log_keep)
        self.cum_t = self.cum.T
        carried = jnp.exp(self.cum) * carry
        left = jnp.exp(self.cum[rows - 1 :] - self.cum) * same_last
        spread = mm(
            halves(jnp.concatenate([self.step, carried, left], axis=0), 1), expand
        )
        self.step_cols = spread[:rows]
        self.carry_cols = spread[rows : 2 * rows]
        self.left_cols = spread[2 * rows :]
        self.keep_all = self.carry_cols[rows - 1 :]

    def decay(self, head):
        return jnp.exp(self.cum[:, head : head + 1] - self.cum_t[head : head + 1] + self.bias)


def head_groups(heads):
    size = 2 if heads % 2 == 0 else 1
    return size, heads // size


def stacked(value, size):
    if size == 1:
        return value.astype(BF16)
    lane = lax.broadcasted_iota(jnp.int32, value.shape, 1)
    first = jnp.where(lane < HEAD_DIM, value, 0.0)
    second = jnp.where(lane < HEAD_DIM, 0.0, value)
    return jnp.concatenate([first, second], axis=0).astype(BF16)


def convolved(ext, micro, rows, taps_ref, same):
    current = ext[micro, 8 : 8 + rows, :]
    total = taps_ref[TAPS : TAPS + 1] + taps_ref[TAPS - 1 : TAPS] * current
    views = []
    for offset in range(1, TAPS):
        view = ext[micro, 8 - offset : 8 - offset + rows, :] * same[offset - 1]
        views.append(view)
        total = total + taps_ref[TAPS - 1 - offset : TAPS - offset] * view
    return current, views, total


def forward_kernel(
    micros,
    heads,
    starts_ref,
    proj_ref,
    dnorm_ref,
    taps_ref,
    head_ref,
    cols_ref,
    expand_ref,
    tri_ref,
    gg_ref,
    mixed_ref,
    states_ref,
    tails_ref,
    sums_ref,
    ext,
    state,
):
    chunk = pl.program_id(0)
    rows = proj_ref.shape[0] // micros
    width = heads * HEAD_DIM
    conv_width = 2 * STATE + width
    size, groups = head_groups(heads)

    @pl.when(chunk == 0)
    def _():
        ext[:, :8, :] = jnp.zeros((micros, 8, conv_width), F32)
        state[...] = jnp.zeros_like(state)

    skip, gain, mask = cols_ref[0:1], cols_ref[1:2], cols_ref[2:3]
    sums = []
    for micro in range(micros):
        part = slice(micro * rows, (micro + 1) * rows)
        tails_ref[micro] = ext[micro, :8, :]
        ext[micro, 8 : 8 + rows, :] = proj_ref[part, :conv_width].astype(F32)
        raw_dt = proj_ref[part, conv_width + width :].astype(F32)
        at = Chunk(
            starts_ref, micro, chunk, rows, raw_dt, head_ref, expand_ref[...], tri_ref[...]
        )
        conv = convolved(ext, micro, rows, taps_ref, at.same)[2]
        act = conv * sigmoid(conv)
        write = act[:, :STATE].astype(BF16)
        read = act[:, STATE : 2 * STATE].astype(BF16)
        x_heads = act[:, 2 * STATE :]
        scores = mm_nt(read, write)
        inputs = x_heads * at.step_cols
        state_in = state[micro]
        state_low = state_in.astype(BF16)
        states_ref[micro] = state_low
        outs = []
        for group in range(groups):
            matrices = [
                (at.decay(group * size + item) * scores).astype(BF16) for item in range(size)
            ]
            span = slice(group * size * HEAD_DIM, (group + 1) * size * HEAD_DIM)
            outs.append(mm(jnp.concatenate(matrices, axis=1), stacked(inputs[:, span], size)))
        mixed = jnp.concatenate(outs, axis=1) + at.carry_cols * mm(read, state_low)
        state[micro] = at.keep_all * state_in + mm_tn(
            write, (inputs * at.left_cols).astype(BF16)
        )
        mixed = mixed + skip * x_heads
        mixed_ref[part, :] = mixed
        gate = proj_ref[part, conv_width : conv_width + width].astype(F32)
        gated = mask * mixed * (gate * sigmoid(gate))
        gg_ref[part, :] = (gated * gain).astype(BF16)
        square = jnp.sum(gated * gated, axis=1, keepdims=True)
        cross = jnp.sum(dnorm_ref[part, :] * gain * gated, axis=1, keepdims=True)
        lane = lax.broadcasted_iota(jnp.int32, (rows, LANES), 1)
        both = jnp.where(lane == 0, square, jnp.where(lane == 1, cross, 0.0))
        sums.append(both.T[:2])
        ext[micro, :8, :] = ext[micro, rows : rows + 8, :]
    pad = sums_ref.shape[0] - 2 * micros
    if pad:
        sums.append(jnp.zeros((pad, rows), F32))
    sums_ref[...] = jnp.concatenate(sums, axis=0)


def backward_kernel(
    micros,
    heads,
    starts_ref,
    active_ref,
    proj_ref,
    dnorm_ref,
    mixed_ref,
    states_ref,
    tails_ref,
    sums_ref,
    taps_ref,
    head_ref,
    cols_ref,
    expand_ref,
    gather_ref,
    tri_ref,
    dproj_ref,
    gnorm_ref,
    gconv_ref,
    gcols_ref,
    ghead_ref,
    ext,
    heads_ext,
    dstate,
):
    chunks = pl.num_programs(0)
    step_index = pl.program_id(0)
    chunk = chunks - 1 - step_index
    rows = proj_ref.shape[0] // micros
    width = heads * HEAD_DIM
    conv_width = 2 * STATE + width
    size, groups = head_groups(heads)

    @pl.when(step_index == 0)
    def _():
        heads_ext[:, :, rows:, :] = jnp.zeros((micros, TAPS - 1, 8, conv_width), F32)
        dstate[...] = jnp.zeros_like(dstate)
        gconv_ref[...] = jnp.zeros_like(gconv_ref)
        gcols_ref[...] = jnp.zeros_like(gcols_ref)
        ghead_ref[...] = jnp.zeros_like(ghead_ref)

    skip, gain, mask = cols_ref[0:1], cols_ref[1:2], cols_ref[2:3]
    tri = tri_ref[...]
    gather = gather_ref[...]
    inverse_active = 1.0 / active_ref[0]
    sums = jnp.concatenate(
        [sums_ref[...], jnp.zeros((LANES - sums_ref.shape[0], rows), F32)], axis=0
    ).T
    for micro in range(micros):
        part = slice(micro * rows, (micro + 1) * rows)
        ext[micro, :8, :] = tails_ref[micro]
        ext[micro, 8 : 8 + rows, :] = proj_ref[part, :conv_width].astype(F32)
        raw_dt = proj_ref[part, conv_width + width :].astype(F32)
        at = Chunk(starts_ref, micro, chunk, rows, raw_dt, head_ref, expand_ref[...], tri)
        current, views, conv = convolved(ext, micro, rows, taps_ref, at.same)
        conv_sig = sigmoid(conv)
        act = conv * conv_sig
        write = act[:, :STATE].astype(BF16)
        read = act[:, STATE : 2 * STATE].astype(BF16)
        x_heads = act[:, 2 * STATE :]
        scores = mm_nt(read, write)
        inputs = x_heads * at.step_cols

        gate = proj_ref[part, conv_width : conv_width + width].astype(F32)
        gate_sig = sigmoid(gate)
        gate_act = gate * gate_sig
        masked = mask * mixed_ref[part, :]
        gated = masked * gate_act
        root = lax.rsqrt(sums[:, 2 * micro : 2 * micro + 1] * inverse_active + EPSILON)
        pull = root * root * root * sums[:, 2 * micro + 1 : 2 * micro + 2] * inverse_active
        dnorm = dnorm_ref[part, :]
        scaled = gated * root
        gnorm_ref[part, :] = (scaled * gain).astype(BF16)
        d_gated = root * dnorm * gain - gated * pull
        d_gate = d_gated * masked * (gate_sig * (1.0 + gate * (1.0 - gate_sig)))
        d_mixed = mask * d_gated * gate_act
        gcols_ref[0:1] += jnp.sum(d_mixed * x_heads, axis=0, keepdims=True)
        gcols_ref[1:2] += jnp.sum(dnorm * scaled, axis=0, keepdims=True)

        state_low = states_ref[micro]
        d_state = dstate[micro]
        d_state_low = d_state.astype(BF16)
        from_state = (d_mixed * at.carry_cols).astype(BF16)
        left = inputs * at.left_cols
        left_low = left.astype(BF16)
        d_left = mm(write, d_state_low)
        state_out = mm(read, state_low)
        d_read = mm_nt(from_state, state_low)
        d_write = mm_nt(left_low, d_state_low)
        d_mixed_low = d_mixed.astype(BF16).astype(F32)
        inputs_low = inputs.astype(BF16).astype(F32)
        d_scores = jnp.zeros((rows, rows), F32)
        locals_out, d_locals = [], []
        for group in range(groups):
            span = slice(group * size * HEAD_DIM, (group + 1) * size * HEAD_DIM)
            decays = [at.decay(group * size + item) for item in range(size)]
            matrices = [(decay * scores).astype(BF16) for decay in decays]
            in_stack = stacked(inputs[:, span], size)
            out_stack = stacked(d_mixed[:, span], size)
            locals_out.append(mm(jnp.concatenate(matrices, axis=1), in_stack))
            d_locals.append(mm_tn(jnp.concatenate(matrices, axis=0), out_stack))
            d_matrices = mm_nt(out_stack, inputs[:, span].astype(BF16))
            for item in range(size):
                d_scores = (
                    d_scores + d_matrices[item * rows : (item + 1) * rows] * decays[item]
                )
        local_out = jnp.concatenate(locals_out, axis=1)
        d_local = jnp.concatenate(d_locals, axis=1)
        d_scores_low = d_scores.astype(BF16)
        d_read = d_read + mm(d_scores_low, write)
        d_write = d_write + mm_tn(d_scores_low, read)
        d_inputs = d_local + at.left_cols * d_left
        d_x = skip * d_mixed + d_inputs * at.step_cols

        passed = left * d_left
        cum_terms = (
            d_mixed_low * local_out
            + d_mixed * at.carry_cols * state_out
            - inputs_low * d_local
            - passed
        )
        kept = jnp.sum(d_state * at.keep_all * state_low.astype(F32), axis=0, keepdims=True)
        final = jnp.sum(passed, axis=0, keepdims=True) + kept
        stack = jnp.concatenate(
            [cum_terms, d_inputs * x_heads, jnp.broadcast_to(final, (8, width))], axis=0
        )
        reduced = mm(halves(stack, 1), gather)
        d_cum = reduced[:rows]
        d_step = reduced[rows : 2 * rows]
        final_row = reduced[2 * rows : 2 * rows + 1]
        total = jnp.sum(d_cum, axis=0, keepdims=True) + final_row
        d_log = total - prefix_sum(tri, d_cum) + d_cum
        d_step = d_step + d_log * head_ref[1:2]
        d_dt = d_step * sigmoid(at.shifted_dt)
        ghead_ref[0:1] += jnp.sum(d_log * at.log_keep, axis=0, keepdims=True)
        ghead_ref[1:2] += jnp.sum(d_dt, axis=0, keepdims=True)
        dstate[micro] = at.keep_all * d_state + mm_tn(read, from_state)

        d_conv = jnp.concatenate([d_write, d_read, d_x], axis=1) * (
            conv_sig * (1.0 + conv * (1.0 - conv_sig))
        )
        gconv_ref[TAPS : TAPS + 1] += jnp.sum(d_conv, axis=0, keepdims=True)
        gconv_ref[TAPS - 1 : TAPS] += jnp.sum(d_conv * current, axis=0, keepdims=True)
        d_raw = taps_ref[TAPS - 1 : TAPS] * d_conv
        for offset in range(1, TAPS):
            tap = TAPS - 1 - offset
            gconv_ref[tap : tap + 1] += jnp.sum(
                d_conv * views[offset - 1], axis=0, keepdims=True
            )
            heads_ext[micro, offset - 1, :rows, :] = d_conv * at.same[offset - 1]
            d_raw = d_raw + taps_ref[tap : tap + 1] * (
                heads_ext[micro, offset - 1, offset : offset + rows, :]
            )
            heads_ext[micro, offset - 1, rows:, :] = heads_ext[micro, offset - 1, :8, :]
        dproj_ref[part, :conv_width] = d_raw.astype(BF16)
        dproj_ref[part, conv_width : conv_width + width] = d_gate.astype(BF16)
        dproj_ref[part, conv_width + width :] = d_dt.astype(BF16)


def constant(shape):
    return pl.BlockSpec(shape, lambda index: (0,) * len(shape))


def run_forward(micros, heads, rows, chunks, starts, proj, dnorm, taps, head, cols, expand, tri):
    width = heads * HEAD_DIM
    conv_width = 2 * STATE + width
    block = micros * rows
    sum_rows = -(-2 * micros // 8) * 8
    return pl.pallas_call(
        partial(forward_kernel, micros, heads),
        grid=(chunks,),
        in_specs=[
            pl.BlockSpec(memory_space=pltpu.SMEM),
            pl.BlockSpec((block, proj.shape[1]), lambda index: (index, 0)),
            pl.BlockSpec((block, width), lambda index: (index, 0)),
            constant(taps.shape),
            constant(head.shape),
            constant(cols.shape),
            constant(expand.shape),
            constant(tri.shape),
        ],
        out_specs=[
            pl.BlockSpec((block, width), lambda index: (index, 0)),
            pl.BlockSpec((block, width), lambda index: (index, 0)),
            pl.BlockSpec((None, micros, STATE, width), lambda index: (index, 0, 0, 0)),
            pl.BlockSpec((None, micros, 8, conv_width), lambda index: (index, 0, 0, 0)),
            pl.BlockSpec((None, sum_rows, rows), lambda index: (index, 0, 0)),
        ],
        out_shape=[
            jax.ShapeDtypeStruct((chunks * block, width), BF16),
            jax.ShapeDtypeStruct((chunks * block, width), F32),
            jax.ShapeDtypeStruct((chunks, micros, STATE, width), BF16),
            jax.ShapeDtypeStruct((chunks, micros, 8, conv_width), F32),
            jax.ShapeDtypeStruct((chunks, sum_rows, rows), F32),
        ],
        scratch_shapes=[
            pltpu.VMEM((micros, rows + 8, conv_width), F32),
            pltpu.VMEM((micros, STATE, width), F32),
        ],
        compiler_params=pltpu.CompilerParams(vmem_limit_bytes=48 << 20),
        name="mixer_forward",
    )(starts, proj, dnorm, taps, head, cols, expand, tri)


def run_backward(
    micros,
    heads,
    rows,
    chunks,
    starts,
    active,
    proj,
    dnorm,
    mixed,
    states,
    tails,
    sums,
    taps,
    head,
    cols,
    expand,
    gather,
    tri,
):
    width = heads * HEAD_DIM
    conv_width = 2 * STATE + width
    block = micros * rows

    def back(index):
        return (chunks - 1 - index, 0)

    return pl.pallas_call(
        partial(backward_kernel, micros, heads),
        grid=(chunks,),
        in_specs=[
            pl.BlockSpec(memory_space=pltpu.SMEM),
            pl.BlockSpec(memory_space=pltpu.SMEM),
            pl.BlockSpec((block, proj.shape[1]), back),
            pl.BlockSpec((block, width), back),
            pl.BlockSpec((block, width), back),
            pl.BlockSpec(
                (None, micros, STATE, width), lambda index: (chunks - 1 - index, 0, 0, 0)
            ),
            pl.BlockSpec(
                (None, micros, 8, conv_width), lambda index: (chunks - 1 - index, 0, 0, 0)
            ),
            pl.BlockSpec((None, sums.shape[1], rows), lambda index: (chunks - 1 - index, 0, 0)),
            constant(taps.shape),
            constant(head.shape),
            constant(cols.shape),
            constant(expand.shape),
            constant(gather.shape),
            constant(tri.shape),
        ],
        out_specs=[
            pl.BlockSpec((block, proj.shape[1]), back),
            pl.BlockSpec((block, width), back),
            constant((8, conv_width)),
            constant((8, width)),
            constant((8, LANES)),
        ],
        out_shape=[
            jax.ShapeDtypeStruct((chunks * block, proj.shape[1]), BF16),
            jax.ShapeDtypeStruct((chunks * block, width), BF16),
            jax.ShapeDtypeStruct((8, conv_width), F32),
            jax.ShapeDtypeStruct((8, width), F32),
            jax.ShapeDtypeStruct((8, LANES), F32),
        ],
        scratch_shapes=[
            pltpu.VMEM((micros, rows + 8, conv_width), F32),
            pltpu.VMEM((micros, TAPS - 1, rows + 8, conv_width), F32),
            pltpu.VMEM((micros, STATE, width), F32),
        ],
        compiler_params=pltpu.CompilerParams(vmem_limit_bytes=48 << 20),
        name="mixer_backward",
    )(
        starts,
        active,
        proj,
        dnorm,
        mixed,
        states,
        tails,
        sums,
        taps,
        head,
        cols,
        expand,
        gather,
        tri,
    )


def tables(heads, rows):
    width = heads * HEAD_DIM
    expand = (
        jnp.arange(LANES)[:, None] == jnp.arange(width)[None, :] // HEAD_DIM
    ).astype(BF16)
    tri = (jnp.arange(rows)[:, None] >= jnp.arange(rows)[None, :]).astype(BF16)
    return (
        jnp.concatenate([expand, expand], axis=0),
        jnp.concatenate([expand.T, expand.T], axis=0),
        tri,
    )


def input_norm(hidden, in_gain):
    return hidden * lax.rsqrt(jnp.mean(hidden * hidden, axis=1, keepdims=True) + EPSILON) * in_gain


def own(value, start, count, axis=0):
    return lax.dynamic_slice_in_dim(value, start, count, axis)


def placed(value, total, start):
    whole = jnp.zeros(value.shape[:-1] + (total,), F32)
    return lax.dynamic_update_slice_in_dim(whole, value, start, value.ndim - 1)


def per_device(
    hidden_in,
    starts,
    in_gain,
    in_weight,
    conv_weight,
    conv_bias,
    step_bias,
    decay_log,
    skip_gain,
    gate_gain,
    out_weight,
    cotangent,
):
    seq_total = lax.axis_size("seq")
    seq_index = lax.axis_index("seq")
    group_index = lax.axis_index("width")
    micros, rows, model_width = hidden_in.shape[1:]
    heads = HEADS // seq_total
    width = heads * HEAD_DIM
    head_first = seq_index * heads
    col_first = seq_index * width
    depth = in_weight.shape[0]
    head_count = HEADS // 8 * jnp.left_shift(jnp.int32(1), group_index)
    active = head_count.astype(F32) * HEAD_DIM

    flat_hidden = hidden_in[0].reshape(micros * rows, model_width).astype(F32)
    flat_grad = cotangent[0].reshape(micros * rows, model_width)
    normed, norm_back = jax.vjp(input_norm, flat_hidden, in_gain)
    all_normed = lax.all_gather(normed.astype(BF16), "seq", axis=0, tiled=True)
    all_grad = lax.all_gather(flat_grad, "seq", axis=0, tiled=True)

    dt_pad = LANES
    gates = in_weight[:, :INNER].reshape(depth, seq_total, width)
    xs = in_weight[:, INNER : 2 * INNER].reshape(depth, seq_total, width)
    bc = jnp.broadcast_to(
        in_weight[:, None, 2 * INNER : INNER + CONV], (depth, seq_total, 2 * STATE)
    )
    dts = in_weight[:, INNER + CONV :].reshape(depth, seq_total, heads)
    dts = jnp.pad(dts, ((0, 0), (0, 0), (0, dt_pad - heads)))
    pieces = jnp.concatenate([bc, xs, gates, dts], axis=2).transpose(1, 0, 2)
    columns = lax.all_to_all(pieces, "seq", split_axis=0, concat_axis=0)
    columns = columns.reshape(seq_total * depth, columns.shape[2])

    conv_width = 2 * STATE + width

    def conv_columns(value):
        return jnp.concatenate(
            [value[..., INNER:], own(value, col_first, width, value.ndim - 1)], axis=-1
        )

    taps = jnp.concatenate(
        [
            conv_columns(conv_weight),
            conv_columns(conv_bias[None]),
            jnp.zeros((8 - TAPS - 1, conv_width), F32),
        ],
        axis=0,
    )
    head_rows = jnp.stack(
        [own(step_bias, head_first, heads), -jnp.exp(own(decay_log, head_first, heads))]
    )
    head_table = jnp.pad(head_rows, ((0, 6), (0, LANES - heads)))
    head_mask = (head_first + jnp.arange(heads, dtype=jnp.int32) < head_count).astype(F32)
    cols = jnp.stack(
        [
            jnp.repeat(own(skip_gain, head_first, heads), HEAD_DIM),
            own(gate_gain, col_first, width),
            jnp.repeat(head_mask, HEAD_DIM),
        ]
    )
    cols = jnp.pad(cols, ((0, 5), (0, 0)))
    expand, gather, tri = tables(heads, rows)

    proj = mm(all_normed, columns).astype(BF16)
    dnorm = mm_nt(all_grad, out_weight)
    gg, mixed, states, tails, sums = run_forward(
        micros, heads, rows, seq_total, starts[0], proj, dnorm, taps, head_table, cols, expand, tri
    )
    sums = lax.psum(sums, "seq")
    branch = lax.psum_scatter(
        mm(gg, out_weight).astype(BF16), "seq", scatter_dimension=0, tiled=True
    )
    squares = own(sums, seq_index, 1)[0, : 2 * micros : 2].reshape(micros * rows, 1)
    output = flat_hidden + branch.astype(F32) * lax.rsqrt(squares / active + EPSILON)

    dproj, gnorm, gconv, gcols, ghead = run_backward(
        micros,
        heads,
        rows,
        seq_total,
        starts[0],
        active[None],
        proj,
        dnorm,
        mixed,
        states,
        tails,
        sums,
        taps,
        head_table,
        cols,
        expand,
        gather,
        tri,
    )
    grad_normed = lax.psum_scatter(
        mm_nt(dproj, columns).astype(BF16), "seq", scatter_dimension=0, tiled=True
    ).astype(F32)
    grad_hidden, grad_gain_in = norm_back(grad_normed)
    hidden_grads = (flat_grad.astype(F32) + grad_hidden).astype(BF16)

    grad_out = mm_tn(gnorm, all_grad).astype(BF16)
    grad_out = grad_out.reshape(width, seq_total, model_width // seq_total).transpose(1, 0, 2)
    grad_out = lax.all_to_all(grad_out, "seq", split_axis=0, concat_axis=0)
    grad_out = grad_out.reshape(seq_total * width, model_width // seq_total)
    shard_out = lax.psum_scatter(
        grad_out.astype(F32), "width", scatter_dimension=0, tiled=True
    )

    grad_in = mm_tn(all_normed, dproj).astype(BF16)[:, : conv_width + width + heads]
    grad_in = grad_in.reshape(seq_total, depth, grad_in.shape[1])
    grad_in = lax.all_to_all(grad_in, "seq", split_axis=0, concat_axis=0)
    grad_in = grad_in.astype(F32)

    def joined(value):
        return value.transpose(1, 0, 2).reshape(depth, seq_total * value.shape[2])

    grad_in = jnp.concatenate(
        [
            joined(grad_in[:, :, conv_width : conv_width + width]),
            joined(grad_in[:, :, 2 * STATE : conv_width]),
            jnp.sum(grad_in[:, :, : 2 * STATE], axis=0),
            joined(grad_in[:, :, conv_width + width :]),
        ],
        axis=1,
    )
    shard_in = lax.psum_scatter(grad_in, "width", scatter_dimension=1, tiled=True)

    skip_heads = jnp.sum(gcols[0].reshape(heads, HEAD_DIM), axis=1)
    conv_small = jnp.concatenate(
        [placed(gconv[:5, 2 * STATE :], INNER, col_first), gconv[:5, : 2 * STATE]], axis=1
    )
    small = jnp.concatenate(
        [
            conv_small.reshape(-1),
            grad_gain_in,
            placed(gcols[1], INNER, col_first),
            placed(ghead[1, :heads], HEADS, head_first),
            placed(ghead[0, :heads], HEADS, head_first),
            placed(skip_heads, HEADS, head_first),
        ]
    )
    small = lax.psum(small, ("width", "seq"))
    edge = 5 * CONV
    conv_small = small[:edge].reshape(5, CONV)
    in_gain_sum = small[edge : edge + model_width]
    edge = edge + model_width
    gain_sum = small[edge : edge + INNER]
    edge = edge + INNER
    shape = hidden_in.shape
    return (
        output.astype(BF16).reshape(shape),
        hidden_grads.reshape(shape),
        in_gain_sum,
        shard_in,
        conv_small[:4],
        conv_small[4],
        small[edge : edge + HEADS],
        small[edge + HEADS : edge + 2 * HEADS],
        small[edge + 2 * HEADS : edge + 3 * HEADS],
        gain_sum,
        shard_out,
    )


def solution(mesh):
    in_specs = (
        P("width", None, "seq", None),
        P("width", None, None),
        P(),
        P("seq", None),
        P(),
        P(),
        P(),
        P(),
        P(),
        P(),
        P("seq", None),
        P("width", None, "seq", None),
    )
    out_specs = (
        P("width", None, "seq", None),
        P("width", None, "seq", None),
        P(),
        P("seq", "width"),
        P(),
        P(),
        P(),
        P(),
        P(),
        P(),
        P("width", "seq"),
    )
    return jax.shard_map(
        per_device, mesh=mesh, in_specs=in_specs, out_specs=out_specs, check_vma=False
    )
```

```python
from functools import partial

import jax
import jax.numpy as jnp
from jax import lax
from jax.experimental import pallas as pl
from jax.experimental.pallas import tpu as pltpu
from jax.sharding import PartitionSpec as P

INNER = 4096
HEADS = 64
HEAD_DIM = 64
STATE = 128
CONV = 4352
EPSILON = 1e-05
LANES = 128
TAPS = 4
NEG = -1e30
F32 = jnp.float32
BF16 = jnp.bfloat16


def mm(a, b):
    return lax.dot_general(a, b, (((1,), (0,)), ((), ())), preferred_element_type=F32)


def mm_nt(a, b):
    return lax.dot_general(a, b, (((1,), (1,)), ((), ())), preferred_element_type=F32)


def mm_tn(a, b):
    return lax.dot_general(a, b, (((0,), (0,)), ((), ())), preferred_element_type=F32)


def halves(value, axis):
    high = value.astype(BF16)
    low = (value - high.astype(F32)).astype(BF16)
    return jnp.concatenate([high, low], axis=axis)


def sigmoid(value):
    return 0.5 * jnp.tanh(0.5 * value) + 0.5


def prefix_sum(tri, value):
    high = value.astype(BF16)
    rest = value - high.astype(F32)
    middle = rest.astype(BF16)
    low = (rest - middle.astype(F32)).astype(BF16)
    parts = mm(tri, jnp.concatenate([high, middle, low], axis=1))
    width = value.shape[1]
    return parts[:, :width] + parts[:, width : 2 * width] + parts[:, 2 * width :]


def doc_number(starts_ref, micro, positions):
    count = jnp.zeros_like(positions)
    for item in range(starts_ref.shape[1]):
        count = count + (starts_ref[micro, item] <= positions).astype(jnp.int32)
    return count


class Chunk:
    def __init__(self, starts_ref, micro, chunk, rows, raw_dt, head_ref, expand, tri):
        first = chunk * rows
        column = lax.broadcasted_iota(jnp.int32, (rows, 1), 0) + first
        line = lax.broadcasted_iota(jnp.int32, (1, rows), 1) + first
        doc_col = doc_number(starts_ref, micro, column)
        doc_row = doc_number(starts_ref, micro, line)
        self.same = [
            (doc_number(starts_ref, micro, column - offset) == doc_col).astype(F32)
            for offset in range(1, TAPS)
        ]
        before = jnp.int32(0)
        last = jnp.int32(0)
        for item in range(starts_ref.shape[1]):
            before = before + (starts_ref[micro, item] <= first - 1).astype(jnp.int32)
            last = last + (starts_ref[micro, item] <= first + rows - 1).astype(jnp.int32)
        carry = (doc_col == before).astype(F32)
        same_last = (doc_col == last).astype(F32)
        self.bias = jnp.where((column >= line) & (doc_col == doc_row), 0.0, NEG)
        self.shifted_dt = raw_dt + head_ref[0:1]
        self.step = jnp.maximum(self.shifted_dt, 0.0) + jnp.log1p(
            jnp.exp(-jnp.abs(self.shifted_dt))
        )
        self.log_keep = self.step * head_ref[1:2]
        self.cum = prefix_sum(tri, self.log_keep)
        self.cum_t = self.cum.T
        carried = jnp.exp(self.cum) * carry
        left = jnp.exp(self.cum[rows - 1 :] - self.cum) * same_last
        spread = mm(
            halves(jnp.concatenate([self.step, carried, left], axis=0), 1), expand
        )
        self.step_cols = spread[:rows]
        self.carry_cols = spread[rows : 2 * rows]
        self.left_cols = spread[2 * rows :]
        self.keep_all = self.carry_cols[rows - 1 :]

    def decay(self, head):
        return jnp.exp(self.cum[:, head : head + 1] - self.cum_t[head : head + 1] + self.bias)


def head_groups(heads):
    size = 2 if heads % 2 == 0 else 1
    return size, heads // size


def stacked(value, size):
    if size == 1:
        return value.astype(BF16)
    lane = lax.broadcasted_iota(jnp.int32, value.shape, 1)
    first = jnp.where(lane < HEAD_DIM, value, 0.0)
    second = jnp.where(lane < HEAD_DIM, 0.0, value)
    return jnp.concatenate([first, second], axis=0).astype(BF16)


def convolved(ext, micro, rows, taps_ref, same):
    current = ext[micro, 8 : 8 + rows, :]
    total = taps_ref[TAPS : TAPS + 1] + taps_ref[TAPS - 1 : TAPS] * current
    views = []
    for offset in range(1, TAPS):
        view = ext[micro, 8 - offset : 8 - offset + rows, :] * same[offset - 1]
        views.append(view)
        total = total + taps_ref[TAPS - 1 - offset : TAPS - offset] * view
    return current, views, total


def forward_kernel(
    micros,
    heads,
    starts_ref,
    proj_ref,
    dnorm_ref,
    taps_ref,
    head_ref,
    cols_ref,
    expand_ref,
    tri_ref,
    gg_ref,
    mixed_ref,
    states_ref,
    tails_ref,
    sums_ref,
    ext,
    state,
):
    chunk = pl.program_id(0)
    rows = proj_ref.shape[0] // micros
    width = heads * HEAD_DIM
    conv_width = 2 * STATE + width
    size, groups = head_groups(heads)

    @pl.when(chunk == 0)
    def _():
        ext[:, :8, :] = jnp.zeros((micros, 8, conv_width), F32)
        state[...] = jnp.zeros_like(state)

    skip, gain, mask = cols_ref[0:1], cols_ref[1:2], cols_ref[2:3]
    sums = []
    for micro in range(micros):
        part = slice(micro * rows, (micro + 1) * rows)
        tails_ref[micro] = ext[micro, :8, :]
        ext[micro, 8 : 8 + rows, :] = proj_ref[part, :conv_width].astype(F32)
        raw_dt = proj_ref[part, conv_width + width :].astype(F32)
        at = Chunk(
            starts_ref, micro, chunk, rows, raw_dt, head_ref, expand_ref[...], tri_ref[...]
        )
        conv = convolved(ext, micro, rows, taps_ref, at.same)[2]
        act = conv * sigmoid(conv)
        write = act[:, :STATE].astype(BF16)
        read = act[:, STATE : 2 * STATE].astype(BF16)
        x_heads = act[:, 2 * STATE :]
        scores = mm_nt(read, write)
        inputs = x_heads * at.step_cols
        state_in = state[micro]
        state_low = state_in.astype(BF16)
        states_ref[micro] = state_low
        outs = []
        for group in range(groups):
            matrices = [
                (at.decay(group * size + item) * scores).astype(BF16) for item in range(size)
            ]
            span = slice(group * size * HEAD_DIM, (group + 1) * size * HEAD_DIM)
            outs.append(mm(jnp.concatenate(matrices, axis=1), stacked(inputs[:, span], size)))
        mixed = jnp.concatenate(outs, axis=1) + at.carry_cols * mm(read, state_low)
        state[micro] = at.keep_all * state_in + mm_tn(
            write, (inputs * at.left_cols).astype(BF16)
        )
        mixed = mixed + skip * x_heads
        mixed_ref[part, :] = mixed
        gate = proj_ref[part, conv_width : conv_width + width].astype(F32)
        gated = mask * mixed * (gate * sigmoid(gate))
        gg_ref[part, :] = (gated * gain).astype(BF16)
        square = jnp.sum(gated * gated, axis=1, keepdims=True)
        cross = jnp.sum(dnorm_ref[part, :] * gain * gated, axis=1, keepdims=True)
        lane = lax.broadcasted_iota(jnp.int32, (rows, LANES), 1)
        both = jnp.where(lane == 0, square, jnp.where(lane == 1, cross, 0.0))
        sums.append(both.T[:2])
        ext[micro, :8, :] = ext[micro, rows : rows + 8, :]
    pad = sums_ref.shape[0] - 2 * micros
    if pad:
        sums.append(jnp.zeros((pad, rows), F32))
    sums_ref[...] = jnp.concatenate(sums, axis=0)


def backward_kernel(
    micros,
    heads,
    starts_ref,
    active_ref,
    proj_ref,
    dnorm_ref,
    mixed_ref,
    states_ref,
    tails_ref,
    sums_ref,
    taps_ref,
    head_ref,
    cols_ref,
    expand_ref,
    gather_ref,
    tri_ref,
    dproj_ref,
    gnorm_ref,
    gconv_ref,
    gcols_ref,
    ghead_ref,
    ext,
    heads_ext,
    dstate,
):
    chunks = pl.num_programs(0)
    step_index = pl.program_id(0)
    chunk = chunks - 1 - step_index
    rows = proj_ref.shape[0] // micros
    width = heads * HEAD_DIM
    conv_width = 2 * STATE + width
    size, groups = head_groups(heads)

    @pl.when(step_index == 0)
    def _():
        heads_ext[:, :, rows:, :] = jnp.zeros((micros, TAPS - 1, 8, conv_width), F32)
        dstate[...] = jnp.zeros_like(dstate)
        gconv_ref[...] = jnp.zeros_like(gconv_ref)
        gcols_ref[...] = jnp.zeros_like(gcols_ref)
        ghead_ref[...] = jnp.zeros_like(ghead_ref)

    skip, gain, mask = cols_ref[0:1], cols_ref[1:2], cols_ref[2:3]
    tri = tri_ref[...]
    gather = gather_ref[...]
    inverse_active = 1.0 / active_ref[0]
    sums = jnp.concatenate(
        [sums_ref[...], jnp.zeros((LANES - sums_ref.shape[0], rows), F32)], axis=0
    ).T
    for micro in range(micros):
        part = slice(micro * rows, (micro + 1) * rows)
        ext[micro, :8, :] = tails_ref[micro]
        ext[micro, 8 : 8 + rows, :] = proj_ref[part, :conv_width].astype(F32)
        raw_dt = proj_ref[part, conv_width + width :].astype(F32)
        at = Chunk(starts_ref, micro, chunk, rows, raw_dt, head_ref, expand_ref[...], tri)
        current, views, conv = convolved(ext, micro, rows, taps_ref, at.same)
        conv_sig = sigmoid(conv)
        act = conv * conv_sig
        write = act[:, :STATE].astype(BF16)
        read = act[:, STATE : 2 * STATE].astype(BF16)
        x_heads = act[:, 2 * STATE :]
        scores = mm_nt(read, write)
        inputs = x_heads * at.step_cols

        gate = proj_ref[part, conv_width : conv_width + width].astype(F32)
        gate_sig = sigmoid(gate)
        gate_act = gate * gate_sig
        masked = mask * mixed_ref[part, :]
        gated = masked * gate_act
        root = lax.rsqrt(sums[:, 2 * micro : 2 * micro + 1] * inverse_active + EPSILON)
        pull = root * root * root * sums[:, 2 * micro + 1 : 2 * micro + 2] * inverse_active
        dnorm = dnorm_ref[part, :]
        scaled = gated * root
        gnorm_ref[part, :] = (scaled * gain).astype(BF16)
        d_gated = root * dnorm * gain - gated * pull
        d_gate = d_gated * masked * (gate_sig * (1.0 + gate * (1.0 - gate_sig)))
        d_mixed = mask * d_gated * gate_act
        gcols_ref[0:1] += jnp.sum(d_mixed * x_heads, axis=0, keepdims=True)
        gcols_ref[1:2] += jnp.sum(dnorm * scaled, axis=0, keepdims=True)

        state_low = states_ref[micro]
        d_state = dstate[micro]
        d_state_low = d_state.astype(BF16)
        from_state = (d_mixed * at.carry_cols).astype(BF16)
        left = inputs * at.left_cols
        left_low = left.astype(BF16)
        d_left = mm(write, d_state_low)
        state_out = mm(read, state_low)
        d_read = mm_nt(from_state, state_low)
        d_write = mm_nt(left_low, d_state_low)
        d_mixed_low = d_mixed.astype(BF16).astype(F32)
        inputs_low = inputs.astype(BF16).astype(F32)
        d_scores = jnp.zeros((rows, rows), F32)
        locals_out, d_locals = [], []
        for group in range(groups):
            span = slice(group * size * HEAD_DIM, (group + 1) * size * HEAD_DIM)
            decays = [at.decay(group * size + item) for item in range(size)]
            matrices = [(decay * scores).astype(BF16) for decay in decays]
            in_stack = stacked(inputs[:, span], size)
            out_stack = stacked(d_mixed[:, span], size)
            locals_out.append(mm(jnp.concatenate(matrices, axis=1), in_stack))
            d_locals.append(mm_tn(jnp.concatenate(matrices, axis=0), out_stack))
            d_matrices = mm_nt(out_stack, inputs[:, span].astype(BF16))
            for item in range(size):
                d_scores = (
                    d_scores + d_matrices[item * rows : (item + 1) * rows] * decays[item]
                )
        local_out = jnp.concatenate(locals_out, axis=1)
        d_local = jnp.concatenate(d_locals, axis=1)
        d_scores_low = d_scores.astype(BF16)
        d_read = d_read + mm(d_scores_low, write)
        d_write = d_write + mm_tn(d_scores_low, read)
        d_inputs = d_local + at.left_cols * d_left
        d_x = skip * d_mixed + d_inputs * at.step_cols

        passed = left * d_left
        cum_terms = (
            d_mixed_low * local_out
            + d_mixed * at.carry_cols * state_out
            - inputs_low * d_local
            - passed
        )
        kept = jnp.sum(d_state * at.keep_all * state_low.astype(F32), axis=0, keepdims=True)
        final = jnp.sum(passed, axis=0, keepdims=True) + kept
        stack = jnp.concatenate(
            [cum_terms, d_inputs * x_heads, jnp.broadcast_to(final, (8, width))], axis=0
        )
        reduced = mm(halves(stack, 1), gather)
        d_cum = reduced[:rows]
        d_step = reduced[rows : 2 * rows]
        final_row = reduced[2 * rows : 2 * rows + 1]
        total = jnp.sum(d_cum, axis=0, keepdims=True) + final_row
        d_log = total - prefix_sum(tri, d_cum) + d_cum
        d_step = d_step + d_log * head_ref[1:2]
        d_dt = d_step * sigmoid(at.shifted_dt)
        ghead_ref[0:1] += jnp.sum(d_log * at.log_keep, axis=0, keepdims=True)
        ghead_ref[1:2] += jnp.sum(d_dt, axis=0, keepdims=True)
        dstate[micro] = at.keep_all * d_state + mm_tn(read, from_state)

        d_conv = jnp.concatenate([d_write, d_read, d_x], axis=1) * (
            conv_sig * (1.0 + conv * (1.0 - conv_sig))
        )
        gconv_ref[TAPS : TAPS + 1] += jnp.sum(d_conv, axis=0, keepdims=True)
        gconv_ref[TAPS - 1 : TAPS] += jnp.sum(d_conv * current, axis=0, keepdims=True)
        d_raw = taps_ref[TAPS - 1 : TAPS] * d_conv
        for offset in range(1, TAPS):
            tap = TAPS - 1 - offset
            gconv_ref[tap : tap + 1] += jnp.sum(
                d_conv * views[offset - 1], axis=0, keepdims=True
            )
            heads_ext[micro, offset - 1, :rows, :] = d_conv * at.same[offset - 1]
            d_raw = d_raw + taps_ref[tap : tap + 1] * (
                heads_ext[micro, offset - 1, offset : offset + rows, :]
            )
            heads_ext[micro, offset - 1, rows:, :] = heads_ext[micro, offset - 1, :8, :]
        dproj_ref[part, :conv_width] = d_raw.astype(BF16)
        dproj_ref[part, conv_width : conv_width + width] = d_gate.astype(BF16)
        dproj_ref[part, conv_width + width :] = d_dt.astype(BF16)


def constant(shape):
    return pl.BlockSpec(shape, lambda index: (0,) * len(shape))


def run_forward(micros, heads, rows, chunks, starts, proj, dnorm, taps, head, cols, expand, tri):
    width = heads * HEAD_DIM
    conv_width = 2 * STATE + width
    block = micros * rows
    sum_rows = -(-2 * micros // 8) * 8
    return pl.pallas_call(
        partial(forward_kernel, micros, heads),
        grid=(chunks,),
        in_specs=[
            pl.BlockSpec(memory_space=pltpu.SMEM),
            pl.BlockSpec((block, proj.shape[1]), lambda index: (index, 0)),
            pl.BlockSpec((block, width), lambda index: (index, 0)),
            constant(taps.shape),
            constant(head.shape),
            constant(cols.shape),
            constant(expand.shape),
            constant(tri.shape),
        ],
        out_specs=[
            pl.BlockSpec((block, width), lambda index: (index, 0)),
            pl.BlockSpec((block, width), lambda index: (index, 0)),
            pl.BlockSpec((None, micros, STATE, width), lambda index: (index, 0, 0, 0)),
            pl.BlockSpec((None, micros, 8, conv_width), lambda index: (index, 0, 0, 0)),
            pl.BlockSpec((None, sum_rows, rows), lambda index: (index, 0, 0)),
        ],
        out_shape=[
            jax.ShapeDtypeStruct((chunks * block, width), BF16),
            jax.ShapeDtypeStruct((chunks * block, width), F32),
            jax.ShapeDtypeStruct((chunks, micros, STATE, width), BF16),
            jax.ShapeDtypeStruct((chunks, micros, 8, conv_width), F32),
            jax.ShapeDtypeStruct((chunks, sum_rows, rows), F32),
        ],
        scratch_shapes=[
            pltpu.VMEM((micros, rows + 8, conv_width), F32),
            pltpu.VMEM((micros, STATE, width), F32),
        ],
        compiler_params=pltpu.CompilerParams(vmem_limit_bytes=48 << 20),
        name="mixer_forward",
    )(starts, proj, dnorm, taps, head, cols, expand, tri)


def run_backward(
    micros,
    heads,
    rows,
    chunks,
    starts,
    active,
    proj,
    dnorm,
    mixed,
    states,
    tails,
    sums,
    taps,
    head,
    cols,
    expand,
    gather,
    tri,
):
    width = heads * HEAD_DIM
    conv_width = 2 * STATE + width
    block = micros * rows

    def back(index):
        return (chunks - 1 - index, 0)

    return pl.pallas_call(
        partial(backward_kernel, micros, heads),
        grid=(chunks,),
        in_specs=[
            pl.BlockSpec(memory_space=pltpu.SMEM),
            pl.BlockSpec(memory_space=pltpu.SMEM),
            pl.BlockSpec((block, proj.shape[1]), back),
            pl.BlockSpec((block, width), back),
            pl.BlockSpec((block, width), back),
            pl.BlockSpec(
                (None, micros, STATE, width), lambda index: (chunks - 1 - index, 0, 0, 0)
            ),
            pl.BlockSpec(
                (None, micros, 8, conv_width), lambda index: (chunks - 1 - index, 0, 0, 0)
            ),
            pl.BlockSpec((None, sums.shape[1], rows), lambda index: (chunks - 1 - index, 0, 0)),
            constant(taps.shape),
            constant(head.shape),
            constant(cols.shape),
            constant(expand.shape),
            constant(gather.shape),
            constant(tri.shape),
        ],
        out_specs=[
            pl.BlockSpec((block, proj.shape[1]), back),
            pl.BlockSpec((block, width), back),
            constant((8, conv_width)),
            constant((8, width)),
            constant((8, LANES)),
        ],
        out_shape=[
            jax.ShapeDtypeStruct((chunks * block, proj.shape[1]), BF16),
            jax.ShapeDtypeStruct((chunks * block, width), BF16),
            jax.ShapeDtypeStruct((8, conv_width), F32),
            jax.ShapeDtypeStruct((8, width), F32),
            jax.ShapeDtypeStruct((8, LANES), F32),
        ],
        scratch_shapes=[
            pltpu.VMEM((micros, rows + 8, conv_width), F32),
            pltpu.VMEM((micros, TAPS - 1, rows + 8, conv_width), F32),
            pltpu.VMEM((micros, STATE, width), F32),
        ],
        compiler_params=pltpu.CompilerParams(vmem_limit_bytes=48 << 20),
        name="mixer_backward",
    )(
        starts,
        active,
        proj,
        dnorm,
        mixed,
        states,
        tails,
        sums,
        taps,
        head,
        cols,
        expand,
        gather,
        tri,
    )


def tables(heads, rows):
    width = heads * HEAD_DIM
    expand = (
        jnp.arange(LANES)[:, None] == jnp.arange(width)[None, :] // HEAD_DIM
    ).astype(BF16)
    tri = (jnp.arange(rows)[:, None] >= jnp.arange(rows)[None, :]).astype(BF16)
    return (
        jnp.concatenate([expand, expand], axis=0),
        jnp.concatenate([expand.T, expand.T], axis=0),
        tri,
    )

MESH = pl.DeviceIdType.MESH
ANY = pl.BlockSpec(memory_space=pl.ANY)


def greet(axes):
    barrier = pltpu.get_barrier_semaphore()
    waits = 0
    for axis in axes:
        count, me = lax.axis_size(axis), lax.axis_index(axis)

        def hello(turn, carry):
            pl.semaphore_signal(
                barrier,
                inc=1,
                device_id={axis: lax.rem(me + turn, count)},
                device_id_type=MESH,
            )
            return carry

        lax.fori_loop(1, count, hello, 0)
        waits += count - 1
    pl.semaphore_wait(barrier, waits)


def remote(source, target, send, receive, device):
    return pltpu.make_async_remote_copy(
        src_ref=source,
        dst_ref=target,
        send_sem=send,
        recv_sem=receive,
        device_id=device,
        device_id_type=MESH,
    )


def exchange_kernel(axis, total, *refs):
    ins, outs = refs[:total], refs[total : 2 * total]
    send, receive, keep = refs[2 * total :]
    count, me = lax.axis_size(axis), lax.axis_index(axis)
    greet((axis,))

    def copy(item, turn, slot):
        peer = lax.rem(me + turn, count)
        owner = me if slot is None else slot
        return remote(
            ins[item].at[peer],
            outs[item].at[owner],
            send.at[item, peer],
            receive.at[item, owner],
            {axis: peer},
        )

    def start(turn, carry):
        for item in range(total):
            copy(item, turn, None).start()
        return carry

    def finish(turn, carry):
        for item in range(total):
            copy(item, turn, None).wait_send()
            copy(item, turn, lax.rem(me + turn, count)).wait_recv()
        return carry

    lax.fori_loop(1, count, start, 0)
    stays = [
        pltpu.make_async_copy(ins[item].at[me], outs[item].at[me], keep.at[item])
        for item in range(total)
    ]
    for stay in stays:
        stay.start()
    lax.fori_loop(1, count, finish, 0)
    for stay in stays:
        stay.wait()


def exchange(arrays, axis, collective_id):
    total, count = len(arrays), arrays[0].shape[0]
    return pl.pallas_call(
        partial(exchange_kernel, axis, total),
        in_specs=[ANY] * total,
        out_specs=[ANY] * total,
        out_shape=[jax.ShapeDtypeStruct(item.shape, item.dtype) for item in arrays],
        scratch_shapes=[
            pltpu.SemaphoreType.DMA((total, count)),
            pltpu.SemaphoreType.DMA((total, count)),
            pltpu.SemaphoreType.DMA((total,)),
        ],
        compiler_params=pltpu.CompilerParams(
            collective_id=collective_id, has_side_effects=True
        ),
        name="exchange_" + axis,
    )(*arrays)


def share_kernel(axis, in_ref, out_ref, slots, send, receive):
    count, me = lax.axis_size(axis), lax.axis_index(axis)
    greet((axis,))

    def copy(turn, owner):
        peer = lax.rem(me + turn, count)
        return remote(in_ref, slots.at[owner], send.at[peer], receive.at[owner], {axis: peer})

    def start(turn, carry):
        copy(turn, me).start()
        return carry

    def finish(turn, carry):
        copy(turn, me).wait_send()
        copy(turn, lax.rem(me + turn, count)).wait_recv()
        return carry

    lax.fori_loop(1, count, start, 0)
    slots[me] = in_ref[...]
    lax.fori_loop(1, count, finish, 0)

    def add(owner, total):
        return total + slots[owner]

    out_ref[...] = lax.fori_loop(1, count, add, slots[0])


def share(value, axis, collective_id):
    count = lax.axis_size(axis)
    return pl.pallas_call(
        partial(share_kernel, axis),
        in_specs=[pl.BlockSpec(memory_space=pltpu.VMEM)],
        out_specs=pl.BlockSpec(memory_space=pltpu.VMEM),
        out_shape=jax.ShapeDtypeStruct(value.shape, value.dtype),
        scratch_shapes=[
            pltpu.VMEM((count,) + value.shape, value.dtype),
            pltpu.SemaphoreType.DMA((count,)),
            pltpu.SemaphoreType.DMA((count,)),
        ],
        compiler_params=pltpu.CompilerParams(
            collective_id=collective_id, has_side_effects=True, vmem_limit_bytes=48 << 20
        ),
        name="share_" + axis,
    )(value)


def total_kernel(in_ref, out_ref, slots, sent, send, receive, send_back, receive_back):
    seq_total, width_total = lax.axis_size("seq"), lax.axis_size("width")
    count = seq_total * width_total
    me = lax.axis_index("width") * seq_total + lax.axis_index("seq")
    barrier = pltpu.get_barrier_semaphore()

    def device(turn):
        peer = lax.rem(me + turn, count)
        return peer, {"width": peer // seq_total, "seq": lax.rem(peer, seq_total)}

    def hello(turn, carry):
        pl.semaphore_signal(barrier, inc=1, device_id=device(turn)[1], device_id_type=MESH)
        return carry

    lax.fori_loop(1, count, hello, 0)
    pl.semaphore_wait(barrier, count - 1)

    def first(turn, from_peer):
        peer, where = device(turn)
        owner = peer if from_peer else me
        return remote(
            in_ref.at[peer], slots.at[owner], send.at[peer], receive.at[owner], where
        )

    def second(turn, from_peer):
        peer, where = device(turn)
        owner = peer if from_peer else me
        return remote(
            sent, out_ref.at[owner], send_back.at[peer], receive_back.at[owner], where
        )

    def loop(make, action):
        def body(turn, carry):
            action(make, turn)
            return carry

        lax.fori_loop(1, count, body, 0)

    def start(make, turn):
        make(turn, False).start()

    def finish(make, turn):
        make(turn, False).wait_send()
        make(turn, True).wait_recv()

    loop(first, start)
    slots[me] = in_ref[me]
    loop(first, finish)

    def add(owner, total):
        return total + slots[owner]

    sent[...] = lax.fori_loop(1, count, add, slots[0])
    loop(second, start)
    out_ref[me] = sent[...]
    loop(second, finish)


def total_over_all(vector, collective_id):
    count = lax.axis_size("seq") * lax.axis_size("width")
    length = vector.shape[0]
    tiles = -(-length // (count * 8 * LANES))
    padded = jnp.pad(vector, (0, count * tiles * 8 * LANES - length))
    shape = (count, tiles * 8, LANES)
    summed = pl.pallas_call(
        total_kernel,
        in_specs=[pl.BlockSpec(memory_space=pltpu.VMEM)],
        out_specs=pl.BlockSpec(memory_space=pltpu.VMEM),
        out_shape=jax.ShapeDtypeStruct(shape, F32),
        scratch_shapes=[
            pltpu.VMEM(shape, F32),
            pltpu.VMEM(shape[1:], F32),
            pltpu.SemaphoreType.DMA((count,)),
            pltpu.SemaphoreType.DMA((count,)),
            pltpu.SemaphoreType.DMA((count,)),
            pltpu.SemaphoreType.DMA((count,)),
        ],
        compiler_params=pltpu.CompilerParams(
            collective_id=collective_id, has_side_effects=True, vmem_limit_bytes=16 << 20
        ),
        name="total_over_all",
    )(padded.reshape(shape))
    return summed.reshape(-1)[:length]


PARTS = 2


def gather_kernel(
    x_ref,
    g_ref,
    w_ref,
    x_out,
    g_out,
    w_out,
    w_send,
    w_receive,
    f_send,
    f_receive,
    up_send,
    down_send,
    line_receive,
    side_send,
    side_receive,
    keep,
):
    seq_total, width_total = lax.axis_size("seq"), lax.axis_size("width")
    me, mine = lax.axis_index("seq"), lax.axis_index("width")
    chips, chip, core = seq_total // 2, me // 2, lax.rem(me, 2)
    sibling = me + 1 - 2 * core
    quarter = w_ref.shape[1]
    depth = quarter * width_total
    block = x_ref.shape[0]
    piece = block // PARTS
    greet(("seq", "width"))

    def rows(source, group):
        return pl.ds(pl.multiple_of(source * depth + group * quarter, 8), quarter)

    def deal(turn, from_peer):
        peer = lax.rem(me + turn, seq_total)
        owner = peer if from_peer else me
        return remote(
            w_ref.at[peer],
            w_out.at[rows(owner, mine)],
            w_send.at[peer],
            w_receive.at[owner],
            {"seq": peer},
        )

    def deal_start(turn, carry):
        deal(turn, False).start()
        return carry

    lax.fori_loop(1, seq_total, deal_start, 0)
    w_own = pltpu.make_async_copy(w_ref.at[me], w_out.at[rows(me, mine)], keep.at[0])
    w_own.start()
    x_own = pltpu.make_async_copy(x_ref, x_out.at[pl.ds(me * block, block)], keep.at[1])
    g_own = pltpu.make_async_copy(g_ref, g_out.at[pl.ds(me * block, block)], keep.at[2])
    x_own.start()
    g_own.start()

    def at(out, owner, part):
        return out.at[pl.ds(pl.multiple_of(owner * block + part * piece, 8), piece)]

    def line(item, out, source, owner_chip, part, target_chip, sems):
        owner = owner_chip * 2 + core
        return remote(
            source,
            at(out, owner, part),
            sems.at[item, owner_chip, part],
            line_receive.at[item, owner_chip, part],
            {"seq": target_chip * 2 + core},
        )

    def side(item, out, source, owner_chip, part, from_sibling):
        owner = owner_chip * 2 + (1 - core if from_sibling else core)
        return remote(
            source,
            at(out, owner, part),
            side_send.at[item, owner_chip, part],
            side_receive.at[item, owner_chip, part],
            {"seq": sibling},
        )

    pairs = ((x_ref, x_out), (g_ref, g_out))

    def own_start(item):
        source, out = pairs[item]
        for part in range(PARTS):
            here = source.at[pl.ds(part * piece, piece)]

            @pl.when(chip + 1 < chips)
            def _():
                line(item, out, here, chip, part, chip + 1, up_send).start()

            @pl.when(chip >= 1)
            def _():
                line(item, out, here, chip, part, chip - 1, down_send).start()

            side(item, out, here, chip, part, False).start()

    def pass_on(item):
        out = pairs[item][1]

        def hop(turn, carry):
            below, above = chip - turn, chip + turn
            for part in range(PARTS):

                @pl.when(below >= 0)
                def _():
                    here = at(out, below * 2 + core, part)
                    line(item, out, here, below, part, chip, up_send).wait_recv()

                    @pl.when(chip + 1 < chips)
                    def _():
                        line(item, out, here, below, part, chip + 1, up_send).start()

                    side(item, out, here, below, part, False).start()

                @pl.when(above < chips)
                def _():
                    here = at(out, above * 2 + core, part)
                    line(item, out, here, above, part, chip, down_send).wait_recv()

                    @pl.when(chip >= 1)
                    def _():
                        line(item, out, here, above, part, chip - 1, down_send).start()

                    side(item, out, here, above, part, False).start()

            return carry

        lax.fori_loop(1, chips, hop, 0)

    def forward(source, turn, from_peer):
        peer = lax.rem(mine + turn, width_total)
        group = peer if from_peer else mine
        where = w_out.at[rows(source, group)]
        return remote(
            where, where, f_send.at[peer, source], f_receive.at[group, source], {"width": peer}
        )

    def forward_start(source):
        for turn in range(1, width_total):
            forward(source, turn, False).start()

    def deal_pass(turn, carry):
        deal(turn, True).wait_recv()
        forward_start(lax.rem(me + turn, seq_total))
        return carry

    own_start(0)
    w_own.wait()
    forward_start(me)
    lax.fori_loop(1, seq_total, deal_pass, 0)
    pass_on(0)
    own_start(1)
    pass_on(1)

    def deal_end(turn, carry):
        deal(turn, False).wait_send()
        return carry

    lax.fori_loop(1, seq_total, deal_end, 0)

    def forward_end(source, carry):
        for turn in range(1, width_total):
            forward(source, turn, False).wait_send()
            forward(source, turn, True).wait_recv()
        return carry

    lax.fori_loop(0, seq_total, forward_end, 0)
    for item in range(2):
        out = pairs[item][1]

        def line_end(owner_chip, carry):
            for part in range(PARTS):
                here = at(out, owner_chip * 2 + core, part)

                @pl.when((owner_chip <= chip) & (chip + 1 < chips))
                def _():
                    line(item, out, here, owner_chip, part, chip + 1, up_send).wait_send()

                @pl.when((owner_chip >= chip) & (chip >= 1))
                def _():
                    line(item, out, here, owner_chip, part, chip - 1, down_send).wait_send()

                side(item, out, here, owner_chip, part, False).wait_send()
                side(item, out, here, owner_chip, part, True).wait_recv()
            return carry

        lax.fori_loop(0, chips, line_end, 0)
    x_own.wait()
    g_own.wait()


def gather_rows(x, g, pieces, collective_id):
    seq_total, width_total = lax.axis_size("seq"), lax.axis_size("width")
    chips = seq_total // 2
    whole = (x.shape[0] * seq_total, x.shape[1])
    weight = (seq_total * width_total * pieces.shape[1], pieces.shape[2])
    dma = pltpu.SemaphoreType.DMA
    return pl.pallas_call(
        gather_kernel,
        in_specs=[ANY] * 3,
        out_specs=[ANY] * 3,
        out_shape=[
            jax.ShapeDtypeStruct(whole, x.dtype),
            jax.ShapeDtypeStruct(whole, g.dtype),
            jax.ShapeDtypeStruct(weight, pieces.dtype),
        ],
        scratch_shapes=[
            dma((seq_total,)),
            dma((seq_total,)),
            dma((width_total, seq_total)),
            dma((width_total, seq_total)),
            dma((2, chips, PARTS)),
            dma((2, chips, PARTS)),
            dma((2, chips, PARTS)),
            dma((2, chips, PARTS)),
            dma((2, chips, PARTS)),
            dma((3,)),
        ],
        compiler_params=pltpu.CompilerParams(
            collective_id=collective_id, has_side_effects=True
        ),
        name="gather_rows",
    )(x, g, pieces)


def input_norm(hidden, in_gain):
    return hidden * lax.rsqrt(jnp.mean(hidden * hidden, axis=1, keepdims=True) + EPSILON) * in_gain


def own(value, start, count, axis=0):
    return lax.dynamic_slice_in_dim(value, start, count, axis)


def placed(value, total, start):
    whole = jnp.zeros(value.shape[:-1] + (total,), F32)
    return lax.dynamic_update_slice_in_dim(whole, value, start, value.ndim - 1)


def per_device(
    hidden_in,
    starts,
    in_gain,
    in_weight,
    conv_weight,
    conv_bias,
    step_bias,
    decay_log,
    skip_gain,
    gate_gain,
    out_weight,
    cotangent,
):
    seq_total = lax.axis_size("seq")
    seq_index = lax.axis_index("seq")
    group_index = lax.axis_index("width")
    micros, rows, model_width = hidden_in.shape[1:]
    heads = HEADS // seq_total
    width = heads * HEAD_DIM
    head_first = seq_index * heads
    col_first = seq_index * width
    depth = in_weight.shape[0]
    head_count = HEADS // 8 * jnp.left_shift(jnp.int32(1), group_index)
    active = head_count.astype(F32) * HEAD_DIM

    flat_hidden = hidden_in[0].reshape(micros * rows, model_width).astype(F32)
    flat_grad = cotangent[0].reshape(micros * rows, model_width)
    normed, norm_back = jax.vjp(input_norm, flat_hidden, in_gain)
    dt_pad = LANES
    width_total = lax.axis_size("width")
    quarter = depth // width_total
    in_quarter = own(in_weight, group_index * quarter, quarter)
    gates = in_quarter[:, :INNER].reshape(quarter, seq_total, width)
    xs = in_quarter[:, INNER : 2 * INNER].reshape(quarter, seq_total, width)
    bc = jnp.broadcast_to(
        in_quarter[:, None, 2 * INNER : INNER + CONV], (quarter, seq_total, 2 * STATE)
    )
    dts = in_quarter[:, INNER + CONV :].reshape(quarter, seq_total, heads)
    dts = jnp.pad(dts, ((0, 0), (0, 0), (0, dt_pad - heads)))
    pieces = jnp.concatenate([bc, xs, gates, dts], axis=2).transpose(1, 0, 2)
    all_normed, all_grad, columns = gather_rows(normed.astype(BF16), flat_grad, pieces, 0)

    conv_width = 2 * STATE + width

    def conv_columns(value):
        return jnp.concatenate(
            [value[..., INNER:], own(value, col_first, width, value.ndim - 1)], axis=-1
        )

    taps = jnp.concatenate(
        [
            conv_columns(conv_weight),
            conv_columns(conv_bias[None]),
            jnp.zeros((8 - TAPS - 1, conv_width), F32),
        ],
        axis=0,
    )
    head_rows = jnp.stack(
        [own(step_bias, head_first, heads), -jnp.exp(own(decay_log, head_first, heads))]
    )
    head_table = jnp.pad(head_rows, ((0, 6), (0, LANES - heads)))
    head_mask = (head_first + jnp.arange(heads, dtype=jnp.int32) < head_count).astype(F32)
    cols = jnp.stack(
        [
            jnp.repeat(own(skip_gain, head_first, heads), HEAD_DIM),
            own(gate_gain, col_first, width),
            jnp.repeat(head_mask, HEAD_DIM),
        ]
    )
    cols = jnp.pad(cols, ((0, 5), (0, 0)))
    expand, gather, tri = tables(heads, rows)

    proj = mm(all_normed, columns).astype(BF16)
    dnorm = mm_nt(all_grad, out_weight)
    gg, mixed, states, tails, sums = run_forward(
        micros, heads, rows, seq_total, starts[0], proj, dnorm, taps, head_table, cols, expand, tri
    )
    sums = share(sums, "seq", 1)
    branch = lax.psum_scatter(
        mm(gg, out_weight).astype(BF16), "seq", scatter_dimension=0, tiled=True
    )
    squares = own(sums, seq_index, 1)[0, : 2 * micros : 2].reshape(micros * rows, 1)
    output = flat_hidden + branch.astype(F32) * lax.rsqrt(squares / active + EPSILON)

    dproj, gnorm, gconv, gcols, ghead = run_backward(
        micros,
        heads,
        rows,
        seq_total,
        starts[0],
        active[None],
        proj,
        dnorm,
        mixed,
        states,
        tails,
        sums,
        taps,
        head_table,
        cols,
        expand,
        gather,
        tri,
    )
    grad_normed = lax.psum_scatter(
        mm_nt(dproj, columns).astype(BF16), "seq", scatter_dimension=0, tiled=True
    ).astype(F32)
    grad_hidden, grad_gain_in = norm_back(grad_normed)
    hidden_grads = (flat_grad.astype(F32) + grad_hidden).astype(BF16)

    sub = width // width_total
    grad_out = mm_tn(gnorm, all_grad).astype(BF16).reshape(width_total, sub, model_width)
    grad_in = mm_tn(all_normed, dproj).astype(BF16)
    grad_in = grad_in.reshape(seq_total, width_total, quarter, grad_in.shape[1])
    grad_in = grad_in.transpose(1, 0, 2, 3)
    grad_out, grad_in = exchange([grad_out, grad_in], "width", 2)

    def added(value):
        return jnp.sum(value.astype(F32), axis=0).astype(BF16)

    grad_in = added(grad_in)
    grad_out = added(grad_out).reshape(sub, seq_total, model_width // seq_total)
    grad_out, grad_in = exchange([grad_out.transpose(1, 0, 2), grad_in], "seq", 3)

    def joined(value):
        return value.transpose(1, 0, 2).reshape(quarter, seq_total * value.shape[2])

    grad_in = jnp.concatenate(
        [
            joined(grad_in[:, :, conv_width : conv_width + width]),
            joined(grad_in[:, :, 2 * STATE : conv_width]),
            jnp.sum(grad_in[:, :, : 2 * STATE].astype(F32), axis=0).astype(BF16),
            joined(grad_in[:, :, conv_width + width : conv_width + width + heads]),
        ],
        axis=1,
    )
    shard_cols = grad_in.shape[1] // width_total
    grad_in = grad_in.reshape(quarter, width_total, shard_cols).transpose(1, 0, 2)
    blocks = seq_total // width_total
    grad_out = grad_out.reshape(width_total, blocks, sub, model_width // seq_total)
    grad_out, grad_in = exchange([grad_out, grad_in], "width", 4)
    shard_in = grad_in.reshape(depth, shard_cols).astype(F32)
    shard_out = grad_out.transpose(1, 0, 2, 3).reshape(blocks * width, -1).astype(F32)

    skip_heads = jnp.sum(gcols[0].reshape(heads, HEAD_DIM), axis=1)
    conv_small = jnp.concatenate(
        [placed(gconv[:5, 2 * STATE :], INNER, col_first), gconv[:5, : 2 * STATE]], axis=1
    )
    small = jnp.concatenate(
        [
            conv_small.reshape(-1),
            grad_gain_in,
            placed(gcols[1], INNER, col_first),
            placed(ghead[1, :heads], HEADS, head_first),
            placed(ghead[0, :heads], HEADS, head_first),
            placed(skip_heads, HEADS, head_first),
        ]
    )
    small = total_over_all(small, 5)
    edge = 5 * CONV
    conv_small = small[:edge].reshape(5, CONV)
    in_gain_sum = small[edge : edge + model_width]
    edge = edge + model_width
    gain_sum = small[edge : edge + INNER]
    edge = edge + INNER
    shape = hidden_in.shape
    return (
        output.astype(BF16).reshape(shape),
        hidden_grads.reshape(shape),
        in_gain_sum,
        shard_in,
        conv_small[:4],
        conv_small[4],
        small[edge : edge + HEADS],
        small[edge + HEADS : edge + 2 * HEADS],
        small[edge + 2 * HEADS : edge + 3 * HEADS],
        gain_sum,
        shard_out,
    )


def solution(mesh):
    in_specs = (
        P("width", None, "seq", None),
        P("width", None, None),
        P(),
        P("seq", None),
        P(),
        P(),
        P(),
        P(),
        P(),
        P(),
        P("seq", None),
        P("width", None, "seq", None),
    )
    out_specs = (
        P("width", None, "seq", None),
        P("width", None, "seq", None),
        P(),
        P("seq", "width"),
        P(),
        P(),
        P(),
        P(),
        P(),
        P(),
        P("width", "seq"),
    )
    return jax.shard_map(
        per_device, mesh=mesh, in_specs=in_specs, out_specs=out_specs, check_vma=False
    )
```

```python
from functools import partial

import jax
import jax.numpy as jnp
from jax import lax
from jax.experimental import pallas as pl
from jax.experimental.pallas import tpu as pltpu
from jax.sharding import PartitionSpec as P

INNER = 4096
HEADS = 64
HEAD_DIM = 64
STATE = 128
CONV = 4352
EPSILON = 1e-05
LANES = 128
TAPS = 4
NEG = -1e30
F32 = jnp.float32
BF16 = jnp.bfloat16


def mm(a, b):
    return lax.dot_general(a, b, (((1,), (0,)), ((), ())), preferred_element_type=F32)


def mm_nt(a, b):
    return lax.dot_general(a, b, (((1,), (1,)), ((), ())), preferred_element_type=F32)


def mm_tn(a, b):
    return lax.dot_general(a, b, (((0,), (0,)), ((), ())), preferred_element_type=F32)


def halves(value, axis):
    high = value.astype(BF16)
    low = (value - high.astype(F32)).astype(BF16)
    return jnp.concatenate([high, low], axis=axis)


def sigmoid(value):
    return 0.5 * jnp.tanh(0.5 * value) + 0.5


def prefix_sum(tri, value):
    high = value.astype(BF16)
    rest = value - high.astype(F32)
    middle = rest.astype(BF16)
    low = (rest - middle.astype(F32)).astype(BF16)
    parts = mm(tri, jnp.concatenate([high, middle, low], axis=1))
    width = value.shape[1]
    return parts[:, :width] + parts[:, width : 2 * width] + parts[:, 2 * width :]


def doc_number(starts_ref, micro, positions):
    count = jnp.zeros_like(positions)
    for item in range(starts_ref.shape[1]):
        count = count + (starts_ref[micro, item] <= positions).astype(jnp.int32)
    return count


MESH = pl.DeviceIdType.MESH
ANY = pl.BlockSpec(memory_space=pl.ANY)


def greet(axes):
    barrier = pltpu.get_barrier_semaphore()
    waits = 0
    for axis in axes:
        count, me = lax.axis_size(axis), lax.axis_index(axis)

        def hello(turn, carry):
            pl.semaphore_signal(
                barrier,
                inc=1,
                device_id={axis: lax.rem(me + turn, count)},
                device_id_type=MESH,
            )
            return carry

        lax.fori_loop(1, count, hello, 0)
        waits += count - 1
    pl.semaphore_wait(barrier, waits)


def remote(source, target, send, receive, device):
    return pltpu.make_async_remote_copy(
        src_ref=source,
        dst_ref=target,
        send_sem=send,
        recv_sem=receive,
        device_id=device,
        device_id_type=MESH,
    )


def share_kernel(axis, in_ref, out_ref, slots, send, receive):
    count, me = lax.axis_size(axis), lax.axis_index(axis)
    greet((axis,))

    def copy(turn, owner):
        peer = lax.rem(me + turn, count)
        return remote(in_ref, slots.at[owner], send.at[peer], receive.at[owner], {axis: peer})

    def start(turn, carry):
        copy(turn, me).start()
        return carry

    def finish(turn, carry):
        copy(turn, me).wait_send()
        copy(turn, lax.rem(me + turn, count)).wait_recv()
        return carry

    lax.fori_loop(1, count, start, 0)
    slots[me] = in_ref[...]
    lax.fori_loop(1, count, finish, 0)

    def add(owner, total):
        return total + slots[owner]

    out_ref[...] = lax.fori_loop(1, count, add, slots[0])


def share(value, axis, collective_id):
    count = lax.axis_size(axis)
    return pl.pallas_call(
        partial(share_kernel, axis),
        in_specs=[pl.BlockSpec(memory_space=pltpu.VMEM)],
        out_specs=pl.BlockSpec(memory_space=pltpu.VMEM),
        out_shape=jax.ShapeDtypeStruct(value.shape, value.dtype),
        scratch_shapes=[
            pltpu.VMEM((count,) + value.shape, value.dtype),
            pltpu.SemaphoreType.DMA((count,)),
            pltpu.SemaphoreType.DMA((count,)),
        ],
        compiler_params=pltpu.CompilerParams(
            collective_id=collective_id, has_side_effects=True, vmem_limit_bytes=48 << 20
        ),
        name="share_" + axis,
    )(value)


PARTS = 2


class Line:
    def __init__(self, source, out, sems):
        self.source, self.out = source, out
        self.up, self.down, self.receive, self.side_send, self.side_receive, self.keep = sems
        self.me = lax.axis_index("seq")
        self.chips = lax.axis_size("seq") // 2
        self.chip, self.core = self.me // 2, lax.rem(self.me, 2)
        self.block = source.shape[0]
        self.piece = self.block // PARTS

    def at(self, owner, part):
        first = pl.multiple_of(owner * self.block + part * self.piece, 8)
        return self.out.at[pl.ds(first, self.piece)]

    def line(self, source, owner_chip, part, target_chip, sems):
        return remote(
            source,
            self.at(owner_chip * 2 + self.core, part),
            sems.at[owner_chip, part],
            self.receive.at[owner_chip, part],
            {"seq": target_chip * 2 + self.core},
        )

    def side(self, source, owner_chip, part, from_sibling):
        core = 1 - self.core if from_sibling else self.core
        return remote(
            source,
            self.at(owner_chip * 2 + core, part),
            self.side_send.at[owner_chip, part],
            self.side_receive.at[owner_chip, part],
            {"seq": self.chip * 2 + 1 - self.core},
        )

    def stay(self):
        first = pl.multiple_of(self.me * self.block, 8)
        return pltpu.make_async_copy(
            self.source, self.out.at[pl.ds(first, self.block)], self.keep.at[0]
        )

    def start(self):
        for part in range(PARTS):
            here = self.source.at[pl.ds(part * self.piece, self.piece)]

            @pl.when(self.chip + 1 < self.chips)
            def _():
                self.line(here, self.chip, part, self.chip + 1, self.up).start()

            @pl.when(self.chip >= 1)
            def _():
                self.line(here, self.chip, part, self.chip - 1, self.down).start()

            self.side(here, self.chip, part, False).start()
        self.stay().start()

    def events(self):
        return (self.chips - 1) * PARTS

    def hop(self, event):
        turn, part = event // PARTS + 1, lax.rem(event, PARTS)
        below, above = self.chip - turn, self.chip + turn

        @pl.when(below >= 0)
        def _():
            here = self.at(below * 2 + self.core, part)
            self.line(here, below, part, self.chip, self.up).wait_recv()

            @pl.when(self.chip + 1 < self.chips)
            def _():
                self.line(here, below, part, self.chip + 1, self.up).start()

            self.side(here, below, part, False).start()

        @pl.when(above < self.chips)
        def _():
            here = self.at(above * 2 + self.core, part)
            self.line(here, above, part, self.chip, self.down).wait_recv()

            @pl.when(self.chip >= 1)
            def _():
                self.line(here, above, part, self.chip - 1, self.down).start()

            self.side(here, above, part, False).start()

    def hops(self, first):
        def body(event, carry):
            self.hop(event)
            return carry

        lax.fori_loop(first, self.events(), body, 0)

    def finish(self):
        def body(owner_chip, carry):
            for part in range(PARTS):
                here = self.at(owner_chip * 2 + self.core, part)

                @pl.when((owner_chip <= self.chip) & (self.chip + 1 < self.chips))
                def _():
                    self.line(here, owner_chip, part, self.chip + 1, self.up).wait_send()

                @pl.when((owner_chip >= self.chip) & (self.chip >= 1))
                def _():
                    self.line(here, owner_chip, part, self.chip - 1, self.down).wait_send()

                self.side(here, owner_chip, part, False).wait_send()
                self.side(here, owner_chip, part, True).wait_recv()
            return carry

        lax.fori_loop(0, self.chips, body, 0)
        self.stay().wait()


def line_sems(chips):
    return [pltpu.SemaphoreType.DMA((chips, PARTS))] * 5 + [pltpu.SemaphoreType.DMA((1,))]


class Chunk:
    def __init__(self, starts_ref, micro, chunk, rows, raw_dt, head_ref, expand, tri):
        first = chunk * rows
        column = lax.broadcasted_iota(jnp.int32, (rows, 1), 0) + first
        line = lax.broadcasted_iota(jnp.int32, (1, rows), 1) + first
        doc_col = doc_number(starts_ref, micro, column)
        doc_row = doc_number(starts_ref, micro, line)
        self.same = [
            (doc_number(starts_ref, micro, column - offset) == doc_col).astype(F32)
            for offset in range(1, TAPS)
        ]
        before = jnp.int32(0)
        last = jnp.int32(0)
        for item in range(starts_ref.shape[1]):
            before = before + (starts_ref[micro, item] <= first - 1).astype(jnp.int32)
            last = last + (starts_ref[micro, item] <= first + rows - 1).astype(jnp.int32)
        carry = (doc_col == before).astype(F32)
        same_last = (doc_col == last).astype(F32)
        self.bias = jnp.where((column >= line) & (doc_col == doc_row), 0.0, NEG)
        self.shifted_dt = raw_dt + head_ref[0:1]
        self.step = jnp.maximum(self.shifted_dt, 0.0) + jnp.log1p(
            jnp.exp(-jnp.abs(self.shifted_dt))
        )
        self.log_keep = self.step * head_ref[1:2]
        self.cum = prefix_sum(tri, self.log_keep)
        self.cum_t = self.cum.T
        carried = jnp.exp(self.cum) * carry
        left = jnp.exp(self.cum[rows - 1 :] - self.cum) * same_last
        spread = mm(
            halves(jnp.concatenate([self.step, carried, left], axis=0), 1), expand
        )
        self.step_cols = spread[:rows]
        self.carry_cols = spread[rows : 2 * rows]
        self.left_cols = spread[2 * rows :]
        self.keep_all = self.carry_cols[rows - 1 :]

    def decay(self, head):
        return jnp.exp(self.cum[:, head : head + 1] - self.cum_t[head : head + 1] + self.bias)


def head_groups(heads):
    size = 2 if heads % 2 == 0 else 1
    return size, heads // size


def stacked(value, size):
    if size == 1:
        return value.astype(BF16)
    lane = lax.broadcasted_iota(jnp.int32, value.shape, 1)
    first = jnp.where(lane < HEAD_DIM, value, 0.0)
    second = jnp.where(lane < HEAD_DIM, 0.0, value)
    return jnp.concatenate([first, second], axis=0).astype(BF16)


def convolved(ext, micro, rows, taps_ref, same):
    current = ext[micro, 8 : 8 + rows, :]
    total = taps_ref[TAPS : TAPS + 1] + taps_ref[TAPS - 1 : TAPS] * current
    views = []
    for offset in range(1, TAPS):
        view = ext[micro, 8 - offset : 8 - offset + rows, :] * same[offset - 1]
        views.append(view)
        total = total + taps_ref[TAPS - 1 - offset : TAPS - offset] * view
    return current, views, total


def forward_kernel(
    micros,
    heads,
    starts_ref,
    x_ref,
    weight_ref,
    out_weight_ref,
    g_ref,
    taps_ref,
    head_ref,
    cols_ref,
    expand_ref,
    tri_ref,
    proj_ref,
    gg_ref,
    branch_ref,
    mixed_ref,
    states_ref,
    tails_ref,
    sums_ref,
    g_out,
    ext,
    state,
    *sems,
):
    chunk, chunks = pl.program_id(0), pl.num_programs(0)
    rows = x_ref.shape[0] // micros
    width = heads * HEAD_DIM
    conv_width = 2 * STATE + width
    size, groups = head_groups(heads)
    line = Line(g_ref, g_out, sems)
    early = min((g_out.shape[0] // g_ref.shape[0] - 1) // 2, line.events())

    @pl.when(chunk == 0)
    def _():
        greet(("seq",))
        line.start()

    @pl.when((lax.rem(chunk, 2) == 0) & (chunk >= 2) & (chunk // 2 - 1 < early))
    def _():
        line.hop(chunk // 2 - 1)

    @pl.when(chunk == 0)
    def _():
        ext[:, :8, :] = jnp.zeros((micros, 8, conv_width), F32)
        state[...] = jnp.zeros_like(state)

    skip, gain, mask = cols_ref[0:1], cols_ref[1:2], cols_ref[2:3]
    proj_ref[...] = mm(x_ref[...], weight_ref[...]).astype(BF16)
    sums = []
    for micro in range(micros):
        part = slice(micro * rows, (micro + 1) * rows)
        tails_ref[micro] = ext[micro, :8, :]
        ext[micro, 8 : 8 + rows, :] = proj_ref[part, :conv_width].astype(F32)
        raw_dt = proj_ref[part, conv_width + width :].astype(F32)
        at = Chunk(
            starts_ref, micro, chunk, rows, raw_dt, head_ref, expand_ref[...], tri_ref[...]
        )
        conv = convolved(ext, micro, rows, taps_ref, at.same)[2]
        act = conv * sigmoid(conv)
        write = act[:, :STATE].astype(BF16)
        read = act[:, STATE : 2 * STATE].astype(BF16)
        x_heads = act[:, 2 * STATE :]
        scores = mm_nt(read, write)
        inputs = x_heads * at.step_cols
        state_in = state[micro]
        state_low = state_in.astype(BF16)
        states_ref[micro] = state_low
        outs = []
        for group in range(groups):
            matrices = [
                (at.decay(group * size + item) * scores).astype(BF16) for item in range(size)
            ]
            span = slice(group * size * HEAD_DIM, (group + 1) * size * HEAD_DIM)
            outs.append(mm(jnp.concatenate(matrices, axis=1), stacked(inputs[:, span], size)))
        mixed = jnp.concatenate(outs, axis=1) + at.carry_cols * mm(read, state_low)
        state[micro] = at.keep_all * state_in + mm_tn(
            write, (inputs * at.left_cols).astype(BF16)
        )
        mixed = mixed + skip * x_heads
        mixed_ref[part, :] = mixed
        gate = proj_ref[part, conv_width : conv_width + width].astype(F32)
        gated = mask * mixed * (gate * sigmoid(gate))
        gg_ref[part, :] = (gated * gain).astype(BF16)
        square = jnp.sum(gated * gated, axis=1, keepdims=True)
        lane = lax.broadcasted_iota(jnp.int32, (rows, LANES), 1)
        sums.append(jnp.where(lane == 0, square, 0.0).T[:2])
        ext[micro, :8, :] = ext[micro, rows : rows + 8, :]
    pad = sums_ref.shape[0] - 2 * micros
    if pad:
        sums.append(jnp.zeros((pad, rows), F32))
    sums_ref[...] = jnp.concatenate(sums, axis=0)
    branch_ref[...] = mm(gg_ref[...], out_weight_ref[...]).astype(BF16)

    @pl.when(chunk == chunks - 1)
    def _():
        line.hops(early)
        line.finish()


def cross_kernel(micros, g_ref, out_weight_ref, gg_ref, sums_ref, dnorm_ref, both_ref):
    rows = g_ref.shape[0] // micros
    dnorm = mm_nt(g_ref[...], out_weight_ref[...])
    dnorm_ref[...] = dnorm
    cross = jnp.sum(dnorm * gg_ref[...].astype(F32), axis=1, keepdims=True)
    lane = lax.broadcasted_iota(jnp.int32, (rows, LANES), 1)
    lines = []
    for micro in range(micros):
        part = cross[micro * rows : (micro + 1) * rows]
        lines.append(jnp.where(lane == 1, part, 0.0).T[:2])
    pad = sums_ref.shape[0] - 2 * micros
    if pad:
        lines.append(jnp.zeros((pad, rows), F32))
    both_ref[...] = sums_ref[...] + jnp.concatenate(lines, axis=0)


def backward_kernel(
    micros,
    heads,
    starts_ref,
    active_ref,
    proj_ref,
    dnorm_ref,
    mixed_ref,
    states_ref,
    tails_ref,
    sums_ref,
    taps_ref,
    head_ref,
    cols_ref,
    expand_ref,
    gather_ref,
    tri_ref,
    dproj_ref,
    gconv_ref,
    gcols_ref,
    ghead_ref,
    ext,
    heads_ext,
    dstate,
):
    chunks = pl.num_programs(0)
    step_index = pl.program_id(0)
    chunk = chunks - 1 - step_index
    rows = proj_ref.shape[0] // micros
    width = heads * HEAD_DIM
    conv_width = 2 * STATE + width
    size, groups = head_groups(heads)

    @pl.when(step_index == 0)
    def _():
        heads_ext[:, :, rows:, :] = jnp.zeros((micros, TAPS - 1, 8, conv_width), F32)
        dstate[...] = jnp.zeros_like(dstate)
        gconv_ref[...] = jnp.zeros_like(gconv_ref)
        gcols_ref[...] = jnp.zeros_like(gcols_ref)
        ghead_ref[...] = jnp.zeros_like(ghead_ref)

    skip, gain, mask = cols_ref[0:1], cols_ref[1:2], cols_ref[2:3]
    tri = tri_ref[...]
    gather = gather_ref[...]
    inverse_active = 1.0 / active_ref[0]
    sums = jnp.concatenate(
        [sums_ref[...], jnp.zeros((LANES - sums_ref.shape[0], rows), F32)], axis=0
    ).T
    for micro in range(micros):
        part = slice(micro * rows, (micro + 1) * rows)
        ext[micro, :8, :] = tails_ref[micro]
        ext[micro, 8 : 8 + rows, :] = proj_ref[part, :conv_width].astype(F32)
        raw_dt = proj_ref[part, conv_width + width :].astype(F32)
        at = Chunk(starts_ref, micro, chunk, rows, raw_dt, head_ref, expand_ref[...], tri)
        current, views, conv = convolved(ext, micro, rows, taps_ref, at.same)
        conv_sig = sigmoid(conv)
        act = conv * conv_sig
        write = act[:, :STATE].astype(BF16)
        read = act[:, STATE : 2 * STATE].astype(BF16)
        x_heads = act[:, 2 * STATE :]
        scores = mm_nt(read, write)
        inputs = x_heads * at.step_cols

        gate = proj_ref[part, conv_width : conv_width + width].astype(F32)
        gate_sig = sigmoid(gate)
        gate_act = gate * gate_sig
        masked = mask * mixed_ref[part, :]
        gated = masked * gate_act
        root = lax.rsqrt(sums[:, 2 * micro : 2 * micro + 1] * inverse_active + EPSILON)
        pull = root * root * root * sums[:, 2 * micro + 1 : 2 * micro + 2] * inverse_active
        dnorm = dnorm_ref[part, :]
        scaled = gated * root
        d_gated = root * dnorm * gain - gated * pull
        d_gate = d_gated * masked * (gate_sig * (1.0 + gate * (1.0 - gate_sig)))
        d_mixed = mask * d_gated * gate_act
        gcols_ref[0:1] += jnp.sum(d_mixed * x_heads, axis=0, keepdims=True)
        gcols_ref[1:2] += jnp.sum(dnorm * scaled, axis=0, keepdims=True)

        state_low = states_ref[micro]
        d_state = dstate[micro]
        d_state_low = d_state.astype(BF16)
        from_state = (d_mixed * at.carry_cols).astype(BF16)
        left = inputs * at.left_cols
        left_low = left.astype(BF16)
        d_left = mm(write, d_state_low)
        state_out = mm(read, state_low)
        d_read = mm_nt(from_state, state_low)
        d_write = mm_nt(left_low, d_state_low)
        d_mixed_low = d_mixed.astype(BF16).astype(F32)
        inputs_low = inputs.astype(BF16).astype(F32)
        d_scores = jnp.zeros((rows, rows), F32)
        locals_out, d_locals = [], []
        for group in range(groups):
            span = slice(group * size * HEAD_DIM, (group + 1) * size * HEAD_DIM)
            decays = [at.decay(group * size + item) for item in range(size)]
            matrices = [(decay * scores).astype(BF16) for decay in decays]
            in_stack = stacked(inputs[:, span], size)
            out_stack = stacked(d_mixed[:, span], size)
            locals_out.append(mm(jnp.concatenate(matrices, axis=1), in_stack))
            d_locals.append(mm_tn(jnp.concatenate(matrices, axis=0), out_stack))
            d_matrices = mm_nt(out_stack, inputs[:, span].astype(BF16))
            for item in range(size):
                d_scores = (
                    d_scores + d_matrices[item * rows : (item + 1) * rows] * decays[item]
                )
        local_out = jnp.concatenate(locals_out, axis=1)
        d_local = jnp.concatenate(d_locals, axis=1)
        d_scores_low = d_scores.astype(BF16)
        d_read = d_read + mm(d_scores_low, write)
        d_write = d_write + mm_tn(d_scores_low, read)
        d_inputs = d_local + at.left_cols * d_left
        d_x = skip * d_mixed + d_inputs * at.step_cols

        passed = left * d_left
        cum_terms = (
            d_mixed_low * local_out
            + d_mixed * at.carry_cols * state_out
            - inputs_low * d_local
            - passed
        )
        kept = jnp.sum(d_state * at.keep_all * state_low.astype(F32), axis=0, keepdims=True)
        final = jnp.sum(passed, axis=0, keepdims=True) + kept
        stack = jnp.concatenate(
            [cum_terms, d_inputs * x_heads, jnp.broadcast_to(final, (8, width))], axis=0
        )
        reduced = mm(halves(stack, 1), gather)
        d_cum = reduced[:rows]
        d_step = reduced[rows : 2 * rows]
        final_row = reduced[2 * rows : 2 * rows + 1]
        total = jnp.sum(d_cum, axis=0, keepdims=True) + final_row
        d_log = total - prefix_sum(tri, d_cum) + d_cum
        d_step = d_step + d_log * head_ref[1:2]
        d_dt = d_step * sigmoid(at.shifted_dt)
        ghead_ref[0:1] += jnp.sum(d_log * at.log_keep, axis=0, keepdims=True)
        ghead_ref[1:2] += jnp.sum(d_dt, axis=0, keepdims=True)
        dstate[micro] = at.keep_all * d_state + mm_tn(read, from_state)

        d_conv = jnp.concatenate([d_write, d_read, d_x], axis=1) * (
            conv_sig * (1.0 + conv * (1.0 - conv_sig))
        )
        gconv_ref[TAPS : TAPS + 1] += jnp.sum(d_conv, axis=0, keepdims=True)
        gconv_ref[TAPS - 1 : TAPS] += jnp.sum(d_conv * current, axis=0, keepdims=True)
        d_raw = taps_ref[TAPS - 1 : TAPS] * d_conv
        for offset in range(1, TAPS):
            tap = TAPS - 1 - offset
            gconv_ref[tap : tap + 1] += jnp.sum(
                d_conv * views[offset - 1], axis=0, keepdims=True
            )
            heads_ext[micro, offset - 1, :rows, :] = d_conv * at.same[offset - 1]
            d_raw = d_raw + taps_ref[tap : tap + 1] * (
                heads_ext[micro, offset - 1, offset : offset + rows, :]
            )
            heads_ext[micro, offset - 1, rows:, :] = heads_ext[micro, offset - 1, :8, :]
        dproj_ref[part, :conv_width] = d_raw.astype(BF16)
        dproj_ref[part, conv_width : conv_width + width] = d_gate.astype(BF16)
        dproj_ref[part, conv_width + width :] = d_dt.astype(BF16)


def constant(shape):
    return pl.BlockSpec(shape, lambda index: (0,) * len(shape))


def run_forward(
    micros, heads, rows, chunks, starts, x, weight, out_weight, g, taps, head, cols, expand, tri, collective_id
):
    width = heads * HEAD_DIM
    conv_width = 2 * STATE + width
    block = micros * rows
    sum_rows = -(-2 * micros // 8) * 8
    columns = weight.shape[1]
    model_width = x.shape[1]

    def whole(value):
        return pl.BlockSpec(
            value.shape, lambda index: (0,) * value.ndim, pipeline_mode=pl.Buffered(1)
        )

    def row_block(size):
        return pl.BlockSpec((block, size), lambda index: (index, 0))

    return pl.pallas_call(
        partial(forward_kernel, micros, heads),
        grid=(chunks,),
        in_specs=[
            pl.BlockSpec(memory_space=pltpu.SMEM),
            row_block(model_width),
            whole(weight),
            whole(out_weight),
            ANY,
            whole(taps),
            whole(head),
            whole(cols),
            whole(expand),
            whole(tri),
        ],
        out_specs=[
            row_block(columns),
            row_block(width),
            row_block(model_width),
            row_block(width),
            pl.BlockSpec((None, micros, STATE, width), lambda index: (index, 0, 0, 0)),
            pl.BlockSpec((None, micros, 8, conv_width), lambda index: (index, 0, 0, 0)),
            pl.BlockSpec((None, sum_rows, rows), lambda index: (index, 0, 0)),
            ANY,
        ],
        out_shape=[
            jax.ShapeDtypeStruct((chunks * block, columns), BF16),
            jax.ShapeDtypeStruct((chunks * block, width), BF16),
            jax.ShapeDtypeStruct((chunks * block, model_width), BF16),
            jax.ShapeDtypeStruct((chunks * block, width), F32),
            jax.ShapeDtypeStruct((chunks, micros, STATE, width), BF16),
            jax.ShapeDtypeStruct((chunks, micros, 8, conv_width), F32),
            jax.ShapeDtypeStruct((chunks, sum_rows, rows), F32),
            jax.ShapeDtypeStruct((chunks * block, model_width), BF16),
        ],
        scratch_shapes=[
            pltpu.VMEM((micros, rows + 8, conv_width), F32),
            pltpu.VMEM((micros, STATE, width), F32),
        ]
        + line_sems(chunks // 2),
        compiler_params=pltpu.CompilerParams(
            collective_id=collective_id, has_side_effects=True, vmem_limit_bytes=48 << 20
        ),
        cost_estimate=pl.CostEstimate(
            flops=60 * 10**9, bytes_accessed=150 * 10**6, transcendentals=0
        ),
        name="mixer_forward",
    )(starts, x, weight, out_weight, g, taps, head, cols, expand, tri)


def run_cross(micros, chunks, g, out_weight, gg, sums):
    block = g.shape[0] // chunks
    width = gg.shape[1]
    sum_block = pl.BlockSpec((None,) + sums.shape[1:], lambda index: (index, 0, 0))
    return pl.pallas_call(
        partial(cross_kernel, micros),
        grid=(chunks,),
        in_specs=[
            pl.BlockSpec((block, g.shape[1]), lambda index: (index, 0)),
            constant(out_weight.shape),
            pl.BlockSpec((block, width), lambda index: (index, 0)),
            sum_block,
        ],
        out_specs=[pl.BlockSpec((block, width), lambda index: (index, 0)), sum_block],
        out_shape=[
            jax.ShapeDtypeStruct((g.shape[0], width), F32),
            jax.ShapeDtypeStruct(sums.shape, F32),
        ],
        compiler_params=pltpu.CompilerParams(vmem_limit_bytes=32 << 20),
        cost_estimate=pl.CostEstimate(
            flops=8 * 10**9, bytes_accessed=16 * 10**6, transcendentals=0
        ),
        name="cross_sums",
    )(g, out_weight, gg, sums)


def run_backward(
    micros,
    heads,
    rows,
    chunks,
    starts,
    active,
    proj,
    dnorm,
    mixed,
    states,
    tails,
    sums,
    taps,
    head,
    cols,
    expand,
    gather,
    tri,
):
    width = heads * HEAD_DIM
    conv_width = 2 * STATE + width
    block = micros * rows

    def back(index):
        return (chunks - 1 - index, 0)

    return pl.pallas_call(
        partial(backward_kernel, micros, heads),
        grid=(chunks,),
        in_specs=[
            pl.BlockSpec(memory_space=pltpu.SMEM),
            pl.BlockSpec(memory_space=pltpu.SMEM),
            pl.BlockSpec((block, proj.shape[1]), back),
            pl.BlockSpec((block, width), back),
            pl.BlockSpec((block, width), back),
            pl.BlockSpec(
                (None, micros, STATE, width), lambda index: (chunks - 1 - index, 0, 0, 0)
            ),
            pl.BlockSpec(
                (None, micros, 8, conv_width), lambda index: (chunks - 1 - index, 0, 0, 0)
            ),
            pl.BlockSpec((None, sums.shape[1], rows), lambda index: (chunks - 1 - index, 0, 0)),
            constant(taps.shape),
            constant(head.shape),
            constant(cols.shape),
            constant(expand.shape),
            constant(gather.shape),
            constant(tri.shape),
        ],
        out_specs=[
            pl.BlockSpec((block, proj.shape[1]), back),
            constant((8, conv_width)),
            constant((8, width)),
            constant((8, LANES)),
        ],
        out_shape=[
            jax.ShapeDtypeStruct((chunks * block, proj.shape[1]), BF16),
            jax.ShapeDtypeStruct((8, conv_width), F32),
            jax.ShapeDtypeStruct((8, width), F32),
            jax.ShapeDtypeStruct((8, LANES), F32),
        ],
        scratch_shapes=[
            pltpu.VMEM((micros, rows + 8, conv_width), F32),
            pltpu.VMEM((micros, TAPS - 1, rows + 8, conv_width), F32),
            pltpu.VMEM((micros, STATE, width), F32),
        ],
        compiler_params=pltpu.CompilerParams(vmem_limit_bytes=48 << 20),
        cost_estimate=pl.CostEstimate(
            flops=40 * 10**9, bytes_accessed=80 * 10**6, transcendentals=0
        ),
        name="mixer_backward",
    )(
        starts,
        active,
        proj,
        dnorm,
        mixed,
        states,
        tails,
        sums,
        taps,
        head,
        cols,
        expand,
        gather,
        tri,
    )


def tables(heads, rows):
    width = heads * HEAD_DIM
    expand = (
        jnp.arange(LANES)[:, None] == jnp.arange(width)[None, :] // HEAD_DIM
    ).astype(BF16)
    tri = (jnp.arange(rows)[:, None] >= jnp.arange(rows)[None, :]).astype(BF16)
    return (
        jnp.concatenate([expand, expand], axis=0),
        jnp.concatenate([expand.T, expand.T], axis=0),
        tri,
    )


def gather_kernel(
    x_ref,
    w_ref,
    x_out,
    w_out,
    w_send,
    w_receive,
    f_send,
    f_receive,
    keep,
    *sems,
):
    seq_total, width_total = lax.axis_size("seq"), lax.axis_size("width")
    me, mine = lax.axis_index("seq"), lax.axis_index("width")
    quarter = w_ref.shape[1]
    depth = quarter * width_total
    line = Line(x_ref, x_out, sems)
    greet(("seq", "width"))

    def rows(source, group):
        return pl.ds(pl.multiple_of(source * depth + group * quarter, 8), quarter)

    def deal(turn, from_peer):
        peer = lax.rem(me + turn, seq_total)
        owner = peer if from_peer else me
        return remote(
            w_ref.at[peer],
            w_out.at[rows(owner, mine)],
            w_send.at[peer],
            w_receive.at[owner],
            {"seq": peer},
        )

    def deal_start(turn, carry):
        deal(turn, False).start()
        return carry

    lax.fori_loop(1, seq_total, deal_start, 0)
    w_own = pltpu.make_async_copy(w_ref.at[me], w_out.at[rows(me, mine)], keep.at[0])
    w_own.start()
    line.start()

    def forward(source, turn, from_peer):
        peer = lax.rem(mine + turn, width_total)
        group = peer if from_peer else mine
        where = w_out.at[rows(source, group)]
        return remote(
            where, where, f_send.at[peer, source], f_receive.at[group, source], {"width": peer}
        )

    def forward_start(source):
        for turn in range(1, width_total):
            forward(source, turn, False).start()

    def deal_pass(turn, carry):
        deal(turn, True).wait_recv()
        forward_start(lax.rem(me + turn, seq_total))
        return carry

    w_own.wait()
    forward_start(me)
    lax.fori_loop(1, seq_total, deal_pass, 0)
    line.hops(0)

    def deal_end(turn, carry):
        deal(turn, False).wait_send()
        return carry

    lax.fori_loop(1, seq_total, deal_end, 0)

    def forward_end(source, carry):
        for turn in range(1, width_total):
            forward(source, turn, False).wait_send()
            forward(source, turn, True).wait_recv()
        return carry

    lax.fori_loop(0, seq_total, forward_end, 0)
    line.finish()


def gather_rows(x, pieces, collective_id):
    seq_total, width_total = lax.axis_size("seq"), lax.axis_size("width")
    whole = (x.shape[0] * seq_total, x.shape[1])
    weight = (seq_total * width_total * pieces.shape[1], pieces.shape[2])
    dma = pltpu.SemaphoreType.DMA
    return pl.pallas_call(
        gather_kernel,
        in_specs=[ANY] * 2,
        out_specs=[ANY] * 2,
        out_shape=[
            jax.ShapeDtypeStruct(whole, x.dtype),
            jax.ShapeDtypeStruct(weight, pieces.dtype),
        ],
        scratch_shapes=[
            dma((seq_total,)),
            dma((seq_total,)),
            dma((width_total, seq_total)),
            dma((width_total, seq_total)),
            dma((1,)),
        ]
        + line_sems(seq_total // 2),
        compiler_params=pltpu.CompilerParams(
            collective_id=collective_id, has_side_effects=True
        ),
        cost_estimate=pl.CostEstimate(
            flops=80 * 10**9, bytes_accessed=200 * 10**6, transcendentals=0
        ),
        name="gather_rows",
    )(x, pieces)


TILE = 256


def home_kernel(
    layout,
    normed_ref,
    dproj_ref,
    columns_ref,
    small_ref,
    grad_ref,
    gnorm_ref,
    zx_ref,
    bc_ref,
    go_ref,
    small_out,
    blocks_in,
    acc,
    out_acc,
    stage,
    arrived,
    sum_x,
    sum_z,
    sum_b,
    out_stage,
    out_arrived,
    sum_out,
    small_stage,
    small_slots,
    fetch,
    hop_send,
    hop_receive,
    zx_send,
    zx_receive,
    bc_send,
    bc_receive,
    oh_send,
    oh_receive,
    go_send,
    go_receive,
    small_send,
    small_receive,
    last_send,
    last_receive,
):
    seq_total, width_total, quarter, width, slots, shard, gain_row = layout
    me, mine = lax.axis_index("seq"), lax.axis_index("width")
    depth = quarter * width_total
    conv_width = 2 * STATE + width
    per_tile = TILE // depth
    tiles = seq_total // per_tile
    chunk_rows = blocks_in.shape[1]
    chunks = normed_ref.shape[0] // chunk_rows
    owners = seq_total // width_total
    barrier = pltpu.get_barrier_semaphore()
    count = seq_total * width_total
    place = mine * seq_total + me

    def fetch_copy(source, step):
        tile, chunk = step // chunks, lax.rem(step, chunks)
        return pltpu.make_async_copy(
            source.at[
                pl.ds(pl.multiple_of(chunk * chunk_rows, 8), chunk_rows),
                pl.ds(pl.multiple_of(tile * TILE, TILE), TILE),
            ],
            blocks_in.at[lax.rem(step, 2)],
            fetch.at[lax.rem(step, 2)],
        )

    fetch_copy(grad_ref, 0).start()

    def hello(turn, carry):
        peer = lax.rem(place + turn, count)
        pl.semaphore_signal(
            barrier,
            inc=1,
            device_id={"width": peer // seq_total, "seq": lax.rem(peer, seq_total)},
            device_id_type=MESH,
        )
        return carry

    lax.fori_loop(1, count, hello, 0)
    pl.semaphore_wait(barrier, count - 1)

    def both(is_here, source, target, send, receive, device, action):
        if action != "send":

            @pl.when(is_here)
            def _():
                stay = pltpu.make_async_copy(source, target, receive)
                if action == "start":
                    stay.start()
                else:
                    stay.wait()

        @pl.when(jnp.logical_not(is_here))
        def _():
            away = remote(source, target, send, receive, device)
            if action == "start":
                away.start()
            elif action == "receive":
                away.wait_recv()
            else:
                away.wait_send()

    sub, cols = out_stage.shape[2:]
    per_out = TILE // cols

    def out_hop(block, turn, from_peer):
        peer = lax.rem(mine + turn, width_total)
        group = peer if from_peer else mine
        return remote(
            out_stage.at[block, peer],
            out_arrived.at[block, group],
            oh_send.at[block, peer],
            oh_receive.at[block, group],
            {"width": peer},
        )

    def place_of(step):
        tile, chunk = step // chunks, lax.rem(step, chunks)
        first = pl.ds(pl.multiple_of(chunk * chunk_rows, 8), chunk_rows)
        return tile, chunk, first, lax.rem(step, 2)

    def out_multiply(step, carry):
        tile, chunk, first, slot = place_of(step)
        fetch_copy(grad_ref, step).wait()

        @pl.when(step + 1 < tiles * chunks)
        def _():
            fetch_copy(grad_ref, step + 1).start()

        @pl.when(step + 1 == tiles * chunks)
        def _():
            fetch_copy(normed_ref, 0).start()

        part = mm_tn(gnorm_ref[first, :], blocks_in[slot])
        if chunks > 1:
            out_acc[...] = jnp.where(chunk == 0, part, out_acc[...] + part)
        else:
            out_acc[...] = part

        @pl.when(chunk == chunks - 1)
        def _():
            for item in range(per_out):
                block = tile * per_out + item
                for group in range(width_total):
                    out_stage[block, group] = out_acc[
                        group * sub : (group + 1) * sub, item * cols : (item + 1) * cols
                    ].astype(BF16)
                for turn in range(1, width_total):
                    out_hop(block, turn, False).start()

        return carry

    lax.fori_loop(0, tiles * chunks, out_multiply, 0)
    go_owner = me // owners

    def go_copy(target, action):
        both(
            (go_owner == mine) & (target == me),
            sum_out.at[target],
            go_ref.at[lax.rem(me, owners), mine],
            go_send.at[target],
            go_receive.at[lax.rem(me, owners), mine],
            {"width": go_owner, "seq": target},
            action,
        )

    small_stage[...] = small_ref[...]

    def hop(block, turn, from_peer):
        peer = lax.rem(mine + turn, width_total)
        group = peer if from_peer else mine
        return remote(
            stage.at[block, peer],
            arrived.at[block, group],
            hop_send.at[block, peer],
            hop_receive.at[block, group],
            {"width": peer},
        )

    def multiply(step, carry):
        tile, chunk, first, _ = place_of(step)
        slot = lax.rem(step + tiles * chunks, 2)
        fetch_copy(normed_ref, step).wait()

        @pl.when(step + 1 < tiles * chunks)
        def _():
            fetch_copy(normed_ref, step + 1).start()

        part = mm_tn(blocks_in[slot], dproj_ref[first, :])
        if chunks > 1:
            acc[...] = jnp.where(chunk == 0, part, acc[...] + part)
        else:
            acc[...] = part

        @pl.when(chunk == chunks - 1)
        def _():
            for item in range(per_tile):
                block = tile * per_tile + item
                for group in range(width_total):
                    row = item * depth + group * quarter
                    stage[block, group] = acc[row : row + quarter].astype(BF16)
                for turn in range(1, width_total):
                    hop(block, turn, False).start()
            weights = columns_ref[pl.ds(pl.multiple_of(tile * TILE, TILE), TILE), :]
            product = (acc[...] * weights.astype(F32)).astype(BF16)
            line = mm_nt(jnp.ones((8, product.shape[1]), BF16), product)
            for item in range(TILE // LANES):
                small_stage[pl.ds(gain_row + tile * (TILE // LANES) + item, 1), :] = line[
                    :1, item * LANES : (item + 1) * LANES
                ]

        return carry

    lax.fori_loop(0, tiles * chunks, multiply, 0)

    def small_hop(turn, from_peer):
        peer = lax.rem(mine + turn, width_total)
        group = peer if from_peer else mine
        return remote(
            small_stage,
            small_slots.at[group],
            small_send.at[peer],
            small_receive.at[group],
            {"width": peer},
        )

    for turn in range(1, width_total):
        small_hop(turn, False).start()
    small_slots[mine] = small_stage[...]

    def block_copy(sums, sem_row, number, block, second, action):
        low = (number * width) // shard
        high = ((number + 1) * width - 1) // shard
        owner = high if second else low
        slot = number - (owner * shard) // width

        def act():
            both(
                (owner == mine) & (block == me),
                sums.at[block],
                zx_ref.at[slot, mine],
                zx_send.at[sem_row, block],
                zx_receive.at[slot, mine],
                {"width": owner, "seq": block},
                action,
            )

        if second:
            pl.when(high != low)(act)
        else:
            act()

    def bc_copy(block, action):
        both(
            (mine == width_total - 1) & (block == me),
            sum_b.at[block],
            bc_ref.at[me, mine],
            bc_send.at[block],
            bc_receive.at[me, mine],
            {"width": width_total - 1, "seq": block},
            action,
        )

    def pieces_of(block, action):
        for second in (False, True):
            block_copy(sum_z, int(second), me, block, second, action)
            block_copy(sum_x, 2 + int(second), seq_total + me, block, second, action)
        bc_copy(block, action)

    def out_combine(block, carry):
        total = out_stage[block, mine].astype(F32)
        for turn in range(1, width_total):
            out_hop(block, turn, True).wait_recv()
            total = total + out_arrived[block, lax.rem(mine + turn, width_total)].astype(F32)
        sum_out[block] = total.astype(BF16)
        go_copy(block, "start")
        return carry

    lax.fori_loop(0, seq_total, out_combine, 0)

    def combine(block, carry):
        total = stage[block, mine].astype(F32)
        for turn in range(1, width_total):
            hop(block, turn, True).wait_recv()
            total = total + arrived[block, lax.rem(mine + turn, width_total)].astype(F32)
        low = total.astype(BF16)
        sum_b[block, :, : 2 * STATE] = low[:, : 2 * STATE]
        sum_x[block] = low[:, 2 * STATE : conv_width]
        sum_z[block] = low[:, conv_width : conv_width + width]
        sum_b[block, :, 2 * STATE :] = low[:, conv_width + width :]
        pieces_of(block, "start")
        return carry

    lax.fori_loop(0, seq_total, combine, 0)

    for turn in range(1, width_total):
        small_hop(turn, True).wait_recv()
        small_hop(turn, False).wait_send()
    total = small_slots[0]
    for group in range(1, width_total):
        total = total + small_slots[group]
    small_stage[...] = total

    def last_hop(turn, from_peer):
        peer = lax.rem(me + turn, seq_total)
        owner = peer if from_peer else me
        return remote(
            small_stage,
            small_out.at[owner],
            last_send.at[peer],
            last_receive.at[owner],
            {"seq": peer},
        )

    def last_start(turn, carry):
        last_hop(turn, False).start()
        return carry

    lax.fori_loop(1, seq_total, last_start, 0)
    small_out[me] = small_stage[...]

    def sent(block, carry):
        for turn in range(1, width_total):
            hop(block, turn, False).wait_send()
            out_hop(block, turn, False).wait_send()
        pieces_of(block, "send")
        go_copy(block, "send")
        return carry

    lax.fori_loop(0, seq_total, sent, 0)

    first = (mine * shard) // width

    def landed(slot, carry):
        number = first + slot
        source = lax.rem(number, seq_total)

        @pl.when((number < 2 * seq_total) & (number * width < (mine + 1) * shard))
        def _():
            for group in range(width_total):
                both(
                    (source == me) & (mine == group),
                    sum_z.at[me],
                    zx_ref.at[slot, group],
                    zx_send.at[0, me],
                    zx_receive.at[slot, group],
                    {"width": group, "seq": source},
                    "receive",
                )

        return carry

    lax.fori_loop(0, slots, landed, 0)

    @pl.when(mine == width_total - 1)
    def _():
        def bc_landed(source, carry):
            for group in range(width_total):
                both(
                    (source == me) & (mine == group),
                    sum_b.at[me],
                    bc_ref.at[source, group],
                    bc_send.at[me],
                    bc_receive.at[source, group],
                    {"width": group, "seq": source},
                    "receive",
                )
            return carry

        lax.fori_loop(0, seq_total, bc_landed, 0)

    for item in range(owners):
        for group in range(width_total):
            source = mine * owners + item
            both(
                (source == me) & (mine == group),
                sum_out.at[me],
                go_ref.at[item, group],
                go_send.at[me],
                go_receive.at[item, group],
                {"width": group, "seq": source},
                "receive",
            )

    def last_end(turn, carry):
        last_hop(turn, False).wait_send()
        last_hop(turn, True).wait_recv()
        return carry

    lax.fori_loop(1, seq_total, last_end, 0)


def bring_home(normed, dproj, columns, small, grad, gnorm, heads, gain_row, collective_id):
    seq_total, width_total = lax.axis_size("seq"), lax.axis_size("width")
    width = heads * HEAD_DIM
    total_rows, model_width = normed.shape
    depth = model_width // seq_total
    quarter = depth // width_total
    shard = (INNER + CONV + HEADS) // width_total
    slots = max(
        ((group + 1) * shard - 1) // width - group * shard // width + 1
        for group in range(width_total)
    )
    all_columns = dproj.shape[1]
    layout = (seq_total, width_total, quarter, width, slots, shard, gain_row)
    rest = all_columns - 2 * width
    sub, cols = width // width_total, model_width // seq_total
    owners = seq_total // width_total
    dma = pltpu.SemaphoreType.DMA
    vmem = pl.BlockSpec(memory_space=pltpu.VMEM)
    flops = 2 * total_rows * model_width * all_columns
    return layout, pl.pallas_call(
        partial(home_kernel, layout),
        in_specs=[ANY, vmem, vmem, vmem, ANY, vmem],
        out_specs=[ANY, ANY, ANY, vmem],
        out_shape=[
            jax.ShapeDtypeStruct((slots, width_total, quarter, width), BF16),
            jax.ShapeDtypeStruct((seq_total, width_total, quarter, rest), BF16),
            jax.ShapeDtypeStruct((owners, width_total, sub, cols), BF16),
            jax.ShapeDtypeStruct((seq_total,) + small.shape, F32),
        ],
        scratch_shapes=[
            pltpu.VMEM((2, min(total_rows, 2048), TILE), BF16),
            pltpu.VMEM((TILE, all_columns), F32),
            pltpu.VMEM((width, TILE), F32),
            pltpu.VMEM((seq_total, width_total, quarter, all_columns), BF16),
            pltpu.VMEM((seq_total, width_total, quarter, all_columns), BF16),
            pltpu.VMEM((seq_total, quarter, width), BF16),
            pltpu.VMEM((seq_total, quarter, width), BF16),
            pltpu.VMEM((seq_total, quarter, rest), BF16),
            pltpu.VMEM((seq_total, width_total, sub, cols), BF16),
            pltpu.VMEM((seq_total, width_total, sub, cols), BF16),
            pltpu.VMEM((seq_total, sub, cols), BF16),
            pltpu.VMEM(small.shape, F32),
            pltpu.VMEM((width_total,) + small.shape, F32),
            dma((2,)),
            dma((seq_total, width_total)),
            dma((seq_total, width_total)),
            dma((4, seq_total)),
            dma((slots, width_total)),
            dma((seq_total,)),
            dma((seq_total, width_total)),
            dma((seq_total, width_total)),
            dma((seq_total, width_total)),
            dma((seq_total,)),
            dma((owners, width_total)),
            dma((width_total,)),
            dma((width_total,)),
            dma((seq_total,)),
            dma((seq_total,)),
        ],
        compiler_params=pltpu.CompilerParams(
            collective_id=collective_id, has_side_effects=True, vmem_limit_bytes=56 << 20
        ),
        cost_estimate=pl.CostEstimate(
            flops=4 * flops, bytes_accessed=8 * normed.size, transcendentals=0
        ),
        name="bring_home",
    )(normed, dproj, columns, small, grad, gnorm)


def input_norm(hidden, in_gain):
    return hidden * lax.rsqrt(jnp.mean(hidden * hidden, axis=1, keepdims=True) + EPSILON) * in_gain


def own(value, start, count, axis=0):
    return lax.dynamic_slice_in_dim(value, start, count, axis)


def per_device(
    hidden_in,
    starts,
    in_gain,
    in_weight,
    conv_weight,
    conv_bias,
    step_bias,
    decay_log,
    skip_gain,
    gate_gain,
    out_weight,
    cotangent,
):
    seq_total = lax.axis_size("seq")
    seq_index = lax.axis_index("seq")
    group_index = lax.axis_index("width")
    micros, rows, model_width = hidden_in.shape[1:]
    heads = HEADS // seq_total
    width = heads * HEAD_DIM
    head_first = seq_index * heads
    col_first = seq_index * width
    depth = in_weight.shape[0]
    head_count = HEADS // 8 * jnp.left_shift(jnp.int32(1), group_index)
    active = head_count.astype(F32) * HEAD_DIM

    flat_hidden = hidden_in[0].reshape(micros * rows, model_width).astype(F32)
    flat_grad = cotangent[0].reshape(micros * rows, model_width)
    normed, norm_back = jax.vjp(input_norm, flat_hidden, in_gain)
    dt_pad = LANES
    width_total = lax.axis_size("width")
    quarter = depth // width_total
    in_quarter = own(in_weight, group_index * quarter, quarter)
    gates = in_quarter[:, :INNER].reshape(quarter, seq_total, width)
    xs = in_quarter[:, INNER : 2 * INNER].reshape(quarter, seq_total, width)
    bc = jnp.broadcast_to(
        in_quarter[:, None, 2 * INNER : INNER + CONV], (quarter, seq_total, 2 * STATE)
    )
    dts = in_quarter[:, INNER + CONV :].reshape(quarter, seq_total, heads)
    dts = jnp.pad(dts, ((0, 0), (0, 0), (0, dt_pad - heads)))
    pieces = jnp.concatenate([bc, xs, gates, dts], axis=2).transpose(1, 0, 2)
    all_normed, columns = gather_rows(normed.astype(BF16), pieces, 0)

    conv_width = 2 * STATE + width

    def conv_columns(value):
        return jnp.concatenate(
            [value[..., INNER:], own(value, col_first, width, value.ndim - 1)], axis=-1
        )

    taps = jnp.concatenate(
        [
            conv_columns(conv_weight),
            conv_columns(conv_bias[None]),
            jnp.zeros((8 - TAPS - 1, conv_width), F32),
        ],
        axis=0,
    )
    head_rows = jnp.stack(
        [own(step_bias, head_first, heads), -jnp.exp(own(decay_log, head_first, heads))]
    )
    head_table = jnp.pad(head_rows, ((0, 6), (0, LANES - heads)))
    head_mask = (head_first + jnp.arange(heads, dtype=jnp.int32) < head_count).astype(F32)
    cols = jnp.stack(
        [
            jnp.repeat(own(skip_gain, head_first, heads), HEAD_DIM),
            own(gate_gain, col_first, width),
            jnp.repeat(head_mask, HEAD_DIM),
        ]
    )
    cols = jnp.pad(cols, ((0, 5), (0, 0)))
    expand, gather, tri = tables(heads, rows)

    proj, gg, branch, mixed, states, tails, sums, all_grad = run_forward(
        micros,
        heads,
        rows,
        seq_total,
        starts[0],
        all_normed,
        columns,
        out_weight,
        flat_grad,
        taps,
        head_table,
        cols,
        expand,
        tri,
        3,
    )
    branch = lax.psum_scatter(branch, "seq", scatter_dimension=0, tiled=True)
    dnorm, sums = run_cross(micros, seq_total, all_grad, out_weight, gg, sums)
    sums = share(sums, "seq", 1)
    roots = lax.rsqrt(sums[:, : 2 * micros : 2] / active + EPSILON)
    own_roots = own(roots, seq_index, 1).reshape(micros * rows, 1)

    gnorm = (gg.astype(F32) * roots.reshape(seq_total * micros * rows, 1)).astype(BF16)
    dproj, gconv, gcols, ghead = run_backward(
        micros,
        heads,
        rows,
        seq_total,
        starts[0],
        active[None],
        proj,
        dnorm,
        mixed,
        states,
        tails,
        sums,
        taps,
        head_table,
        cols,
        expand,
        gather,
        tri,
    )
    grad_normed = lax.psum_scatter(
        mm_nt(dproj, columns).astype(BF16), "seq", scatter_dimension=0, tiled=True
    ).astype(F32)
    grad_hidden = norm_back(grad_normed)[0]
    hidden_grads = (flat_grad.astype(F32) + grad_hidden).astype(BF16)

    skip_heads = jnp.sum(gcols[0].reshape(heads, HEAD_DIM), axis=1)
    shared_part = gconv[:5, : 2 * STATE].reshape(-1)
    gain_row = shared_part.shape[0] // LANES
    own_part = jnp.concatenate(
        [
            gconv[:5, 2 * STATE :].reshape(-1),
            gcols[1],
            ghead[1, :heads],
            ghead[0, :heads],
            skip_heads,
        ]
    )
    small = jnp.concatenate([shared_part, jnp.zeros(model_width, F32), own_part])
    length = small.shape[0]
    small = jnp.pad(small, (0, -length % (8 * LANES))).reshape(-1, LANES)
    small, branch = lax.optimization_barrier((small, branch))
    layout, (zx, bcs, grad_out, small) = bring_home(
        all_normed, dproj, columns, small, all_grad, gnorm, heads, gain_row, 2
    )
    output = flat_hidden + branch.astype(F32) * own_roots
    slots, shard = layout[4], layout[5]
    tail = 2 * STATE + HEADS
    bcs = bcs.reshape(seq_total, depth, bcs.shape[3])
    bc_sum = jnp.sum(bcs[:, :, : 2 * STATE].astype(F32), axis=0).astype(BF16)
    dt_sum = bcs[:, :, 2 * STATE : 2 * STATE + heads].transpose(1, 0, 2).reshape(depth, HEADS)
    tail_slots = -(-tail // width)
    ends = jnp.pad(
        jnp.concatenate([bc_sum, dt_sum], axis=1), ((0, 0), (0, tail_slots * width - tail))
    )
    zx = zx.reshape(slots, depth, width).transpose(1, 0, 2).reshape(depth, slots * width)
    is_last = group_index == width_total - 1
    edge = (slots - tail_slots) * width
    zx = jnp.concatenate([zx[:, :edge], jnp.where(is_last, ends, zx[:, edge:])], axis=1)
    start = lax.rem(group_index * shard, width)
    shard_in = own(zx, start, shard, 1).astype(F32)
    shard_out = grad_out.reshape(seq_total // width_total * width, -1).astype(F32)
    small = small.reshape(seq_total, -1)
    shared_part = jnp.sum(small[:, : gain_row * LANES + model_width], axis=0)
    own_part = small[:, gain_row * LANES + model_width : length]

    bc_small = shared_part[: 10 * STATE].reshape(5, 2 * STATE)
    in_gain_sum = shared_part[10 * STATE :] / in_gain
    x_small = own_part[:, : 5 * width].reshape(seq_total, 5, width)
    x_small = x_small.transpose(1, 0, 2).reshape(5, INNER)
    conv_small = jnp.concatenate([x_small, bc_small], axis=1)
    gain_sum = own_part[:, 5 * width : 6 * width].reshape(INNER)
    head_sums = own_part[:, 6 * width :].reshape(seq_total, 3, heads)
    head_sums = head_sums.transpose(1, 0, 2).reshape(3, HEADS)
    shape = hidden_in.shape
    return (
        output.astype(BF16).reshape(shape),
        hidden_grads.reshape(shape),
        in_gain_sum,
        shard_in,
        conv_small[:4],
        conv_small[4],
        head_sums[0],
        head_sums[1],
        head_sums[2],
        gain_sum,
        shard_out,
    )


def solution(mesh):
    in_specs = (
        P("width", None, "seq", None),
        P("width", None, None),
        P(),
        P("seq", None),
        P(),
        P(),
        P(),
        P(),
        P(),
        P(),
        P("seq", None),
        P("width", None, "seq", None),
    )
    out_specs = (
        P("width", None, "seq", None),
        P("width", None, "seq", None),
        P(),
        P("seq", "width"),
        P(),
        P(),
        P(),
        P(),
        P(),
        P(),
        P("width", "seq"),
    )
    return jax.shard_map(
        per_device, mesh=mesh, in_specs=in_specs, out_specs=out_specs, check_vma=False
    )
```

```python
from functools import partial

import jax
import jax.numpy as jnp
from jax import lax
from jax.experimental import pallas as pl
from jax.experimental.pallas import tpu as pltpu
from jax.sharding import PartitionSpec as P

INNER = 4096
HEADS = 64
HEAD_DIM = 64
STATE = 128
CONV = 4352
EPSILON = 1e-05
LANES = 128
TAPS = 4
NEG = -1e30
F32 = jnp.float32
BF16 = jnp.bfloat16


def mm(a, b):
    return lax.dot_general(a, b, (((1,), (0,)), ((), ())), preferred_element_type=F32)


def mm_nt(a, b):
    return lax.dot_general(a, b, (((1,), (1,)), ((), ())), preferred_element_type=F32)


def mm_tn(a, b):
    return lax.dot_general(a, b, (((0,), (0,)), ((), ())), preferred_element_type=F32)


def halves(value, axis):
    high = value.astype(BF16)
    low = (value - high.astype(F32)).astype(BF16)
    return jnp.concatenate([high, low], axis=axis)


def sigmoid(value):
    return 0.5 * jnp.tanh(0.5 * value) + 0.5


def prefix_sum(tri, value):
    high = value.astype(BF16)
    rest = value - high.astype(F32)
    middle = rest.astype(BF16)
    low = (rest - middle.astype(F32)).astype(BF16)
    parts = mm(tri, jnp.concatenate([high, middle, low], axis=1))
    width = value.shape[1]
    return parts[:, :width] + parts[:, width : 2 * width] + parts[:, 2 * width :]


def doc_number(starts_ref, micro, positions):
    count = jnp.zeros_like(positions)
    for item in range(starts_ref.shape[1]):
        count = count + (starts_ref[micro, item] <= positions).astype(jnp.int32)
    return count


MESH = pl.DeviceIdType.MESH
ANY = pl.BlockSpec(memory_space=pl.ANY)


def greet(axes):
    barrier = pltpu.get_barrier_semaphore()
    waits = 0
    for axis in axes:
        count, me = lax.axis_size(axis), lax.axis_index(axis)

        def hello(turn, carry):
            pl.semaphore_signal(
                barrier,
                inc=1,
                device_id={axis: lax.rem(me + turn, count)},
                device_id_type=MESH,
            )
            return carry

        lax.fori_loop(1, count, hello, 0)
        waits += count - 1
    pl.semaphore_wait(barrier, waits)


def remote(source, target, send, receive, device):
    return pltpu.make_async_remote_copy(
        src_ref=source,
        dst_ref=target,
        send_sem=send,
        recv_sem=receive,
        device_id=device,
        device_id_type=MESH,
    )


class Line:
    def __init__(self, source, out, sems):
        self.source, self.out = source, out
        self.up, self.down, self.receive, self.side_send, self.side_receive, self.keep = sems
        self.me = lax.axis_index("seq")
        self.chips = lax.axis_size("seq") // 2
        self.chip, self.core = self.me // 2, lax.rem(self.me, 2)
        self.parts, self.rows = source.shape[:2]

    def at(self, owner, part):
        return self.out.at[part, pl.ds(pl.multiple_of(owner * self.rows, 8), self.rows)]

    def line(self, source, owner_chip, part, target_chip, sems):
        return remote(
            source,
            self.at(owner_chip * 2 + self.core, part),
            sems.at[owner_chip, part],
            self.receive.at[owner_chip, part],
            {"seq": target_chip * 2 + self.core},
        )

    def side(self, source, owner_chip, part, from_sibling):
        core = 1 - self.core if from_sibling else self.core
        return remote(
            source,
            self.at(owner_chip * 2 + core, part),
            self.side_send.at[owner_chip, part],
            self.side_receive.at[owner_chip, part],
            {"seq": self.chip * 2 + 1 - self.core},
        )

    def stay(self, part):
        return pltpu.make_async_copy(
            self.source.at[part], self.at(self.me, part), self.keep.at[part]
        )

    def start(self):
        for part in range(self.parts):
            here = self.source.at[part]

            @pl.when(self.chip + 1 < self.chips)
            def _():
                self.line(here, self.chip, part, self.chip + 1, self.up).start()

            @pl.when(self.chip >= 1)
            def _():
                self.line(here, self.chip, part, self.chip - 1, self.down).start()

            self.side(here, self.chip, part, False).start()
            self.stay(part).start()

    def events(self):
        return (self.chips - 1) * self.parts

    def hop(self, event):
        turn, part = event // self.parts + 1, lax.rem(event, self.parts)
        below, above = self.chip - turn, self.chip + turn

        @pl.when(below >= 0)
        def _():
            here = self.at(below * 2 + self.core, part)
            self.line(here, below, part, self.chip, self.up).wait_recv()

            @pl.when(self.chip + 1 < self.chips)
            def _():
                self.line(here, below, part, self.chip + 1, self.up).start()

            self.side(here, below, part, False).start()

        @pl.when(above < self.chips)
        def _():
            here = self.at(above * 2 + self.core, part)
            self.line(here, above, part, self.chip, self.down).wait_recv()

            @pl.when(self.chip >= 1)
            def _():
                self.line(here, above, part, self.chip - 1, self.down).start()

            self.side(here, above, part, False).start()

    def hops(self, first):
        def body(event, carry):
            self.hop(event)
            return carry

        lax.fori_loop(first, self.events(), body, 0)

    def finish(self):
        def body(owner_chip, carry):
            for part in range(self.parts):
                here = self.at(owner_chip * 2 + self.core, part)

                @pl.when((owner_chip <= self.chip) & (self.chip + 1 < self.chips))
                def _():
                    self.line(here, owner_chip, part, self.chip + 1, self.up).wait_send()

                @pl.when((owner_chip >= self.chip) & (self.chip >= 1))
                def _():
                    self.line(here, owner_chip, part, self.chip - 1, self.down).wait_send()

                self.side(here, owner_chip, part, False).wait_send()
                self.side(here, owner_chip, part, True).wait_recv()
            return carry

        lax.fori_loop(0, self.chips, body, 0)
        for part in range(self.parts):
            self.stay(part).wait()


def line_sems(chips, parts):
    return [pltpu.SemaphoreType.DMA((chips, parts))] * 5 + [pltpu.SemaphoreType.DMA((parts,))]


class Chunk:
    def __init__(self, starts_ref, micro, chunk, rows, raw_dt, head_ref, expand, tri):
        first = chunk * rows
        column = lax.broadcasted_iota(jnp.int32, (rows, 1), 0) + first
        line = lax.broadcasted_iota(jnp.int32, (1, rows), 1) + first
        doc_col = doc_number(starts_ref, micro, column)
        doc_row = doc_number(starts_ref, micro, line)
        self.same = [
            (doc_number(starts_ref, micro, column - offset) == doc_col).astype(F32)
            for offset in range(1, TAPS)
        ]
        before = jnp.int32(0)
        last = jnp.int32(0)
        for item in range(starts_ref.shape[1]):
            before = before + (starts_ref[micro, item] <= first - 1).astype(jnp.int32)
            last = last + (starts_ref[micro, item] <= first + rows - 1).astype(jnp.int32)
        carry = (doc_col == before).astype(F32)
        same_last = (doc_col == last).astype(F32)
        self.bias = jnp.where((column >= line) & (doc_col == doc_row), 0.0, NEG)
        self.shifted_dt = raw_dt + head_ref[0:1]
        self.step = jnp.maximum(self.shifted_dt, 0.0) + jnp.log1p(
            jnp.exp(-jnp.abs(self.shifted_dt))
        )
        self.log_keep = self.step * head_ref[1:2]
        self.cum = prefix_sum(tri, self.log_keep)
        self.cum_t = self.cum.T
        carried = jnp.exp(self.cum) * carry
        left = jnp.exp(self.cum[rows - 1 :] - self.cum) * same_last
        spread = mm(
            halves(jnp.concatenate([self.step, carried, left], axis=0), 1), expand
        )
        self.step_cols = spread[:rows]
        self.carry_cols = spread[rows : 2 * rows]
        self.left_cols = spread[2 * rows :]
        self.keep_all = self.carry_cols[rows - 1 :]

    def decay(self, head):
        return jnp.exp(self.cum[:, head : head + 1] - self.cum_t[head : head + 1] + self.bias)


def head_groups(heads):
    size = 2 if heads % 2 == 0 else 1
    return size, heads // size


def stacked(value, size):
    if size == 1:
        return value.astype(BF16)
    lane = lax.broadcasted_iota(jnp.int32, value.shape, 1)
    first = jnp.where(lane < HEAD_DIM, value, 0.0)
    second = jnp.where(lane < HEAD_DIM, 0.0, value)
    return jnp.concatenate([first, second], axis=0).astype(BF16)


def convolved(ext, micro, rows, taps_ref, same):
    current = ext[micro, 8 : 8 + rows, :]
    total = taps_ref[TAPS : TAPS + 1] + taps_ref[TAPS - 1 : TAPS] * current
    views = []
    for offset in range(1, TAPS):
        view = ext[micro, 8 - offset : 8 - offset + rows, :] * same[offset - 1]
        views.append(view)
        total = total + taps_ref[TAPS - 1 - offset : TAPS - offset] * view
    return current, views, total


def forward_kernel(
    micros,
    heads,
    starts_ref,
    x_ref,
    weight_ref,
    out_weight_ref,
    g_ref,
    table_ref,
    heads_ref,
    expand_ref,
    tri_ref,
    proj_ref,
    gg_ref,
    branch_ref,
    mixed_ref,
    states_ref,
    tails_ref,
    sums_ref,
    taps_ref,
    cols_ref,
    head_ref,
    g_out,
    ext,
    state,
    *sems,
):
    chunk, chunks = pl.program_id(0), pl.num_programs(0)
    rows = x_ref.shape[1]
    width = heads * HEAD_DIM
    conv_width = 2 * STATE + width
    size, groups = head_groups(heads)
    line = Line(g_ref, g_out, sems)
    early = min((g_out.shape[1] // g_ref.shape[1] - 1) // 2, line.events())

    @pl.when(chunk == 0)
    def _():
        greet(("seq",))
        line.start()

    @pl.when((lax.rem(chunk, 2) == 0) & (chunk >= 2) & (chunk // 2 - 1 < early))
    def _():
        line.hop(chunk // 2 - 1)

    @pl.when(chunk == 0)
    def _():
        ext[:, :8, :] = jnp.zeros((micros, 8, conv_width), F32)
        state[...] = jnp.zeros_like(state)
        me = lax.axis_index("seq")
        local = pltpu.roll(
            table_ref[:, :INNER], lax.rem(INNER - me * width, jnp.int32(INNER)), 1
        )[:, :width]
        taps_ref[:, : 2 * STATE] = table_ref[:, INNER:]
        taps_ref[:, 2 * STATE :] = local
        head_row = me * heads + (
            lax.broadcasted_iota(jnp.int32, (1, width), 1) // HEAD_DIM
        )
        limit = HEADS // 8 * jnp.left_shift(jnp.int32(1), lax.axis_index("width"))
        cols_ref[0:1] = local[6:7]
        cols_ref[1:2] = local[5:6]
        cols_ref[2:3] = (head_row < limit).astype(F32)
        cols_ref[3:8] = jnp.zeros((5, width), F32)
        head_ref[...] = pltpu.roll(
            heads_ref[...], lax.rem(LANES - me * heads, jnp.int32(LANES)), 1
        )

    skip, gain, mask = cols_ref[0:1], cols_ref[1:2], cols_ref[2:3]
    rows_in = x_ref[...].reshape(micros * rows, x_ref.shape[2])
    proj_ref[...] = mm(rows_in, weight_ref[...]).astype(BF16).reshape(proj_ref.shape)
    sums, gated_gains = [], []
    for micro in range(micros):
        tails_ref[micro] = ext[micro, :8, :]
        ext[micro, 8 : 8 + rows, :] = proj_ref[micro, :, :conv_width].astype(F32)
        raw_dt = proj_ref[micro, :, conv_width + width :].astype(F32)
        at = Chunk(
            starts_ref, micro, chunk, rows, raw_dt, head_ref, expand_ref[...], tri_ref[...]
        )
        conv = convolved(ext, micro, rows, taps_ref, at.same)[2]
        act = conv * sigmoid(conv)
        write = act[:, :STATE].astype(BF16)
        read = act[:, STATE : 2 * STATE].astype(BF16)
        x_heads = act[:, 2 * STATE :]
        scores = mm_nt(read, write)
        inputs = x_heads * at.step_cols
        state_in = state[micro]
        state_low = state_in.astype(BF16)
        states_ref[micro] = state_low
        outs = []
        for group in range(groups):
            matrices = [
                (at.decay(group * size + item) * scores).astype(BF16) for item in range(size)
            ]
            span = slice(group * size * HEAD_DIM, (group + 1) * size * HEAD_DIM)
            outs.append(mm(jnp.concatenate(matrices, axis=1), stacked(inputs[:, span], size)))
        mixed = jnp.concatenate(outs, axis=1) + at.carry_cols * mm(read, state_low)
        state[micro] = at.keep_all * state_in + mm_tn(
            write, (inputs * at.left_cols).astype(BF16)
        )
        mixed = mixed + skip * x_heads
        mixed_ref[micro] = mixed
        gate = proj_ref[micro, :, conv_width : conv_width + width].astype(F32)
        gated = mask * mixed * (gate * sigmoid(gate))
        gated_gain = (gated * gain).astype(BF16)
        gg_ref[micro] = gated_gain
        gated_gains.append(gated_gain)
        square = jnp.sum(gated * gated, axis=1, keepdims=True)
        lane = lax.broadcasted_iota(jnp.int32, (rows, LANES), 1)
        sums.append(jnp.where(lane == 0, square, 0.0).T[:2])
        ext[micro, :8, :] = ext[micro, rows : rows + 8, :]
    pad = sums_ref.shape[0] - 2 * micros
    if pad:
        sums.append(jnp.zeros((pad, rows), F32))
    sums_ref[...] = jnp.concatenate(sums, axis=0)
    branch_ref[...] = mm(jnp.concatenate(gated_gains, axis=0), out_weight_ref[...]).astype(BF16)

    @pl.when(chunk == chunks - 1)
    def _():
        line.hops(early)
        line.finish()


def cross_kernel(
    g_ref, out_weight_ref, gg_ref, sums_ref, dnorm_ref, total_ref, mine, slots, send, receive
):
    chunk, chunks = pl.program_id(0), pl.num_programs(0)
    micros, rows, model_width = g_ref.shape
    me = lax.axis_index("seq")

    @pl.when(chunk == 0)
    def _():
        greet(("seq",))

    grads = g_ref[...].reshape(micros * rows, model_width)
    dnorm = mm_nt(grads, out_weight_ref[...])
    gg = gg_ref[...].reshape(micros * rows, dnorm.shape[1])
    dnorm_ref[...] = dnorm.reshape(dnorm_ref.shape)
    cross = jnp.sum(dnorm * gg.astype(F32), axis=1, keepdims=True)
    lane = lax.broadcasted_iota(jnp.int32, (rows, LANES), 1)
    lines = []
    for micro in range(micros):
        part = cross[micro * rows : (micro + 1) * rows]
        lines.append(jnp.where(lane == 1, part, 0.0).T[:2])
    pad = sums_ref.shape[0] - 2 * micros
    if pad:
        lines.append(jnp.zeros((pad, rows), F32))
    mine[chunk] = sums_ref[...] + jnp.concatenate(lines, axis=0)

    @pl.when(chunk == chunks - 1)
    def _():
        def copy(turn, owner):
            peer = lax.rem(me + turn, chunks)
            return remote(
                mine, slots.at[owner], send.at[peer], receive.at[owner], {"seq": peer}
            )

        def start(turn, carry):
            copy(turn, me).start()
            return carry

        def finish(turn, carry):
            copy(turn, me).wait_send()
            copy(turn, lax.rem(me + turn, chunks)).wait_recv()
            return carry

        lax.fori_loop(1, chunks, start, 0)
        slots[me] = mine[...]
        lax.fori_loop(1, chunks, finish, 0)

        def add(owner, total):
            return total + slots[owner]

        total_ref[...] = lax.fori_loop(1, chunks, add, slots[0])


def backward_kernel(
    micros,
    heads,
    starts_ref,
    active_ref,
    proj_ref,
    dnorm_ref,
    mixed_ref,
    states_ref,
    tails_ref,
    sums_ref,
    weight_ref,
    taps_ref,
    head_ref,
    cols_ref,
    expand_ref,
    gather_ref,
    tri_ref,
    dproj_ref,
    partial_ref,
    gconv_ref,
    gcols_ref,
    ghead_ref,
    ext,
    heads_ext,
    dstate,
):
    chunks = pl.num_programs(0)
    step_index = pl.program_id(0)
    rows = proj_ref.shape[1]

    @pl.when(step_index == 0)
    def _():
        heads_ext[:, :, rows:, :] = jnp.zeros((micros, TAPS - 1, 8, ext.shape[2]), F32)
        dstate[...] = jnp.zeros_like(dstate)
        gconv_ref[...] = jnp.zeros_like(gconv_ref)
        gcols_ref[...] = jnp.zeros_like(gcols_ref)
        ghead_ref[...] = jnp.zeros_like(ghead_ref)

    for micro in range(micros):
        backward_rows(
            micro,
            heads,
            chunks - 1 - step_index,
            starts_ref,
            active_ref,
            proj_ref.at[micro],
            dnorm_ref.at[micro],
            mixed_ref.at[micro],
            states_ref.at[micro],
            tails_ref.at[micro],
            sums_ref,
            taps_ref,
            head_ref,
            cols_ref,
            expand_ref,
            gather_ref,
            tri_ref,
            dproj_ref.at[micro],
            gconv_ref,
            gcols_ref,
            ghead_ref,
            ext,
            heads_ext.at[micro],
            dstate.at[micro],
        )
    d_rows = dproj_ref[...].reshape(micros * rows, dproj_ref.shape[2])
    partial_ref[...] = mm_nt(d_rows, weight_ref[...]).astype(BF16)

    @pl.when(step_index == chunks - 1)
    def _():
        ghead_ref[2:3] = mm(halves(gcols_ref[...], 1), gather_ref[...])[0:1]


def backward_rows(
    micro,
    heads,
    chunk,
    starts_ref,
    active_ref,
    proj_ref,
    dnorm_ref,
    mixed_ref,
    states_ref,
    tails_ref,
    sums_ref,
    taps_ref,
    head_ref,
    cols_ref,
    expand_ref,
    gather_ref,
    tri_ref,
    dproj_ref,
    gconv_ref,
    gcols_ref,
    ghead_ref,
    ext,
    heads_ext,
    dstate,
):
    rows = proj_ref.shape[0]
    width = heads * HEAD_DIM
    conv_width = 2 * STATE + width
    size, groups = head_groups(heads)
    skip, gain, mask = cols_ref[0:1], cols_ref[1:2], cols_ref[2:3]
    tri = tri_ref[...]
    gather = gather_ref[...]
    inverse_active = 1.0 / active_ref[0]
    sums = jnp.concatenate(
        [sums_ref[...], jnp.zeros((LANES - sums_ref.shape[0], rows), F32)], axis=0
    ).T
    ext[micro, :8, :] = tails_ref[...]
    ext[micro, 8 : 8 + rows, :] = proj_ref[:, :conv_width].astype(F32)
    raw_dt = proj_ref[:, conv_width + width :].astype(F32)
    at = Chunk(starts_ref, micro, chunk, rows, raw_dt, head_ref, expand_ref[...], tri)
    current, views, conv = convolved(ext, micro, rows, taps_ref, at.same)
    conv_sig = sigmoid(conv)
    act = conv * conv_sig
    write = act[:, :STATE].astype(BF16)
    read = act[:, STATE : 2 * STATE].astype(BF16)
    x_heads = act[:, 2 * STATE :]
    scores = mm_nt(read, write)
    inputs = x_heads * at.step_cols

    gate = proj_ref[:, conv_width : conv_width + width].astype(F32)
    gate_sig = sigmoid(gate)
    gate_act = gate * gate_sig
    masked = mask * mixed_ref[...]
    gated = masked * gate_act
    root = lax.rsqrt(sums[:, 2 * micro : 2 * micro + 1] * inverse_active + EPSILON)
    pull = root * root * root * sums[:, 2 * micro + 1 : 2 * micro + 2] * inverse_active
    dnorm = dnorm_ref[...]
    scaled = gated * root
    d_gated = root * dnorm * gain - gated * pull
    d_gate = d_gated * masked * (gate_sig * (1.0 + gate * (1.0 - gate_sig)))
    d_mixed = mask * d_gated * gate_act
    gcols_ref[0:1] += jnp.sum(d_mixed * x_heads, axis=0, keepdims=True)
    gcols_ref[1:2] += jnp.sum(dnorm * scaled, axis=0, keepdims=True)

    state_low = states_ref[...]
    d_state = dstate[...]
    d_state_low = d_state.astype(BF16)
    from_state = (d_mixed * at.carry_cols).astype(BF16)
    left = inputs * at.left_cols
    left_low = left.astype(BF16)
    d_left = mm(write, d_state_low)
    state_out = mm(read, state_low)
    d_read = mm_nt(from_state, state_low)
    d_write = mm_nt(left_low, d_state_low)
    d_mixed_low = d_mixed.astype(BF16).astype(F32)
    inputs_low = inputs.astype(BF16).astype(F32)
    d_scores = jnp.zeros((rows, rows), F32)
    locals_out, d_locals = [], []
    for group in range(groups):
        span = slice(group * size * HEAD_DIM, (group + 1) * size * HEAD_DIM)
        decays = [at.decay(group * size + item) for item in range(size)]
        matrices = [(decay * scores).astype(BF16) for decay in decays]
        in_stack = stacked(inputs[:, span], size)
        out_stack = stacked(d_mixed[:, span], size)
        locals_out.append(mm(jnp.concatenate(matrices, axis=1), in_stack))
        d_locals.append(mm_tn(jnp.concatenate(matrices, axis=0), out_stack))
        d_matrices = mm_nt(out_stack, inputs[:, span].astype(BF16))
        for item in range(size):
            d_scores = (
                d_scores + d_matrices[item * rows : (item + 1) * rows] * decays[item]
            )
    local_out = jnp.concatenate(locals_out, axis=1)
    d_local = jnp.concatenate(d_locals, axis=1)
    d_scores_low = d_scores.astype(BF16)
    d_read = d_read + mm(d_scores_low, write)
    d_write = d_write + mm_tn(d_scores_low, read)
    d_inputs = d_local + at.left_cols * d_left
    d_x = skip * d_mixed + d_inputs * at.step_cols

    passed = left * d_left
    cum_terms = (
        d_mixed_low * local_out
        + d_mixed * at.carry_cols * state_out
        - inputs_low * d_local
        - passed
    )
    kept = jnp.sum(d_state * at.keep_all * state_low.astype(F32), axis=0, keepdims=True)
    final = jnp.sum(passed, axis=0, keepdims=True) + kept
    stack = jnp.concatenate(
        [cum_terms, d_inputs * x_heads, jnp.broadcast_to(final, (8, width))], axis=0
    )
    reduced = mm(halves(stack, 1), gather)
    d_cum = reduced[:rows]
    d_step = reduced[rows : 2 * rows]
    final_row = reduced[2 * rows : 2 * rows + 1]
    total = jnp.sum(d_cum, axis=0, keepdims=True) + final_row
    d_log = total - prefix_sum(tri, d_cum) + d_cum
    d_step = d_step + d_log * head_ref[1:2]
    d_dt = d_step * sigmoid(at.shifted_dt)
    ghead_ref[0:1] += jnp.sum(d_log * at.log_keep, axis=0, keepdims=True)
    ghead_ref[1:2] += jnp.sum(d_dt, axis=0, keepdims=True)
    dstate[...] = at.keep_all * d_state + mm_tn(read, from_state)

    d_conv = jnp.concatenate([d_write, d_read, d_x], axis=1) * (
        conv_sig * (1.0 + conv * (1.0 - conv_sig))
    )
    gconv_ref[TAPS : TAPS + 1] += jnp.sum(d_conv, axis=0, keepdims=True)
    gconv_ref[TAPS - 1 : TAPS] += jnp.sum(d_conv * current, axis=0, keepdims=True)
    d_raw = taps_ref[TAPS - 1 : TAPS] * d_conv
    for offset in range(1, TAPS):
        tap = TAPS - 1 - offset
        gconv_ref[tap : tap + 1] += jnp.sum(
            d_conv * views[offset - 1], axis=0, keepdims=True
        )
        heads_ext[offset - 1, :rows, :] = d_conv * at.same[offset - 1]
        d_raw = d_raw + taps_ref[tap : tap + 1] * (
            heads_ext[offset - 1, offset : offset + rows, :]
        )
        heads_ext[offset - 1, rows:, :] = heads_ext[offset - 1, :8, :]
    dproj_ref[:, :conv_width] = d_raw.astype(BF16)
    dproj_ref[:, conv_width : conv_width + width] = d_gate.astype(BF16)
    dproj_ref[:, conv_width + width :] = d_dt.astype(BF16)


def constant(shape):
    return pl.BlockSpec(shape, lambda index: (0,) * len(shape))


def run_forward(
    heads, starts, x, weight, out_weight, g, table, head_table, expand, tri, collective_id
):
    micros, rows, model_width = g.shape
    chunks = x.shape[1] // rows
    width = heads * HEAD_DIM
    conv_width = 2 * STATE + width
    block = micros * rows
    sum_rows = -(-2 * micros // 8) * 8
    columns = weight.shape[1]

    def whole(value):
        return pl.BlockSpec(
            value.shape, lambda index: (0,) * value.ndim, pipeline_mode=pl.Buffered(1)
        )

    def row_block(size):
        return pl.BlockSpec((micros, rows, size), lambda index: (0, index, 0))

    return pl.pallas_call(
        partial(forward_kernel, micros, heads),
        grid=(chunks,),
        in_specs=[
            pl.BlockSpec(memory_space=pltpu.SMEM),
            row_block(model_width),
            whole(weight),
            whole(out_weight),
            ANY,
            whole(table),
            whole(head_table),
            whole(expand),
            whole(tri),
        ],
        out_specs=[
            row_block(columns),
            row_block(width),
            pl.BlockSpec((block, model_width), lambda index: (index, 0)),
            row_block(width),
            pl.BlockSpec((None, micros, STATE, width), lambda index: (index, 0, 0, 0)),
            pl.BlockSpec((None, micros, 8, conv_width), lambda index: (index, 0, 0, 0)),
            pl.BlockSpec((None, sum_rows, rows), lambda index: (index, 0, 0)),
            constant((8, conv_width)),
            constant((8, width)),
            constant((8, LANES)),
            ANY,
        ],
        out_shape=[
            jax.ShapeDtypeStruct((micros, chunks * rows, columns), BF16),
            jax.ShapeDtypeStruct((micros, chunks * rows, width), BF16),
            jax.ShapeDtypeStruct((chunks * block, model_width), BF16),
            jax.ShapeDtypeStruct((micros, chunks * rows, width), F32),
            jax.ShapeDtypeStruct((chunks, micros, STATE, width), BF16),
            jax.ShapeDtypeStruct((chunks, micros, 8, conv_width), F32),
            jax.ShapeDtypeStruct((chunks, sum_rows, rows), F32),
            jax.ShapeDtypeStruct((8, conv_width), F32),
            jax.ShapeDtypeStruct((8, width), F32),
            jax.ShapeDtypeStruct((8, LANES), F32),
            jax.ShapeDtypeStruct((micros, chunks * rows, model_width), BF16),
        ],
        scratch_shapes=[
            pltpu.VMEM((micros, rows + 8, conv_width), F32),
            pltpu.VMEM((micros, STATE, width), F32),
        ]
        + line_sems(chunks // 2, micros),
        compiler_params=pltpu.CompilerParams(
            collective_id=collective_id, has_side_effects=True, vmem_limit_bytes=56 << 20
        ),
        cost_estimate=pl.CostEstimate(
            flops=60 * 10**9, bytes_accessed=150 * 10**6, transcendentals=0
        ),
        name="mixer_forward",
    )(starts, x, weight, out_weight, g, table, head_table, expand, tri)


def run_cross(g, out_weight, gg, sums, collective_id):
    chunks = sums.shape[0]
    micros, all_rows, model_width = g.shape
    rows, width = all_rows // chunks, gg.shape[2]

    def row_block(size):
        return pl.BlockSpec((micros, rows, size), lambda index: (0, index, 0))

    return pl.pallas_call(
        cross_kernel,
        grid=(chunks,),
        in_specs=[
            row_block(model_width),
            pl.BlockSpec(out_weight.shape, lambda index: (0, 0), pipeline_mode=pl.Buffered(1)),
            row_block(width),
            pl.BlockSpec((None,) + sums.shape[1:], lambda index: (index, 0, 0)),
        ],
        out_specs=[row_block(width), constant(sums.shape)],
        out_shape=[
            jax.ShapeDtypeStruct((micros, all_rows, width), F32),
            jax.ShapeDtypeStruct(sums.shape, F32),
        ],
        scratch_shapes=[
            pltpu.VMEM(sums.shape, F32),
            pltpu.VMEM((chunks,) + sums.shape, F32),
            pltpu.SemaphoreType.DMA((chunks,)),
            pltpu.SemaphoreType.DMA((chunks,)),
        ],
        compiler_params=pltpu.CompilerParams(
            collective_id=collective_id, has_side_effects=True, vmem_limit_bytes=60 << 20
        ),
        cost_estimate=pl.CostEstimate(
            flops=12 * 10**9, bytes_accessed=16 * 10**6, transcendentals=0
        ),
        name="cross_sums",
    )(g, out_weight, gg, sums)


def run_backward(
    heads, starts, active, proj, dnorm, mixed, states, tails, sums, weight, shared
):
    micros, all_rows, columns = proj.shape
    chunks = sums.shape[0]
    rows = all_rows // chunks
    width = heads * HEAD_DIM
    conv_width = 2 * STATE + width
    model_width = weight.shape[0]

    def row_block(size):
        return pl.BlockSpec((micros, rows, size), lambda index: (0, chunks - 1 - index, 0))

    def chunk_block(shape):
        return pl.BlockSpec((None, micros) + shape, lambda index: (chunks - 1 - index, 0, 0, 0))

    return pl.pallas_call(
        partial(backward_kernel, micros, heads),
        grid=(chunks,),
        in_specs=[
            pl.BlockSpec(memory_space=pltpu.SMEM),
            pl.BlockSpec(memory_space=pltpu.SMEM),
            row_block(columns),
            row_block(width),
            row_block(width),
            chunk_block((STATE, width)),
            chunk_block((8, conv_width)),
            pl.BlockSpec((None, sums.shape[1], rows), lambda index: (chunks - 1 - index, 0, 0)),
            pl.BlockSpec(weight.shape, lambda index: (0, 0), pipeline_mode=pl.Buffered(1)),
        ]
        + [constant(item.shape) for item in shared],
        out_specs=[
            row_block(columns),
            pl.BlockSpec((micros * rows, model_width), lambda index: (chunks - 1 - index, 0)),
            constant((8, conv_width)),
            constant((8, width)),
            constant((8, LANES)),
        ],
        out_shape=[
            jax.ShapeDtypeStruct((micros, all_rows, columns), BF16),
            jax.ShapeDtypeStruct((micros * all_rows, model_width), BF16),
            jax.ShapeDtypeStruct((8, conv_width), F32),
            jax.ShapeDtypeStruct((8, width), F32),
            jax.ShapeDtypeStruct((8, LANES), F32),
        ],
        scratch_shapes=[
            pltpu.VMEM((micros, rows + 8, conv_width), F32),
            pltpu.VMEM((micros, TAPS - 1, rows + 8, conv_width), F32),
            pltpu.VMEM((micros, STATE, width), F32),
        ],
        compiler_params=pltpu.CompilerParams(vmem_limit_bytes=56 << 20),
        cost_estimate=pl.CostEstimate(
            flops=60 * 10**9, bytes_accessed=60 * 10**6, transcendentals=0
        ),
        name="mixer_backward",
    )(starts, active, proj, dnorm, mixed, states, tails, sums, weight, *shared)


def tables(heads, rows):
    width = heads * HEAD_DIM
    expand = (
        jnp.arange(LANES)[:, None] == jnp.arange(width)[None, :] // HEAD_DIM
    ).astype(BF16)
    tri = (jnp.arange(rows)[:, None] >= jnp.arange(rows)[None, :]).astype(BF16)
    return (
        jnp.concatenate([expand, expand], axis=0),
        jnp.concatenate([expand.T, expand.T], axis=0),
        tri,
    )


def gather_kernel(
    x_ref,
    w_ref,
    x_out,
    w_out,
    w_send,
    w_receive,
    f_send,
    f_receive,
    keep,
    *sems,
):
    seq_total, width_total = lax.axis_size("seq"), lax.axis_size("width")
    me, mine = lax.axis_index("seq"), lax.axis_index("width")
    quarter = w_ref.shape[1]
    depth = quarter * width_total
    line = Line(x_ref, x_out, sems)
    greet(("seq", "width"))

    def rows(source, group):
        return pl.ds(pl.multiple_of(source * depth + group * quarter, 8), quarter)

    def deal(turn, from_peer):
        peer = lax.rem(me + turn, seq_total)
        owner = peer if from_peer else me
        return remote(
            w_ref.at[peer],
            w_out.at[rows(owner, mine)],
            w_send.at[peer],
            w_receive.at[owner],
            {"seq": peer},
        )

    def deal_start(turn, carry):
        deal(turn, False).start()
        return carry

    lax.fori_loop(1, seq_total, deal_start, 0)
    w_own = pltpu.make_async_copy(w_ref.at[me], w_out.at[rows(me, mine)], keep.at[0])
    w_own.start()
    line.start()

    def forward(source, turn, from_peer):
        peer = lax.rem(mine + turn, width_total)
        group = peer if from_peer else mine
        where = w_out.at[rows(source, group)]
        return remote(
            where, where, f_send.at[peer, source], f_receive.at[group, source], {"width": peer}
        )

    def forward_start(source):
        for turn in range(1, width_total):
            forward(source, turn, False).start()

    def deal_pass(turn, carry):
        deal(turn, True).wait_recv()
        forward_start(lax.rem(me + turn, seq_total))
        return carry

    w_own.wait()
    forward_start(me)
    lax.fori_loop(1, seq_total, deal_pass, 0)
    line.hops(0)

    def deal_end(turn, carry):
        deal(turn, False).wait_send()
        return carry

    lax.fori_loop(1, seq_total, deal_end, 0)

    def forward_end(source, carry):
        for turn in range(1, width_total):
            forward(source, turn, False).wait_send()
            forward(source, turn, True).wait_recv()
        return carry

    lax.fori_loop(0, seq_total, forward_end, 0)
    line.finish()


def gather_rows(x, pieces, collective_id):
    seq_total, width_total = lax.axis_size("seq"), lax.axis_size("width")
    parts, rows, model_width = x.shape
    whole = (parts, rows * seq_total, model_width)
    weight = (seq_total * width_total * pieces.shape[1], pieces.shape[2])
    dma = pltpu.SemaphoreType.DMA
    return pl.pallas_call(
        gather_kernel,
        in_specs=[ANY] * 2,
        out_specs=[ANY] * 2,
        out_shape=[
            jax.ShapeDtypeStruct(whole, x.dtype),
            jax.ShapeDtypeStruct(weight, pieces.dtype),
        ],
        scratch_shapes=[
            dma((seq_total,)),
            dma((seq_total,)),
            dma((width_total, seq_total)),
            dma((width_total, seq_total)),
            dma((1,)),
        ]
        + line_sems(seq_total // 2, parts),
        compiler_params=pltpu.CompilerParams(
            collective_id=collective_id, has_side_effects=True
        ),
        cost_estimate=pl.CostEstimate(
            flops=80 * 10**9, bytes_accessed=200 * 10**6, transcendentals=0
        ),
        name="gather_rows",
    )(x, pieces)


TILE = 256
MIDDLE = 2
LAST = 4


def home_kernel(
    layout,
    normed_ref,
    columns_ref,
    gconv_ref,
    gcols_ref,
    ghead_ref,
    in_gain_ref,
    grad_ref,
    gnorm_ref,
    dproj_ref,
    shard_in_ref,
    shard_out_ref,
    taps_out,
    bias_out,
    gain_out,
    head_out,
    in_gain_out,
    zx_ref,
    bc_ref,
    go_ref,
    small_out,
    line_buffer,
    blocks_in,
    acc,
    out_acc,
    stage,
    arrived,
    last_arrived,
    sum_x,
    sum_z,
    sum_b,
    out_stage,
    out_arrived,
    out_last,
    sum_out,
    small_stage,
    small_slots,
    fetch,
    in_sems,
    zx_send,
    zx_receive,
    bc_send,
    bc_receive,
    out_sems,
    go_send,
    go_receive,
    small_send,
    small_receive,
    last_send,
    last_receive,
):
    seq_total, width_total, quarter, width, slots, shard, heads = layout
    micros = normed_ref.shape[0]
    me, mine = lax.axis_index("seq"), lax.axis_index("width")
    depth = quarter * width_total
    conv_width = 2 * STATE + width
    per_tile = TILE // depth
    tiles = seq_total // per_tile
    chunk_rows = blocks_in.shape[1]
    pieces = normed_ref.shape[1] // chunk_rows
    chunks = micros * pieces
    owners = seq_total // width_total
    barrier = pltpu.get_barrier_semaphore()
    count = seq_total * width_total
    place = mine * seq_total + me

    def turned(turn):
        return lax.rem(turn + me // per_tile, tiles)

    def fetch_copy(source, turn, chunk):
        tile = turned(turn)
        first = chunk % pieces * chunk_rows
        return pltpu.make_async_copy(
            source.at[
                chunk // pieces,
                pl.ds(first, chunk_rows),
                pl.ds(pl.multiple_of(tile * TILE, TILE), TILE),
            ],
            blocks_in.at[chunk % 2],
            fetch.at[chunk % 2],
        )

    def fetched(source, following, turn, chunk):
        fetch_copy(source, turn, chunk).wait()
        if chunk + 1 < chunks:
            fetch_copy(source, turn, chunk + 1).start()
        else:

            @pl.when(turn + 1 < tiles)
            def _():
                fetch_copy(source, turn + 1, 0).start()

            if following is not None:

                @pl.when(turn + 1 == tiles)
                def _():
                    fetch_copy(following, 0, 0).start()

        return blocks_in[chunk % 2]

    fetch_copy(grad_ref, 0, 0).start()

    def hello(turn, carry):
        peer = lax.rem(place + turn, count)
        pl.semaphore_signal(
            barrier,
            inc=1,
            device_id={"width": peer // seq_total, "seq": lax.rem(peer, seq_total)},
            device_id_type=MESH,
        )
        return carry

    lax.fori_loop(1, count, hello, 0)
    pl.semaphore_wait(barrier, count - 1)

    def both(is_here, source, target, send, receive, device, action):
        if action != "send":

            @pl.when(is_here)
            def _():
                stay = pltpu.make_async_copy(source, target, receive)
                if action == "start":
                    stay.start()
                else:
                    stay.wait()

        @pl.when(jnp.logical_not(is_here))
        def _():
            away = remote(source, target, send, receive, device)
            if action == "start":
                away.start()
            elif action == "receive":
                away.wait_recv()
            else:
                away.wait_send()

    sub, cols = out_stage.shape[2:]
    per_out = TILE // cols

    upper, lower = mine // 2, lax.rem(mine, 2)

    def order(block):
        odd = lax.rem(block, 2)
        even = 1 - odd
        first = odd * upper + even * lower
        second = odd * lower + even * upper
        across = 2 * (1 - upper) + lower
        beside = 2 * upper + 1 - lower
        return first, second, odd * across + even * beside, odd * beside + even * across

    def slot_of(block, group):
        odd = lax.rem(block, 2)
        return odd * group + (1 - odd) * (group % 2 * 2 + group // 2)

    class Meeting:
        def __init__(self, parts, come, last, sems):
            self.parts, self.come, self.last, self.sems = parts, come, last, sems

        def first(self, block):
            side, _, partner, _ = order(block)
            return remote(
                self.parts.at[block, pl.ds(2 * (1 - side), 2)],
                self.come.at[block],
                self.sems.at[0, block],
                self.sems.at[1, block],
                {"width": partner},
            )

        def second(self, block):
            side, place, _, partner = order(block)
            return remote(
                self.parts.at[block, 2 * side + 1 - place],
                self.last.at[block],
                self.sems.at[2, block],
                self.sems.at[3, block],
                {"width": partner},
            )

        def middle(self, block):
            self.first(block).wait_recv()
            side = order(block)[0]
            for item in range(2):
                slot = 2 * side + item
                total = self.parts[block, slot].astype(F32) + self.come[block, item].astype(F32)
                self.parts[block, slot] = total.astype(BF16)
            self.second(block).start()

        def total(self, block):
            self.second(block).wait_recv()
            side, place = order(block)[:2]
            return self.parts[block, 2 * side + place].astype(F32) + self.last[block].astype(F32)

        def sent(self, block):
            self.first(block).wait_send()
            self.second(block).wait_send()

    out_meeting = Meeting(out_stage, out_arrived, out_last, out_sems)
    in_meeting = Meeting(stage, arrived, last_arrived, in_sems)

    def each(turn, per, act):
        for item in range(per):
            act(turned(turn) * per + item)

    go_owner = me // owners

    def go_copy(target, action):
        both(
            (go_owner == mine) & (target == me),
            sum_out.at[target],
            go_ref.at[lax.rem(me, owners), mine],
            go_send.at[target],
            go_receive.at[lax.rem(me, owners), mine],
            {"width": go_owner, "seq": target},
            action,
        )

    def out_combine(block):
        sum_out[block] = out_meeting.total(block).astype(BF16)
        go_copy(block, "start")

    def out_multiply(turn, carry):
        tile = turned(turn)
        for chunk in range(chunks):
            block = fetched(grad_ref, normed_ref, turn, chunk)
            first = chunk % pieces * chunk_rows
            part = mm_tn(gnorm_ref[chunk // pieces, first : first + chunk_rows, :], block)
            out_acc[...] = part if chunk == 0 else out_acc[...] + part
        for item in range(per_out):
            block = tile * per_out + item
            for group in range(width_total):
                out_stage[block, slot_of(block, group)] = out_acc[
                    group * sub : (group + 1) * sub, item * cols : (item + 1) * cols
                ].astype(BF16)
            out_meeting.first(block).start()

        @pl.when(turn >= MIDDLE)
        def _():
            each(turn - MIDDLE, per_out, out_meeting.middle)

        @pl.when(turn >= LAST)
        def _():
            each(turn - LAST, per_out, out_combine)

        return carry

    lax.fori_loop(0, tiles, out_multiply, 0)
    conv_end = conv_width + width
    small_stage[:, :conv_width] = gconv_ref[...]
    small_stage[:, conv_width:conv_end] = gcols_ref[...]
    small_stage[:, conv_end : conv_end + LANES] = ghead_ref[...]

    def block_copy(sums, sem_row, number, block, second, action):
        low = (number * width) // shard
        high = ((number + 1) * width - 1) // shard
        owner = high if second else low
        slot = number - (owner * shard) // width

        def act():
            both(
                (owner == mine) & (block == me),
                sums.at[block],
                zx_ref.at[slot, mine],
                zx_send.at[sem_row, block],
                zx_receive.at[slot, mine],
                {"width": owner, "seq": block},
                action,
            )

        if second:
            pl.when(high != low)(act)
        else:
            act()

    def bc_copy(block, action):
        both(
            (mine == width_total - 1) & (block == me),
            sum_b.at[block],
            bc_ref.at[me, mine],
            bc_send.at[block],
            bc_receive.at[me, mine],
            {"width": width_total - 1, "seq": block},
            action,
        )

    def pieces_of(block, action):
        for second in (False, True):
            block_copy(sum_z, int(second), me, block, second, action)
            block_copy(sum_x, 2 + int(second), seq_total + me, block, second, action)
        bc_copy(block, action)

    def combine(block):
        low = in_meeting.total(block).astype(BF16)
        sum_b[block, :, : 2 * STATE] = low[:, : 2 * STATE]
        sum_x[block] = low[:, 2 * STATE : conv_width]
        sum_z[block] = low[:, conv_width : conv_width + width]
        sum_b[block, :, 2 * STATE :] = low[:, conv_width + width :]
        pieces_of(block, "start")

    def multiply(turn, carry):
        tile = turned(turn)
        for chunk in range(chunks):
            block = fetched(normed_ref, None, turn, chunk)
            first = chunk % pieces * chunk_rows
            part = mm_tn(
                block, dproj_ref[chunk // pieces, first : first + chunk_rows, :]
            )
            acc[...] = part if chunk == 0 else acc[...] + part
        for item in range(per_tile):
            block = tile * per_tile + item
            for group in range(width_total):
                row = item * depth + group * quarter
                stage[block, slot_of(block, group)] = acc[row : row + quarter].astype(BF16)
            in_meeting.first(block).start()
        weights = columns_ref[pl.ds(pl.multiple_of(tile * TILE, TILE), TILE), :]
        product = (acc[...] * weights.astype(F32)).astype(BF16)
        line = mm_nt(jnp.ones((8, product.shape[1]), BF16), product)
        small_stage[pl.ds(tile, 1), conv_end + LANES :] = line[:1]

        @pl.when(turn < MIDDLE)
        def _():
            each(tiles - MIDDLE + turn, per_out, out_meeting.middle)

        @pl.when(turn >= MIDDLE)
        def _():
            each(turn - MIDDLE, per_tile, in_meeting.middle)

        @pl.when(turn < LAST)
        def _():
            each(tiles - LAST + turn, per_out, out_combine)

        @pl.when(turn >= LAST)
        def _():
            each(turn - LAST, per_tile, combine)

        return carry

    lax.fori_loop(0, tiles, multiply, 0)

    def small_hop(turn, from_peer):
        peer = lax.rem(mine + turn, width_total)
        group = peer if from_peer else mine
        return remote(
            small_stage,
            small_slots.at[group],
            small_send.at[peer],
            small_receive.at[group],
            {"width": peer},
        )

    for turn in range(1, width_total):
        small_hop(turn, False).start()
    small_slots[mine] = small_stage[...]

    for tile in range(tiles - LAST, tiles):
        if tile >= tiles - MIDDLE:
            each(tile, per_tile, in_meeting.middle)
    for tile in range(tiles - LAST, tiles):
        each(tile, per_tile, combine)

    for turn in range(1, width_total):
        small_hop(turn, True).wait_recv()
        small_hop(turn, False).wait_send()
    total = small_slots[0]
    for group in range(1, width_total):
        total = total + small_slots[group]
    small_stage[...] = total

    def last_hop(turn, from_peer):
        peer = lax.rem(me + turn, seq_total)
        owner = peer if from_peer else me
        return remote(
            small_stage,
            small_out.at[owner],
            last_send.at[peer],
            last_receive.at[owner],
            {"seq": peer},
        )

    def last_start(turn, carry):
        last_hop(turn, False).start()
        return carry

    lax.fori_loop(1, seq_total, last_start, 0)
    small_out[me] = small_stage[...]

    def sent(block, carry):
        in_meeting.sent(block)
        out_meeting.sent(block)
        pieces_of(block, "send")
        go_copy(block, "send")
        return carry

    lax.fori_loop(0, seq_total, sent, 0)

    first = (mine * shard) // width

    def landed(slot, carry):
        number = first + slot
        source = lax.rem(number, seq_total)

        @pl.when((number < 2 * seq_total) & (number * width < (mine + 1) * shard))
        def _():
            for group in range(width_total):
                both(
                    (source == me) & (mine == group),
                    sum_z.at[me],
                    zx_ref.at[slot, group],
                    zx_send.at[0, me],
                    zx_receive.at[slot, group],
                    {"width": group, "seq": source},
                    "receive",
                )

        return carry

    lax.fori_loop(0, slots, landed, 0)

    @pl.when(mine == width_total - 1)
    def _():
        def bc_landed(source, carry):
            for group in range(width_total):
                both(
                    (source == me) & (mine == group),
                    sum_b.at[me],
                    bc_ref.at[source, group],
                    bc_send.at[me],
                    bc_receive.at[source, group],
                    {"width": group, "seq": source},
                    "receive",
                )
            return carry

        lax.fori_loop(0, seq_total, bc_landed, 0)

    for item in range(owners):
        for group in range(width_total):
            source = mine * owners + item
            both(
                (source == me) & (mine == group),
                sum_out.at[me],
                go_ref.at[item, group],
                go_send.at[me],
                go_receive.at[item, group],
                {"width": group, "seq": source},
                "receive",
            )

    def last_end(turn, carry):
        last_hop(turn, False).wait_send()
        last_hop(turn, True).wait_recv()
        return carry

    lax.fori_loop(1, seq_total, last_end, 0)

    edge = (slots - -(-(2 * STATE + HEADS) // width)) * width
    for group in range(width_total):
        for slot in range(slots):
            line_buffer[:, slot * width : (slot + 1) * width] = zx_ref[slot, group].astype(F32)

        @pl.when(mine == width_total - 1)
        def _():
            def bc_add(source, total):
                return total + bc_ref[source, group, :, : 2 * STATE].astype(F32)

            first_sum = bc_ref[0, group, :, : 2 * STATE].astype(F32)
            line_buffer[:, edge : edge + 2 * STATE] = lax.fori_loop(
                1, seq_total, bc_add, first_sum
            )
            for source in range(seq_total):
                at = edge + 2 * STATE + source * heads
                line_buffer[:, at : at + heads] = bc_ref[
                    source, group, :, 2 * STATE : 2 * STATE + heads
                ].astype(F32)

        total_lanes = line_buffer.shape[1]
        start = lax.rem(mine * shard, jnp.int32(width))
        rolled = pltpu.roll(
            line_buffer[...], lax.rem(total_lanes - start, jnp.int32(total_lanes)), 1
        )
        shard_in_ref[group * quarter : (group + 1) * quarter, :] = rolled[:, :shard]
    for item in range(owners):
        for group in range(width_total):
            row = item * width + group * sub
            shard_out_ref[row : row + sub, :] = go_ref[item, group].astype(F32)

    def small_add(source, total):
        return total + small_out[source]

    total = lax.fori_loop(1, seq_total, small_add, small_out[0])
    taps_out[:, INNER:] = total[:TAPS, : 2 * STATE]
    bias_out[:, INNER:] = total[TAPS : TAPS + 1, : 2 * STATE]
    in_gain_out[...] = total[:, conv_end + LANES :] / in_gain_ref[...]
    for source in range(seq_total):
        first = source * width
        taps_out[:, first : first + width] = small_out[source, :TAPS, 2 * STATE : conv_width]
        bias_out[:, first : first + width] = small_out[
            source, TAPS : TAPS + 1, 2 * STATE : conv_width
        ]
        gain_out[:, first : first + width] = small_out[source, 1:2, conv_width:conv_end]
        head_out[:, source * heads : (source + 1) * heads] = small_out[
            source, :, conv_end : conv_end + heads
        ]


def bring_home(normed, dproj, columns, smalls, in_gain, grad, gnorm, heads, collective_id):
    seq_total, width_total = lax.axis_size("seq"), lax.axis_size("width")
    width = heads * HEAD_DIM
    micros, group_rows, model_width = normed.shape
    depth = model_width // seq_total
    quarter = depth // width_total
    shard = (INNER + CONV + HEADS) // width_total
    slots = max(
        ((group + 1) * shard - 1) // width - group * shard // width + 1
        for group in range(width_total)
    )
    all_columns = dproj.shape[2]
    layout = (seq_total, width_total, quarter, width, slots, shard, heads)
    rest = all_columns - 2 * width
    sub, cols = width // width_total, model_width // seq_total
    owners = seq_total // width_total
    small = (8, 2 * STATE + 2 * width + LANES + TILE)
    lanes = -(-slots * width // LANES) * LANES
    dma = pltpu.SemaphoreType.DMA
    vmem = pl.BlockSpec(memory_space=pltpu.VMEM)
    return pl.pallas_call(
        partial(home_kernel, layout),
        in_specs=[ANY, vmem, vmem, vmem, vmem, vmem, ANY, vmem, vmem],
        out_specs=[vmem] * 7,
        out_shape=[
            jax.ShapeDtypeStruct((depth, shard), F32),
            jax.ShapeDtypeStruct((owners * width, cols), F32),
            jax.ShapeDtypeStruct((TAPS, CONV), F32),
            jax.ShapeDtypeStruct((1, CONV), F32),
            jax.ShapeDtypeStruct((1, INNER), F32),
            jax.ShapeDtypeStruct((8, HEADS), F32),
            jax.ShapeDtypeStruct(in_gain.shape, F32),
        ],
        scratch_shapes=[
            pltpu.VMEM((slots, width_total, quarter, width), BF16),
            pltpu.VMEM((seq_total, width_total, quarter, rest), BF16),
            pltpu.VMEM((owners, width_total, sub, cols), BF16),
            pltpu.VMEM((seq_total,) + small, F32),
            pltpu.VMEM((quarter, lanes), F32),
            pltpu.VMEM((2, min(group_rows, 1024), TILE), BF16),
            pltpu.VMEM((TILE, all_columns), F32),
            pltpu.VMEM((width, TILE), F32),
            pltpu.VMEM((seq_total, width_total, quarter, all_columns), BF16),
            pltpu.VMEM((seq_total, 2, quarter, all_columns), BF16),
            pltpu.VMEM((seq_total, quarter, all_columns), BF16),
            pltpu.VMEM((seq_total, quarter, width), BF16),
            pltpu.VMEM((seq_total, quarter, width), BF16),
            pltpu.VMEM((seq_total, quarter, rest), BF16),
            pltpu.VMEM((seq_total, width_total, sub, cols), BF16),
            pltpu.VMEM((seq_total, 2, sub, cols), BF16),
            pltpu.VMEM((seq_total, sub, cols), BF16),
            pltpu.VMEM((seq_total, sub, cols), BF16),
            pltpu.VMEM(small, F32),
            pltpu.VMEM((width_total,) + small, F32),
            dma((2,)),
            dma((4, seq_total)),
            dma((4, seq_total)),
            dma((slots, width_total)),
            dma((seq_total,)),
            dma((seq_total, width_total)),
            dma((4, seq_total)),
            dma((seq_total,)),
            dma((owners, width_total)),
            dma((width_total,)),
            dma((width_total,)),
            dma((seq_total,)),
            dma((seq_total,)),
        ],
        compiler_params=pltpu.CompilerParams(
            collective_id=collective_id, has_side_effects=True, vmem_limit_bytes=60 << 20
        ),
        cost_estimate=pl.CostEstimate(
            flops=150 * 10**9, bytes_accessed=8 * normed.size, transcendentals=0
        ),
        name="bring_home",
    )(normed, columns, *smalls, in_gain, grad, gnorm, dproj)


def own(value, start, count, axis=0):
    return lax.dynamic_slice_in_dim(value, start, count, axis)


def per_device(
    hidden_in,
    starts,
    in_gain,
    in_weight,
    conv_weight,
    conv_bias,
    step_bias,
    decay_log,
    skip_gain,
    gate_gain,
    out_weight,
    cotangent,
):
    seq_total = lax.axis_size("seq")
    seq_index = lax.axis_index("seq")
    group_index = lax.axis_index("width")
    micros, rows, model_width = hidden_in.shape[1:]
    heads = HEADS // seq_total
    width = heads * HEAD_DIM
    depth = in_weight.shape[0]
    head_count = HEADS // 8 * jnp.left_shift(jnp.int32(1), group_index)
    active = head_count.astype(F32) * HEAD_DIM

    hidden = hidden_in[0].astype(F32)
    grads = cotangent[0]
    root_in = lax.rsqrt(jnp.mean(hidden * hidden, axis=2, keepdims=True) + EPSILON)
    normed = (hidden * root_in * in_gain).astype(BF16)

    dt_pad = LANES
    width_total = lax.axis_size("width")
    quarter = depth // width_total
    in_quarter = own(in_weight, group_index * quarter, quarter)
    gates = in_quarter[:, :INNER].reshape(quarter, seq_total, width)
    xs = in_quarter[:, INNER : 2 * INNER].reshape(quarter, seq_total, width)
    bc = jnp.broadcast_to(
        in_quarter[:, None, 2 * INNER : INNER + CONV], (quarter, seq_total, 2 * STATE)
    )
    dts = in_quarter[:, INNER + CONV :].reshape(quarter, seq_total, heads)
    dts = jnp.pad(dts, ((0, 0), (0, 0), (0, dt_pad - heads)))
    pieces = jnp.concatenate([bc, xs, gates, dts], axis=2).transpose(1, 0, 2)
    all_normed, columns = gather_rows(normed, pieces, 0)

    def lane_pad(value):
        return jnp.pad(value, (0, CONV - INNER))[None]

    table = jnp.concatenate(
        [
            conv_weight,
            conv_bias[None],
            lane_pad(gate_gain),
            lane_pad(jnp.repeat(skip_gain, HEAD_DIM)),
            jnp.zeros((1, CONV), F32),
        ],
        axis=0,
    )
    head_table = jnp.pad(
        jnp.stack([step_bias, -jnp.exp(decay_log)]), ((0, 6), (0, LANES - HEADS))
    )
    expand, gather, tri = tables(heads, rows)

    proj, gg, branch, mixed, states, tails, sums, taps, cols, head, all_grad = run_forward(
        heads,
        starts[0],
        all_normed,
        columns,
        out_weight,
        grads,
        table,
        head_table,
        expand,
        tri,
        3,
    )
    branch = lax.psum_scatter(branch, "seq", scatter_dimension=0, tiled=True)
    dnorm, sums = run_cross(all_grad, out_weight, gg, sums, 1)
    roots = lax.rsqrt(sums[:, : 2 * micros : 2] / active + EPSILON)
    own_roots = own(roots, seq_index, 1).reshape(micros, rows, 1)
    all_roots = roots.transpose(1, 0, 2).reshape(micros, seq_total * rows, 1)
    gnorm = (gg.astype(F32) * all_roots).astype(BF16)

    dproj, partial_rows, *smalls = run_backward(
        heads,
        starts[0],
        active[None],
        proj,
        dnorm,
        mixed,
        states,
        tails,
        sums,
        columns,
        [taps, head, cols, expand, gather, tri],
    )
    scattered = lax.psum_scatter(partial_rows, "seq", scatter_dimension=0, tiled=True)
    head_sums, branch = lax.optimization_barrier((smalls[2], branch))
    home = bring_home(
        all_normed,
        dproj,
        columns,
        [smalls[0], smalls[1], head_sums],
        in_gain.reshape(-1, TILE),
        all_grad,
        gnorm,
        heads,
        2,
    )
    shard_in, shard_out, taps_sum, bias_sum, gain_sum, head_sums, in_gain_sum = home
    output = hidden + branch.reshape(hidden.shape).astype(F32) * own_roots
    scattered, in_gain_sum = lax.optimization_barrier((scattered, in_gain_sum))
    gained = scattered.reshape(hidden.shape).astype(F32) * in_gain
    pull = jnp.mean(gained * hidden, axis=2, keepdims=True) * (root_in * root_in * root_in)
    hidden_grads = grads.astype(F32) + root_in * gained - hidden * pull
    shape = hidden_in.shape
    return (
        output.astype(BF16).reshape(shape),
        hidden_grads.astype(BF16).reshape(shape),
        in_gain_sum.reshape(-1),
        shard_in,
        taps_sum,
        bias_sum[0],
        head_sums[1],
        head_sums[0],
        head_sums[2],
        gain_sum[0],
        shard_out,
    )


def solution(mesh):
    in_specs = (
        P("width", None, "seq", None),
        P("width", None, None),
        P(),
        P("seq", None),
        P(),
        P(),
        P(),
        P(),
        P(),
        P(),
        P("seq", None),
        P("width", None, "seq", None),
    )
    out_specs = (
        P("width", None, "seq", None),
        P("width", None, "seq", None),
        P(),
        P("seq", "width"),
        P(),
        P(),
        P(),
        P(),
        P(),
        P(),
        P("width", "seq"),
    )
    return jax.shard_map(
        per_device, mesh=mesh, in_specs=in_specs, out_specs=out_specs, check_vma=False
    )
```

```python
from functools import partial

import jax
import jax.numpy as jnp
from jax import lax
from jax.experimental import pallas as pl
from jax.experimental.pallas import tpu as pltpu
from jax.sharding import PartitionSpec as P

INNER = 4096
HEADS = 64
HEAD_DIM = 64
STATE = 128
CONV = 4352
EPSILON = 1e-05
LANES = 128
TAPS = 4
NEG = -1e30
F32 = jnp.float32
BF16 = jnp.bfloat16


def mm(a, b):
    return lax.dot_general(a, b, (((1,), (0,)), ((), ())), preferred_element_type=F32)


def mm_nt(a, b):
    return lax.dot_general(a, b, (((1,), (1,)), ((), ())), preferred_element_type=F32)


def mm_tn(a, b):
    return lax.dot_general(a, b, (((0,), (0,)), ((), ())), preferred_element_type=F32)


def halves(value, axis):
    high = value.astype(BF16)
    low = (value - high.astype(F32)).astype(BF16)
    return jnp.concatenate([high, low], axis=axis)


def sigmoid(value):
    return 0.5 * jnp.tanh(0.5 * value) + 0.5


def prefix_sum(tri, value):
    high = value.astype(BF16)
    rest = value - high.astype(F32)
    middle = rest.astype(BF16)
    low = (rest - middle.astype(F32)).astype(BF16)
    parts = mm(tri, jnp.concatenate([high, middle, low], axis=1))
    width = value.shape[1]
    return parts[:, :width] + parts[:, width : 2 * width] + parts[:, 2 * width :]


def doc_number(starts_ref, micro, positions):
    count = jnp.zeros_like(positions)
    for item in range(starts_ref.shape[1]):
        count = count + (starts_ref[micro, item] <= positions).astype(jnp.int32)
    return count


MESH = pl.DeviceIdType.MESH
ANY = pl.BlockSpec(memory_space=pl.ANY)


def greet(axes):
    barrier = pltpu.get_barrier_semaphore()
    waits = 0
    for axis in axes:
        count, me = lax.axis_size(axis), lax.axis_index(axis)

        def hello(turn, carry):
            pl.semaphore_signal(
                barrier,
                inc=1,
                device_id={axis: lax.rem(me + turn, count)},
                device_id_type=MESH,
            )
            return carry

        lax.fori_loop(1, count, hello, 0)
        waits += count - 1
    pl.semaphore_wait(barrier, waits)


def remote(source, target, send, receive, device):
    return pltpu.make_async_remote_copy(
        src_ref=source,
        dst_ref=target,
        send_sem=send,
        recv_sem=receive,
        device_id=device,
        device_id_type=MESH,
    )


class Line:
    def __init__(self, source, out, sems):
        self.source, self.out = source, out
        self.up, self.down, self.receive, self.side_send, self.side_receive, self.keep = sems
        self.me = lax.axis_index("seq")
        self.chips = lax.axis_size("seq") // 2
        self.chip, self.core = self.me // 2, lax.rem(self.me, 2)
        self.parts, self.rows = source.shape[:2]

    def at(self, owner, part):
        return self.out.at[part, pl.ds(pl.multiple_of(owner * self.rows, 8), self.rows)]

    def line(self, source, owner_chip, part, target_chip, sems):
        return remote(
            source,
            self.at(owner_chip * 2 + self.core, part),
            sems.at[owner_chip, part],
            self.receive.at[owner_chip, part],
            {"seq": target_chip * 2 + self.core},
        )

    def side(self, source, owner_chip, part, from_sibling):
        core = 1 - self.core if from_sibling else self.core
        return remote(
            source,
            self.at(owner_chip * 2 + core, part),
            self.side_send.at[owner_chip, part],
            self.side_receive.at[owner_chip, part],
            {"seq": self.chip * 2 + 1 - self.core},
        )

    def stay(self, part):
        return pltpu.make_async_copy(
            self.source.at[part], self.at(self.me, part), self.keep.at[part]
        )

    def start(self):
        for part in range(self.parts):
            here = self.source.at[part]

            @pl.when(self.chip + 1 < self.chips)
            def _():
                self.line(here, self.chip, part, self.chip + 1, self.up).start()

            @pl.when(self.chip >= 1)
            def _():
                self.line(here, self.chip, part, self.chip - 1, self.down).start()

            self.side(here, self.chip, part, False).start()
            self.stay(part).start()

    def events(self):
        return (self.chips - 1) * self.parts

    def hop(self, event):
        turn, part = event // self.parts + 1, lax.rem(event, self.parts)
        below, above = self.chip - turn, self.chip + turn

        @pl.when(below >= 0)
        def _():
            here = self.at(below * 2 + self.core, part)
            self.line(here, below, part, self.chip, self.up).wait_recv()

            @pl.when(self.chip + 1 < self.chips)
            def _():
                self.line(here, below, part, self.chip + 1, self.up).start()

            self.side(here, below, part, False).start()

        @pl.when(above < self.chips)
        def _():
            here = self.at(above * 2 + self.core, part)
            self.line(here, above, part, self.chip, self.down).wait_recv()

            @pl.when(self.chip >= 1)
            def _():
                self.line(here, above, part, self.chip - 1, self.down).start()

            self.side(here, above, part, False).start()

    def hops(self, first):
        def body(event, carry):
            self.hop(event)
            return carry

        lax.fori_loop(first, self.events(), body, 0)

    def finish(self):
        def body(owner_chip, carry):
            for part in range(self.parts):
                here = self.at(owner_chip * 2 + self.core, part)

                @pl.when((owner_chip <= self.chip) & (self.chip + 1 < self.chips))
                def _():
                    self.line(here, owner_chip, part, self.chip + 1, self.up).wait_send()

                @pl.when((owner_chip >= self.chip) & (self.chip >= 1))
                def _():
                    self.line(here, owner_chip, part, self.chip - 1, self.down).wait_send()

                self.side(here, owner_chip, part, False).wait_send()
                self.side(here, owner_chip, part, True).wait_recv()
            return carry

        lax.fori_loop(0, self.chips, body, 0)
        for part in range(self.parts):
            self.stay(part).wait()


def line_sems(chips, parts):
    return [pltpu.SemaphoreType.DMA((chips, parts))] * 5 + [pltpu.SemaphoreType.DMA((parts,))]


TILE = 256
MIDDLE = 2
LAST = 4


def greet_all():
    seq_total, width_total = lax.axis_size("seq"), lax.axis_size("width")
    count = seq_total * width_total
    place = lax.axis_index("width") * seq_total + lax.axis_index("seq")
    barrier = pltpu.get_barrier_semaphore()

    def hello(turn, carry):
        peer = lax.rem(place + turn, count)
        pl.semaphore_signal(
            barrier,
            inc=1,
            device_id={"width": peer // seq_total, "seq": lax.rem(peer, seq_total)},
            device_id_type=MESH,
        )
        return carry

    lax.fori_loop(1, count, hello, 0)
    pl.semaphore_wait(barrier, count - 1)


def both(is_here, source, target, send, receive, device, action):
    if action != "send":

        @pl.when(is_here)
        def _():
            stay = pltpu.make_async_copy(source, target, receive)
            if action == "start":
                stay.start()
            else:
                stay.wait()

    @pl.when(jnp.logical_not(is_here))
    def _():
        away = remote(source, target, send, receive, device)
        if action == "start":
            away.start()
        elif action == "receive":
            away.wait_recv()
        else:
            away.wait_send()


class Meeting:
    def __init__(self, parts, come, last, sems):
        self.parts, self.come, self.last, self.sems = parts, come, last, sems
        mine = lax.axis_index("width")
        self.upper, self.lower = mine // 2, lax.rem(mine, 2)

    def order(self, block):
        odd = lax.rem(block, 2)
        even = 1 - odd
        first = odd * self.upper + even * self.lower
        second = odd * self.lower + even * self.upper
        across = 2 * (1 - self.upper) + self.lower
        beside = 2 * self.upper + 1 - self.lower
        return first, second, odd * across + even * beside, odd * beside + even * across

    def slot(self, block, group):
        odd = lax.rem(block, 2)
        return odd * group + (1 - odd) * (group % 2 * 2 + group // 2)

    def first(self, block):
        side, _, partner, _ = self.order(block)
        return remote(
            self.parts.at[block, pl.ds(2 * (1 - side), 2)],
            self.come.at[block],
            self.sems.at[0, block],
            self.sems.at[1, block],
            {"width": partner},
        )

    def second(self, block):
        side, place, _, partner = self.order(block)
        return remote(
            self.parts.at[block, 2 * side + 1 - place],
            self.last.at[block],
            self.sems.at[2, block],
            self.sems.at[3, block],
            {"width": partner},
        )

    def middle(self, block):
        self.first(block).wait_recv()
        side = self.order(block)[0]
        for item in range(2):
            slot = 2 * side + item
            total = self.parts[block, slot].astype(F32) + self.come[block, item].astype(F32)
            self.parts[block, slot] = total.astype(BF16)
        self.second(block).start()

    def total(self, block):
        self.second(block).wait_recv()
        side, place = self.order(block)[:2]
        return self.parts[block, 2 * side + place].astype(F32) + self.last[block].astype(F32)

    def sent(self, block):
        self.first(block).wait_send()
        self.second(block).wait_send()


class Tiles:
    def __init__(self, source, blocks, sems, per_tile):
        self.source, self.blocks, self.sems, self.per_tile = source, blocks, sems, per_tile
        self.total = source.shape[2] // TILE
        self.chunk_rows = blocks.shape[1]
        self.pieces = source.shape[1] // self.chunk_rows
        self.chunks = source.shape[0] * self.pieces

    def turned(self, turn):
        return lax.rem(turn + lax.axis_index("seq") // self.per_tile, self.total)

    def fetch(self, turn, chunk):
        first = chunk % self.pieces * self.chunk_rows
        return pltpu.make_async_copy(
            self.source.at[
                chunk // self.pieces,
                pl.ds(first, self.chunk_rows),
                pl.ds(pl.multiple_of(self.turned(turn) * TILE, TILE), TILE),
            ],
            self.blocks.at[chunk % 2],
            self.sems.at[chunk % 2],
        )

    def begin(self):
        self.fetch(0, 0).start()
        self.fetch(0, 1).start()

    def block(self, turn, chunk):
        self.fetch(turn, chunk).wait()
        first = chunk % self.pieces * self.chunk_rows
        return chunk // self.pieces, slice(first, first + self.chunk_rows), self.blocks[chunk % 2]

    def used(self, turn, chunk):
        if chunk + 2 < self.chunks:
            self.fetch(turn, chunk + 2).start()
        else:

            @pl.when(turn + 1 < self.total)
            def _():
                self.fetch(turn + 1, chunk + 2 - self.chunks).start()

    def each(self, turn, act):
        for item in range(self.per_tile):
            act(self.turned(turn) * self.per_tile + item)


class OutGrad:
    def __init__(self, grad, gnorm, refs):
        (
            blocks,
            self.acc,
            self.stage,
            come,
            last,
            self.sums,
            self.landing,
            fetch,
            sems,
            self.send,
            self.receive,
        ) = refs
        self.gnorm = gnorm
        self.sub, self.cols = self.stage.shape[2:]
        self.meeting = Meeting(self.stage, come, last, sems)
        self.tiles = Tiles(grad, blocks, fetch, TILE // self.cols)
        self.width_total = lax.axis_size("width")
        self.seq_total = lax.axis_size("seq")
        self.owners = self.seq_total // self.width_total
        self.me, self.mine = lax.axis_index("seq"), lax.axis_index("width")

    def copy(self, target, action):
        owner = self.me // self.owners
        place = self.landing.at[lax.rem(self.me, self.owners), self.mine]
        receive = self.receive.at[lax.rem(self.me, self.owners), self.mine]
        both(
            (owner == self.mine) & (target == self.me),
            self.sums.at[target],
            place,
            self.send.at[target],
            receive,
            {"width": owner, "seq": target},
            action,
        )

    def combine(self, block):
        self.sums[block] = self.meeting.total(block).astype(BF16)
        self.copy(block, "start")

    def multiply(self, turn):
        for chunk in range(self.tiles.chunks):
            micro, rows, block = self.tiles.block(turn, chunk)
            part = mm_tn(self.gnorm[micro, rows, :], block)
            self.acc[...] = part if chunk == 0 else self.acc[...] + part
            self.tiles.used(turn, chunk)
        for item in range(self.tiles.per_tile):
            block = self.tiles.turned(turn) * self.tiles.per_tile + item
            for group in range(self.width_total):
                self.stage[block, self.meeting.slot(block, group)] = self.acc[
                    group * self.sub : (group + 1) * self.sub,
                    item * self.cols : (item + 1) * self.cols,
                ].astype(BF16)
            self.meeting.first(block).start()

    def finish(self, out_ref):
        def sent(block, carry):
            self.meeting.sent(block)
            self.copy(block, "send")
            return carry

        lax.fori_loop(0, self.seq_total, sent, 0)
        for item in range(self.owners):
            for group in range(self.width_total):
                source = self.mine * self.owners + item
                both(
                    (source == self.me) & (self.mine == group),
                    self.sums.at[self.me],
                    self.landing.at[item, group],
                    self.send.at[self.me],
                    self.receive.at[item, group],
                    {"width": group, "seq": source},
                    "receive",
                )
                row = (item * self.width_total + group) * self.sub
                out_ref[row : row + self.sub, :] = self.landing[item, group].astype(F32)


def out_grad_scratch(heads, group_rows, model_width):
    seq_total, width_total = lax.axis_size("seq"), lax.axis_size("width")
    sub, cols = heads * HEAD_DIM // width_total, model_width // seq_total
    owners = seq_total // width_total
    dma = pltpu.SemaphoreType.DMA
    return [
        pltpu.VMEM((2, min(group_rows, 1024), TILE), BF16),
        pltpu.VMEM((heads * HEAD_DIM, TILE), F32),
        pltpu.VMEM((seq_total, width_total, sub, cols), BF16),
        pltpu.VMEM((seq_total, 2, sub, cols), BF16),
        pltpu.VMEM((seq_total, sub, cols), BF16),
        pltpu.VMEM((seq_total, sub, cols), BF16),
        pltpu.VMEM((owners, width_total, sub, cols), BF16),
        dma((2,)),
        dma((4, seq_total)),
        dma((seq_total,)),
        dma((owners, width_total)),
    ]


class PairSum:
    def __init__(self, out, come, refs):
        self.out, self.come = out, come
        self.hold, self.leave, self.load, self.send, self.receive, self.local = refs
        me = lax.axis_index("seq")
        self.core, self.sibling = lax.rem(me, 2), me + 1 - 2 * lax.rem(me, 2)
        self.pairs = out.shape[0]

    def copy(self, pair):
        return remote(
            self.leave.at[lax.rem(pair, 2)],
            self.come.at[pair],
            self.send.at[pair],
            self.receive.at[pair],
            {"seq": self.sibling},
        )

    def put(self, position, earlier, block):
        pair = position // 2
        here = lax.rem(position, 2) == self.core

        @pl.when(here)
        def _():
            self.hold[lax.rem(pair, 2)] = block

        @pl.when(jnp.logical_not(here))
        def _():
            @pl.when((earlier >= 0) & (earlier < self.pairs))
            def _():
                self.copy(earlier).wait_send()

            self.leave[lax.rem(pair, 2)] = block
            self.copy(pair).start()

    def fetch(self, pair):
        return pltpu.make_async_copy(self.come.at[pair], self.load, self.local.at[0])

    def store(self, pair):
        return pltpu.make_async_copy(self.load, self.out.at[pair], self.local.at[1])

    def begin(self, pair, earlier):
        self.copy(pair).wait_recv()

        @pl.when((earlier >= 0) & (earlier < self.pairs))
        def _():
            self.store(earlier).wait()

        self.fetch(pair).start()

    def settle(self, pair):
        self.fetch(pair).wait()
        total = self.hold[lax.rem(pair, 2)].astype(F32) + self.load[...].astype(F32)
        self.load[...] = total.astype(BF16)
        self.store(pair).start()

    def finish(self, last):
        for pair in last:
            self.copy(pair).wait_send()


def pair_scratch(pairs, block, columns):
    dma = pltpu.SemaphoreType.DMA
    return [
        pltpu.VMEM((2, block, columns), BF16),
        pltpu.VMEM((2, block, columns), BF16),
        pltpu.VMEM((block, columns), BF16),
        dma((pairs,)),
        dma((pairs,)),
        dma((2,)),
    ]


def chip_groups(seq_total):
    return [list(range(core, seq_total, 2)) for core in range(2)]


class Chunk:
    def __init__(self, starts_ref, micro, chunk, rows, raw_dt, head_ref, expand, tri):
        first = chunk * rows
        column = lax.broadcasted_iota(jnp.int32, (rows, 1), 0) + first
        line = lax.broadcasted_iota(jnp.int32, (1, rows), 1) + first
        doc_col = doc_number(starts_ref, micro, column)
        doc_row = doc_number(starts_ref, micro, line)
        self.same = [
            (doc_number(starts_ref, micro, column - offset) == doc_col).astype(F32)
            for offset in range(1, TAPS)
        ]
        before = jnp.int32(0)
        last = jnp.int32(0)
        for item in range(starts_ref.shape[1]):
            before = before + (starts_ref[micro, item] <= first - 1).astype(jnp.int32)
            last = last + (starts_ref[micro, item] <= first + rows - 1).astype(jnp.int32)
        carry = (doc_col == before).astype(F32)
        same_last = (doc_col == last).astype(F32)
        self.bias = jnp.where((column >= line) & (doc_col == doc_row), 0.0, NEG)
        self.shifted_dt = raw_dt + head_ref[0:1]
        self.step = jnp.maximum(self.shifted_dt, 0.0) + jnp.log1p(
            jnp.exp(-jnp.abs(self.shifted_dt))
        )
        self.log_keep = self.step * head_ref[1:2]
        self.cum = prefix_sum(tri, self.log_keep)
        self.cum_t = self.cum.T
        carried = jnp.exp(self.cum) * carry
        left = jnp.exp(self.cum[rows - 1 :] - self.cum) * same_last
        spread = mm(
            halves(jnp.concatenate([self.step, carried, left], axis=0), 1), expand
        )
        self.step_cols = spread[:rows]
        self.carry_cols = spread[rows : 2 * rows]
        self.left_cols = spread[2 * rows :]
        self.keep_all = self.carry_cols[rows - 1 :]

    def decay(self, head):
        return jnp.exp(self.cum[:, head : head + 1] - self.cum_t[head : head + 1] + self.bias)


def head_groups(heads):
    size = 2 if heads % 2 == 0 else 1
    return size, heads // size


def stacked(value, size):
    if size == 1:
        return value.astype(BF16)
    lane = lax.broadcasted_iota(jnp.int32, value.shape, 1)
    first = jnp.where(lane < HEAD_DIM, value, 0.0)
    second = jnp.where(lane < HEAD_DIM, 0.0, value)
    return jnp.concatenate([first, second], axis=0).astype(BF16)


def convolved(ext, micro, rows, taps_ref, same):
    current = ext[micro, 8 : 8 + rows, :]
    total = taps_ref[TAPS : TAPS + 1] + taps_ref[TAPS - 1 : TAPS] * current
    views = []
    for offset in range(1, TAPS):
        view = ext[micro, 8 - offset : 8 - offset + rows, :] * same[offset - 1]
        views.append(view)
        total = total + taps_ref[TAPS - 1 - offset : TAPS - offset] * view
    return current, views, total


def forward_kernel(
    micros,
    heads,
    starts_ref,
    x_ref,
    weight_ref,
    out_weight_ref,
    g_ref,
    table_ref,
    heads_ref,
    expand_ref,
    tri_ref,
    proj_ref,
    gg_ref,
    branch_ref,
    mixed_ref,
    states_ref,
    tails_ref,
    sums_ref,
    taps_ref,
    cols_ref,
    head_ref,
    g_out,
    come_ref,
    ext,
    state,
    *sems,
):
    chunk, chunks = pl.program_id(0), pl.num_programs(0)
    rows = x_ref.shape[1]
    width = heads * HEAD_DIM
    conv_width = 2 * STATE + width
    size, groups = head_groups(heads)
    line = Line(g_ref, g_out, sems[:6])
    pairs = PairSum(branch_ref, come_ref, sems[6:])
    early = min((g_out.shape[1] // g_ref.shape[1] - 1) // 2, line.events())

    @pl.when(chunk == 0)
    def _():
        greet(("seq",))
        line.start()

    @pl.when((lax.rem(chunk, 2) == 0) & (chunk >= 2) & (chunk // 2 - 1 < early))
    def _():
        line.hop(chunk // 2 - 1)

    @pl.when((lax.rem(chunk, 2) == 0) & (chunk >= 2))
    def _():
        pairs.begin(chunk // 2 - 1, chunk // 2 - 2)

    @pl.when(chunk == 0)
    def _():
        ext[:, :8, :] = jnp.zeros((micros, 8, conv_width), F32)
        state[...] = jnp.zeros_like(state)
        me = lax.axis_index("seq")
        local = pltpu.roll(
            table_ref[:, :INNER], lax.rem(INNER - me * width, jnp.int32(INNER)), 1
        )[:, :width]
        taps_ref[:, : 2 * STATE] = table_ref[:, INNER:]
        taps_ref[:, 2 * STATE :] = local
        head_row = me * heads + (
            lax.broadcasted_iota(jnp.int32, (1, width), 1) // HEAD_DIM
        )
        limit = HEADS // 8 * jnp.left_shift(jnp.int32(1), lax.axis_index("width"))
        cols_ref[0:1] = local[6:7]
        cols_ref[1:2] = local[5:6]
        cols_ref[2:3] = (head_row < limit).astype(F32)
        cols_ref[3:8] = jnp.zeros((5, width), F32)
        head_ref[...] = pltpu.roll(
            heads_ref[...], lax.rem(LANES - me * heads, jnp.int32(LANES)), 1
        )

    skip, gain, mask = cols_ref[0:1], cols_ref[1:2], cols_ref[2:3]
    rows_in = x_ref[...].reshape(micros * rows, x_ref.shape[2])
    proj_ref[...] = mm(rows_in, weight_ref[...]).astype(BF16).reshape(proj_ref.shape)
    sums, gated_gains = [], []
    for micro in range(micros):
        tails_ref[micro] = ext[micro, :8, :]
        ext[micro, 8 : 8 + rows, :] = proj_ref[micro, :, :conv_width].astype(F32)
        raw_dt = proj_ref[micro, :, conv_width + width :].astype(F32)
        at = Chunk(
            starts_ref, micro, chunk, rows, raw_dt, head_ref, expand_ref[...], tri_ref[...]
        )
        conv = convolved(ext, micro, rows, taps_ref, at.same)[2]
        act = conv * sigmoid(conv)
        write = act[:, :STATE].astype(BF16)
        read = act[:, STATE : 2 * STATE].astype(BF16)
        x_heads = act[:, 2 * STATE :]
        scores = mm_nt(read, write)
        inputs = x_heads * at.step_cols
        state_in = state[micro]
        state_low = state_in.astype(BF16)
        states_ref[micro] = state_low
        outs = []
        for group in range(groups):
            matrices = [
                (at.decay(group * size + item) * scores).astype(BF16) for item in range(size)
            ]
            span = slice(group * size * HEAD_DIM, (group + 1) * size * HEAD_DIM)
            outs.append(mm(jnp.concatenate(matrices, axis=1), stacked(inputs[:, span], size)))
        mixed = jnp.concatenate(outs, axis=1) + at.carry_cols * mm(read, state_low)
        state[micro] = at.keep_all * state_in + mm_tn(
            write, (inputs * at.left_cols).astype(BF16)
        )
        mixed = mixed + skip * x_heads
        mixed_ref[micro] = mixed
        gate = proj_ref[micro, :, conv_width : conv_width + width].astype(F32)
        gated = mask * mixed * (gate * sigmoid(gate))
        gated_gain = (gated * gain).astype(BF16)
        gg_ref[micro] = gated_gain
        gated_gains.append(gated_gain)
        square = jnp.sum(gated * gated, axis=1, keepdims=True)
        lane = lax.broadcasted_iota(jnp.int32, (rows, LANES), 1)
        sums.append(jnp.where(lane == 0, square, 0.0).T[:2])
        ext[micro, :8, :] = ext[micro, rows : rows + 8, :]
    pad = sums_ref.shape[0] - 2 * micros
    if pad:
        sums.append(jnp.zeros((pad, rows), F32))
    sums_ref[...] = jnp.concatenate(sums, axis=0)
    branch = mm(jnp.concatenate(gated_gains, axis=0), out_weight_ref[...]).astype(BF16)

    @pl.when((lax.rem(chunk, 2) == 0) & (chunk >= 2))
    def _():
        pairs.settle(chunk // 2 - 1)

    pairs.put(chunk, chunk // 2 - 2, branch)

    @pl.when(chunk == chunks - 1)
    def _():
        pair_count = branch_ref.shape[0]
        line.hops(early)
        pairs.begin(jnp.int32(pair_count - 1), jnp.int32(pair_count - 2))
        pairs.settle(jnp.int32(pair_count - 1))
        line.finish()
        pairs.store(pair_count - 1).wait()
        pairs.finish(range(max(0, pair_count - 2), pair_count))


def cross_kernel(
    g_ref, out_weight_ref, gg_ref, sums_ref, dnorm_ref, total_ref, mine, slots, send, receive
):
    chunk, chunks = pl.program_id(0), pl.num_programs(0)
    micros, rows, model_width = g_ref.shape
    me = lax.axis_index("seq")

    @pl.when(chunk == 0)
    def _():
        greet(("seq",))

    grads = g_ref[...].reshape(micros * rows, model_width)
    dnorm = mm_nt(grads, out_weight_ref[...])
    gg = gg_ref[...].reshape(micros * rows, dnorm.shape[1])
    dnorm_ref[...] = dnorm.reshape(dnorm_ref.shape)
    cross = jnp.sum(dnorm * gg.astype(F32), axis=1, keepdims=True)
    lane = lax.broadcasted_iota(jnp.int32, (rows, LANES), 1)
    lines = []
    for micro in range(micros):
        part = cross[micro * rows : (micro + 1) * rows]
        lines.append(jnp.where(lane == 1, part, 0.0).T[:2])
    pad = sums_ref.shape[0] - 2 * micros
    if pad:
        lines.append(jnp.zeros((pad, rows), F32))
    mine[chunk] = sums_ref[...] + jnp.concatenate(lines, axis=0)

    @pl.when(chunk == chunks - 1)
    def _():
        def copy(turn, owner):
            peer = lax.rem(me + turn, chunks)
            return remote(
                mine, slots.at[owner], send.at[peer], receive.at[owner], {"seq": peer}
            )

        def start(turn, carry):
            copy(turn, me).start()
            return carry

        def finish(turn, carry):
            copy(turn, me).wait_send()
            copy(turn, lax.rem(me + turn, chunks)).wait_recv()
            return carry

        lax.fori_loop(1, chunks, start, 0)
        slots[me] = mine[...]
        lax.fori_loop(1, chunks, finish, 0)

        def add(owner, total):
            return total + slots[owner]

        total_ref[...] = lax.fori_loop(1, chunks, add, slots[0])


def backward_kernel(
    micros,
    heads,
    starts_ref,
    active_ref,
    proj_ref,
    dnorm_ref,
    mixed_ref,
    states_ref,
    tails_ref,
    sums_ref,
    weight_ref,
    taps_ref,
    head_ref,
    cols_ref,
    expand_ref,
    gather_ref,
    tri_ref,
    dproj_ref,
    partial_ref,
    gconv_ref,
    gcols_ref,
    ghead_ref,
    come_ref,
    ext,
    heads_ext,
    dstate,
    *pair_refs,
):
    chunks = pl.num_programs(0)
    step_index = pl.program_id(0)
    rows = proj_ref.shape[1]
    pairs = PairSum(partial_ref, come_ref, pair_refs)

    @pl.when(step_index == 0)
    def _():
        heads_ext[:, :, rows:, :] = jnp.zeros((micros, TAPS - 1, 8, ext.shape[2]), F32)
        dstate[...] = jnp.zeros_like(dstate)
        gconv_ref[...] = jnp.zeros_like(gconv_ref)
        gcols_ref[...] = jnp.zeros_like(gcols_ref)
        ghead_ref[...] = jnp.zeros_like(ghead_ref)
        barrier = pltpu.get_barrier_semaphore()
        pl.semaphore_signal(
            barrier, inc=1, device_id={"seq": pairs.sibling}, device_id_type=MESH
        )
        pl.semaphore_wait(barrier, 1)

    position = chunks - 1 - step_index

    @pl.when((lax.rem(position, 2) == 1) & (step_index >= 2))
    def _():
        pairs.begin((position + 1) // 2, (position + 1) // 2 + 1)

    for micro in range(micros):
        backward_rows(
            micro,
            heads,
            chunks - 1 - step_index,
            starts_ref,
            active_ref,
            proj_ref.at[micro],
            dnorm_ref.at[micro],
            mixed_ref.at[micro],
            states_ref.at[micro],
            tails_ref.at[micro],
            sums_ref,
            taps_ref,
            head_ref,
            cols_ref,
            expand_ref,
            gather_ref,
            tri_ref,
            dproj_ref.at[micro],
            gconv_ref,
            gcols_ref,
            ghead_ref,
            ext,
            heads_ext.at[micro],
            dstate.at[micro],
        )
    d_rows = dproj_ref[...].reshape(micros * rows, dproj_ref.shape[2])
    partial_rows = mm_nt(d_rows, weight_ref[...]).astype(BF16)

    @pl.when((lax.rem(position, 2) == 1) & (step_index >= 2))
    def _():
        pairs.settle((position + 1) // 2)

    pairs.put(position, position // 2 + 2, partial_rows)

    @pl.when(step_index == chunks - 1)
    def _():
        ghead_ref[2:3] = mm(halves(gcols_ref[...], 1), gather_ref[...])[0:1]
        pairs.begin(jnp.int32(0), jnp.int32(1))
        pairs.settle(jnp.int32(0))
        pairs.store(0).wait()
        pairs.finish(range(min(2, partial_ref.shape[0])))


def backward_rows(
    micro,
    heads,
    chunk,
    starts_ref,
    active_ref,
    proj_ref,
    dnorm_ref,
    mixed_ref,
    states_ref,
    tails_ref,
    sums_ref,
    taps_ref,
    head_ref,
    cols_ref,
    expand_ref,
    gather_ref,
    tri_ref,
    dproj_ref,
    gconv_ref,
    gcols_ref,
    ghead_ref,
    ext,
    heads_ext,
    dstate,
):
    rows = proj_ref.shape[0]
    width = heads * HEAD_DIM
    conv_width = 2 * STATE + width
    size, groups = head_groups(heads)
    skip, gain, mask = cols_ref[0:1], cols_ref[1:2], cols_ref[2:3]
    tri = tri_ref[...]
    gather = gather_ref[...]
    inverse_active = 1.0 / active_ref[0]
    sums = jnp.concatenate(
        [sums_ref[...], jnp.zeros((LANES - sums_ref.shape[0], rows), F32)], axis=0
    ).T
    ext[micro, :8, :] = tails_ref[...]
    ext[micro, 8 : 8 + rows, :] = proj_ref[:, :conv_width].astype(F32)
    raw_dt = proj_ref[:, conv_width + width :].astype(F32)
    at = Chunk(starts_ref, micro, chunk, rows, raw_dt, head_ref, expand_ref[...], tri)
    current, views, conv = convolved(ext, micro, rows, taps_ref, at.same)
    conv_sig = sigmoid(conv)
    act = conv * conv_sig
    write = act[:, :STATE].astype(BF16)
    read = act[:, STATE : 2 * STATE].astype(BF16)
    x_heads = act[:, 2 * STATE :]
    scores = mm_nt(read, write)
    inputs = x_heads * at.step_cols

    gate = proj_ref[:, conv_width : conv_width + width].astype(F32)
    gate_sig = sigmoid(gate)
    gate_act = gate * gate_sig
    masked = mask * mixed_ref[...]
    gated = masked * gate_act
    root = lax.rsqrt(sums[:, 2 * micro : 2 * micro + 1] * inverse_active + EPSILON)
    pull = root * root * root * sums[:, 2 * micro + 1 : 2 * micro + 2] * inverse_active
    dnorm = dnorm_ref[...]
    scaled = gated * root
    d_gated = root * dnorm * gain - gated * pull
    d_gate = d_gated * masked * (gate_sig * (1.0 + gate * (1.0 - gate_sig)))
    d_mixed = mask * d_gated * gate_act
    gcols_ref[0:1] += jnp.sum(d_mixed * x_heads, axis=0, keepdims=True)
    gcols_ref[1:2] += jnp.sum(dnorm * scaled, axis=0, keepdims=True)

    state_low = states_ref[...]
    d_state = dstate[...]
    d_state_low = d_state.astype(BF16)
    from_state = (d_mixed * at.carry_cols).astype(BF16)
    left = inputs * at.left_cols
    left_low = left.astype(BF16)
    d_left = mm(write, d_state_low)
    state_out = mm(read, state_low)
    d_read = mm_nt(from_state, state_low)
    d_write = mm_nt(left_low, d_state_low)
    d_mixed_low = d_mixed.astype(BF16).astype(F32)
    inputs_low = inputs.astype(BF16).astype(F32)
    d_scores = jnp.zeros((rows, rows), F32)
    locals_out, d_locals = [], []
    for group in range(groups):
        span = slice(group * size * HEAD_DIM, (group + 1) * size * HEAD_DIM)
        decays = [at.decay(group * size + item) for item in range(size)]
        matrices = [(decay * scores).astype(BF16) for decay in decays]
        in_stack = stacked(inputs[:, span], size)
        out_stack = stacked(d_mixed[:, span], size)
        locals_out.append(mm(jnp.concatenate(matrices, axis=1), in_stack))
        d_locals.append(mm_tn(jnp.concatenate(matrices, axis=0), out_stack))
        d_matrices = mm_nt(out_stack, inputs[:, span].astype(BF16))
        for item in range(size):
            d_scores = (
                d_scores + d_matrices[item * rows : (item + 1) * rows] * decays[item]
            )
    local_out = jnp.concatenate(locals_out, axis=1)
    d_local = jnp.concatenate(d_locals, axis=1)
    d_scores_low = d_scores.astype(BF16)
    d_read = d_read + mm(d_scores_low, write)
    d_write = d_write + mm_tn(d_scores_low, read)
    d_inputs = d_local + at.left_cols * d_left
    d_x = skip * d_mixed + d_inputs * at.step_cols

    passed = left * d_left
    cum_terms = (
        d_mixed_low * local_out
        + d_mixed * at.carry_cols * state_out
        - inputs_low * d_local
        - passed
    )
    kept = jnp.sum(d_state * at.keep_all * state_low.astype(F32), axis=0, keepdims=True)
    final = jnp.sum(passed, axis=0, keepdims=True) + kept
    stack = jnp.concatenate(
        [cum_terms, d_inputs * x_heads, jnp.broadcast_to(final, (8, width))], axis=0
    )
    reduced = mm(halves(stack, 1), gather)
    d_cum = reduced[:rows]
    d_step = reduced[rows : 2 * rows]
    final_row = reduced[2 * rows : 2 * rows + 1]
    total = jnp.sum(d_cum, axis=0, keepdims=True) + final_row
    d_log = total - prefix_sum(tri, d_cum) + d_cum
    d_step = d_step + d_log * head_ref[1:2]
    d_dt = d_step * sigmoid(at.shifted_dt)
    ghead_ref[0:1] += jnp.sum(d_log * at.log_keep, axis=0, keepdims=True)
    ghead_ref[1:2] += jnp.sum(d_dt, axis=0, keepdims=True)
    dstate[...] = at.keep_all * d_state + mm_tn(read, from_state)

    d_conv = jnp.concatenate([d_write, d_read, d_x], axis=1) * (
        conv_sig * (1.0 + conv * (1.0 - conv_sig))
    )
    gconv_ref[TAPS : TAPS + 1] += jnp.sum(d_conv, axis=0, keepdims=True)
    gconv_ref[TAPS - 1 : TAPS] += jnp.sum(d_conv * current, axis=0, keepdims=True)
    d_raw = taps_ref[TAPS - 1 : TAPS] * d_conv
    for offset in range(1, TAPS):
        tap = TAPS - 1 - offset
        gconv_ref[tap : tap + 1] += jnp.sum(
            d_conv * views[offset - 1], axis=0, keepdims=True
        )
        heads_ext[offset - 1, :rows, :] = d_conv * at.same[offset - 1]
        d_raw = d_raw + taps_ref[tap : tap + 1] * (
            heads_ext[offset - 1, offset : offset + rows, :]
        )
        heads_ext[offset - 1, rows:, :] = heads_ext[offset - 1, :8, :]
    dproj_ref[:, :conv_width] = d_raw.astype(BF16)
    dproj_ref[:, conv_width : conv_width + width] = d_gate.astype(BF16)
    dproj_ref[:, conv_width + width :] = d_dt.astype(BF16)


def constant(shape):
    return pl.BlockSpec(shape, lambda index: (0,) * len(shape))


def run_forward(
    heads, starts, x, weight, out_weight, g, table, head_table, expand, tri, collective_id
):
    micros, rows, model_width = g.shape
    chunks = x.shape[1] // rows
    width = heads * HEAD_DIM
    conv_width = 2 * STATE + width
    block = micros * rows
    sum_rows = -(-2 * micros // 8) * 8
    columns = weight.shape[1]

    def whole(value):
        return pl.BlockSpec(
            value.shape, lambda index: (0,) * value.ndim, pipeline_mode=pl.Buffered(1)
        )

    def row_block(size):
        return pl.BlockSpec((micros, rows, size), lambda index: (0, index, 0))

    return pl.pallas_call(
        partial(forward_kernel, micros, heads),
        grid=(chunks,),
        in_specs=[
            pl.BlockSpec(memory_space=pltpu.SMEM),
            row_block(model_width),
            whole(weight),
            whole(out_weight),
            ANY,
            whole(table),
            whole(head_table),
            whole(expand),
            whole(tri),
        ],
        out_specs=[
            row_block(columns),
            row_block(width),
            ANY,
            row_block(width),
            pl.BlockSpec((None, micros, STATE, width), lambda index: (index, 0, 0, 0)),
            pl.BlockSpec((None, micros, 8, conv_width), lambda index: (index, 0, 0, 0)),
            pl.BlockSpec((None, sum_rows, rows), lambda index: (index, 0, 0)),
            constant((8, conv_width)),
            constant((8, width)),
            constant((8, LANES)),
            ANY,
            ANY,
        ],
        out_shape=[
            jax.ShapeDtypeStruct((micros, chunks * rows, columns), BF16),
            jax.ShapeDtypeStruct((micros, chunks * rows, width), BF16),
            jax.ShapeDtypeStruct((chunks // 2, block, model_width), BF16),
            jax.ShapeDtypeStruct((micros, chunks * rows, width), F32),
            jax.ShapeDtypeStruct((chunks, micros, STATE, width), BF16),
            jax.ShapeDtypeStruct((chunks, micros, 8, conv_width), F32),
            jax.ShapeDtypeStruct((chunks, sum_rows, rows), F32),
            jax.ShapeDtypeStruct((8, conv_width), F32),
            jax.ShapeDtypeStruct((8, width), F32),
            jax.ShapeDtypeStruct((8, LANES), F32),
            jax.ShapeDtypeStruct((micros, chunks * rows, model_width), BF16),
            jax.ShapeDtypeStruct((chunks // 2, block, model_width), BF16),
        ],
        scratch_shapes=[
            pltpu.VMEM((micros, rows + 8, conv_width), F32),
            pltpu.VMEM((micros, STATE, width), F32),
        ]
        + line_sems(chunks // 2, micros)
        + pair_scratch(chunks // 2, block, model_width),
        compiler_params=pltpu.CompilerParams(
            collective_id=collective_id, has_side_effects=True, vmem_limit_bytes=56 << 20
        ),
        cost_estimate=pl.CostEstimate(
            flops=60 * 10**9, bytes_accessed=150 * 10**6, transcendentals=0
        ),
        name="mixer_forward",
    )(starts, x, weight, out_weight, g, table, head_table, expand, tri)


def run_cross(g, out_weight, gg, sums, collective_id):
    chunks = sums.shape[0]
    micros, all_rows, model_width = g.shape
    rows, width = all_rows // chunks, gg.shape[2]

    def row_block(size):
        return pl.BlockSpec((micros, rows, size), lambda index: (0, index, 0))

    return pl.pallas_call(
        cross_kernel,
        grid=(chunks,),
        in_specs=[
            row_block(model_width),
            pl.BlockSpec(out_weight.shape, lambda index: (0, 0), pipeline_mode=pl.Buffered(1)),
            row_block(width),
            pl.BlockSpec((None,) + sums.shape[1:], lambda index: (index, 0, 0)),
        ],
        out_specs=[row_block(width), constant(sums.shape)],
        out_shape=[
            jax.ShapeDtypeStruct((micros, all_rows, width), F32),
            jax.ShapeDtypeStruct(sums.shape, F32),
        ],
        scratch_shapes=[
            pltpu.VMEM(sums.shape, F32),
            pltpu.VMEM((chunks,) + sums.shape, F32),
            pltpu.SemaphoreType.DMA((chunks,)),
            pltpu.SemaphoreType.DMA((chunks,)),
        ],
        compiler_params=pltpu.CompilerParams(
            collective_id=collective_id, has_side_effects=True, vmem_limit_bytes=60 << 20
        ),
        cost_estimate=pl.CostEstimate(
            flops=12 * 10**9, bytes_accessed=16 * 10**6, transcendentals=0
        ),
        name="cross_sums",
    )(g, out_weight, gg, sums)


def run_backward(
    heads,
    starts,
    active,
    proj,
    dnorm,
    mixed,
    states,
    tails,
    sums,
    weight,
    shared,
    collective_id,
):
    micros, all_rows, columns = proj.shape
    chunks = sums.shape[0]
    rows = all_rows // chunks
    width = heads * HEAD_DIM
    conv_width = 2 * STATE + width
    model_width = weight.shape[0]

    def row_block(size):
        return pl.BlockSpec((micros, rows, size), lambda index: (0, chunks - 1 - index, 0))

    def chunk_block(shape):
        return pl.BlockSpec((None, micros) + shape, lambda index: (chunks - 1 - index, 0, 0, 0))

    return pl.pallas_call(
        partial(backward_kernel, micros, heads),
        grid=(chunks,),
        in_specs=[
            pl.BlockSpec(memory_space=pltpu.SMEM),
            pl.BlockSpec(memory_space=pltpu.SMEM),
            row_block(columns),
            row_block(width),
            row_block(width),
            chunk_block((STATE, width)),
            chunk_block((8, conv_width)),
            pl.BlockSpec((None, sums.shape[1], rows), lambda index: (chunks - 1 - index, 0, 0)),
            pl.BlockSpec(weight.shape, lambda index: (0, 0), pipeline_mode=pl.Buffered(1)),
        ]
        + [constant(item.shape) for item in shared],
        out_specs=[
            row_block(columns),
            ANY,
            constant((8, conv_width)),
            constant((8, width)),
            constant((8, LANES)),
            ANY,
        ],
        out_shape=[
            jax.ShapeDtypeStruct((micros, all_rows, columns), BF16),
            jax.ShapeDtypeStruct((chunks // 2, micros * rows, model_width), BF16),
            jax.ShapeDtypeStruct((8, conv_width), F32),
            jax.ShapeDtypeStruct((8, width), F32),
            jax.ShapeDtypeStruct((8, LANES), F32),
            jax.ShapeDtypeStruct((chunks // 2, micros * rows, model_width), BF16),
        ],
        scratch_shapes=[
            pltpu.VMEM((micros, rows + 8, conv_width), F32),
            pltpu.VMEM((micros, TAPS - 1, rows + 8, conv_width), F32),
            pltpu.VMEM((micros, STATE, width), F32),
        ]
        + pair_scratch(chunks // 2, micros * rows, model_width),
        compiler_params=pltpu.CompilerParams(
            collective_id=collective_id, has_side_effects=True, vmem_limit_bytes=60 << 20
        ),
        cost_estimate=pl.CostEstimate(
            flops=60 * 10**9, bytes_accessed=60 * 10**6, transcendentals=0
        ),
        name="mixer_backward",
    )(starts, active, proj, dnorm, mixed, states, tails, sums, weight, *shared)


def tables(heads, rows):
    width = heads * HEAD_DIM
    expand = (
        jnp.arange(LANES)[:, None] == jnp.arange(width)[None, :] // HEAD_DIM
    ).astype(BF16)
    tri = (jnp.arange(rows)[:, None] >= jnp.arange(rows)[None, :]).astype(BF16)
    return (
        jnp.concatenate([expand, expand], axis=0),
        jnp.concatenate([expand.T, expand.T], axis=0),
        tri,
    )


def gather_kernel(
    x_ref,
    w_ref,
    x_out,
    w_out,
    w_send,
    w_receive,
    f_send,
    f_receive,
    keep,
    *sems,
):
    seq_total, width_total = lax.axis_size("seq"), lax.axis_size("width")
    me, mine = lax.axis_index("seq"), lax.axis_index("width")
    quarter = w_ref.shape[1]
    depth = quarter * width_total
    line = Line(x_ref, x_out, sems)
    greet(("seq", "width"))

    def rows(source, group):
        return pl.ds(pl.multiple_of(source * depth + group * quarter, 8), quarter)

    def deal(turn, from_peer):
        peer = lax.rem(me + turn, seq_total)
        owner = peer if from_peer else me
        return remote(
            w_ref.at[peer],
            w_out.at[rows(owner, mine)],
            w_send.at[peer],
            w_receive.at[owner],
            {"seq": peer},
        )

    def deal_start(turn, carry):
        deal(turn, False).start()
        return carry

    lax.fori_loop(1, seq_total, deal_start, 0)
    w_own = pltpu.make_async_copy(w_ref.at[me], w_out.at[rows(me, mine)], keep.at[0])
    w_own.start()
    line.start()

    def forward(source, turn, from_peer):
        peer = lax.rem(mine + turn, width_total)
        group = peer if from_peer else mine
        where = w_out.at[rows(source, group)]
        return remote(
            where, where, f_send.at[peer, source], f_receive.at[group, source], {"width": peer}
        )

    def forward_start(source):
        for turn in range(1, width_total):
            forward(source, turn, False).start()

    def deal_pass(turn, carry):
        deal(turn, True).wait_recv()
        forward_start(lax.rem(me + turn, seq_total))
        return carry

    w_own.wait()
    forward_start(me)
    lax.fori_loop(1, seq_total, deal_pass, 0)
    line.hops(0)

    def deal_end(turn, carry):
        deal(turn, False).wait_send()
        return carry

    lax.fori_loop(1, seq_total, deal_end, 0)

    def forward_end(source, carry):
        for turn in range(1, width_total):
            forward(source, turn, False).wait_send()
            forward(source, turn, True).wait_recv()
        return carry

    lax.fori_loop(0, seq_total, forward_end, 0)
    line.finish()


def gather_rows(x, pieces, collective_id):
    seq_total, width_total = lax.axis_size("seq"), lax.axis_size("width")
    parts, rows, model_width = x.shape
    whole = (parts, rows * seq_total, model_width)
    weight = (seq_total * width_total * pieces.shape[1], pieces.shape[2])
    dma = pltpu.SemaphoreType.DMA
    return pl.pallas_call(
        gather_kernel,
        in_specs=[ANY] * 2,
        out_specs=[ANY] * 2,
        out_shape=[
            jax.ShapeDtypeStruct(whole, x.dtype),
            jax.ShapeDtypeStruct(weight, pieces.dtype),
        ],
        scratch_shapes=[
            dma((seq_total,)),
            dma((seq_total,)),
            dma((width_total, seq_total)),
            dma((width_total, seq_total)),
            dma((1,)),
        ]
        + line_sems(seq_total // 2, parts),
        compiler_params=pltpu.CompilerParams(
            collective_id=collective_id, has_side_effects=True
        ),
        cost_estimate=pl.CostEstimate(
            flops=80 * 10**9, bytes_accessed=200 * 10**6, transcendentals=0
        ),
        name="gather_rows",
    )(x, pieces)


def home_kernel(
    layout,
    normed_ref,
    columns_ref,
    gconv_ref,
    gcols_ref,
    ghead_ref,
    in_gain_ref,
    dproj_ref,
    grad_ref,
    gnorm_ref,
    shard_in_ref,
    shard_out_ref,
    taps_out,
    bias_out,
    gain_out,
    head_out,
    in_gain_out,
    zx_ref,
    bc_ref,
    small_out,
    line_buffer,
    blocks_in,
    acc,
    stage,
    arrived,
    last_arrived,
    sum_x,
    sum_z,
    sum_b,
    small_stage,
    small_slots,
    fetch,
    in_sems,
    zx_send,
    zx_receive,
    bc_send,
    bc_receive,
    small_send,
    small_receive,
    last_send,
    last_receive,
    bc_total,
    bc_last,
    bc_last_send,
    bc_last_receive,
    *out_refs,
):
    seq_total, width_total, quarter, width, slots, shard, heads = layout
    micros = normed_ref.shape[0]
    me, mine = lax.axis_index("seq"), lax.axis_index("width")
    depth = quarter * width_total
    conv_width = 2 * STATE + width
    per_tile = TILE // depth
    tiles = seq_total // per_tile
    rows_in = Tiles(normed_ref, blocks_in, fetch, per_tile)
    meeting = Meeting(stage, arrived, last_arrived, in_sems)
    out_grad = OutGrad(grad_ref, gnorm_ref, out_refs)
    out_grad.tiles.begin()
    greet_all()

    def out_multiply(turn, carry):
        out_grad.multiply(turn)

        @pl.when(turn >= MIDDLE)
        def _():
            out_grad.tiles.each(turn - MIDDLE, out_grad.meeting.middle)

        @pl.when(turn >= LAST)
        def _():
            out_grad.tiles.each(turn - LAST, out_grad.combine)

        return carry

    rows_in.begin()
    lax.fori_loop(0, tiles, out_multiply, 0)

    conv_end = conv_width + width
    small_stage[:, :conv_width] = gconv_ref[...]
    small_stage[:, conv_width:conv_end] = gcols_ref[...]
    small_stage[:, conv_end : conv_end + LANES] = ghead_ref[...]

    def block_copy(sums, sem_row, number, block, second, action):
        low = (number * width) // shard
        high = ((number + 1) * width - 1) // shard
        owner = high if second else low
        slot = number - (owner * shard) // width

        def act():
            both(
                (owner == mine) & (block == me),
                sums.at[block],
                zx_ref.at[slot, mine],
                zx_send.at[sem_row, block],
                zx_receive.at[slot, mine],
                {"width": owner, "seq": block},
                action,
            )

        if second:
            pl.when(high != low)(act)
        else:
            act()

    def bc_copy(block, action):
        both(
            block == me,
            sum_b.at[block],
            bc_ref.at[me],
            bc_send.at[block],
            bc_receive.at[me],
            {"seq": block},
            action,
        )

    def bc_home(source, action):
        both(
            (mine == width_total - 1) & (source == mine),
            bc_total,
            bc_last.at[source],
            bc_last_send.at[0],
            bc_last_receive.at[source],
            {"width": width_total - 1},
            action,
        )

    def pieces_of(block, action):
        for second in (False, True):
            block_copy(sum_z, int(second), me, block, second, action)
            block_copy(sum_x, 2 + int(second), seq_total + me, block, second, action)
        bc_copy(block, action)

    def combine(block):
        low = meeting.total(block).astype(BF16)
        sum_b[block, :, : 2 * STATE] = low[:, : 2 * STATE]
        sum_x[block] = low[:, 2 * STATE : conv_width]
        sum_z[block] = low[:, conv_width : conv_width + width]
        sum_b[block, :, 2 * STATE :] = low[:, conv_width + width :]
        pieces_of(block, "start")

    def multiply(turn, carry):
        tile = rows_in.turned(turn)
        for chunk in range(rows_in.chunks):
            micro, rows, block = rows_in.block(turn, chunk)
            part = mm_tn(block, dproj_ref[micro, rows, :])
            acc[...] = part if chunk == 0 else acc[...] + part
            rows_in.used(turn, chunk)
        for item in range(per_tile):
            block = tile * per_tile + item
            for group in range(width_total):
                row = item * depth + group * quarter
                stage[block, meeting.slot(block, group)] = acc[row : row + quarter].astype(BF16)
            meeting.first(block).start()
        weights = columns_ref[pl.ds(pl.multiple_of(tile * TILE, TILE), TILE), :]
        product = (acc[...] * weights.astype(F32)).astype(BF16)
        line = mm_nt(jnp.ones((8, product.shape[1]), BF16), product)
        small_stage[pl.ds(tile, 1), conv_end + LANES :] = line[:1]

        @pl.when(turn < MIDDLE)
        def _():
            out_grad.tiles.each(tiles - MIDDLE + turn, out_grad.meeting.middle)

        @pl.when(turn >= MIDDLE)
        def _():
            rows_in.each(turn - MIDDLE, meeting.middle)

        @pl.when(turn < LAST)
        def _():
            out_grad.tiles.each(tiles - LAST + turn, out_grad.combine)

        @pl.when(turn >= LAST)
        def _():
            rows_in.each(turn - LAST, combine)

        return carry

    lax.fori_loop(0, tiles, multiply, 0)

    def small_hop(turn, from_peer):
        peer = lax.rem(mine + turn, width_total)
        group = peer if from_peer else mine
        return remote(
            small_stage,
            small_slots.at[group],
            small_send.at[peer],
            small_receive.at[group],
            {"width": peer},
        )

    for turn in range(1, width_total):
        small_hop(turn, False).start()
    small_slots[mine] = small_stage[...]

    for turn in range(tiles - MIDDLE, tiles):
        rows_in.each(turn, meeting.middle)
    for turn in range(tiles - LAST, tiles):
        rows_in.each(turn, combine)

    def bc_arrive(turn, carry):
        source = lax.rem(me + turn, seq_total)
        both(
            source == me,
            sum_b.at[me],
            bc_ref.at[source],
            bc_send.at[me],
            bc_receive.at[source],
            {"seq": source},
            "receive",
        )
        return carry

    lax.fori_loop(0, seq_total, bc_arrive, 0)

    def bc_add(source, total):
        return total + bc_ref[source, :, : 2 * STATE].astype(F32)

    bc_sum = lax.fori_loop(1, seq_total, bc_add, bc_ref[0, :, : 2 * STATE].astype(F32))
    bc_total[:, : 2 * STATE] = bc_sum.astype(BF16)
    for source in range(seq_total):
        at = 2 * STATE + source * heads
        bc_total[:, at : at + heads] = bc_ref[source, :, 2 * STATE : 2 * STATE + heads]
    bc_home(mine, "start")

    for turn in range(1, width_total):
        small_hop(turn, True).wait_recv()
        small_hop(turn, False).wait_send()
    total = small_slots[0]
    for group in range(1, width_total):
        total = total + small_slots[group]
    small_stage[...] = total

    def last_hop(turn, from_peer):
        peer = lax.rem(me + turn, seq_total)
        owner = peer if from_peer else me
        return remote(
            small_stage,
            small_out.at[owner],
            last_send.at[peer],
            last_receive.at[owner],
            {"seq": peer},
        )

    def last_start(turn, carry):
        last_hop(turn, False).start()
        return carry

    lax.fori_loop(1, seq_total, last_start, 0)
    small_out[me] = small_stage[...]

    def sent(block, carry):
        meeting.sent(block)
        pieces_of(block, "send")
        return carry

    lax.fori_loop(0, seq_total, sent, 0)

    first = (mine * shard) // width

    def landed(slot, carry):
        number = first + slot
        source = lax.rem(number, seq_total)

        @pl.when((number < 2 * seq_total) & (number * width < (mine + 1) * shard))
        def _():
            for group in range(width_total):
                both(
                    (source == me) & (mine == group),
                    sum_z.at[me],
                    zx_ref.at[slot, group],
                    zx_send.at[0, me],
                    zx_receive.at[slot, group],
                    {"width": group, "seq": source},
                    "receive",
                )

        return carry

    lax.fori_loop(0, slots, landed, 0)

    bc_home(mine, "send")

    @pl.when(mine == width_total - 1)
    def _():
        for source in range(width_total):
            bc_home(source, "receive")

    out_grad.finish(shard_out_ref)

    def last_end(turn, carry):
        last_hop(turn, False).wait_send()
        last_hop(turn, True).wait_recv()
        return carry

    lax.fori_loop(1, seq_total, last_end, 0)

    edge = (slots - -(-(2 * STATE + HEADS) // width)) * width
    for group in range(width_total):
        for slot in range(slots):
            line_buffer[:, slot * width : (slot + 1) * width] = zx_ref[slot, group].astype(F32)

        @pl.when(mine == width_total - 1)
        def _():
            line_buffer[:, edge : edge + 2 * STATE + HEADS] = bc_last[
                group, :, : 2 * STATE + HEADS
            ].astype(F32)

        total_lanes = line_buffer.shape[1]
        start = lax.rem(mine * shard, jnp.int32(width))
        rolled = pltpu.roll(
            line_buffer[...], lax.rem(total_lanes - start, jnp.int32(total_lanes)), 1
        )
        shard_in_ref[group * quarter : (group + 1) * quarter, :] = rolled[:, :shard]
    def small_add(source, total):
        return total + small_out[source]

    total = lax.fori_loop(1, seq_total, small_add, small_out[0])
    taps_out[:, INNER:] = total[:TAPS, : 2 * STATE]
    bias_out[:, INNER:] = total[TAPS : TAPS + 1, : 2 * STATE]
    in_gain_out[...] = total[:, conv_end + LANES :] / in_gain_ref[...]
    for source in range(seq_total):
        first = source * width
        taps_out[:, first : first + width] = small_out[source, :TAPS, 2 * STATE : conv_width]
        bias_out[:, first : first + width] = small_out[
            source, TAPS : TAPS + 1, 2 * STATE : conv_width
        ]
        gain_out[:, first : first + width] = small_out[source, 1:2, conv_width:conv_end]
        head_out[:, source * heads : (source + 1) * heads] = small_out[
            source, :, conv_end : conv_end + heads
        ]


def bring_home(normed, dproj, columns, smalls, in_gain, grad, gnorm, heads, collective_id):
    seq_total, width_total = lax.axis_size("seq"), lax.axis_size("width")
    width = heads * HEAD_DIM
    micros, group_rows, model_width = normed.shape
    depth = model_width // seq_total
    quarter = depth // width_total
    shard = (INNER + CONV + HEADS) // width_total
    slots = max(
        ((group + 1) * shard - 1) // width - group * shard // width + 1
        for group in range(width_total)
    )
    all_columns = dproj.shape[2]
    layout = (seq_total, width_total, quarter, width, slots, shard, heads)
    rest = all_columns - 2 * width
    small = (8, 2 * STATE + 2 * width + LANES + TILE)
    lanes = -(-slots * width // LANES) * LANES
    dma = pltpu.SemaphoreType.DMA
    vmem = pl.BlockSpec(memory_space=pltpu.VMEM)
    return pl.pallas_call(
        partial(home_kernel, layout),
        in_specs=[ANY] + [vmem] * 6 + [ANY, vmem],
        out_specs=[vmem] * 7,
        out_shape=[
            jax.ShapeDtypeStruct((depth, shard), F32),
            jax.ShapeDtypeStruct((seq_total // width_total * width, model_width // seq_total), F32),
            jax.ShapeDtypeStruct((TAPS, CONV), F32),
            jax.ShapeDtypeStruct((1, CONV), F32),
            jax.ShapeDtypeStruct((1, INNER), F32),
            jax.ShapeDtypeStruct((8, HEADS), F32),
            jax.ShapeDtypeStruct(in_gain.shape, F32),
        ],
        scratch_shapes=[
            pltpu.VMEM((slots, width_total, quarter, width), BF16),
            pltpu.VMEM((seq_total, quarter, rest), BF16),
            pltpu.VMEM((seq_total,) + small, F32),
            pltpu.VMEM((quarter, lanes), F32),
            pltpu.VMEM((2, min(group_rows, 1024), TILE), BF16),
            pltpu.VMEM((TILE, all_columns), F32),
            pltpu.VMEM((seq_total, width_total, quarter, all_columns), BF16),
            pltpu.VMEM((seq_total, 2, quarter, all_columns), BF16),
            pltpu.VMEM((seq_total, quarter, all_columns), BF16),
            pltpu.VMEM((seq_total, quarter, width), BF16),
            pltpu.VMEM((seq_total, quarter, width), BF16),
            pltpu.VMEM((seq_total, quarter, rest), BF16),
            pltpu.VMEM(small, F32),
            pltpu.VMEM((width_total,) + small, F32),
            dma((2,)),
            dma((4, seq_total)),
            dma((4, seq_total)),
            dma((slots, width_total)),
            dma((seq_total,)),
            dma((seq_total,)),
            dma((width_total,)),
            dma((width_total,)),
            dma((seq_total,)),
            dma((seq_total,)),
            pltpu.VMEM((quarter, rest), BF16),
            pltpu.VMEM((width_total, quarter, rest), BF16),
            dma((1,)),
            dma((width_total,)),
        ]
        + out_grad_scratch(heads, group_rows, model_width),
        compiler_params=pltpu.CompilerParams(
            collective_id=collective_id, has_side_effects=True, vmem_limit_bytes=62 << 20
        ),
        cost_estimate=pl.CostEstimate(
            flops=150 * 10**9, bytes_accessed=8 * normed.size, transcendentals=0
        ),
        name="bring_home",
    )(normed, columns, *smalls, in_gain, dproj, grad, gnorm)


def own(value, start, count, axis=0):
    return lax.dynamic_slice_in_dim(value, start, count, axis)


def per_device(
    hidden_in,
    starts,
    in_gain,
    in_weight,
    conv_weight,
    conv_bias,
    step_bias,
    decay_log,
    skip_gain,
    gate_gain,
    out_weight,
    cotangent,
):
    seq_total = lax.axis_size("seq")
    seq_index = lax.axis_index("seq")
    group_index = lax.axis_index("width")
    micros, rows, model_width = hidden_in.shape[1:]
    heads = HEADS // seq_total
    width = heads * HEAD_DIM
    depth = in_weight.shape[0]
    head_count = HEADS // 8 * jnp.left_shift(jnp.int32(1), group_index)
    active = head_count.astype(F32) * HEAD_DIM

    hidden = hidden_in[0].astype(F32)
    grads = cotangent[0]
    root_in = lax.rsqrt(jnp.mean(hidden * hidden, axis=2, keepdims=True) + EPSILON)
    normed = (hidden * root_in * in_gain).astype(BF16)

    dt_pad = LANES
    width_total = lax.axis_size("width")
    quarter = depth // width_total
    in_quarter = own(in_weight, group_index * quarter, quarter)
    gates = in_quarter[:, :INNER].reshape(quarter, seq_total, width)
    xs = in_quarter[:, INNER : 2 * INNER].reshape(quarter, seq_total, width)
    bc = jnp.broadcast_to(
        in_quarter[:, None, 2 * INNER : INNER + CONV], (quarter, seq_total, 2 * STATE)
    )
    dts = in_quarter[:, INNER + CONV :].reshape(quarter, seq_total, heads)
    dts = jnp.pad(dts, ((0, 0), (0, 0), (0, dt_pad - heads)))
    pieces = jnp.concatenate([bc, xs, gates, dts], axis=2).transpose(1, 0, 2)
    all_normed, columns = gather_rows(normed, pieces, 0)

    def lane_pad(value):
        return jnp.pad(value, (0, CONV - INNER))[None]

    table = jnp.concatenate(
        [
            conv_weight,
            conv_bias[None],
            lane_pad(gate_gain),
            lane_pad(jnp.repeat(skip_gain, HEAD_DIM)),
            jnp.zeros((1, CONV), F32),
        ],
        axis=0,
    )
    head_table = jnp.pad(
        jnp.stack([step_bias, -jnp.exp(decay_log)]), ((0, 6), (0, LANES - HEADS))
    )
    expand, gather, tri = tables(heads, rows)

    proj, gg, branch, mixed, states, tails, sums, taps, cols, head, all_grad, _ = run_forward(
        heads,
        starts[0],
        all_normed,
        columns,
        out_weight,
        grads,
        table,
        head_table,
        expand,
        tri,
        3,
    )
    chip_wise = dict(axis_index_groups=chip_groups(seq_total), scatter_dimension=0, tiled=True)
    branch = lax.psum_scatter(branch, "seq", **chip_wise)
    dnorm, sums = run_cross(all_grad, out_weight, gg, sums, 1)
    roots = lax.rsqrt(sums[:, : 2 * micros : 2] / active + EPSILON)
    own_roots = own(roots, seq_index, 1).reshape(micros, rows, 1)
    all_roots = roots.transpose(1, 0, 2).reshape(micros, seq_total * rows, 1)
    gnorm = (gg.astype(F32) * all_roots).astype(BF16)

    dproj, partial_rows, *smalls = run_backward(
        heads,
        starts[0],
        active[None],
        proj,
        dnorm,
        mixed,
        states,
        tails,
        sums,
        columns,
        [taps, head, cols, expand, gather, tri],
        4,
    )
    smalls.pop()
    scattered = lax.psum_scatter(partial_rows, "seq", **chip_wise)
    head_sums, branch = lax.optimization_barrier((smalls[2], branch))
    home = bring_home(
        all_normed,
        dproj,
        columns,
        [smalls[0], smalls[1], head_sums],
        in_gain.reshape(-1, TILE),
        all_grad,
        gnorm,
        heads,
        2,
    )
    shard_in, shard_out, taps_sum, bias_sum, gain_sum, head_sums, in_gain_sum = home
    output = hidden + branch.reshape(hidden.shape).astype(F32) * own_roots
    scattered, in_gain_sum = lax.optimization_barrier((scattered, in_gain_sum))
    gained = scattered.reshape(hidden.shape).astype(F32) * in_gain
    pull = jnp.mean(gained * hidden, axis=2, keepdims=True) * (root_in * root_in * root_in)
    hidden_grads = grads.astype(F32) + root_in * gained - hidden * pull
    shape = hidden_in.shape
    return (
        output.astype(BF16).reshape(shape),
        hidden_grads.astype(BF16).reshape(shape),
        in_gain_sum.reshape(-1),
        shard_in,
        taps_sum,
        bias_sum[0],
        head_sums[1],
        head_sums[0],
        head_sums[2],
        gain_sum[0],
        shard_out,
    )


def solution(mesh):
    in_specs = (
        P("width", None, "seq", None),
        P("width", None, None),
        P(),
        P("seq", None),
        P(),
        P(),
        P(),
        P(),
        P(),
        P(),
        P("seq", None),
        P("width", None, "seq", None),
    )
    out_specs = (
        P("width", None, "seq", None),
        P("width", None, "seq", None),
        P(),
        P("seq", "width"),
        P(),
        P(),
        P(),
        P(),
        P(),
        P(),
        P("width", "seq"),
    )
    return jax.shard_map(
        per_device, mesh=mesh, in_specs=in_specs, out_specs=out_specs, check_vma=False
    )
```

```python
from functools import partial

import jax
import jax.numpy as jnp
from jax import lax
from jax.experimental import pallas as pl
from jax.experimental.pallas import tpu as pltpu
from jax.sharding import PartitionSpec as P

INNER = 4096
HEADS = 64
HEAD_DIM = 64
STATE = 128
CONV = 4352
EPSILON = 1e-05
LANES = 128
TAPS = 4
NEG = -1e30
F32 = jnp.float32
BF16 = jnp.bfloat16


def mm(a, b):
    return lax.dot_general(a, b, (((1,), (0,)), ((), ())), preferred_element_type=F32)


def mm_nt(a, b):
    return lax.dot_general(a, b, (((1,), (1,)), ((), ())), preferred_element_type=F32)


def mm_tn(a, b):
    return lax.dot_general(a, b, (((0,), (0,)), ((), ())), preferred_element_type=F32)


def halves(value, axis):
    high = value.astype(BF16)
    low = (value - high.astype(F32)).astype(BF16)
    return jnp.concatenate([high, low], axis=axis)


def sigmoid(value):
    return 0.5 * jnp.tanh(0.5 * value) + 0.5


def prefix_sum(tri, value):
    high = value.astype(BF16)
    rest = value - high.astype(F32)
    middle = rest.astype(BF16)
    low = (rest - middle.astype(F32)).astype(BF16)
    parts = mm(tri, jnp.concatenate([high, middle, low], axis=1))
    width = value.shape[1]
    return parts[:, :width] + parts[:, width : 2 * width] + parts[:, 2 * width :]


def doc_number(starts_ref, micro, positions):
    count = jnp.zeros_like(positions)
    for item in range(starts_ref.shape[1]):
        count = count + (starts_ref[micro, item] <= positions).astype(jnp.int32)
    return count


MESH = pl.DeviceIdType.MESH
ANY = pl.BlockSpec(memory_space=pl.ANY)


def greet(axes):
    barrier = pltpu.get_barrier_semaphore()
    waits = 0
    for axis in axes:
        count, me = lax.axis_size(axis), lax.axis_index(axis)

        def hello(turn, carry):
            pl.semaphore_signal(
                barrier,
                inc=1,
                device_id={axis: lax.rem(me + turn, count)},
                device_id_type=MESH,
            )
            return carry

        lax.fori_loop(1, count, hello, 0)
        waits += count - 1
    pl.semaphore_wait(barrier, waits)


def remote(source, target, send, receive, device):
    return pltpu.make_async_remote_copy(
        src_ref=source,
        dst_ref=target,
        send_sem=send,
        recv_sem=receive,
        device_id=device,
        device_id_type=MESH,
    )


class Line:
    def __init__(self, source, out, sems):
        self.source, self.out = source, out
        self.up, self.down, self.receive, self.side_send, self.side_receive, self.keep = sems
        self.me = lax.axis_index("seq")
        self.chips = lax.axis_size("seq") // 2
        self.chip, self.core = self.me // 2, lax.rem(self.me, 2)
        self.parts, self.rows = source.shape[:2]

    def at(self, owner, part):
        return self.out.at[part, pl.ds(pl.multiple_of(owner * self.rows, 8), self.rows)]

    def line(self, source, owner_chip, part, target_chip, sems):
        return remote(
            source,
            self.at(owner_chip * 2 + self.core, part),
            sems.at[owner_chip, part],
            self.receive.at[owner_chip, part],
            {"seq": target_chip * 2 + self.core},
        )

    def side(self, source, owner_chip, part, from_sibling):
        core = 1 - self.core if from_sibling else self.core
        return remote(
            source,
            self.at(owner_chip * 2 + core, part),
            self.side_send.at[owner_chip, part],
            self.side_receive.at[owner_chip, part],
            {"seq": self.chip * 2 + 1 - self.core},
        )

    def stay(self, part):
        return pltpu.make_async_copy(
            self.source.at[part], self.at(self.me, part), self.keep.at[part]
        )

    def start(self):
        for part in range(self.parts):
            here = self.source.at[part]

            @pl.when(self.chip + 1 < self.chips)
            def _():
                self.line(here, self.chip, part, self.chip + 1, self.up).start()

            @pl.when(self.chip >= 1)
            def _():
                self.line(here, self.chip, part, self.chip - 1, self.down).start()

            self.side(here, self.chip, part, False).start()
            self.stay(part).start()

    def events(self):
        return (self.chips - 1) * self.parts

    def hop(self, event):
        turn, part = event // self.parts + 1, lax.rem(event, self.parts)
        below, above = self.chip - turn, self.chip + turn

        @pl.when(below >= 0)
        def _():
            here = self.at(below * 2 + self.core, part)
            self.line(here, below, part, self.chip, self.up).wait_recv()

            @pl.when(self.chip + 1 < self.chips)
            def _():
                self.line(here, below, part, self.chip + 1, self.up).start()

            self.side(here, below, part, False).start()

        @pl.when(above < self.chips)
        def _():
            here = self.at(above * 2 + self.core, part)
            self.line(here, above, part, self.chip, self.down).wait_recv()

            @pl.when(self.chip >= 1)
            def _():
                self.line(here, above, part, self.chip - 1, self.down).start()

            self.side(here, above, part, False).start()

    def hops(self, first):
        def body(event, carry):
            self.hop(event)
            return carry

        lax.fori_loop(first, self.events(), body, 0)

    def finish(self):
        def body(owner_chip, carry):
            for part in range(self.parts):
                here = self.at(owner_chip * 2 + self.core, part)

                @pl.when((owner_chip <= self.chip) & (self.chip + 1 < self.chips))
                def _():
                    self.line(here, owner_chip, part, self.chip + 1, self.up).wait_send()

                @pl.when((owner_chip >= self.chip) & (self.chip >= 1))
                def _():
                    self.line(here, owner_chip, part, self.chip - 1, self.down).wait_send()

                self.side(here, owner_chip, part, False).wait_send()
                self.side(here, owner_chip, part, True).wait_recv()
            return carry

        lax.fori_loop(0, self.chips, body, 0)
        for part in range(self.parts):
            self.stay(part).wait()


def line_sems(chips, parts):
    return [pltpu.SemaphoreType.DMA((chips, parts))] * 5 + [pltpu.SemaphoreType.DMA((parts,))]


TILE = 256
MIDDLE = 2
LAST = 4


def greet_all():
    seq_total, width_total = lax.axis_size("seq"), lax.axis_size("width")
    count = seq_total * width_total
    place = lax.axis_index("width") * seq_total + lax.axis_index("seq")
    barrier = pltpu.get_barrier_semaphore()

    def hello(turn, carry):
        peer = lax.rem(place + turn, count)
        pl.semaphore_signal(
            barrier,
            inc=1,
            device_id={"width": peer // seq_total, "seq": lax.rem(peer, seq_total)},
            device_id_type=MESH,
        )
        return carry

    lax.fori_loop(1, count, hello, 0)
    pl.semaphore_wait(barrier, count - 1)


def both(is_here, source, target, send, receive, device, action):
    if action != "send":

        @pl.when(is_here)
        def _():
            stay = pltpu.make_async_copy(source, target, receive)
            if action == "start":
                stay.start()
            else:
                stay.wait()

    @pl.when(jnp.logical_not(is_here))
    def _():
        away = remote(source, target, send, receive, device)
        if action == "start":
            away.start()
        elif action == "receive":
            away.wait_recv()
        else:
            away.wait_send()


class Meeting:
    def __init__(self, parts, come, last, sems):
        self.parts, self.come, self.last, self.sems = parts, come, last, sems
        mine = lax.axis_index("width")
        self.upper, self.lower = mine // 2, lax.rem(mine, 2)

    def order(self, block):
        odd = lax.rem(block, 2)
        even = 1 - odd
        first = odd * self.upper + even * self.lower
        second = odd * self.lower + even * self.upper
        across = 2 * (1 - self.upper) + self.lower
        beside = 2 * self.upper + 1 - self.lower
        return first, second, odd * across + even * beside, odd * beside + even * across

    def slot(self, block, group):
        odd = lax.rem(block, 2)
        return odd * group + (1 - odd) * (group % 2 * 2 + group // 2)

    def first(self, block):
        side, _, partner, _ = self.order(block)
        return remote(
            self.parts.at[block, pl.ds(2 * (1 - side), 2)],
            self.come.at[block],
            self.sems.at[0, block],
            self.sems.at[1, block],
            {"width": partner},
        )

    def second(self, block):
        side, place, _, partner = self.order(block)
        return remote(
            self.parts.at[block, 2 * side + 1 - place],
            self.last.at[block],
            self.sems.at[2, block],
            self.sems.at[3, block],
            {"width": partner},
        )

    def middle(self, block):
        self.first(block).wait_recv()
        side = self.order(block)[0]
        for item in range(2):
            slot = 2 * side + item
            total = self.parts[block, slot].astype(F32) + self.come[block, item].astype(F32)
            self.parts[block, slot] = total.astype(BF16)
        self.second(block).start()

    def total(self, block):
        self.second(block).wait_recv()
        side, place = self.order(block)[:2]
        return self.parts[block, 2 * side + place].astype(F32) + self.last[block].astype(F32)

    def sent(self, block):
        self.first(block).wait_send()
        self.second(block).wait_send()


class Tiles:
    def __init__(self, source, blocks, sems, per_tile):
        self.source, self.blocks, self.sems, self.per_tile = source, blocks, sems, per_tile
        self.total = source.shape[2] // TILE
        self.chunk_rows = blocks.shape[1]
        self.pieces = source.shape[1] // self.chunk_rows
        self.chunks = source.shape[0] * self.pieces

    def turned(self, turn):
        return lax.rem(turn + lax.axis_index("seq") // self.per_tile, self.total)

    def fetch(self, turn, chunk):
        first = chunk % self.pieces * self.chunk_rows
        return pltpu.make_async_copy(
            self.source.at[
                chunk // self.pieces,
                pl.ds(first, self.chunk_rows),
                pl.ds(pl.multiple_of(self.turned(turn) * TILE, TILE), TILE),
            ],
            self.blocks.at[chunk % 2],
            self.sems.at[chunk % 2],
        )

    def begin(self):
        self.fetch(0, 0).start()
        self.fetch(0, 1).start()

    def block(self, turn, chunk):
        self.fetch(turn, chunk).wait()
        first = chunk % self.pieces * self.chunk_rows
        return chunk // self.pieces, slice(first, first + self.chunk_rows), self.blocks[chunk % 2]

    def used(self, turn, chunk):
        if chunk + 2 < self.chunks:
            self.fetch(turn, chunk + 2).start()
        else:

            @pl.when(turn + 1 < self.total)
            def _():
                self.fetch(turn + 1, chunk + 2 - self.chunks).start()

    def each(self, turn, act):
        for item in range(self.per_tile):
            act(self.turned(turn) * self.per_tile + item)


class OutGrad:
    def __init__(self, grad, gnorm, refs):
        (
            blocks,
            self.acc,
            self.stage,
            come,
            last,
            self.sums,
            self.landing,
            fetch,
            sems,
            self.send,
            self.receive,
        ) = refs
        self.gnorm = gnorm
        self.sub, self.cols = self.stage.shape[2:]
        self.meeting = Meeting(self.stage, come, last, sems)
        self.tiles = Tiles(grad, blocks, fetch, TILE // self.cols)
        self.width_total = lax.axis_size("width")
        self.seq_total = lax.axis_size("seq")
        self.owners = self.seq_total // self.width_total
        self.me, self.mine = lax.axis_index("seq"), lax.axis_index("width")

    def copy(self, target, action):
        owner = self.me // self.owners
        place = self.landing.at[lax.rem(self.me, self.owners), self.mine]
        receive = self.receive.at[lax.rem(self.me, self.owners), self.mine]
        both(
            (owner == self.mine) & (target == self.me),
            self.sums.at[target],
            place,
            self.send.at[target],
            receive,
            {"width": owner, "seq": target},
            action,
        )

    def combine(self, block):
        self.sums[block] = self.meeting.total(block).astype(BF16)
        self.copy(block, "start")

    def multiply(self, turn):
        for chunk in range(self.tiles.chunks):
            micro, rows, block = self.tiles.block(turn, chunk)
            part = mm_tn(self.gnorm[micro, rows, :], block)
            self.acc[...] = part if chunk == 0 else self.acc[...] + part
            self.tiles.used(turn, chunk)
        for item in range(self.tiles.per_tile):
            block = self.tiles.turned(turn) * self.tiles.per_tile + item
            for group in range(self.width_total):
                self.stage[block, self.meeting.slot(block, group)] = self.acc[
                    group * self.sub : (group + 1) * self.sub,
                    item * self.cols : (item + 1) * self.cols,
                ].astype(BF16)
            self.meeting.first(block).start()

    def finish(self, out_ref):
        def sent(block, carry):
            self.meeting.sent(block)
            self.copy(block, "send")
            return carry

        lax.fori_loop(0, self.seq_total, sent, 0)
        for item in range(self.owners):
            for group in range(self.width_total):
                source = self.mine * self.owners + item
                both(
                    (source == self.me) & (self.mine == group),
                    self.sums.at[self.me],
                    self.landing.at[item, group],
                    self.send.at[self.me],
                    self.receive.at[item, group],
                    {"width": group, "seq": source},
                    "receive",
                )
                row = (item * self.width_total + group) * self.sub
                out_ref[row : row + self.sub, :] = self.landing[item, group].astype(F32)


def out_grad_scratch(heads, group_rows, model_width):
    seq_total, width_total = lax.axis_size("seq"), lax.axis_size("width")
    sub, cols = heads * HEAD_DIM // width_total, model_width // seq_total
    owners = seq_total // width_total
    dma = pltpu.SemaphoreType.DMA
    return [
        pltpu.VMEM((2, min(group_rows, 1024), TILE), BF16),
        pltpu.VMEM((heads * HEAD_DIM, TILE), F32),
        pltpu.VMEM((seq_total, width_total, sub, cols), BF16),
        pltpu.VMEM((seq_total, 2, sub, cols), BF16),
        pltpu.VMEM((seq_total, sub, cols), BF16),
        pltpu.VMEM((seq_total, sub, cols), BF16),
        pltpu.VMEM((owners, width_total, sub, cols), BF16),
        dma((2,)),
        dma((4, seq_total)),
        dma((seq_total,)),
        dma((owners, width_total)),
    ]


class PairSum:
    def __init__(self, out, come, refs):
        self.out, self.come = out, come
        self.hold, self.leave, self.load, self.send, self.receive, self.local = refs
        me = lax.axis_index("seq")
        self.core, self.sibling = lax.rem(me, 2), me + 1 - 2 * lax.rem(me, 2)
        self.pairs = out.shape[0]

    def copy(self, pair):
        return remote(
            self.leave.at[lax.rem(pair, 2)],
            self.come.at[pair],
            self.send.at[pair],
            self.receive.at[pair],
            {"seq": self.sibling},
        )

    def put(self, position, earlier, block):
        pair = position // 2
        here = lax.rem(position, 2) == self.core

        @pl.when(here)
        def _():
            self.hold[lax.rem(pair, 2)] = block

        @pl.when(jnp.logical_not(here))
        def _():
            @pl.when((earlier >= 0) & (earlier < self.pairs))
            def _():
                self.copy(earlier).wait_send()

            self.leave[lax.rem(pair, 2)] = block
            self.copy(pair).start()

    def fetch(self, pair):
        return pltpu.make_async_copy(self.come.at[pair], self.load, self.local.at[0])

    def store(self, pair):
        return pltpu.make_async_copy(self.load, self.out.at[pair], self.local.at[1])

    def begin(self, pair, earlier):
        self.copy(pair).wait_recv()

        @pl.when((earlier >= 0) & (earlier < self.pairs))
        def _():
            self.store(earlier).wait()

        self.fetch(pair).start()

    def settle(self, pair):
        self.fetch(pair).wait()
        total = self.hold[lax.rem(pair, 2)].astype(F32) + self.load[...].astype(F32)
        self.load[...] = total.astype(BF16)
        self.store(pair).start()

    def finish(self, last):
        for pair in last:
            self.copy(pair).wait_send()


def pair_scratch(pairs, block, columns):
    dma = pltpu.SemaphoreType.DMA
    return [
        pltpu.VMEM((2, block, columns), BF16),
        pltpu.VMEM((2, block, columns), BF16),
        pltpu.VMEM((block, columns), BF16),
        dma((pairs,)),
        dma((pairs,)),
        dma((2,)),
    ]


def chip_groups(seq_total):
    return [list(range(core, seq_total, 2)) for core in range(2)]


class Chunk:
    def __init__(self, starts_ref, micro, chunk, rows, raw_dt, head_ref, expand, tri):
        first = chunk * rows
        column = lax.broadcasted_iota(jnp.int32, (rows, 1), 0) + first
        line = lax.broadcasted_iota(jnp.int32, (1, rows), 1) + first
        doc_col = doc_number(starts_ref, micro, column)
        doc_row = doc_number(starts_ref, micro, line)
        self.same = [
            (doc_number(starts_ref, micro, column - offset) == doc_col).astype(F32)
            for offset in range(1, TAPS)
        ]
        before = jnp.int32(0)
        last = jnp.int32(0)
        for item in range(starts_ref.shape[1]):
            before = before + (starts_ref[micro, item] <= first - 1).astype(jnp.int32)
            last = last + (starts_ref[micro, item] <= first + rows - 1).astype(jnp.int32)
        carry = (doc_col == before).astype(F32)
        same_last = (doc_col == last).astype(F32)
        self.bias = jnp.where((column >= line) & (doc_col == doc_row), 0.0, NEG)
        self.shifted_dt = raw_dt + head_ref[0:1]
        self.step = jnp.maximum(self.shifted_dt, 0.0) + jnp.log1p(
            jnp.exp(-jnp.abs(self.shifted_dt))
        )
        self.log_keep = self.step * head_ref[1:2]
        self.cum = prefix_sum(tri, self.log_keep)
        self.cum_t = self.cum.T
        carried = jnp.exp(self.cum) * carry
        left = jnp.exp(self.cum[rows - 1 :] - self.cum) * same_last
        spread = mm(
            halves(jnp.concatenate([self.step, carried, left], axis=0), 1), expand
        )
        self.step_cols = spread[:rows]
        self.carry_cols = spread[rows : 2 * rows]
        self.left_cols = spread[2 * rows :]
        self.keep_all = self.carry_cols[rows - 1 :]

    def decay(self, head):
        return jnp.exp(self.cum[:, head : head + 1] - self.cum_t[head : head + 1] + self.bias)


def head_groups(heads):
    size = 2 if heads % 2 == 0 else 1
    return size, heads // size


def stacked(value, size):
    if size == 1:
        return value.astype(BF16)
    lane = lax.broadcasted_iota(jnp.int32, value.shape, 1)
    first = jnp.where(lane < HEAD_DIM, value, 0.0)
    second = jnp.where(lane < HEAD_DIM, 0.0, value)
    return jnp.concatenate([first, second], axis=0).astype(BF16)


def convolved(ext, micro, rows, taps_ref, same):
    current = ext[micro, 8 : 8 + rows, :]
    total = taps_ref[TAPS : TAPS + 1] + taps_ref[TAPS - 1 : TAPS] * current
    views = []
    for offset in range(1, TAPS):
        view = ext[micro, 8 - offset : 8 - offset + rows, :] * same[offset - 1]
        views.append(view)
        total = total + taps_ref[TAPS - 1 - offset : TAPS - offset] * view
    return current, views, total


def forward_kernel(
    micros,
    heads,
    starts_ref,
    x_ref,
    weight_ref,
    out_weight_ref,
    g_ref,
    conv_weight_ref,
    conv_bias_ref,
    gate_gain_ref,
    skip_ref,
    step_bias_ref,
    decay_ref,
    proj_ref,
    gg_ref,
    branch_ref,
    mixed_ref,
    states_ref,
    tails_ref,
    sums_ref,
    taps_ref,
    cols_ref,
    head_ref,
    expand_ref,
    gather_ref,
    tri_ref,
    g_out,
    come_ref,
    ext,
    state,
    table,
    *sems,
):
    chunk, chunks = pl.program_id(0), pl.num_programs(0)
    rows = x_ref.shape[1]
    width = heads * HEAD_DIM
    conv_width = 2 * STATE + width
    size, groups = head_groups(heads)
    line = Line(g_ref, g_out, sems[:6])
    pairs = PairSum(branch_ref, come_ref, sems[6:])
    early = min((g_out.shape[1] // g_ref.shape[1] - 1) // 2, line.events())

    @pl.when(chunk == 0)
    def _():
        greet(("seq",))
        line.start()

    @pl.when((lax.rem(chunk, 2) == 0) & (chunk >= 2) & (chunk // 2 - 1 < early))
    def _():
        line.hop(chunk // 2 - 1)

    @pl.when((lax.rem(chunk, 2) == 0) & (chunk >= 2))
    def _():
        pairs.begin(chunk // 2 - 1, chunk // 2 - 2)

    @pl.when(chunk == 0)
    def _():
        ext[:, :8, :] = jnp.zeros((micros, 8, conv_width), F32)
        state[...] = jnp.zeros_like(state)
        me = lax.axis_index("seq")
        lane_of = lax.broadcasted_iota(jnp.int32, (LANES, width), 0)
        head_of = lax.broadcasted_iota(jnp.int32, (LANES, width), 1) // HEAD_DIM
        spread = (lane_of == head_of).astype(F32).astype(BF16)
        expand_ref[:LANES] = spread
        expand_ref[LANES:] = spread
        lane_of = lax.broadcasted_iota(jnp.int32, (width, LANES), 1)
        head_of = lax.broadcasted_iota(jnp.int32, (width, LANES), 0) // HEAD_DIM
        folded = (lane_of == head_of).astype(F32).astype(BF16)
        gather_ref[:width] = folded
        gather_ref[width:] = folded
        later = lax.broadcasted_iota(jnp.int32, (rows, rows), 0)
        sooner = lax.broadcasted_iota(jnp.int32, (rows, rows), 1)
        tri_ref[...] = (later >= sooner).astype(F32).astype(BF16)

        table[...] = jnp.zeros_like(table)
        table[0:TAPS] = conv_weight_ref[:, :INNER]
        table[TAPS : TAPS + 1] = conv_bias_ref[:, :INNER]
        table[TAPS + 1 : TAPS + 2] = gate_gain_ref[...]
        local = pltpu.roll(table[...], lax.rem(INNER - me * width, jnp.int32(INNER)), 1)[
            :, :width
        ]
        taps_ref[...] = jnp.zeros_like(taps_ref)
        taps_ref[0:TAPS, : 2 * STATE] = conv_weight_ref[:, INNER:]
        taps_ref[TAPS : TAPS + 1, : 2 * STATE] = conv_bias_ref[:, INNER:]
        taps_ref[0 : TAPS + 1, 2 * STATE :] = local[: TAPS + 1]
        head_ref[...] = jnp.zeros_like(head_ref)
        head_ref[0:1, :HEADS] = step_bias_ref[...]
        head_ref[1:2, :HEADS] = -jnp.exp(decay_ref[...])
        head_ref[2:3, :HEADS] = skip_ref[...]
        own_heads = pltpu.roll(
            head_ref[...], lax.rem(LANES - me * heads, jnp.int32(LANES)), 1
        )
        head_ref[...] = own_heads
        head_row = me * heads + (
            lax.broadcasted_iota(jnp.int32, (1, width), 1) // HEAD_DIM
        )
        limit = HEADS // 8 * jnp.left_shift(jnp.int32(1), lax.axis_index("width"))
        cols_ref[0:1] = mm(halves(own_heads, 1), expand_ref[...])[2:3]
        cols_ref[1:2] = local[TAPS + 1 : TAPS + 2]
        cols_ref[2:3] = (head_row < limit).astype(F32)
        cols_ref[3:8] = jnp.zeros((5, width), F32)

    skip, gain, mask = cols_ref[0:1], cols_ref[1:2], cols_ref[2:3]
    rows_in = x_ref[...].reshape(micros * rows, x_ref.shape[2])
    proj_ref[...] = mm(rows_in, weight_ref[...]).astype(BF16).reshape(proj_ref.shape)
    sums, gated_gains = [], []
    for micro in range(micros):
        tails_ref[micro] = ext[micro, :8, :]
        ext[micro, 8 : 8 + rows, :] = proj_ref[micro, :, :conv_width].astype(F32)
        raw_dt = proj_ref[micro, :, conv_width + width :].astype(F32)
        at = Chunk(
            starts_ref, micro, chunk, rows, raw_dt, head_ref, expand_ref[...], tri_ref[...]
        )
        conv = convolved(ext, micro, rows, taps_ref, at.same)[2]
        act = conv * sigmoid(conv)
        write = act[:, :STATE].astype(BF16)
        read = act[:, STATE : 2 * STATE].astype(BF16)
        x_heads = act[:, 2 * STATE :]
        scores = mm_nt(read, write)
        inputs = x_heads * at.step_cols
        state_in = state[micro]
        state_low = state_in.astype(BF16)
        states_ref[micro] = state_low
        outs = []
        for group in range(groups):
            matrices = [
                (at.decay(group * size + item) * scores).astype(BF16) for item in range(size)
            ]
            span = slice(group * size * HEAD_DIM, (group + 1) * size * HEAD_DIM)
            outs.append(mm(jnp.concatenate(matrices, axis=1), stacked(inputs[:, span], size)))
        mixed = jnp.concatenate(outs, axis=1) + at.carry_cols * mm(read, state_low)
        state[micro] = at.keep_all * state_in + mm_tn(
            write, (inputs * at.left_cols).astype(BF16)
        )
        mixed = mixed + skip * x_heads
        mixed_ref[micro] = mixed
        gate = proj_ref[micro, :, conv_width : conv_width + width].astype(F32)
        gated = mask * mixed * (gate * sigmoid(gate))
        gated_gain = (gated * gain).astype(BF16)
        gg_ref[micro] = gated_gain
        gated_gains.append(gated_gain)
        square = jnp.sum(gated * gated, axis=1, keepdims=True)
        lane = lax.broadcasted_iota(jnp.int32, (rows, LANES), 1)
        sums.append(jnp.where(lane == 0, square, 0.0).T[:2])
        ext[micro, :8, :] = ext[micro, rows : rows + 8, :]
    pad = sums_ref.shape[0] - 2 * micros
    if pad:
        sums.append(jnp.zeros((pad, rows), F32))
    sums_ref[...] = jnp.concatenate(sums, axis=0)
    branch = mm(jnp.concatenate(gated_gains, axis=0), out_weight_ref[...]).astype(BF16)

    @pl.when((lax.rem(chunk, 2) == 0) & (chunk >= 2))
    def _():
        pairs.settle(chunk // 2 - 1)

    pairs.put(chunk, chunk // 2 - 2, branch)

    @pl.when(chunk == chunks - 1)
    def _():
        pair_count = branch_ref.shape[0]
        line.hops(early)
        pairs.begin(jnp.int32(pair_count - 1), jnp.int32(pair_count - 2))
        pairs.settle(jnp.int32(pair_count - 1))
        line.finish()
        pairs.store(pair_count - 1).wait()
        pairs.finish(range(max(0, pair_count - 2), pair_count))


def cross_kernel(
    g_ref, out_weight_ref, gg_ref, sums_ref, dnorm_ref, total_ref, mine, slots, send, receive
):
    chunk, chunks = pl.program_id(0), pl.num_programs(0)
    micros, rows, model_width = g_ref.shape
    me = lax.axis_index("seq")

    @pl.when(chunk == 0)
    def _():
        greet(("seq",))

    grads = g_ref[...].reshape(micros * rows, model_width)
    dnorm = mm_nt(grads, out_weight_ref[...])
    gg = gg_ref[...].reshape(micros * rows, dnorm.shape[1])
    dnorm_ref[...] = dnorm.reshape(dnorm_ref.shape)
    cross = jnp.sum(dnorm * gg.astype(F32), axis=1, keepdims=True)
    lane = lax.broadcasted_iota(jnp.int32, (rows, LANES), 1)
    lines = []
    for micro in range(micros):
        part = cross[micro * rows : (micro + 1) * rows]
        lines.append(jnp.where(lane == 1, part, 0.0).T[:2])
    pad = sums_ref.shape[0] - 2 * micros
    if pad:
        lines.append(jnp.zeros((pad, rows), F32))
    mine[chunk] = sums_ref[...] + jnp.concatenate(lines, axis=0)

    @pl.when(chunk == chunks - 1)
    def _():
        def copy(turn, owner):
            peer = lax.rem(me + turn, chunks)
            return remote(
                mine, slots.at[owner], send.at[peer], receive.at[owner], {"seq": peer}
            )

        def start(turn, carry):
            copy(turn, me).start()
            return carry

        def finish(turn, carry):
            copy(turn, me).wait_send()
            copy(turn, lax.rem(me + turn, chunks)).wait_recv()
            return carry

        lax.fori_loop(1, chunks, start, 0)
        slots[me] = mine[...]
        lax.fori_loop(1, chunks, finish, 0)

        def add(owner, total):
            return total + slots[owner]

        total_ref[...] = lax.fori_loop(1, chunks, add, slots[0])


def backward_kernel(
    micros,
    heads,
    starts_ref,
    active_ref,
    proj_ref,
    dnorm_ref,
    mixed_ref,
    states_ref,
    tails_ref,
    sums_ref,
    weight_ref,
    taps_ref,
    head_ref,
    cols_ref,
    expand_ref,
    gather_ref,
    tri_ref,
    dproj_ref,
    partial_ref,
    gconv_ref,
    gcols_ref,
    ghead_ref,
    come_ref,
    ext,
    heads_ext,
    dstate,
    *pair_refs,
):
    chunks = pl.num_programs(0)
    step_index = pl.program_id(0)
    rows = proj_ref.shape[1]
    pairs = PairSum(partial_ref, come_ref, pair_refs)

    @pl.when(step_index == 0)
    def _():
        heads_ext[:, :, rows:, :] = jnp.zeros((micros, TAPS - 1, 8, ext.shape[2]), F32)
        dstate[...] = jnp.zeros_like(dstate)
        gconv_ref[...] = jnp.zeros_like(gconv_ref)
        gcols_ref[...] = jnp.zeros_like(gcols_ref)
        ghead_ref[...] = jnp.zeros_like(ghead_ref)
        barrier = pltpu.get_barrier_semaphore()
        pl.semaphore_signal(
            barrier, inc=1, device_id={"seq": pairs.sibling}, device_id_type=MESH
        )
        pl.semaphore_wait(barrier, 1)

    position = chunks - 1 - step_index

    @pl.when((lax.rem(position, 2) == 1) & (step_index >= 2))
    def _():
        pairs.begin((position + 1) // 2, (position + 1) // 2 + 1)

    for micro in range(micros):
        backward_rows(
            micro,
            heads,
            chunks - 1 - step_index,
            starts_ref,
            active_ref,
            proj_ref.at[micro],
            dnorm_ref.at[micro],
            mixed_ref.at[micro],
            states_ref.at[micro],
            tails_ref.at[micro],
            sums_ref,
            taps_ref,
            head_ref,
            cols_ref,
            expand_ref,
            gather_ref,
            tri_ref,
            dproj_ref.at[micro],
            gconv_ref,
            gcols_ref,
            ghead_ref,
            ext,
            heads_ext.at[micro],
            dstate.at[micro],
        )
    d_rows = dproj_ref[...].reshape(micros * rows, dproj_ref.shape[2])
    partial_rows = mm_nt(d_rows, weight_ref[...]).astype(BF16)

    @pl.when((lax.rem(position, 2) == 1) & (step_index >= 2))
    def _():
        pairs.settle((position + 1) // 2)

    pairs.put(position, position // 2 + 2, partial_rows)

    @pl.when(step_index == chunks - 1)
    def _():
        ghead_ref[2:3] = mm(halves(gcols_ref[...], 1), gather_ref[...])[0:1]
        pairs.begin(jnp.int32(0), jnp.int32(1))
        pairs.settle(jnp.int32(0))
        pairs.store(0).wait()
        pairs.finish(range(min(2, partial_ref.shape[0])))


def backward_rows(
    micro,
    heads,
    chunk,
    starts_ref,
    active_ref,
    proj_ref,
    dnorm_ref,
    mixed_ref,
    states_ref,
    tails_ref,
    sums_ref,
    taps_ref,
    head_ref,
    cols_ref,
    expand_ref,
    gather_ref,
    tri_ref,
    dproj_ref,
    gconv_ref,
    gcols_ref,
    ghead_ref,
    ext,
    heads_ext,
    dstate,
):
    rows = proj_ref.shape[0]
    width = heads * HEAD_DIM
    conv_width = 2 * STATE + width
    size, groups = head_groups(heads)
    skip, gain, mask = cols_ref[0:1], cols_ref[1:2], cols_ref[2:3]
    tri = tri_ref[...]
    gather = gather_ref[...]
    inverse_active = 1.0 / active_ref[0]
    sums = jnp.concatenate(
        [sums_ref[...], jnp.zeros((LANES - sums_ref.shape[0], rows), F32)], axis=0
    ).T
    ext[micro, :8, :] = tails_ref[...]
    ext[micro, 8 : 8 + rows, :] = proj_ref[:, :conv_width].astype(F32)
    raw_dt = proj_ref[:, conv_width + width :].astype(F32)
    at = Chunk(starts_ref, micro, chunk, rows, raw_dt, head_ref, expand_ref[...], tri)
    current, views, conv = convolved(ext, micro, rows, taps_ref, at.same)
    conv_sig = sigmoid(conv)
    act = conv * conv_sig
    write = act[:, :STATE].astype(BF16)
    read = act[:, STATE : 2 * STATE].astype(BF16)
    x_heads = act[:, 2 * STATE :]
    scores = mm_nt(read, write)
    inputs = x_heads * at.step_cols

    gate = proj_ref[:, conv_width : conv_width + width].astype(F32)
    gate_sig = sigmoid(gate)
    gate_act = gate * gate_sig
    masked = mask * mixed_ref[...]
    gated = masked * gate_act
    root = lax.rsqrt(sums[:, 2 * micro : 2 * micro + 1] * inverse_active + EPSILON)
    pull = root * root * root * sums[:, 2 * micro + 1 : 2 * micro + 2] * inverse_active
    dnorm = dnorm_ref[...]
    scaled = gated * root
    d_gated = root * dnorm * gain - gated * pull
    d_gate = d_gated * masked * (gate_sig * (1.0 + gate * (1.0 - gate_sig)))
    d_mixed = mask * d_gated * gate_act
    gcols_ref[0:1] += jnp.sum(d_mixed * x_heads, axis=0, keepdims=True)
    gcols_ref[1:2] += jnp.sum(dnorm * scaled, axis=0, keepdims=True)

    state_low = states_ref[...]
    d_state = dstate[...]
    d_state_low = d_state.astype(BF16)
    from_state = (d_mixed * at.carry_cols).astype(BF16)
    left = inputs * at.left_cols
    left_low = left.astype(BF16)
    d_left = mm(write, d_state_low)
    state_out = mm(read, state_low)
    d_read = mm_nt(from_state, state_low)
    d_write = mm_nt(left_low, d_state_low)
    d_mixed_low = d_mixed.astype(BF16).astype(F32)
    inputs_low = inputs.astype(BF16).astype(F32)
    d_scores = jnp.zeros((rows, rows), F32)
    locals_out, d_locals = [], []
    for group in range(groups):
        span = slice(group * size * HEAD_DIM, (group + 1) * size * HEAD_DIM)
        decays = [at.decay(group * size + item) for item in range(size)]
        matrices = [(decay * scores).astype(BF16) for decay in decays]
        in_stack = stacked(inputs[:, span], size)
        out_stack = stacked(d_mixed[:, span], size)
        locals_out.append(mm(jnp.concatenate(matrices, axis=1), in_stack))
        d_locals.append(mm_tn(jnp.concatenate(matrices, axis=0), out_stack))
        d_matrices = mm_nt(out_stack, inputs[:, span].astype(BF16))
        for item in range(size):
            d_scores = (
                d_scores + d_matrices[item * rows : (item + 1) * rows] * decays[item]
            )
    local_out = jnp.concatenate(locals_out, axis=1)
    d_local = jnp.concatenate(d_locals, axis=1)
    d_scores_low = d_scores.astype(BF16)
    d_read = d_read + mm(d_scores_low, write)
    d_write = d_write + mm_tn(d_scores_low, read)
    d_inputs = d_local + at.left_cols * d_left
    d_x = skip * d_mixed + d_inputs * at.step_cols

    passed = left * d_left
    cum_terms = (
        d_mixed_low * local_out
        + d_mixed * at.carry_cols * state_out
        - inputs_low * d_local
        - passed
    )
    kept = jnp.sum(d_state * at.keep_all * state_low.astype(F32), axis=0, keepdims=True)
    final = jnp.sum(passed, axis=0, keepdims=True) + kept
    stack = jnp.concatenate(
        [cum_terms, d_inputs * x_heads, jnp.broadcast_to(final, (8, width))], axis=0
    )
    reduced = mm(halves(stack, 1), gather)
    d_cum = reduced[:rows]
    d_step = reduced[rows : 2 * rows]
    final_row = reduced[2 * rows : 2 * rows + 1]
    total = jnp.sum(d_cum, axis=0, keepdims=True) + final_row
    d_log = total - prefix_sum(tri, d_cum) + d_cum
    d_step = d_step + d_log * head_ref[1:2]
    d_dt = d_step * sigmoid(at.shifted_dt)
    ghead_ref[0:1] += jnp.sum(d_log * at.log_keep, axis=0, keepdims=True)
    ghead_ref[1:2] += jnp.sum(d_dt, axis=0, keepdims=True)
    dstate[...] = at.keep_all * d_state + mm_tn(read, from_state)

    d_conv = jnp.concatenate([d_write, d_read, d_x], axis=1) * (
        conv_sig * (1.0 + conv * (1.0 - conv_sig))
    )
    gconv_ref[TAPS : TAPS + 1] += jnp.sum(d_conv, axis=0, keepdims=True)
    gconv_ref[TAPS - 1 : TAPS] += jnp.sum(d_conv * current, axis=0, keepdims=True)
    d_raw = taps_ref[TAPS - 1 : TAPS] * d_conv
    for offset in range(1, TAPS):
        tap = TAPS - 1 - offset
        gconv_ref[tap : tap + 1] += jnp.sum(
            d_conv * views[offset - 1], axis=0, keepdims=True
        )
        heads_ext[offset - 1, :rows, :] = d_conv * at.same[offset - 1]
        d_raw = d_raw + taps_ref[tap : tap + 1] * (
            heads_ext[offset - 1, offset : offset + rows, :]
        )
        heads_ext[offset - 1, rows:, :] = heads_ext[offset - 1, :8, :]
    dproj_ref[:, :conv_width] = d_raw.astype(BF16)
    dproj_ref[:, conv_width : conv_width + width] = d_gate.astype(BF16)
    dproj_ref[:, conv_width + width :] = d_dt.astype(BF16)


def constant(shape):
    return pl.BlockSpec(shape, lambda index: (0,) * len(shape))


def run_forward(
    heads, starts, x, weight, out_weight, g, smalls, collective_id
):
    micros, rows, model_width = g.shape
    chunks = x.shape[1] // rows
    width = heads * HEAD_DIM
    conv_width = 2 * STATE + width
    block = micros * rows
    sum_rows = -(-2 * micros // 8) * 8
    columns = weight.shape[1]

    def whole(value):
        return pl.BlockSpec(
            value.shape, lambda index: (0,) * value.ndim, pipeline_mode=pl.Buffered(1)
        )

    def row_block(size):
        return pl.BlockSpec((micros, rows, size), lambda index: (0, index, 0))

    return pl.pallas_call(
        partial(forward_kernel, micros, heads),
        grid=(chunks,),
        in_specs=[
            pl.BlockSpec(memory_space=pltpu.SMEM),
            row_block(model_width),
            whole(weight),
            whole(out_weight),
            ANY,
        ]
        + [whole(item) for item in smalls],
        out_specs=[
            row_block(columns),
            row_block(width),
            ANY,
            row_block(width),
            pl.BlockSpec((None, micros, STATE, width), lambda index: (index, 0, 0, 0)),
            pl.BlockSpec((None, micros, 8, conv_width), lambda index: (index, 0, 0, 0)),
            pl.BlockSpec((None, sum_rows, rows), lambda index: (index, 0, 0)),
            constant((8, conv_width)),
            constant((8, width)),
            constant((8, LANES)),
            constant((2 * LANES, width)),
            constant((2 * width, LANES)),
            constant((rows, rows)),
            ANY,
            ANY,
        ],
        out_shape=[
            jax.ShapeDtypeStruct((micros, chunks * rows, columns), BF16),
            jax.ShapeDtypeStruct((micros, chunks * rows, width), BF16),
            jax.ShapeDtypeStruct((chunks // 2, block, model_width), BF16),
            jax.ShapeDtypeStruct((micros, chunks * rows, width), F32),
            jax.ShapeDtypeStruct((chunks, micros, STATE, width), BF16),
            jax.ShapeDtypeStruct((chunks, micros, 8, conv_width), F32),
            jax.ShapeDtypeStruct((chunks, sum_rows, rows), F32),
            jax.ShapeDtypeStruct((8, conv_width), F32),
            jax.ShapeDtypeStruct((8, width), F32),
            jax.ShapeDtypeStruct((8, LANES), F32),
            jax.ShapeDtypeStruct((2 * LANES, width), BF16),
            jax.ShapeDtypeStruct((2 * width, LANES), BF16),
            jax.ShapeDtypeStruct((rows, rows), BF16),
            jax.ShapeDtypeStruct((micros, chunks * rows, model_width), BF16),
            jax.ShapeDtypeStruct((chunks // 2, block, model_width), BF16),
        ],
        scratch_shapes=[
            pltpu.VMEM((micros, rows + 8, conv_width), F32),
            pltpu.VMEM((micros, STATE, width), F32),
            pltpu.VMEM((8, INNER), F32),
        ]
        + line_sems(chunks // 2, micros)
        + pair_scratch(chunks // 2, block, model_width),
        compiler_params=pltpu.CompilerParams(
            collective_id=collective_id, has_side_effects=True, vmem_limit_bytes=56 << 20
        ),
        cost_estimate=pl.CostEstimate(
            flops=60 * 10**9, bytes_accessed=150 * 10**6, transcendentals=0
        ),
        name="mixer_forward",
    )(starts, x, weight, out_weight, g, *smalls)


def run_cross(g, out_weight, gg, sums, collective_id):
    chunks = sums.shape[0]
    micros, all_rows, model_width = g.shape
    rows, width = all_rows // chunks, gg.shape[2]

    def row_block(size):
        return pl.BlockSpec((micros, rows, size), lambda index: (0, index, 0))

    return pl.pallas_call(
        cross_kernel,
        grid=(chunks,),
        in_specs=[
            row_block(model_width),
            pl.BlockSpec(out_weight.shape, lambda index: (0, 0), pipeline_mode=pl.Buffered(1)),
            row_block(width),
            pl.BlockSpec((None,) + sums.shape[1:], lambda index: (index, 0, 0)),
        ],
        out_specs=[row_block(width), constant(sums.shape)],
        out_shape=[
            jax.ShapeDtypeStruct((micros, all_rows, width), F32),
            jax.ShapeDtypeStruct(sums.shape, F32),
        ],
        scratch_shapes=[
            pltpu.VMEM(sums.shape, F32),
            pltpu.VMEM((chunks,) + sums.shape, F32),
            pltpu.SemaphoreType.DMA((chunks,)),
            pltpu.SemaphoreType.DMA((chunks,)),
        ],
        compiler_params=pltpu.CompilerParams(
            collective_id=collective_id, has_side_effects=True, vmem_limit_bytes=60 << 20
        ),
        cost_estimate=pl.CostEstimate(
            flops=12 * 10**9, bytes_accessed=16 * 10**6, transcendentals=0
        ),
        name="cross_sums",
    )(g, out_weight, gg, sums)


def run_backward(
    heads,
    starts,
    active,
    proj,
    dnorm,
    mixed,
    states,
    tails,
    sums,
    weight,
    shared,
    collective_id,
):
    micros, all_rows, columns = proj.shape
    chunks = sums.shape[0]
    rows = all_rows // chunks
    width = heads * HEAD_DIM
    conv_width = 2 * STATE + width
    model_width = weight.shape[0]

    def row_block(size):
        return pl.BlockSpec((micros, rows, size), lambda index: (0, chunks - 1 - index, 0))

    def chunk_block(shape):
        return pl.BlockSpec((None, micros) + shape, lambda index: (chunks - 1 - index, 0, 0, 0))

    return pl.pallas_call(
        partial(backward_kernel, micros, heads),
        grid=(chunks,),
        in_specs=[
            pl.BlockSpec(memory_space=pltpu.SMEM),
            pl.BlockSpec(memory_space=pltpu.SMEM),
            row_block(columns),
            row_block(width),
            row_block(width),
            chunk_block((STATE, width)),
            chunk_block((8, conv_width)),
            pl.BlockSpec((None, sums.shape[1], rows), lambda index: (chunks - 1 - index, 0, 0)),
            pl.BlockSpec(weight.shape, lambda index: (0, 0), pipeline_mode=pl.Buffered(1)),
        ]
        + [constant(item.shape) for item in shared],
        out_specs=[
            row_block(columns),
            ANY,
            constant((8, conv_width)),
            constant((8, width)),
            constant((8, LANES)),
            ANY,
        ],
        out_shape=[
            jax.ShapeDtypeStruct((micros, all_rows, columns), BF16),
            jax.ShapeDtypeStruct((chunks // 2, micros * rows, model_width), BF16),
            jax.ShapeDtypeStruct((8, conv_width), F32),
            jax.ShapeDtypeStruct((8, width), F32),
            jax.ShapeDtypeStruct((8, LANES), F32),
            jax.ShapeDtypeStruct((chunks // 2, micros * rows, model_width), BF16),
        ],
        scratch_shapes=[
            pltpu.VMEM((micros, rows + 8, conv_width), F32),
            pltpu.VMEM((micros, TAPS - 1, rows + 8, conv_width), F32),
            pltpu.VMEM((micros, STATE, width), F32),
        ]
        + pair_scratch(chunks // 2, micros * rows, model_width),
        compiler_params=pltpu.CompilerParams(
            collective_id=collective_id, has_side_effects=True, vmem_limit_bytes=60 << 20
        ),
        cost_estimate=pl.CostEstimate(
            flops=60 * 10**9, bytes_accessed=60 * 10**6, transcendentals=0
        ),
        name="mixer_backward",
    )(starts, active, proj, dnorm, mixed, states, tails, sums, weight, *shared)


def gather_kernel(
    x_ref,
    w_ref,
    x_out,
    w_out,
    w_send,
    w_receive,
    f_send,
    f_receive,
    keep,
    *sems,
):
    seq_total, width_total = lax.axis_size("seq"), lax.axis_size("width")
    me, mine = lax.axis_index("seq"), lax.axis_index("width")
    quarter = w_ref.shape[1]
    depth = quarter * width_total
    line = Line(x_ref, x_out, sems)
    greet(("seq", "width"))

    def rows(source, group):
        return pl.ds(pl.multiple_of(source * depth + group * quarter, 8), quarter)

    def deal(turn, from_peer):
        peer = lax.rem(me + turn, seq_total)
        owner = peer if from_peer else me
        return remote(
            w_ref.at[peer],
            w_out.at[rows(owner, mine)],
            w_send.at[peer],
            w_receive.at[owner],
            {"seq": peer},
        )

    def deal_start(turn, carry):
        deal(turn, False).start()
        return carry

    lax.fori_loop(1, seq_total, deal_start, 0)
    w_own = pltpu.make_async_copy(w_ref.at[me], w_out.at[rows(me, mine)], keep.at[0])
    w_own.start()
    line.start()

    def forward(source, turn, from_peer):
        peer = lax.rem(mine + turn, width_total)
        group = peer if from_peer else mine
        where = w_out.at[rows(source, group)]
        return remote(
            where, where, f_send.at[peer, source], f_receive.at[group, source], {"width": peer}
        )

    def forward_start(source):
        for turn in range(1, width_total):
            forward(source, turn, False).start()

    def deal_pass(turn, carry):
        deal(turn, True).wait_recv()
        forward_start(lax.rem(me + turn, seq_total))
        return carry

    w_own.wait()
    forward_start(me)
    lax.fori_loop(1, seq_total, deal_pass, 0)
    line.hops(0)

    def deal_end(turn, carry):
        deal(turn, False).wait_send()
        return carry

    lax.fori_loop(1, seq_total, deal_end, 0)

    def forward_end(source, carry):
        for turn in range(1, width_total):
            forward(source, turn, False).wait_send()
            forward(source, turn, True).wait_recv()
        return carry

    lax.fori_loop(0, seq_total, forward_end, 0)
    line.finish()


def gather_rows(x, pieces, collective_id):
    seq_total, width_total = lax.axis_size("seq"), lax.axis_size("width")
    parts, rows, model_width = x.shape
    whole = (parts, rows * seq_total, model_width)
    weight = (seq_total * width_total * pieces.shape[1], pieces.shape[2])
    dma = pltpu.SemaphoreType.DMA
    return pl.pallas_call(
        gather_kernel,
        in_specs=[ANY] * 2,
        out_specs=[ANY] * 2,
        out_shape=[
            jax.ShapeDtypeStruct(whole, x.dtype),
            jax.ShapeDtypeStruct(weight, pieces.dtype),
        ],
        scratch_shapes=[
            dma((seq_total,)),
            dma((seq_total,)),
            dma((width_total, seq_total)),
            dma((width_total, seq_total)),
            dma((1,)),
        ]
        + line_sems(seq_total // 2, parts),
        compiler_params=pltpu.CompilerParams(
            collective_id=collective_id, has_side_effects=True
        ),
        cost_estimate=pl.CostEstimate(
            flops=80 * 10**9, bytes_accessed=200 * 10**6, transcendentals=0
        ),
        name="gather_rows",
    )(x, pieces)


def home_kernel(
    layout,
    normed_ref,
    columns_ref,
    gconv_ref,
    gcols_ref,
    ghead_ref,
    in_gain_ref,
    dproj_ref,
    grad_ref,
    gnorm_ref,
    shard_in_ref,
    shard_out_ref,
    taps_out,
    bias_out,
    gain_out,
    head_out,
    in_gain_out,
    zx_ref,
    bc_ref,
    small_out,
    line_buffer,
    blocks_in,
    acc,
    stage,
    arrived,
    last_arrived,
    sum_x,
    sum_z,
    sum_b,
    small_stage,
    small_slots,
    fetch,
    in_sems,
    zx_send,
    zx_receive,
    bc_send,
    bc_receive,
    small_send,
    small_receive,
    last_send,
    last_receive,
    bc_total,
    bc_last,
    bc_last_send,
    bc_last_receive,
    *out_refs,
):
    seq_total, width_total, quarter, width, slots, shard, heads = layout
    micros = normed_ref.shape[0]
    me, mine = lax.axis_index("seq"), lax.axis_index("width")
    depth = quarter * width_total
    conv_width = 2 * STATE + width
    per_tile = TILE // depth
    tiles = seq_total // per_tile
    rows_in = Tiles(normed_ref, blocks_in, fetch, per_tile)
    meeting = Meeting(stage, arrived, last_arrived, in_sems)
    out_grad = OutGrad(grad_ref, gnorm_ref, out_refs)
    out_grad.tiles.begin()
    greet_all()

    def out_multiply(turn, carry):
        out_grad.multiply(turn)

        @pl.when(turn >= MIDDLE)
        def _():
            out_grad.tiles.each(turn - MIDDLE, out_grad.meeting.middle)

        @pl.when(turn >= LAST)
        def _():
            out_grad.tiles.each(turn - LAST, out_grad.combine)

        return carry

    rows_in.begin()
    lax.fori_loop(0, tiles, out_multiply, 0)

    conv_end = conv_width + width
    small_stage[:, :conv_width] = gconv_ref[...]
    small_stage[:, conv_width:conv_end] = gcols_ref[...]
    small_stage[:, conv_end : conv_end + LANES] = ghead_ref[...]

    def block_copy(sums, sem_row, number, block, second, action):
        low = (number * width) // shard
        high = ((number + 1) * width - 1) // shard
        owner = high if second else low
        slot = number - (owner * shard) // width

        def act():
            both(
                (owner == mine) & (block == me),
                sums.at[block],
                zx_ref.at[slot, mine],
                zx_send.at[sem_row, block],
                zx_receive.at[slot, mine],
                {"width": owner, "seq": block},
                action,
            )

        if second:
            pl.when(high != low)(act)
        else:
            act()

    def bc_copy(block, action):
        both(
            block == me,
            sum_b.at[block],
            bc_ref.at[me],
            bc_send.at[block],
            bc_receive.at[me],
            {"seq": block},
            action,
        )

    def bc_home(source, action):
        both(
            (mine == width_total - 1) & (source == mine),
            bc_total,
            bc_last.at[source],
            bc_last_send.at[0],
            bc_last_receive.at[source],
            {"width": width_total - 1},
            action,
        )

    def pieces_of(block, action):
        for second in (False, True):
            block_copy(sum_z, int(second), me, block, second, action)
            block_copy(sum_x, 2 + int(second), seq_total + me, block, second, action)
        bc_copy(block, action)

    def combine(block):
        low = meeting.total(block).astype(BF16)
        sum_b[block, :, : 2 * STATE] = low[:, : 2 * STATE]
        sum_x[block] = low[:, 2 * STATE : conv_width]
        sum_z[block] = low[:, conv_width : conv_width + width]
        sum_b[block, :, 2 * STATE :] = low[:, conv_width + width :]
        pieces_of(block, "start")

    def multiply(turn, carry):
        tile = rows_in.turned(turn)
        for chunk in range(rows_in.chunks):
            micro, rows, block = rows_in.block(turn, chunk)
            part = mm_tn(block, dproj_ref[micro, rows, :])
            acc[...] = part if chunk == 0 else acc[...] + part
            rows_in.used(turn, chunk)
        for item in range(per_tile):
            block = tile * per_tile + item
            for group in range(width_total):
                row = item * depth + group * quarter
                stage[block, meeting.slot(block, group)] = acc[row : row + quarter].astype(BF16)
            meeting.first(block).start()
        weights = columns_ref[pl.ds(pl.multiple_of(tile * TILE, TILE), TILE), :]
        product = (acc[...] * weights.astype(F32)).astype(BF16)
        line = mm_nt(jnp.ones((8, product.shape[1]), BF16), product)
        small_stage[pl.ds(tile, 1), conv_end + LANES :] = line[:1]

        @pl.when(turn < MIDDLE)
        def _():
            out_grad.tiles.each(tiles - MIDDLE + turn, out_grad.meeting.middle)

        @pl.when(turn >= MIDDLE)
        def _():
            rows_in.each(turn - MIDDLE, meeting.middle)

        @pl.when(turn < LAST)
        def _():
            out_grad.tiles.each(tiles - LAST + turn, out_grad.combine)

        @pl.when(turn >= LAST)
        def _():
            rows_in.each(turn - LAST, combine)

        return carry

    lax.fori_loop(0, tiles, multiply, 0)

    def small_hop(turn, from_peer):
        peer = lax.rem(mine + turn, width_total)
        group = peer if from_peer else mine
        return remote(
            small_stage,
            small_slots.at[group],
            small_send.at[peer],
            small_receive.at[group],
            {"width": peer},
        )

    for turn in range(1, width_total):
        small_hop(turn, False).start()
    small_slots[mine] = small_stage[...]

    for turn in range(tiles - MIDDLE, tiles):
        rows_in.each(turn, meeting.middle)
    for turn in range(tiles - LAST, tiles):
        rows_in.each(turn, combine)

    for turn in range(1, width_total):
        small_hop(turn, True).wait_recv()
        small_hop(turn, False).wait_send()
    total = small_slots[0]
    for group in range(1, width_total):
        total = total + small_slots[group]
    small_stage[...] = total

    def last_hop(turn, from_peer):
        peer = lax.rem(me + turn, seq_total)
        owner = peer if from_peer else me
        return remote(
            small_stage,
            small_out.at[owner],
            last_send.at[peer],
            last_receive.at[owner],
            {"seq": peer},
        )

    def last_start(turn, carry):
        last_hop(turn, False).start()
        return carry

    lax.fori_loop(1, seq_total, last_start, 0)
    small_out[me] = small_stage[...]

    out_grad.finish(shard_out_ref)

    def bc_arrive(turn, carry):
        source = lax.rem(me + turn, seq_total)
        both(
            source == me,
            sum_b.at[me],
            bc_ref.at[source],
            bc_send.at[me],
            bc_receive.at[source],
            {"seq": source},
            "receive",
        )
        return carry

    lax.fori_loop(0, seq_total, bc_arrive, 0)

    def bc_add(source, total):
        return total + bc_ref[source, :, : 2 * STATE].astype(F32)

    bc_sum = lax.fori_loop(1, seq_total, bc_add, bc_ref[0, :, : 2 * STATE].astype(F32))
    bc_total[:, : 2 * STATE] = bc_sum.astype(BF16)
    for source in range(seq_total):
        at = 2 * STATE + source * heads
        bc_total[:, at : at + heads] = bc_ref[source, :, 2 * STATE : 2 * STATE + heads]
    bc_home(mine, "start")

    def last_end(turn, carry):
        last_hop(turn, False).wait_send()
        last_hop(turn, True).wait_recv()
        return carry

    lax.fori_loop(1, seq_total, last_end, 0)

    def small_add(source, total):
        return total + small_out[source]

    total = lax.fori_loop(1, seq_total, small_add, small_out[0])
    taps_out[:, INNER:] = total[:TAPS, : 2 * STATE]
    bias_out[:, INNER:] = total[TAPS : TAPS + 1, : 2 * STATE]
    in_gain_out[...] = total[:, conv_end + LANES :] / in_gain_ref[...]
    for source in range(seq_total):
        first = source * width
        taps_out[:, first : first + width] = small_out[source, :TAPS, 2 * STATE : conv_width]
        bias_out[:, first : first + width] = small_out[
            source, TAPS : TAPS + 1, 2 * STATE : conv_width
        ]
        gain_out[:, first : first + width] = small_out[source, 1:2, conv_width:conv_end]
        head_out[:, source * heads : (source + 1) * heads] = small_out[
            source, :, conv_end : conv_end + heads
        ]

    first = (mine * shard) // width

    def landed(slot, carry):
        number = first + slot
        source = lax.rem(number, seq_total)

        @pl.when((number < 2 * seq_total) & (number * width < (mine + 1) * shard))
        def _():
            for group in range(width_total):
                both(
                    (source == me) & (mine == group),
                    sum_z.at[me],
                    zx_ref.at[slot, group],
                    zx_send.at[0, me],
                    zx_receive.at[slot, group],
                    {"width": group, "seq": source},
                    "receive",
                )

        return carry

    lax.fori_loop(0, slots, landed, 0)

    @pl.when(mine == width_total - 1)
    def _():
        for source in range(width_total):
            bc_home(source, "receive")

    edge = (slots - -(-(2 * STATE + HEADS) // width)) * width
    for group in range(width_total):
        for slot in range(slots):
            line_buffer[:, slot * width : (slot + 1) * width] = zx_ref[slot, group].astype(F32)

        @pl.when(mine == width_total - 1)
        def _():
            line_buffer[:, edge : edge + 2 * STATE + HEADS] = bc_last[
                group, :, : 2 * STATE + HEADS
            ].astype(F32)

        total_lanes = line_buffer.shape[1]
        start = lax.rem(mine * shard, jnp.int32(width))
        rolled = pltpu.roll(
            line_buffer[...], lax.rem(total_lanes - start, jnp.int32(total_lanes)), 1
        )
        shard_in_ref[group * quarter : (group + 1) * quarter, :] = rolled[:, :shard].astype(BF16)

    def sent(block, carry):
        meeting.sent(block)
        pieces_of(block, "send")
        return carry

    lax.fori_loop(0, seq_total, sent, 0)
    bc_home(mine, "send")


def bring_home(normed, dproj, columns, smalls, in_gain, grad, gnorm, heads, collective_id):
    seq_total, width_total = lax.axis_size("seq"), lax.axis_size("width")
    width = heads * HEAD_DIM
    micros, group_rows, model_width = normed.shape
    depth = model_width // seq_total
    quarter = depth // width_total
    shard = (INNER + CONV + HEADS) // width_total
    slots = max(
        ((group + 1) * shard - 1) // width - group * shard // width + 1
        for group in range(width_total)
    )
    all_columns = dproj.shape[2]
    layout = (seq_total, width_total, quarter, width, slots, shard, heads)
    rest = all_columns - 2 * width
    small = (8, 2 * STATE + 2 * width + LANES + TILE)
    lanes = -(-slots * width // LANES) * LANES
    dma = pltpu.SemaphoreType.DMA
    vmem = pl.BlockSpec(memory_space=pltpu.VMEM)
    return pl.pallas_call(
        partial(home_kernel, layout),
        in_specs=[ANY] + [vmem] * 6 + [ANY, vmem],
        out_specs=[vmem] * 7,
        out_shape=[
            jax.ShapeDtypeStruct((depth, shard), BF16),
            jax.ShapeDtypeStruct((seq_total // width_total * width, model_width // seq_total), F32),
            jax.ShapeDtypeStruct((TAPS, CONV), F32),
            jax.ShapeDtypeStruct((1, CONV), F32),
            jax.ShapeDtypeStruct((1, INNER), F32),
            jax.ShapeDtypeStruct((8, HEADS), F32),
            jax.ShapeDtypeStruct(in_gain.shape, F32),
        ],
        scratch_shapes=[
            pltpu.VMEM((slots, width_total, quarter, width), BF16),
            pltpu.VMEM((seq_total, quarter, rest), BF16),
            pltpu.VMEM((seq_total,) + small, F32),
            pltpu.VMEM((quarter, lanes), F32),
            pltpu.VMEM((2, min(group_rows, 1024), TILE), BF16),
            pltpu.VMEM((TILE, all_columns), F32),
            pltpu.VMEM((seq_total, width_total, quarter, all_columns), BF16),
            pltpu.VMEM((seq_total, 2, quarter, all_columns), BF16),
            pltpu.VMEM((seq_total, quarter, all_columns), BF16),
            pltpu.VMEM((seq_total, quarter, width), BF16),
            pltpu.VMEM((seq_total, quarter, width), BF16),
            pltpu.VMEM((seq_total, quarter, rest), BF16),
            pltpu.VMEM(small, F32),
            pltpu.VMEM((width_total,) + small, F32),
            dma((2,)),
            dma((4, seq_total)),
            dma((4, seq_total)),
            dma((slots, width_total)),
            dma((seq_total,)),
            dma((seq_total,)),
            dma((width_total,)),
            dma((width_total,)),
            dma((seq_total,)),
            dma((seq_total,)),
            pltpu.VMEM((quarter, rest), BF16),
            pltpu.VMEM((width_total, quarter, rest), BF16),
            dma((1,)),
            dma((width_total,)),
        ]
        + out_grad_scratch(heads, group_rows, model_width),
        compiler_params=pltpu.CompilerParams(
            collective_id=collective_id, has_side_effects=True, vmem_limit_bytes=62 << 20
        ),
        cost_estimate=pl.CostEstimate(
            flops=150 * 10**9, bytes_accessed=8 * normed.size, transcendentals=0
        ),
        name="bring_home",
    )(normed, columns, *smalls, in_gain, dproj, grad, gnorm)


def own(value, start, count, axis=0):
    return lax.dynamic_slice_in_dim(value, start, count, axis)


def per_device(
    hidden_in,
    starts,
    in_gain,
    in_weight,
    conv_weight,
    conv_bias,
    step_bias,
    decay_log,
    skip_gain,
    gate_gain,
    out_weight,
    cotangent,
):
    seq_total = lax.axis_size("seq")
    seq_index = lax.axis_index("seq")
    group_index = lax.axis_index("width")
    micros, rows, model_width = hidden_in.shape[1:]
    heads = HEADS // seq_total
    width = heads * HEAD_DIM
    depth = in_weight.shape[0]
    head_count = HEADS // 8 * jnp.left_shift(jnp.int32(1), group_index)
    active = head_count.astype(F32) * HEAD_DIM

    hidden = hidden_in[0].astype(F32)
    grads = cotangent[0]
    root_in = lax.rsqrt(jnp.mean(hidden * hidden, axis=2, keepdims=True) + EPSILON)
    normed = (hidden * root_in * in_gain).astype(BF16)

    dt_pad = LANES
    width_total = lax.axis_size("width")
    quarter = depth // width_total
    in_quarter = own(in_weight, group_index * quarter, quarter)
    gates = in_quarter[:, :INNER].reshape(quarter, seq_total, width)
    xs = in_quarter[:, INNER : 2 * INNER].reshape(quarter, seq_total, width)
    bc = jnp.broadcast_to(
        in_quarter[:, None, 2 * INNER : INNER + CONV], (quarter, seq_total, 2 * STATE)
    )
    dts = in_quarter[:, INNER + CONV :].reshape(quarter, seq_total, heads)
    dts = jnp.pad(dts, ((0, 0), (0, 0), (0, dt_pad - heads)))
    pieces = jnp.concatenate([bc, xs, gates, dts], axis=2).transpose(1, 0, 2)
    all_normed, columns = gather_rows(normed, pieces, 0)

    smalls = [
        conv_weight,
        conv_bias[None],
        gate_gain[None],
        skip_gain[None],
        step_bias[None],
        decay_log[None],
    ]
    forward = run_forward(
        heads, starts[0], all_normed, columns, out_weight, grads, smalls, 3
    )
    proj, gg, branch, mixed, states, tails, sums = forward[:7]
    taps, cols, head, expand, gather, tri, all_grad = forward[7:14]
    chip_wise = dict(axis_index_groups=chip_groups(seq_total), scatter_dimension=0, tiled=True)
    branch = lax.psum_scatter(branch, "seq", **chip_wise)
    dnorm, sums = run_cross(all_grad, out_weight, gg, sums, 1)
    roots = lax.rsqrt(sums[:, : 2 * micros : 2] / active + EPSILON)
    own_roots = own(roots, seq_index, 1).reshape(micros, rows, 1)
    all_roots = roots.transpose(1, 0, 2).reshape(micros, seq_total * rows, 1)
    gnorm = (gg.astype(F32) * all_roots).astype(BF16)

    dproj, partial_rows, *smalls = run_backward(
        heads,
        starts[0],
        active[None],
        proj,
        dnorm,
        mixed,
        states,
        tails,
        sums,
        columns,
        [taps, head, cols, expand, gather, tri],
        4,
    )
    smalls.pop()
    scattered = lax.psum_scatter(partial_rows, "seq", **chip_wise)
    head_sums, branch = lax.optimization_barrier((smalls[2], branch))
    home = bring_home(
        all_normed,
        dproj,
        columns,
        [smalls[0], smalls[1], head_sums],
        in_gain.reshape(-1, TILE),
        all_grad,
        gnorm,
        heads,
        2,
    )
    shard_in, shard_out, taps_sum, bias_sum, gain_sum, head_sums, in_gain_sum = home
    output = hidden + branch.reshape(hidden.shape).astype(F32) * own_roots
    scattered, in_gain_sum = lax.optimization_barrier((scattered, in_gain_sum))
    gained = scattered.reshape(hidden.shape).astype(F32) * in_gain
    pull = jnp.mean(gained * hidden, axis=2, keepdims=True) * (root_in * root_in * root_in)
    hidden_grads = grads.astype(F32) + root_in * gained - hidden * pull
    shape = hidden_in.shape
    return (
        output.astype(BF16).reshape(shape),
        hidden_grads.astype(BF16).reshape(shape),
        in_gain_sum.reshape(-1),
        shard_in.astype(F32),
        taps_sum,
        bias_sum[0],
        head_sums[1],
        head_sums[0],
        head_sums[2],
        gain_sum[0],
        shard_out,
    )


def solution(mesh):
    in_specs = (
        P("width", None, "seq", None),
        P("width", None, None),
        P(),
        P("seq", None),
        P(),
        P(),
        P(),
        P(),
        P(),
        P(),
        P("seq", None),
        P("width", None, "seq", None),
    )
    out_specs = (
        P("width", None, "seq", None),
        P("width", None, "seq", None),
        P(),
        P("seq", "width"),
        P(),
        P(),
        P(),
        P(),
        P(),
        P(),
        P("width", "seq"),
    )
    return jax.shard_map(
        per_device, mesh=mesh, in_specs=in_specs, out_specs=out_specs, check_vma=False
    )
```

```python
from functools import partial

import jax
import jax.numpy as jnp
from jax import lax
from jax.experimental import pallas as pl
from jax.experimental.pallas import tpu as pltpu
from jax.sharding import PartitionSpec as P

INNER = 4096
HEADS = 64
HEAD_DIM = 64
STATE = 128
CONV = 4352
EPSILON = 1e-05
LANES = 128
TAPS = 4
NEG = -1e30
F32 = jnp.float32
BF16 = jnp.bfloat16


def mm(a, b):
    return lax.dot_general(a, b, (((1,), (0,)), ((), ())), preferred_element_type=F32)


def mm_nt(a, b):
    return lax.dot_general(a, b, (((1,), (1,)), ((), ())), preferred_element_type=F32)


def mm_tn(a, b):
    return lax.dot_general(a, b, (((0,), (0,)), ((), ())), preferred_element_type=F32)


def halves(value, axis):
    high = value.astype(BF16)
    low = (value - high.astype(F32)).astype(BF16)
    return jnp.concatenate([high, low], axis=axis)


def sigmoid(value):
    return 0.5 * jnp.tanh(0.5 * value) + 0.5


def prefix_sum(tri, value):
    high = value.astype(BF16)
    rest = value - high.astype(F32)
    middle = rest.astype(BF16)
    low = (rest - middle.astype(F32)).astype(BF16)
    parts = mm(tri, jnp.concatenate([high, middle, low], axis=1))
    width = value.shape[1]
    return parts[:, :width] + parts[:, width : 2 * width] + parts[:, 2 * width :]


def doc_number(starts_ref, micro, positions):
    count = jnp.zeros_like(positions)
    for item in range(starts_ref.shape[1]):
        count = count + (starts_ref[micro, item] <= positions).astype(jnp.int32)
    return count


MESH = pl.DeviceIdType.MESH
ANY = pl.BlockSpec(memory_space=pl.ANY)


def hear(axes):
    waits = sum(lax.axis_size(axis) - 1 for axis in axes)
    pl.semaphore_wait(pltpu.get_barrier_semaphore(), waits)


def greet(axes, hear=True):
    barrier = pltpu.get_barrier_semaphore()
    waits = 0
    for axis in axes:
        count, me = lax.axis_size(axis), lax.axis_index(axis)

        def hello(turn, carry):
            pl.semaphore_signal(
                barrier,
                inc=1,
                device_id={axis: lax.rem(me + turn, count)},
                device_id_type=MESH,
            )
            return carry

        lax.fori_loop(1, count, hello, 0)
        waits += count - 1
    if hear:
        pl.semaphore_wait(barrier, waits)


def remote(source, target, send, receive, device):
    return pltpu.make_async_remote_copy(
        src_ref=source,
        dst_ref=target,
        send_sem=send,
        recv_sem=receive,
        device_id=device,
        device_id_type=MESH,
    )


class Line:
    def __init__(self, source, out, sems):
        self.source, self.out = source, out
        self.up, self.down, self.receive, self.side_send, self.side_receive, self.keep = sems
        self.me = lax.axis_index("seq")
        self.chips = lax.axis_size("seq") // 2
        self.chip, self.core = self.me // 2, lax.rem(self.me, 2)
        self.parts, self.rows = source.shape[:2]

    def at(self, owner, part):
        return self.out.at[part, pl.ds(pl.multiple_of(owner * self.rows, 8), self.rows)]

    def line(self, source, owner_chip, part, target_chip, sems):
        return remote(
            source,
            self.at(owner_chip * 2 + self.core, part),
            sems.at[owner_chip, part],
            self.receive.at[owner_chip, part],
            {"seq": target_chip * 2 + self.core},
        )

    def side(self, source, owner_chip, part, from_sibling):
        core = 1 - self.core if from_sibling else self.core
        return remote(
            source,
            self.at(owner_chip * 2 + core, part),
            self.side_send.at[owner_chip, part],
            self.side_receive.at[owner_chip, part],
            {"seq": self.chip * 2 + 1 - self.core},
        )

    def stay(self, part):
        return pltpu.make_async_copy(
            self.source.at[part], self.at(self.me, part), self.keep.at[part]
        )

    def start(self):
        for part in range(self.parts):
            here = self.source.at[part]

            @pl.when(self.chip + 1 < self.chips)
            def _():
                self.line(here, self.chip, part, self.chip + 1, self.up).start()

            @pl.when(self.chip >= 1)
            def _():
                self.line(here, self.chip, part, self.chip - 1, self.down).start()

            self.side(here, self.chip, part, False).start()
            self.stay(part).start()

    def events(self):
        return (self.chips - 1) * self.parts

    def hop(self, event):
        turn, part = event // self.parts + 1, lax.rem(event, self.parts)
        below, above = self.chip - turn, self.chip + turn

        @pl.when(below >= 0)
        def _():
            here = self.at(below * 2 + self.core, part)
            self.line(here, below, part, self.chip, self.up).wait_recv()

            @pl.when(self.chip + 1 < self.chips)
            def _():
                self.line(here, below, part, self.chip + 1, self.up).start()

            self.side(here, below, part, False).start()

        @pl.when(above < self.chips)
        def _():
            here = self.at(above * 2 + self.core, part)
            self.line(here, above, part, self.chip, self.down).wait_recv()

            @pl.when(self.chip >= 1)
            def _():
                self.line(here, above, part, self.chip - 1, self.down).start()

            self.side(here, above, part, False).start()

    def hops(self, first):
        def body(event, carry):
            self.hop(event)
            return carry

        lax.fori_loop(first, self.events(), body, 0)

    def finish(self):
        def body(owner_chip, carry):
            for part in range(self.parts):
                here = self.at(owner_chip * 2 + self.core, part)

                @pl.when((owner_chip <= self.chip) & (self.chip + 1 < self.chips))
                def _():
                    self.line(here, owner_chip, part, self.chip + 1, self.up).wait_send()

                @pl.when((owner_chip >= self.chip) & (self.chip >= 1))
                def _():
                    self.line(here, owner_chip, part, self.chip - 1, self.down).wait_send()

                self.side(here, owner_chip, part, False).wait_send()
                self.side(here, owner_chip, part, True).wait_recv()
            return carry

        lax.fori_loop(0, self.chips, body, 0)
        for part in range(self.parts):
            self.stay(part).wait()


def line_sems(chips, parts):
    return [pltpu.SemaphoreType.DMA((chips, parts))] * 5 + [pltpu.SemaphoreType.DMA((parts,))]


TILE = 256
MIDDLE = 2
LAST = 4


def call_all():
    seq_total, width_total = lax.axis_size("seq"), lax.axis_size("width")
    count = seq_total * width_total
    place = lax.axis_index("width") * seq_total + lax.axis_index("seq")
    barrier = pltpu.get_barrier_semaphore()

    def hello(turn, carry):
        peer = lax.rem(place + turn, count)
        pl.semaphore_signal(
            barrier,
            inc=1,
            device_id={"width": peer // seq_total, "seq": lax.rem(peer, seq_total)},
            device_id_type=MESH,
        )
        return carry

    lax.fori_loop(1, count, hello, 0)


def hear_all():
    count = lax.axis_size("seq") * lax.axis_size("width")
    pl.semaphore_wait(pltpu.get_barrier_semaphore(), count - 1)


def both(is_here, source, target, send, receive, device, action):
    if action != "send":

        @pl.when(is_here)
        def _():
            stay = pltpu.make_async_copy(source, target, receive)
            if action == "start":
                stay.start()
            else:
                stay.wait()

    @pl.when(jnp.logical_not(is_here))
    def _():
        away = remote(source, target, send, receive, device)
        if action == "start":
            away.start()
        elif action == "receive":
            away.wait_recv()
        else:
            away.wait_send()


class Meeting:
    def __init__(self, parts, come, last, sems):
        self.parts, self.come, self.last, self.sems = parts, come, last, sems
        mine = lax.axis_index("width")
        self.upper, self.lower = mine // 2, lax.rem(mine, 2)

    def order(self, block):
        odd = lax.rem(block, 2)
        even = 1 - odd
        first = odd * self.upper + even * self.lower
        second = odd * self.lower + even * self.upper
        across = 2 * (1 - self.upper) + self.lower
        beside = 2 * self.upper + 1 - self.lower
        return first, second, odd * across + even * beside, odd * beside + even * across

    def slot(self, block, group):
        odd = lax.rem(block, 2)
        return odd * group + (1 - odd) * (group % 2 * 2 + group // 2)

    def first(self, block):
        side, _, partner, _ = self.order(block)
        return remote(
            self.parts.at[block, pl.ds(2 * (1 - side), 2)],
            self.come.at[block],
            self.sems.at[0, block],
            self.sems.at[1, block],
            {"width": partner},
        )

    def second(self, block):
        side, place, _, partner = self.order(block)
        return remote(
            self.parts.at[block, 2 * side + 1 - place],
            self.last.at[block],
            self.sems.at[2, block],
            self.sems.at[3, block],
            {"width": partner},
        )

    def middle(self, block):
        self.first(block).wait_recv()
        side = self.order(block)[0]
        for item in range(2):
            slot = 2 * side + item
            total = self.parts[block, slot].astype(F32) + self.come[block, item].astype(F32)
            self.parts[block, slot] = total.astype(BF16)
        self.second(block).start()

    def total(self, block):
        self.second(block).wait_recv()
        side, place = self.order(block)[:2]
        return self.parts[block, 2 * side + place].astype(F32) + self.last[block].astype(F32)

    def sent(self, block):
        self.first(block).wait_send()
        self.second(block).wait_send()


class Tiles:
    def __init__(self, source, blocks, sems, per_tile):
        self.source, self.blocks, self.sems, self.per_tile = source, blocks, sems, per_tile
        self.total = source.shape[2] // TILE
        self.chunk_rows = blocks.shape[1]
        self.pieces = source.shape[1] // self.chunk_rows
        self.chunks = source.shape[0] * self.pieces

    def turned(self, turn):
        return lax.rem(turn + lax.axis_index("seq") // self.per_tile, self.total)

    def fetch(self, turn, chunk):
        first = chunk % self.pieces * self.chunk_rows
        return pltpu.make_async_copy(
            self.source.at[
                chunk // self.pieces,
                pl.ds(first, self.chunk_rows),
                pl.ds(pl.multiple_of(self.turned(turn) * TILE, TILE), TILE),
            ],
            self.blocks.at[chunk % 2],
            self.sems.at[chunk % 2],
        )

    def begin(self):
        self.fetch(0, 0).start()
        self.fetch(0, 1).start()

    def block(self, turn, chunk):
        self.fetch(turn, chunk).wait()
        first = chunk % self.pieces * self.chunk_rows
        return chunk // self.pieces, slice(first, first + self.chunk_rows), self.blocks[chunk % 2]

    def used(self, turn, chunk):
        if chunk + 2 < self.chunks:
            self.fetch(turn, chunk + 2).start()
        else:

            @pl.when(turn + 1 < self.total)
            def _():
                self.fetch(turn + 1, chunk + 2 - self.chunks).start()

    def each(self, turn, act):
        for item in range(self.per_tile):
            act(self.turned(turn) * self.per_tile + item)


class OutGrad:
    def __init__(self, grad, gnorm, refs):
        (
            blocks,
            self.acc,
            self.stage,
            come,
            last,
            self.sums,
            self.landing,
            fetch,
            sems,
            self.send,
            self.receive,
        ) = refs
        self.gnorm = gnorm
        self.sub, self.cols = self.stage.shape[2:]
        self.meeting = Meeting(self.stage, come, last, sems)
        self.tiles = Tiles(grad, blocks, fetch, TILE // self.cols)
        self.width_total = lax.axis_size("width")
        self.seq_total = lax.axis_size("seq")
        self.owners = self.seq_total // self.width_total
        self.me, self.mine = lax.axis_index("seq"), lax.axis_index("width")

    def copy(self, target, action):
        owner = self.me // self.owners
        place = self.landing.at[lax.rem(self.me, self.owners), self.mine]
        receive = self.receive.at[lax.rem(self.me, self.owners), self.mine]
        both(
            (owner == self.mine) & (target == self.me),
            self.sums.at[target],
            place,
            self.send.at[target],
            receive,
            {"width": owner, "seq": target},
            action,
        )

    def combine(self, block):
        self.sums[block] = self.meeting.total(block).astype(BF16)
        self.copy(block, "start")

    def multiply(self, turn):
        for chunk in range(self.tiles.chunks):
            micro, rows, block = self.tiles.block(turn, chunk)
            part = mm_tn(self.gnorm[micro, rows, :], block)
            self.acc[...] = part if chunk == 0 else self.acc[...] + part
            self.tiles.used(turn, chunk)
        pl.when(turn == 0)(hear_all)
        for item in range(self.tiles.per_tile):
            block = self.tiles.turned(turn) * self.tiles.per_tile + item
            for group in range(self.width_total):
                self.stage[block, self.meeting.slot(block, group)] = self.acc[
                    group * self.sub : (group + 1) * self.sub,
                    item * self.cols : (item + 1) * self.cols,
                ].astype(BF16)
            self.meeting.first(block).start()

    def finish(self, out_ref):
        def sent(block, carry):
            self.meeting.sent(block)
            self.copy(block, "send")
            return carry

        lax.fori_loop(0, self.seq_total, sent, 0)
        for item in range(self.owners):
            for group in range(self.width_total):
                source = self.mine * self.owners + item
                both(
                    (source == self.me) & (self.mine == group),
                    self.sums.at[self.me],
                    self.landing.at[item, group],
                    self.send.at[self.me],
                    self.receive.at[item, group],
                    {"width": group, "seq": source},
                    "receive",
                )
                row = (item * self.width_total + group) * self.sub
                out_ref[row : row + self.sub, :] = self.landing[item, group].astype(F32)


def out_grad_scratch(heads, group_rows, model_width):
    seq_total, width_total = lax.axis_size("seq"), lax.axis_size("width")
    sub, cols = heads * HEAD_DIM // width_total, model_width // seq_total
    owners = seq_total // width_total
    dma = pltpu.SemaphoreType.DMA
    return [
        pltpu.VMEM((2, min(group_rows, 1024), TILE), BF16),
        pltpu.VMEM((heads * HEAD_DIM, TILE), F32),
        pltpu.VMEM((seq_total, width_total, sub, cols), BF16),
        pltpu.VMEM((seq_total, 2, sub, cols), BF16),
        pltpu.VMEM((seq_total, sub, cols), BF16),
        pltpu.VMEM((seq_total, sub, cols), BF16),
        pltpu.VMEM((owners, width_total, sub, cols), BF16),
        dma((2,)),
        dma((4, seq_total)),
        dma((seq_total,)),
        dma((owners, width_total)),
    ]


class PairSum:
    def __init__(self, out, come, refs):
        self.out, self.come = out, come
        self.hold, self.leave, self.load, self.send, self.receive, self.local = refs
        me = lax.axis_index("seq")
        self.core, self.sibling = lax.rem(me, 2), me + 1 - 2 * lax.rem(me, 2)
        self.pairs = out.shape[0]

    def copy(self, pair):
        return remote(
            self.leave.at[lax.rem(pair, 2)],
            self.come.at[pair],
            self.send.at[pair],
            self.receive.at[pair],
            {"seq": self.sibling},
        )

    def put(self, position, earlier, block):
        pair = position // 2
        here = lax.rem(position, 2) == self.core

        @pl.when(here)
        def _():
            self.hold[lax.rem(pair, 2)] = block

        @pl.when(jnp.logical_not(here))
        def _():
            @pl.when((earlier >= 0) & (earlier < self.pairs))
            def _():
                self.copy(earlier).wait_send()

            self.leave[lax.rem(pair, 2)] = block
            self.copy(pair).start()

    def fetch(self, pair):
        return pltpu.make_async_copy(self.come.at[pair], self.load, self.local.at[0])

    def store(self, pair):
        return pltpu.make_async_copy(self.load, self.out.at[pair], self.local.at[1])

    def begin(self, pair, earlier):
        self.copy(pair).wait_recv()

        @pl.when((earlier >= 0) & (earlier < self.pairs))
        def _():
            self.store(earlier).wait()

        self.fetch(pair).start()

    def settle(self, pair):
        self.fetch(pair).wait()
        total = self.hold[lax.rem(pair, 2)].astype(F32) + self.load[...].astype(F32)
        self.load[...] = total.astype(BF16)
        self.store(pair).start()

    def finish(self, last):
        for pair in last:
            self.copy(pair).wait_send()


def pair_scratch(pairs, block, columns):
    dma = pltpu.SemaphoreType.DMA
    return [
        pltpu.VMEM((2, block, columns), BF16),
        pltpu.VMEM((2, block, columns), BF16),
        pltpu.VMEM((block, columns), BF16),
        dma((pairs,)),
        dma((pairs,)),
        dma((2,)),
    ]


def chip_groups(seq_total):
    return [list(range(core, seq_total, 2)) for core in range(2)]


class Chunk:
    def __init__(self, starts_ref, micro, chunk, rows, raw_dt, head_ref, expand, tri):
        first = chunk * rows
        column = lax.broadcasted_iota(jnp.int32, (rows, 1), 0) + first
        line = lax.broadcasted_iota(jnp.int32, (1, rows), 1) + first
        doc_col = doc_number(starts_ref, micro, column)
        doc_row = doc_number(starts_ref, micro, line)
        self.same = [
            (doc_number(starts_ref, micro, column - offset) == doc_col).astype(F32)
            for offset in range(1, TAPS)
        ]
        before = jnp.int32(0)
        last = jnp.int32(0)
        for item in range(starts_ref.shape[1]):
            before = before + (starts_ref[micro, item] <= first - 1).astype(jnp.int32)
            last = last + (starts_ref[micro, item] <= first + rows - 1).astype(jnp.int32)
        carry = (doc_col == before).astype(F32)
        same_last = (doc_col == last).astype(F32)
        self.bias = jnp.where((column >= line) & (doc_col == doc_row), 0.0, NEG)
        self.shifted_dt = raw_dt + head_ref[0:1]
        self.step = jnp.maximum(self.shifted_dt, 0.0) + jnp.log1p(
            jnp.exp(-jnp.abs(self.shifted_dt))
        )
        self.log_keep = self.step * head_ref[1:2]
        self.cum = prefix_sum(tri, self.log_keep)
        self.cum_t = self.cum.T
        carried = jnp.exp(self.cum) * carry
        left = jnp.exp(self.cum[rows - 1 :] - self.cum) * same_last
        spread = mm(
            halves(jnp.concatenate([self.step, carried, left], axis=0), 1), expand
        )
        self.step_cols = spread[:rows]
        self.carry_cols = spread[rows : 2 * rows]
        self.left_cols = spread[2 * rows :]
        self.keep_all = self.carry_cols[rows - 1 :]

    def decay(self, head):
        return jnp.exp(self.cum[:, head : head + 1] - self.cum_t[head : head + 1] + self.bias)


def head_groups(heads):
    size = 2 if heads % 2 == 0 else 1
    return size, heads // size


def stacked(value, size):
    if size == 1:
        return value.astype(BF16)
    lane = lax.broadcasted_iota(jnp.int32, value.shape, 1)
    first = jnp.where(lane < HEAD_DIM, value, 0.0)
    second = jnp.where(lane < HEAD_DIM, 0.0, value)
    return jnp.concatenate([first, second], axis=0).astype(BF16)


def convolved(ext, micro, rows, taps_ref, same):
    current = ext[micro, 8 : 8 + rows, :]
    total = taps_ref[TAPS : TAPS + 1] + taps_ref[TAPS - 1 : TAPS] * current
    views = []
    for offset in range(1, TAPS):
        view = ext[micro, 8 - offset : 8 - offset + rows, :] * same[offset - 1]
        views.append(view)
        total = total + taps_ref[TAPS - 1 - offset : TAPS - offset] * view
    return current, views, total


def forward_kernel(
    micros,
    heads,
    starts_ref,
    x_ref,
    weight_ref,
    out_weight_ref,
    g_ref,
    conv_weight_ref,
    conv_bias_ref,
    gate_gain_ref,
    skip_ref,
    step_bias_ref,
    decay_ref,
    proj_ref,
    gg_ref,
    branch_ref,
    mixed_ref,
    states_ref,
    tails_ref,
    sums_ref,
    taps_ref,
    cols_ref,
    head_ref,
    expand_ref,
    gather_ref,
    tri_ref,
    g_out,
    come_ref,
    ext,
    state,
    table,
    *sems,
):
    chunk, chunks = pl.program_id(0), pl.num_programs(0)
    rows = x_ref.shape[1]
    width = heads * HEAD_DIM
    conv_width = 2 * STATE + width
    size, groups = head_groups(heads)
    line = Line(g_ref, g_out, sems[:6])
    pairs = PairSum(branch_ref, come_ref, sems[6:])
    early = min((g_out.shape[1] // g_ref.shape[1] - 1) // 2, line.events())

    @pl.when(chunk == 0)
    def _():
        greet(("seq",))
        line.start()

    @pl.when((lax.rem(chunk, 2) == 0) & (chunk >= 2) & (chunk // 2 - 1 < early))
    def _():
        line.hop(chunk // 2 - 1)

    @pl.when((lax.rem(chunk, 2) == 0) & (chunk >= 2))
    def _():
        pairs.begin(chunk // 2 - 1, chunk // 2 - 2)

    @pl.when(chunk == 0)
    def _():
        ext[:, :8, :] = jnp.zeros((micros, 8, conv_width), F32)
        state[...] = jnp.zeros_like(state)
        me = lax.axis_index("seq")
        lane_of = lax.broadcasted_iota(jnp.int32, (LANES, width), 0)
        head_of = lax.broadcasted_iota(jnp.int32, (LANES, width), 1) // HEAD_DIM
        spread = (lane_of == head_of).astype(F32).astype(BF16)
        expand_ref[:LANES] = spread
        expand_ref[LANES:] = spread
        lane_of = lax.broadcasted_iota(jnp.int32, (width, LANES), 1)
        head_of = lax.broadcasted_iota(jnp.int32, (width, LANES), 0) // HEAD_DIM
        folded = (lane_of == head_of).astype(F32).astype(BF16)
        gather_ref[:width] = folded
        gather_ref[width:] = folded
        later = lax.broadcasted_iota(jnp.int32, (rows, rows), 0)
        sooner = lax.broadcasted_iota(jnp.int32, (rows, rows), 1)
        tri_ref[...] = (later >= sooner).astype(F32).astype(BF16)

        table[...] = jnp.zeros_like(table)
        table[0:TAPS] = conv_weight_ref[:, :INNER]
        table[TAPS : TAPS + 1] = conv_bias_ref[:, :INNER]
        table[TAPS + 1 : TAPS + 2] = gate_gain_ref[...]
        local = pltpu.roll(table[...], lax.rem(INNER - me * width, jnp.int32(INNER)), 1)[
            :, :width
        ]
        taps_ref[...] = jnp.zeros_like(taps_ref)
        taps_ref[0:TAPS, : 2 * STATE] = conv_weight_ref[:, INNER:]
        taps_ref[TAPS : TAPS + 1, : 2 * STATE] = conv_bias_ref[:, INNER:]
        taps_ref[0 : TAPS + 1, 2 * STATE :] = local[: TAPS + 1]
        head_ref[...] = jnp.zeros_like(head_ref)
        head_ref[0:1, :HEADS] = step_bias_ref[...]
        head_ref[1:2, :HEADS] = -jnp.exp(decay_ref[...])
        head_ref[2:3, :HEADS] = skip_ref[...]
        own_heads = pltpu.roll(
            head_ref[...], lax.rem(LANES - me * heads, jnp.int32(LANES)), 1
        )
        head_ref[...] = own_heads
        head_row = me * heads + (
            lax.broadcasted_iota(jnp.int32, (1, width), 1) // HEAD_DIM
        )
        limit = HEADS // 8 * jnp.left_shift(jnp.int32(1), lax.axis_index("width"))
        cols_ref[0:1] = mm(halves(own_heads, 1), expand_ref[...])[2:3]
        cols_ref[1:2] = local[TAPS + 1 : TAPS + 2]
        cols_ref[2:3] = (head_row < limit).astype(F32)
        cols_ref[3:8] = jnp.zeros((5, width), F32)

    skip, gain, mask = cols_ref[0:1], cols_ref[1:2], cols_ref[2:3]
    rows_in = x_ref[...].reshape(micros * rows, x_ref.shape[2])
    proj_ref[...] = mm(rows_in, weight_ref[...]).astype(BF16).reshape(proj_ref.shape)
    sums, gated_gains = [], []
    for micro in range(micros):
        tails_ref[micro] = ext[micro, :8, :]
        ext[micro, 8 : 8 + rows, :] = proj_ref[micro, :, :conv_width].astype(F32)
        raw_dt = proj_ref[micro, :, conv_width + width :].astype(F32)
        at = Chunk(
            starts_ref, micro, chunk, rows, raw_dt, head_ref, expand_ref[...], tri_ref[...]
        )
        conv = convolved(ext, micro, rows, taps_ref, at.same)[2]
        act = conv * sigmoid(conv)
        write = act[:, :STATE].astype(BF16)
        read = act[:, STATE : 2 * STATE].astype(BF16)
        x_heads = act[:, 2 * STATE :]
        scores = mm_nt(read, write)
        inputs = x_heads * at.step_cols
        state_in = state[micro]
        state_low = state_in.astype(BF16)
        states_ref[micro] = state_low
        outs = []
        for group in range(groups):
            matrices = [
                (at.decay(group * size + item) * scores).astype(BF16) for item in range(size)
            ]
            span = slice(group * size * HEAD_DIM, (group + 1) * size * HEAD_DIM)
            outs.append(mm(jnp.concatenate(matrices, axis=1), stacked(inputs[:, span], size)))
        mixed = jnp.concatenate(outs, axis=1) + at.carry_cols * mm(read, state_low)
        state[micro] = at.keep_all * state_in + mm_tn(
            write, (inputs * at.left_cols).astype(BF16)
        )
        mixed = mixed + skip * x_heads
        mixed_ref[micro] = mixed
        gate = proj_ref[micro, :, conv_width : conv_width + width].astype(F32)
        gated = mask * mixed * (gate * sigmoid(gate))
        gated_gain = (gated * gain).astype(BF16)
        gg_ref[micro] = gated_gain
        gated_gains.append(gated_gain)
        square = jnp.sum(gated * gated, axis=1, keepdims=True)
        lane = lax.broadcasted_iota(jnp.int32, (rows, LANES), 1)
        sums.append(jnp.where(lane == 0, square, 0.0).T[:2])
        ext[micro, :8, :] = ext[micro, rows : rows + 8, :]
    pad = sums_ref.shape[0] - 2 * micros
    if pad:
        sums.append(jnp.zeros((pad, rows), F32))
    sums_ref[...] = jnp.concatenate(sums, axis=0)
    branch = mm(jnp.concatenate(gated_gains, axis=0), out_weight_ref[...]).astype(BF16)

    @pl.when((lax.rem(chunk, 2) == 0) & (chunk >= 2))
    def _():
        pairs.settle(chunk // 2 - 1)

    pairs.put(chunk, chunk // 2 - 2, branch)

    @pl.when(chunk == chunks - 1)
    def _():
        pair_count = branch_ref.shape[0]
        line.hops(early)
        pairs.begin(jnp.int32(pair_count - 1), jnp.int32(pair_count - 2))
        pairs.settle(jnp.int32(pair_count - 1))
        line.finish()
        pairs.store(pair_count - 1).wait()
        pairs.finish(range(max(0, pair_count - 2), pair_count))


def cross_kernel(
    g_ref, out_weight_ref, gg_ref, sums_ref, dnorm_ref, total_ref, mine, slots, send, receive
):
    chunk, chunks = pl.program_id(0), pl.num_programs(0)
    micros, rows, model_width = g_ref.shape
    me = lax.axis_index("seq")

    @pl.when(chunk == 0)
    def _():
        greet(("seq",), hear=False)

    grads = g_ref[...].reshape(micros * rows, model_width)
    dnorm = mm_nt(grads, out_weight_ref[...])
    gg = gg_ref[...].reshape(micros * rows, dnorm.shape[1])
    dnorm_ref[...] = dnorm.reshape(dnorm_ref.shape)
    cross = jnp.sum(dnorm * gg.astype(F32), axis=1, keepdims=True)
    lane = lax.broadcasted_iota(jnp.int32, (rows, LANES), 1)
    lines = []
    for micro in range(micros):
        part = cross[micro * rows : (micro + 1) * rows]
        lines.append(jnp.where(lane == 1, part, 0.0).T[:2])
    pad = sums_ref.shape[0] - 2 * micros
    if pad:
        lines.append(jnp.zeros((pad, rows), F32))
    mine[chunk] = sums_ref[...] + jnp.concatenate(lines, axis=0)

    @pl.when(chunk == chunks - 1)
    def _():
        hear(("seq",))

        def copy(turn, owner):
            peer = lax.rem(me + turn, chunks)
            return remote(
                mine, slots.at[owner], send.at[peer], receive.at[owner], {"seq": peer}
            )

        def start(turn, carry):
            copy(turn, me).start()
            return carry

        def finish(turn, carry):
            copy(turn, me).wait_send()
            copy(turn, lax.rem(me + turn, chunks)).wait_recv()
            return carry

        lax.fori_loop(1, chunks, start, 0)
        slots[me] = mine[...]
        lax.fori_loop(1, chunks, finish, 0)

        def add(owner, total):
            return total + slots[owner]

        total_ref[...] = lax.fori_loop(1, chunks, add, slots[0])


def backward_kernel(
    micros,
    heads,
    starts_ref,
    active_ref,
    proj_ref,
    dnorm_ref,
    mixed_ref,
    states_ref,
    tails_ref,
    sums_ref,
    weight_ref,
    taps_ref,
    head_ref,
    cols_ref,
    expand_ref,
    gather_ref,
    tri_ref,
    dproj_ref,
    partial_ref,
    gconv_ref,
    gcols_ref,
    ghead_ref,
    come_ref,
    ext,
    heads_ext,
    dstate,
    *pair_refs,
):
    chunks = pl.num_programs(0)
    step_index = pl.program_id(0)
    rows = proj_ref.shape[1]
    pairs = PairSum(partial_ref, come_ref, pair_refs)

    @pl.when(step_index == 0)
    def _():
        heads_ext[:, :, rows:, :] = jnp.zeros((micros, TAPS - 1, 8, ext.shape[2]), F32)
        dstate[...] = jnp.zeros_like(dstate)
        gconv_ref[...] = jnp.zeros_like(gconv_ref)
        gcols_ref[...] = jnp.zeros_like(gcols_ref)
        ghead_ref[...] = jnp.zeros_like(ghead_ref)
        barrier = pltpu.get_barrier_semaphore()
        pl.semaphore_signal(
            barrier, inc=1, device_id={"seq": pairs.sibling}, device_id_type=MESH
        )

    position = chunks - 1 - step_index

    @pl.when((lax.rem(position, 2) == 1) & (step_index >= 2))
    def _():
        pairs.begin((position + 1) // 2, (position + 1) // 2 + 1)

    for micro in range(micros):
        backward_rows(
            micro,
            heads,
            chunks - 1 - step_index,
            starts_ref,
            active_ref,
            proj_ref.at[micro],
            dnorm_ref.at[micro],
            mixed_ref.at[micro],
            states_ref.at[micro],
            tails_ref.at[micro],
            sums_ref,
            taps_ref,
            head_ref,
            cols_ref,
            expand_ref,
            gather_ref,
            tri_ref,
            dproj_ref.at[micro],
            gconv_ref,
            gcols_ref,
            ghead_ref,
            ext,
            heads_ext.at[micro],
            dstate.at[micro],
        )
    d_rows = dproj_ref[...].reshape(micros * rows, dproj_ref.shape[2])
    partial_rows = mm_nt(d_rows, weight_ref[...]).astype(BF16)

    @pl.when(step_index == 0)
    def _():
        pl.semaphore_wait(pltpu.get_barrier_semaphore(), 1)

    @pl.when((lax.rem(position, 2) == 1) & (step_index >= 2))
    def _():
        pairs.settle((position + 1) // 2)

    pairs.put(position, position // 2 + 2, partial_rows)

    @pl.when(step_index == chunks - 1)
    def _():
        ghead_ref[2:3] = mm(halves(gcols_ref[...], 1), gather_ref[...])[0:1]
        pairs.begin(jnp.int32(0), jnp.int32(1))
        pairs.settle(jnp.int32(0))
        pairs.store(0).wait()
        pairs.finish(range(min(2, partial_ref.shape[0])))


def backward_rows(
    micro,
    heads,
    chunk,
    starts_ref,
    active_ref,
    proj_ref,
    dnorm_ref,
    mixed_ref,
    states_ref,
    tails_ref,
    sums_ref,
    taps_ref,
    head_ref,
    cols_ref,
    expand_ref,
    gather_ref,
    tri_ref,
    dproj_ref,
    gconv_ref,
    gcols_ref,
    ghead_ref,
    ext,
    heads_ext,
    dstate,
):
    rows = proj_ref.shape[0]
    width = heads * HEAD_DIM
    conv_width = 2 * STATE + width
    size, groups = head_groups(heads)
    skip, gain, mask = cols_ref[0:1], cols_ref[1:2], cols_ref[2:3]
    tri = tri_ref[...]
    gather = gather_ref[...]
    inverse_active = 1.0 / active_ref[0]
    sums = jnp.concatenate(
        [sums_ref[...], jnp.zeros((LANES - sums_ref.shape[0], rows), F32)], axis=0
    ).T
    ext[micro, :8, :] = tails_ref[...]
    ext[micro, 8 : 8 + rows, :] = proj_ref[:, :conv_width].astype(F32)
    raw_dt = proj_ref[:, conv_width + width :].astype(F32)
    at = Chunk(starts_ref, micro, chunk, rows, raw_dt, head_ref, expand_ref[...], tri)
    current, views, conv = convolved(ext, micro, rows, taps_ref, at.same)
    conv_sig = sigmoid(conv)
    act = conv * conv_sig
    write = act[:, :STATE].astype(BF16)
    read = act[:, STATE : 2 * STATE].astype(BF16)
    x_heads = act[:, 2 * STATE :]
    scores = mm_nt(read, write)
    inputs = x_heads * at.step_cols

    gate = proj_ref[:, conv_width : conv_width + width].astype(F32)
    gate_sig = sigmoid(gate)
    gate_act = gate * gate_sig
    masked = mask * mixed_ref[...]
    gated = masked * gate_act
    root = lax.rsqrt(sums[:, 2 * micro : 2 * micro + 1] * inverse_active + EPSILON)
    pull = root * root * root * sums[:, 2 * micro + 1 : 2 * micro + 2] * inverse_active
    dnorm = dnorm_ref[...]
    scaled = gated * root
    d_gated = root * dnorm * gain - gated * pull
    d_gate = d_gated * masked * (gate_sig * (1.0 + gate * (1.0 - gate_sig)))
    d_mixed = mask * d_gated * gate_act
    gcols_ref[0:1] += jnp.sum(d_mixed * x_heads, axis=0, keepdims=True)
    gcols_ref[1:2] += jnp.sum(dnorm * scaled, axis=0, keepdims=True)

    state_low = states_ref[...]
    d_state = dstate[...]
    d_state_low = d_state.astype(BF16)
    from_state = (d_mixed * at.carry_cols).astype(BF16)
    left = inputs * at.left_cols
    left_low = left.astype(BF16)
    d_left = mm(write, d_state_low)
    state_out = mm(read, state_low)
    d_read = mm_nt(from_state, state_low)
    d_write = mm_nt(left_low, d_state_low)
    d_mixed_low = d_mixed.astype(BF16).astype(F32)
    inputs_low = inputs.astype(BF16).astype(F32)
    d_scores = jnp.zeros((rows, rows), F32)
    locals_out, d_locals = [], []
    for group in range(groups):
        span = slice(group * size * HEAD_DIM, (group + 1) * size * HEAD_DIM)
        decays = [at.decay(group * size + item) for item in range(size)]
        matrices = [(decay * scores).astype(BF16) for decay in decays]
        in_stack = stacked(inputs[:, span], size)
        out_stack = stacked(d_mixed[:, span], size)
        locals_out.append(mm(jnp.concatenate(matrices, axis=1), in_stack))
        d_locals.append(mm_tn(jnp.concatenate(matrices, axis=0), out_stack))
        d_matrices = mm_nt(out_stack, inputs[:, span].astype(BF16))
        for item in range(size):
            d_scores = (
                d_scores + d_matrices[item * rows : (item + 1) * rows] * decays[item]
            )
    local_out = jnp.concatenate(locals_out, axis=1)
    d_local = jnp.concatenate(d_locals, axis=1)
    d_scores_low = d_scores.astype(BF16)
    d_read = d_read + mm(d_scores_low, write)
    d_write = d_write + mm_tn(d_scores_low, read)
    d_inputs = d_local + at.left_cols * d_left
    d_x = skip * d_mixed + d_inputs * at.step_cols

    passed = left * d_left
    cum_terms = (
        d_mixed_low * local_out
        + d_mixed * at.carry_cols * state_out
        - inputs_low * d_local
        - passed
    )
    kept = jnp.sum(d_state * at.keep_all * state_low.astype(F32), axis=0, keepdims=True)
    final = jnp.sum(passed, axis=0, keepdims=True) + kept
    stack = jnp.concatenate(
        [cum_terms, d_inputs * x_heads, jnp.broadcast_to(final, (8, width))], axis=0
    )
    reduced = mm(halves(stack, 1), gather)
    d_cum = reduced[:rows]
    d_step = reduced[rows : 2 * rows]
    final_row = reduced[2 * rows : 2 * rows + 1]
    total = jnp.sum(d_cum, axis=0, keepdims=True) + final_row
    d_log = total - prefix_sum(tri, d_cum) + d_cum
    d_step = d_step + d_log * head_ref[1:2]
    d_dt = d_step * sigmoid(at.shifted_dt)
    ghead_ref[0:1] += jnp.sum(d_log * at.log_keep, axis=0, keepdims=True)
    ghead_ref[1:2] += jnp.sum(d_dt, axis=0, keepdims=True)
    dstate[...] = at.keep_all * d_state + mm_tn(read, from_state)

    d_conv = jnp.concatenate([d_write, d_read, d_x], axis=1) * (
        conv_sig * (1.0 + conv * (1.0 - conv_sig))
    )
    gconv_ref[TAPS : TAPS + 1] += jnp.sum(d_conv, axis=0, keepdims=True)
    gconv_ref[TAPS - 1 : TAPS] += jnp.sum(d_conv * current, axis=0, keepdims=True)
    d_raw = taps_ref[TAPS - 1 : TAPS] * d_conv
    for offset in range(1, TAPS):
        tap = TAPS - 1 - offset
        gconv_ref[tap : tap + 1] += jnp.sum(
            d_conv * views[offset - 1], axis=0, keepdims=True
        )
        heads_ext[offset - 1, :rows, :] = d_conv * at.same[offset - 1]
        d_raw = d_raw + taps_ref[tap : tap + 1] * (
            heads_ext[offset - 1, offset : offset + rows, :]
        )
        heads_ext[offset - 1, rows:, :] = heads_ext[offset - 1, :8, :]
    dproj_ref[:, :conv_width] = d_raw.astype(BF16)
    dproj_ref[:, conv_width : conv_width + width] = d_gate.astype(BF16)
    dproj_ref[:, conv_width + width :] = d_dt.astype(BF16)


def constant(shape):
    return pl.BlockSpec(shape, lambda index: (0,) * len(shape))


def run_forward(
    heads, starts, x, weight, out_weight, g, smalls, collective_id
):
    micros, rows, model_width = g.shape
    chunks = x.shape[1] // rows
    width = heads * HEAD_DIM
    conv_width = 2 * STATE + width
    block = micros * rows
    sum_rows = -(-2 * micros // 8) * 8
    columns = weight.shape[1]

    def whole(value):
        return pl.BlockSpec(
            value.shape, lambda index: (0,) * value.ndim, pipeline_mode=pl.Buffered(1)
        )

    def row_block(size):
        return pl.BlockSpec((micros, rows, size), lambda index: (0, index, 0))

    return pl.pallas_call(
        partial(forward_kernel, micros, heads),
        grid=(chunks,),
        in_specs=[
            pl.BlockSpec(memory_space=pltpu.SMEM),
            row_block(model_width),
            whole(weight),
            whole(out_weight),
            ANY,
        ]
        + [whole(item) for item in smalls],
        out_specs=[
            row_block(columns),
            row_block(width),
            ANY,
            row_block(width),
            pl.BlockSpec((None, micros, STATE, width), lambda index: (index, 0, 0, 0)),
            pl.BlockSpec((None, micros, 8, conv_width), lambda index: (index, 0, 0, 0)),
            pl.BlockSpec((None, sum_rows, rows), lambda index: (index, 0, 0)),
            constant((8, conv_width)),
            constant((8, width)),
            constant((8, LANES)),
            constant((2 * LANES, width)),
            constant((2 * width, LANES)),
            constant((rows, rows)),
            ANY,
            ANY,
        ],
        out_shape=[
            jax.ShapeDtypeStruct((micros, chunks * rows, columns), BF16),
            jax.ShapeDtypeStruct((micros, chunks * rows, width), BF16),
            jax.ShapeDtypeStruct((chunks // 2, block, model_width), BF16),
            jax.ShapeDtypeStruct((micros, chunks * rows, width), F32),
            jax.ShapeDtypeStruct((chunks, micros, STATE, width), BF16),
            jax.ShapeDtypeStruct((chunks, micros, 8, conv_width), F32),
            jax.ShapeDtypeStruct((chunks, sum_rows, rows), F32),
            jax.ShapeDtypeStruct((8, conv_width), F32),
            jax.ShapeDtypeStruct((8, width), F32),
            jax.ShapeDtypeStruct((8, LANES), F32),
            jax.ShapeDtypeStruct((2 * LANES, width), BF16),
            jax.ShapeDtypeStruct((2 * width, LANES), BF16),
            jax.ShapeDtypeStruct((rows, rows), BF16),
            jax.ShapeDtypeStruct((micros, chunks * rows, model_width), BF16),
            jax.ShapeDtypeStruct((chunks // 2, block, model_width), BF16),
        ],
        scratch_shapes=[
            pltpu.VMEM((micros, rows + 8, conv_width), F32),
            pltpu.VMEM((micros, STATE, width), F32),
            pltpu.VMEM((8, INNER), F32),
        ]
        + line_sems(chunks // 2, micros)
        + pair_scratch(chunks // 2, block, model_width),
        compiler_params=pltpu.CompilerParams(
            collective_id=collective_id, has_side_effects=True, vmem_limit_bytes=56 << 20
        ),
        cost_estimate=pl.CostEstimate(
            flops=60 * 10**9, bytes_accessed=150 * 10**6, transcendentals=0
        ),
        name="mixer_forward",
    )(starts, x, weight, out_weight, g, *smalls)


def run_cross(g, out_weight, gg, sums, collective_id):
    chunks = sums.shape[0]
    micros, all_rows, model_width = g.shape
    rows, width = all_rows // chunks, gg.shape[2]

    def row_block(size):
        return pl.BlockSpec((micros, rows, size), lambda index: (0, index, 0))

    return pl.pallas_call(
        cross_kernel,
        grid=(chunks,),
        in_specs=[
            row_block(model_width),
            pl.BlockSpec(out_weight.shape, lambda index: (0, 0), pipeline_mode=pl.Buffered(1)),
            row_block(width),
            pl.BlockSpec((None,) + sums.shape[1:], lambda index: (index, 0, 0)),
        ],
        out_specs=[row_block(width), constant(sums.shape)],
        out_shape=[
            jax.ShapeDtypeStruct((micros, all_rows, width), F32),
            jax.ShapeDtypeStruct(sums.shape, F32),
        ],
        scratch_shapes=[
            pltpu.VMEM(sums.shape, F32),
            pltpu.VMEM((chunks,) + sums.shape, F32),
            pltpu.SemaphoreType.DMA((chunks,)),
            pltpu.SemaphoreType.DMA((chunks,)),
        ],
        compiler_params=pltpu.CompilerParams(
            collective_id=collective_id, has_side_effects=True, vmem_limit_bytes=60 << 20
        ),
        cost_estimate=pl.CostEstimate(
            flops=12 * 10**9, bytes_accessed=16 * 10**6, transcendentals=0
        ),
        name="cross_sums",
    )(g, out_weight, gg, sums)


def run_backward(
    heads,
    starts,
    active,
    proj,
    dnorm,
    mixed,
    states,
    tails,
    sums,
    weight,
    shared,
    collective_id,
):
    micros, all_rows, columns = proj.shape
    chunks = sums.shape[0]
    rows = all_rows // chunks
    width = heads * HEAD_DIM
    conv_width = 2 * STATE + width
    model_width = weight.shape[0]

    def row_block(size):
        return pl.BlockSpec((micros, rows, size), lambda index: (0, chunks - 1 - index, 0))

    def chunk_block(shape):
        return pl.BlockSpec((None, micros) + shape, lambda index: (chunks - 1 - index, 0, 0, 0))

    return pl.pallas_call(
        partial(backward_kernel, micros, heads),
        grid=(chunks,),
        in_specs=[
            pl.BlockSpec(memory_space=pltpu.SMEM),
            pl.BlockSpec(memory_space=pltpu.SMEM),
            row_block(columns),
            row_block(width),
            row_block(width),
            chunk_block((STATE, width)),
            chunk_block((8, conv_width)),
            pl.BlockSpec((None, sums.shape[1], rows), lambda index: (chunks - 1 - index, 0, 0)),
            pl.BlockSpec(weight.shape, lambda index: (0, 0), pipeline_mode=pl.Buffered(1)),
        ]
        + [constant(item.shape) for item in shared],
        out_specs=[
            row_block(columns),
            ANY,
            constant((8, conv_width)),
            constant((8, width)),
            constant((8, LANES)),
            ANY,
        ],
        out_shape=[
            jax.ShapeDtypeStruct((micros, all_rows, columns), BF16),
            jax.ShapeDtypeStruct((chunks // 2, micros * rows, model_width), BF16),
            jax.ShapeDtypeStruct((8, conv_width), F32),
            jax.ShapeDtypeStruct((8, width), F32),
            jax.ShapeDtypeStruct((8, LANES), F32),
            jax.ShapeDtypeStruct((chunks // 2, micros * rows, model_width), BF16),
        ],
        scratch_shapes=[
            pltpu.VMEM((micros, rows + 8, conv_width), F32),
            pltpu.VMEM((micros, TAPS - 1, rows + 8, conv_width), F32),
            pltpu.VMEM((micros, STATE, width), F32),
        ]
        + pair_scratch(chunks // 2, micros * rows, model_width),
        compiler_params=pltpu.CompilerParams(
            collective_id=collective_id, has_side_effects=True, vmem_limit_bytes=60 << 20
        ),
        cost_estimate=pl.CostEstimate(
            flops=60 * 10**9, bytes_accessed=60 * 10**6, transcendentals=0
        ),
        name="mixer_backward",
    )(starts, active, proj, dnorm, mixed, states, tails, sums, weight, *shared)


def gather_kernel(
    x_ref,
    w_ref,
    x_out,
    w_out,
    w_send,
    w_receive,
    f_send,
    f_receive,
    keep,
    *sems,
):
    seq_total, width_total = lax.axis_size("seq"), lax.axis_size("width")
    me, mine = lax.axis_index("seq"), lax.axis_index("width")
    quarter = w_ref.shape[1]
    depth = quarter * width_total
    line = Line(x_ref, x_out, sems)
    greet(("seq", "width"))

    def rows(source, group):
        return pl.ds(pl.multiple_of(source * depth + group * quarter, 8), quarter)

    def deal(turn, from_peer):
        peer = lax.rem(me + turn, seq_total)
        owner = peer if from_peer else me
        return remote(
            w_ref.at[peer],
            w_out.at[rows(owner, mine)],
            w_send.at[peer],
            w_receive.at[owner],
            {"seq": peer},
        )

    def deal_start(turn, carry):
        deal(turn, False).start()
        return carry

    lax.fori_loop(1, seq_total, deal_start, 0)
    w_own = pltpu.make_async_copy(w_ref.at[me], w_out.at[rows(me, mine)], keep.at[0])
    w_own.start()
    line.start()

    def forward(source, turn, from_peer):
        peer = lax.rem(mine + turn, width_total)
        group = peer if from_peer else mine
        where = w_out.at[rows(source, group)]
        return remote(
            where, where, f_send.at[peer, source], f_receive.at[group, source], {"width": peer}
        )

    def forward_start(source):
        for turn in range(1, width_total):
            forward(source, turn, False).start()

    def deal_pass(turn, carry):
        deal(turn, True).wait_recv()
        forward_start(lax.rem(me + turn, seq_total))
        return carry

    w_own.wait()
    forward_start(me)
    lax.fori_loop(1, seq_total, deal_pass, 0)
    line.hops(0)

    def deal_end(turn, carry):
        deal(turn, False).wait_send()
        return carry

    lax.fori_loop(1, seq_total, deal_end, 0)

    def forward_end(source, carry):
        for turn in range(1, width_total):
            forward(source, turn, False).wait_send()
            forward(source, turn, True).wait_recv()
        return carry

    lax.fori_loop(0, seq_total, forward_end, 0)
    line.finish()


def gather_rows(x, pieces, collective_id):
    seq_total, width_total = lax.axis_size("seq"), lax.axis_size("width")
    parts, rows, model_width = x.shape
    whole = (parts, rows * seq_total, model_width)
    weight = (seq_total * width_total * pieces.shape[1], pieces.shape[2])
    dma = pltpu.SemaphoreType.DMA
    return pl.pallas_call(
        gather_kernel,
        in_specs=[ANY] * 2,
        out_specs=[ANY] * 2,
        out_shape=[
            jax.ShapeDtypeStruct(whole, x.dtype),
            jax.ShapeDtypeStruct(weight, pieces.dtype),
        ],
        scratch_shapes=[
            dma((seq_total,)),
            dma((seq_total,)),
            dma((width_total, seq_total)),
            dma((width_total, seq_total)),
            dma((1,)),
        ]
        + line_sems(seq_total // 2, parts),
        compiler_params=pltpu.CompilerParams(
            collective_id=collective_id, has_side_effects=True
        ),
        cost_estimate=pl.CostEstimate(
            flops=80 * 10**9, bytes_accessed=200 * 10**6, transcendentals=0
        ),
        name="gather_rows",
    )(x, pieces)


def home_kernel(
    layout,
    normed_ref,
    columns_ref,
    gconv_ref,
    gcols_ref,
    ghead_ref,
    in_gain_ref,
    dproj_ref,
    grad_ref,
    gnorm_ref,
    shard_in_ref,
    shard_out_ref,
    taps_out,
    bias_out,
    gain_out,
    head_out,
    in_gain_out,
    zx_ref,
    bc_ref,
    small_out,
    line_buffer,
    blocks_in,
    acc,
    stage,
    arrived,
    last_arrived,
    sum_x,
    sum_z,
    sum_b,
    small_stage,
    small_slots,
    fetch,
    in_sems,
    zx_send,
    zx_receive,
    bc_send,
    bc_receive,
    small_send,
    small_receive,
    last_send,
    last_receive,
    bc_total,
    bc_last,
    bc_last_send,
    bc_last_receive,
    *out_refs,
):
    seq_total, width_total, quarter, width, slots, shard, heads = layout
    micros = normed_ref.shape[0]
    me, mine = lax.axis_index("seq"), lax.axis_index("width")
    depth = quarter * width_total
    conv_width = 2 * STATE + width
    per_tile = TILE // depth
    tiles = seq_total // per_tile
    rows_in = Tiles(normed_ref, blocks_in, fetch, per_tile)
    meeting = Meeting(stage, arrived, last_arrived, in_sems)
    out_grad = OutGrad(grad_ref, gnorm_ref, out_refs)
    out_grad.tiles.begin()
    call_all()

    def out_multiply(turn, carry):
        out_grad.multiply(turn)

        @pl.when(turn >= MIDDLE)
        def _():
            out_grad.tiles.each(turn - MIDDLE, out_grad.meeting.middle)

        @pl.when(turn >= LAST)
        def _():
            out_grad.tiles.each(turn - LAST, out_grad.combine)

        return carry

    rows_in.begin()
    lax.fori_loop(0, tiles, out_multiply, 0)

    conv_end = conv_width + width
    small_stage[:, :conv_width] = gconv_ref[...]
    small_stage[:, conv_width:conv_end] = gcols_ref[...]
    small_stage[:, conv_end : conv_end + LANES] = ghead_ref[...]

    def block_copy(sums, sem_row, number, block, second, action):
        low = (number * width) // shard
        high = ((number + 1) * width - 1) // shard
        owner = high if second else low
        slot = number - (owner * shard) // width

        def act():
            both(
                (owner == mine) & (block == me),
                sums.at[block],
                zx_ref.at[slot, mine],
                zx_send.at[sem_row, block],
                zx_receive.at[slot, mine],
                {"width": owner, "seq": block},
                action,
            )

        if second:
            pl.when(high != low)(act)
        else:
            act()

    def bc_copy(block, action):
        both(
            block == me,
            sum_b.at[block],
            bc_ref.at[me],
            bc_send.at[block],
            bc_receive.at[me],
            {"seq": block},
            action,
        )

    def bc_home(source, action):
        both(
            (mine == width_total - 1) & (source == mine),
            bc_total,
            bc_last.at[source],
            bc_last_send.at[0],
            bc_last_receive.at[source],
            {"width": width_total - 1},
            action,
        )

    def pieces_of(block, action):
        for second in (False, True):
            block_copy(sum_z, int(second), me, block, second, action)
            block_copy(sum_x, 2 + int(second), seq_total + me, block, second, action)
        bc_copy(block, action)

    def combine(block):
        low = meeting.total(block).astype(BF16)
        sum_b[block, :, : 2 * STATE] = low[:, : 2 * STATE]
        sum_x[block] = low[:, 2 * STATE : conv_width]
        sum_z[block] = low[:, conv_width : conv_width + width]
        sum_b[block, :, 2 * STATE :] = low[:, conv_width + width :]
        pieces_of(block, "start")

    def multiply(turn, carry):
        tile = rows_in.turned(turn)
        for chunk in range(rows_in.chunks):
            micro, rows, block = rows_in.block(turn, chunk)
            part = mm_tn(block, dproj_ref[micro, rows, :])
            acc[...] = part if chunk == 0 else acc[...] + part
            rows_in.used(turn, chunk)
        for item in range(per_tile):
            block = tile * per_tile + item
            for group in range(width_total):
                row = item * depth + group * quarter
                stage[block, meeting.slot(block, group)] = acc[row : row + quarter].astype(BF16)
            meeting.first(block).start()
        weights = columns_ref[pl.ds(pl.multiple_of(tile * TILE, TILE), TILE), :]
        product = (acc[...] * weights.astype(F32)).astype(BF16)
        line = mm_nt(jnp.ones((8, product.shape[1]), BF16), product)
        small_stage[pl.ds(tile, 1), conv_end + LANES :] = line[:1]

        @pl.when(turn < MIDDLE)
        def _():
            out_grad.tiles.each(tiles - MIDDLE + turn, out_grad.meeting.middle)

        @pl.when(turn >= MIDDLE)
        def _():
            rows_in.each(turn - MIDDLE, meeting.middle)

        @pl.when(turn < LAST)
        def _():
            out_grad.tiles.each(tiles - LAST + turn, out_grad.combine)

        @pl.when(turn >= LAST)
        def _():
            rows_in.each(turn - LAST, combine)

        return carry

    lax.fori_loop(0, tiles, multiply, 0)

    def small_hop(turn, from_peer):
        peer = lax.rem(mine + turn, width_total)
        group = peer if from_peer else mine
        return remote(
            small_stage,
            small_slots.at[group],
            small_send.at[peer],
            small_receive.at[group],
            {"width": peer},
        )

    for turn in range(1, width_total):
        small_hop(turn, False).start()
    small_slots[mine] = small_stage[...]

    for turn in range(tiles - MIDDLE, tiles):
        rows_in.each(turn, meeting.middle)
    for turn in range(tiles - LAST, tiles):
        rows_in.each(turn, combine)

    for turn in range(1, width_total):
        small_hop(turn, True).wait_recv()
        small_hop(turn, False).wait_send()
    total = small_slots[0]
    for group in range(1, width_total):
        total = total + small_slots[group]
    small_stage[...] = total

    def last_hop(turn, from_peer):
        peer = lax.rem(me + turn, seq_total)
        owner = peer if from_peer else me
        return remote(
            small_stage,
            small_out.at[owner],
            last_send.at[peer],
            last_receive.at[owner],
            {"seq": peer},
        )

    def last_start(turn, carry):
        last_hop(turn, False).start()
        return carry

    lax.fori_loop(1, seq_total, last_start, 0)
    small_out[me] = small_stage[...]

    out_grad.finish(shard_out_ref)

    def bc_arrive(turn, carry):
        source = lax.rem(me + turn, seq_total)
        both(
            source == me,
            sum_b.at[me],
            bc_ref.at[source],
            bc_send.at[me],
            bc_receive.at[source],
            {"seq": source},
            "receive",
        )
        return carry

    lax.fori_loop(0, seq_total, bc_arrive, 0)

    def bc_add(source, total):
        return total + bc_ref[source, :, : 2 * STATE].astype(F32)

    bc_sum = lax.fori_loop(1, seq_total, bc_add, bc_ref[0, :, : 2 * STATE].astype(F32))
    bc_total[:, : 2 * STATE] = bc_sum.astype(BF16)
    for source in range(seq_total):
        at = 2 * STATE + source * heads
        bc_total[:, at : at + heads] = bc_ref[source, :, 2 * STATE : 2 * STATE + heads]
    bc_home(mine, "start")

    def last_end(turn, carry):
        last_hop(turn, False).wait_send()
        last_hop(turn, True).wait_recv()
        return carry

    lax.fori_loop(1, seq_total, last_end, 0)

    def small_add(source, total):
        return total + small_out[source]

    total = lax.fori_loop(1, seq_total, small_add, small_out[0])
    taps_out[:, INNER:] = total[:TAPS, : 2 * STATE]
    bias_out[:, INNER:] = total[TAPS : TAPS + 1, : 2 * STATE]
    in_gain_out[...] = total[:, conv_end + LANES :] / in_gain_ref[...]
    for source in range(seq_total):
        first = source * width
        taps_out[:, first : first + width] = small_out[source, :TAPS, 2 * STATE : conv_width]
        bias_out[:, first : first + width] = small_out[
            source, TAPS : TAPS + 1, 2 * STATE : conv_width
        ]
        gain_out[:, first : first + width] = small_out[source, 1:2, conv_width:conv_end]
        head_out[:, source * heads : (source + 1) * heads] = small_out[
            source, :, conv_end : conv_end + heads
        ]

    first = (mine * shard) // width

    def landed(slot, carry):
        number = first + slot
        source = lax.rem(number, seq_total)

        @pl.when((number < 2 * seq_total) & (number * width < (mine + 1) * shard))
        def _():
            for group in range(width_total):
                both(
                    (source == me) & (mine == group),
                    sum_z.at[me],
                    zx_ref.at[slot, group],
                    zx_send.at[0, me],
                    zx_receive.at[slot, group],
                    {"width": group, "seq": source},
                    "receive",
                )

        return carry

    lax.fori_loop(0, slots, landed, 0)

    @pl.when(mine == width_total - 1)
    def _():
        for source in range(width_total):
            bc_home(source, "receive")

    edge = (slots - -(-(2 * STATE + HEADS) // width)) * width
    for group in range(width_total):
        for slot in range(slots):
            line_buffer[:, slot * width : (slot + 1) * width] = zx_ref[slot, group].astype(F32)

        @pl.when(mine == width_total - 1)
        def _():
            line_buffer[:, edge : edge + 2 * STATE + HEADS] = bc_last[
                group, :, : 2 * STATE + HEADS
            ].astype(F32)

        total_lanes = line_buffer.shape[1]
        start = lax.rem(mine * shard, jnp.int32(width))
        rolled = pltpu.roll(
            line_buffer[...], lax.rem(total_lanes - start, jnp.int32(total_lanes)), 1
        )
        shard_in_ref[group * quarter : (group + 1) * quarter, :] = rolled[:, :shard].astype(BF16)

    def sent(block, carry):
        meeting.sent(block)
        pieces_of(block, "send")
        return carry

    lax.fori_loop(0, seq_total, sent, 0)
    bc_home(mine, "send")


def bring_home(normed, dproj, columns, smalls, in_gain, grad, gnorm, heads, collective_id):
    seq_total, width_total = lax.axis_size("seq"), lax.axis_size("width")
    width = heads * HEAD_DIM
    micros, group_rows, model_width = normed.shape
    depth = model_width // seq_total
    quarter = depth // width_total
    shard = (INNER + CONV + HEADS) // width_total
    slots = max(
        ((group + 1) * shard - 1) // width - group * shard // width + 1
        for group in range(width_total)
    )
    all_columns = dproj.shape[2]
    layout = (seq_total, width_total, quarter, width, slots, shard, heads)
    rest = all_columns - 2 * width
    small = (8, 2 * STATE + 2 * width + LANES + TILE)
    lanes = -(-slots * width // LANES) * LANES
    dma = pltpu.SemaphoreType.DMA
    vmem = pl.BlockSpec(memory_space=pltpu.VMEM)
    return pl.pallas_call(
        partial(home_kernel, layout),
        in_specs=[ANY] + [vmem] * 6 + [ANY, vmem],
        out_specs=[vmem] * 7,
        out_shape=[
            jax.ShapeDtypeStruct((depth, shard), BF16),
            jax.ShapeDtypeStruct((seq_total // width_total * width, model_width // seq_total), F32),
            jax.ShapeDtypeStruct((TAPS, CONV), F32),
            jax.ShapeDtypeStruct((1, CONV), F32),
            jax.ShapeDtypeStruct((1, INNER), F32),
            jax.ShapeDtypeStruct((8, HEADS), F32),
            jax.ShapeDtypeStruct(in_gain.shape, F32),
        ],
        scratch_shapes=[
            pltpu.VMEM((slots, width_total, quarter, width), BF16),
            pltpu.VMEM((seq_total, quarter, rest), BF16),
            pltpu.VMEM((seq_total,) + small, F32),
            pltpu.VMEM((quarter, lanes), F32),
            pltpu.VMEM((2, min(group_rows, 1024), TILE), BF16),
            pltpu.VMEM((TILE, all_columns), F32),
            pltpu.VMEM((seq_total, width_total, quarter, all_columns), BF16),
            pltpu.VMEM((seq_total, 2, quarter, all_columns), BF16),
            pltpu.VMEM((seq_total, quarter, all_columns), BF16),
            pltpu.VMEM((seq_total, quarter, width), BF16),
            pltpu.VMEM((seq_total, quarter, width), BF16),
            pltpu.VMEM((seq_total, quarter, rest), BF16),
            pltpu.VMEM(small, F32),
            pltpu.VMEM((width_total,) + small, F32),
            dma((2,)),
            dma((4, seq_total)),
            dma((4, seq_total)),
            dma((slots, width_total)),
            dma((seq_total,)),
            dma((seq_total,)),
            dma((width_total,)),
            dma((width_total,)),
            dma((seq_total,)),
            dma((seq_total,)),
            pltpu.VMEM((quarter, rest), BF16),
            pltpu.VMEM((width_total, quarter, rest), BF16),
            dma((1,)),
            dma((width_total,)),
        ]
        + out_grad_scratch(heads, group_rows, model_width),
        compiler_params=pltpu.CompilerParams(
            collective_id=collective_id, has_side_effects=True, vmem_limit_bytes=62 << 20
        ),
        cost_estimate=pl.CostEstimate(
            flops=150 * 10**9, bytes_accessed=8 * normed.size, transcendentals=0
        ),
        name="bring_home",
    )(normed, columns, *smalls, in_gain, dproj, grad, gnorm)


def own(value, start, count, axis=0):
    return lax.dynamic_slice_in_dim(value, start, count, axis)


def per_device(
    hidden_in,
    starts,
    in_gain,
    in_weight,
    conv_weight,
    conv_bias,
    step_bias,
    decay_log,
    skip_gain,
    gate_gain,
    out_weight,
    cotangent,
):
    seq_total = lax.axis_size("seq")
    seq_index = lax.axis_index("seq")
    group_index = lax.axis_index("width")
    micros, rows, model_width = hidden_in.shape[1:]
    heads = HEADS // seq_total
    width = heads * HEAD_DIM
    depth = in_weight.shape[0]
    head_count = HEADS // 8 * jnp.left_shift(jnp.int32(1), group_index)
    active = head_count.astype(F32) * HEAD_DIM

    hidden = hidden_in[0].astype(F32)
    grads = cotangent[0]
    root_in = lax.rsqrt(jnp.mean(hidden * hidden, axis=2, keepdims=True) + EPSILON)
    normed = (hidden * root_in * in_gain).astype(BF16)

    dt_pad = LANES
    width_total = lax.axis_size("width")
    quarter = depth // width_total
    in_quarter = own(in_weight, group_index * quarter, quarter)
    gates = in_quarter[:, :INNER].reshape(quarter, seq_total, width)
    xs = in_quarter[:, INNER : 2 * INNER].reshape(quarter, seq_total, width)
    bc = jnp.broadcast_to(
        in_quarter[:, None, 2 * INNER : INNER + CONV], (quarter, seq_total, 2 * STATE)
    )
    dts = in_quarter[:, INNER + CONV :].reshape(quarter, seq_total, heads)
    dts = jnp.pad(dts, ((0, 0), (0, 0), (0, dt_pad - heads)))
    pieces = jnp.concatenate([bc, xs, gates, dts], axis=2).transpose(1, 0, 2)
    all_normed, columns = gather_rows(normed, pieces, 0)

    smalls = [
        conv_weight,
        conv_bias[None],
        gate_gain[None],
        skip_gain[None],
        step_bias[None],
        decay_log[None],
    ]
    forward = run_forward(
        heads, starts[0], all_normed, columns, out_weight, grads, smalls, 3
    )
    proj, gg, branch, mixed, states, tails, sums = forward[:7]
    taps, cols, head, expand, gather, tri, all_grad = forward[7:14]
    chip_wise = dict(axis_index_groups=chip_groups(seq_total), scatter_dimension=0, tiled=True)
    branch = lax.psum_scatter(branch, "seq", **chip_wise)
    dnorm, sums = run_cross(all_grad, out_weight, gg, sums, 1)
    roots = lax.rsqrt(sums[:, : 2 * micros : 2] / active + EPSILON)
    own_roots = own(roots, seq_index, 1).reshape(micros, rows, 1)
    all_roots = roots.transpose(1, 0, 2).reshape(micros, seq_total * rows, 1)
    gnorm = (gg.astype(F32) * all_roots).astype(BF16)

    dproj, partial_rows, *smalls = run_backward(
        heads,
        starts[0],
        active[None],
        proj,
        dnorm,
        mixed,
        states,
        tails,
        sums,
        columns,
        [taps, head, cols, expand, gather, tri],
        4,
    )
    smalls.pop()
    scattered = lax.psum_scatter(partial_rows, "seq", **chip_wise)
    head_sums, branch = lax.optimization_barrier((smalls[2], branch))
    home = bring_home(
        all_normed,
        dproj,
        columns,
        [smalls[0], smalls[1], head_sums],
        in_gain.reshape(-1, TILE),
        all_grad,
        gnorm,
        heads,
        2,
    )
    shard_in, shard_out, taps_sum, bias_sum, gain_sum, head_sums, in_gain_sum = home
    output = hidden + branch.reshape(hidden.shape).astype(F32) * own_roots
    scattered, in_gain_sum = lax.optimization_barrier((scattered, in_gain_sum))
    gained = scattered.reshape(hidden.shape).astype(F32) * in_gain
    pull = jnp.mean(gained * hidden, axis=2, keepdims=True) * (root_in * root_in * root_in)
    hidden_grads = grads.astype(F32) + root_in * gained - hidden * pull
    shape = hidden_in.shape
    return (
        output.astype(BF16).reshape(shape),
        hidden_grads.astype(BF16).reshape(shape),
        in_gain_sum.reshape(-1),
        shard_in.astype(F32),
        taps_sum,
        bias_sum[0],
        head_sums[1],
        head_sums[0],
        head_sums[2],
        gain_sum[0],
        shard_out,
    )


def solution(mesh):
    in_specs = (
        P("width", None, "seq", None),
        P("width", None, None),
        P(),
        P("seq", None),
        P(),
        P(),
        P(),
        P(),
        P(),
        P(),
        P("seq", None),
        P("width", None, "seq", None),
    )
    out_specs = (
        P("width", None, "seq", None),
        P("width", None, "seq", None),
        P(),
        P("seq", "width"),
        P(),
        P(),
        P(),
        P(),
        P(),
        P(),
        P("width", "seq"),
    )
    return jax.shard_map(
        per_device, mesh=mesh, in_specs=in_specs, out_specs=out_specs, check_vma=False
    )
```

```python
from functools import partial

import jax
import jax.numpy as jnp
from jax import lax
from jax.experimental import pallas as pl
from jax.experimental.pallas import tpu as pltpu
from jax.sharding import PartitionSpec as P

INNER = 4096
HEADS = 64
HEAD_DIM = 64
STATE = 128
CONV = 4352
EPSILON = 1e-05
LANES = 128
TAPS = 4
NEG = -1e30
F32 = jnp.float32
BF16 = jnp.bfloat16


def mm(a, b):
    return lax.dot_general(a, b, (((1,), (0,)), ((), ())), preferred_element_type=F32)


def mm_nt(a, b):
    return lax.dot_general(a, b, (((1,), (1,)), ((), ())), preferred_element_type=F32)


def mm_tn(a, b):
    return lax.dot_general(a, b, (((0,), (0,)), ((), ())), preferred_element_type=F32)


def halves(value, axis):
    high = value.astype(BF16)
    low = (value - high.astype(F32)).astype(BF16)
    return jnp.concatenate([high, low], axis=axis)


def sigmoid(value):
    return 0.5 * jnp.tanh(0.5 * value) + 0.5


def prefix_sum(tri, value):
    high = value.astype(BF16)
    rest = value - high.astype(F32)
    middle = rest.astype(BF16)
    low = (rest - middle.astype(F32)).astype(BF16)
    parts = mm(tri, jnp.concatenate([high, middle, low], axis=1))
    width = value.shape[1]
    return parts[:, :width] + parts[:, width : 2 * width] + parts[:, 2 * width :]


def doc_number(starts_ref, micro, positions):
    count = jnp.zeros_like(positions)
    for item in range(starts_ref.shape[1]):
        count = count + (starts_ref[micro, item] <= positions).astype(jnp.int32)
    return count


MESH = pl.DeviceIdType.MESH
ANY = pl.BlockSpec(memory_space=pl.ANY)


def hear(axes):
    waits = sum(lax.axis_size(axis) - 1 for axis in axes)
    pl.semaphore_wait(pltpu.get_barrier_semaphore(), waits)


def greet(axes, hear=True):
    barrier = pltpu.get_barrier_semaphore()
    waits = 0
    for axis in axes:
        count, me = lax.axis_size(axis), lax.axis_index(axis)

        def hello(turn, carry):
            pl.semaphore_signal(
                barrier,
                inc=1,
                device_id={axis: lax.rem(me + turn, count)},
                device_id_type=MESH,
            )
            return carry

        lax.fori_loop(1, count, hello, 0)
        waits += count - 1
    if hear:
        pl.semaphore_wait(barrier, waits)


def remote(source, target, send, receive, device):
    return pltpu.make_async_remote_copy(
        src_ref=source,
        dst_ref=target,
        send_sem=send,
        recv_sem=receive,
        device_id=device,
        device_id_type=MESH,
    )


class Line:
    def __init__(self, source, out, sems):
        self.source, self.out = source, out
        self.up, self.down, self.receive, self.side_send, self.side_receive, self.keep = sems
        self.me = lax.axis_index("seq")
        self.chips = lax.axis_size("seq") // 2
        self.chip, self.core = self.me // 2, lax.rem(self.me, 2)
        self.parts, self.rows = source.shape[:2]

    def at(self, owner, part):
        return self.out.at[part, pl.ds(pl.multiple_of(owner * self.rows, 8), self.rows)]

    def line(self, source, owner_chip, part, target_chip, sems):
        return remote(
            source,
            self.at(owner_chip * 2 + self.core, part),
            sems.at[owner_chip, part],
            self.receive.at[owner_chip, part],
            {"seq": target_chip * 2 + self.core},
        )

    def side(self, source, owner_chip, part, from_sibling):
        core = 1 - self.core if from_sibling else self.core
        return remote(
            source,
            self.at(owner_chip * 2 + core, part),
            self.side_send.at[owner_chip, part],
            self.side_receive.at[owner_chip, part],
            {"seq": self.chip * 2 + 1 - self.core},
        )

    def stay(self, part):
        return pltpu.make_async_copy(
            self.source.at[part], self.at(self.me, part), self.keep.at[part]
        )

    def start(self):
        for part in range(self.parts):
            here = self.source.at[part]

            @pl.when(self.chip + 1 < self.chips)
            def _():
                self.line(here, self.chip, part, self.chip + 1, self.up).start()

            @pl.when(self.chip >= 1)
            def _():
                self.line(here, self.chip, part, self.chip - 1, self.down).start()

            self.side(here, self.chip, part, False).start()
            self.stay(part).start()

    def events(self):
        return (self.chips - 1) * self.parts

    def hop(self, event):
        turn, part = event // self.parts + 1, lax.rem(event, self.parts)
        below, above = self.chip - turn, self.chip + turn

        @pl.when(below >= 0)
        def _():
            here = self.at(below * 2 + self.core, part)
            self.line(here, below, part, self.chip, self.up).wait_recv()

            @pl.when(self.chip + 1 < self.chips)
            def _():
                self.line(here, below, part, self.chip + 1, self.up).start()

            self.side(here, below, part, False).start()

        @pl.when(above < self.chips)
        def _():
            here = self.at(above * 2 + self.core, part)
            self.line(here, above, part, self.chip, self.down).wait_recv()

            @pl.when(self.chip >= 1)
            def _():
                self.line(here, above, part, self.chip - 1, self.down).start()

            self.side(here, above, part, False).start()

    def hops(self, first):
        def body(event, carry):
            self.hop(event)
            return carry

        lax.fori_loop(first, self.events(), body, 0)

    def finish(self):
        def body(owner_chip, carry):
            for part in range(self.parts):
                here = self.at(owner_chip * 2 + self.core, part)

                @pl.when((owner_chip <= self.chip) & (self.chip + 1 < self.chips))
                def _():
                    self.line(here, owner_chip, part, self.chip + 1, self.up).wait_send()

                @pl.when((owner_chip >= self.chip) & (self.chip >= 1))
                def _():
                    self.line(here, owner_chip, part, self.chip - 1, self.down).wait_send()

                self.side(here, owner_chip, part, False).wait_send()
                self.side(here, owner_chip, part, True).wait_recv()
            return carry

        lax.fori_loop(0, self.chips, body, 0)
        for part in range(self.parts):
            self.stay(part).wait()


def line_sems(chips, parts):
    return [pltpu.SemaphoreType.DMA((chips, parts))] * 5 + [pltpu.SemaphoreType.DMA((parts,))]


TILE = 256
MIDDLE = 2
LAST = 4


def call_all():
    seq_total, width_total = lax.axis_size("seq"), lax.axis_size("width")
    count = seq_total * width_total
    place = lax.axis_index("width") * seq_total + lax.axis_index("seq")
    barrier = pltpu.get_barrier_semaphore()

    def hello(turn, carry):
        peer = lax.rem(place + turn, count)
        pl.semaphore_signal(
            barrier,
            inc=1,
            device_id={"width": peer // seq_total, "seq": lax.rem(peer, seq_total)},
            device_id_type=MESH,
        )
        return carry

    lax.fori_loop(1, count, hello, 0)


def hear_all():
    count = lax.axis_size("seq") * lax.axis_size("width")
    pl.semaphore_wait(pltpu.get_barrier_semaphore(), count - 1)


def both(is_here, source, target, send, receive, device, action):
    if action != "send":

        @pl.when(is_here)
        def _():
            stay = pltpu.make_async_copy(source, target, receive)
            if action == "start":
                stay.start()
            else:
                stay.wait()

    @pl.when(jnp.logical_not(is_here))
    def _():
        away = remote(source, target, send, receive, device)
        if action == "start":
            away.start()
        elif action == "receive":
            away.wait_recv()
        else:
            away.wait_send()


class Meeting:
    def __init__(self, parts, come, last, sems):
        self.parts, self.come, self.last, self.sems = parts, come, last, sems
        mine = lax.axis_index("width")
        self.upper, self.lower = mine // 2, lax.rem(mine, 2)

    def order(self, block):
        odd = lax.rem(block, 2)
        even = 1 - odd
        first = odd * self.upper + even * self.lower
        second = odd * self.lower + even * self.upper
        across = 2 * (1 - self.upper) + self.lower
        beside = 2 * self.upper + 1 - self.lower
        return first, second, odd * across + even * beside, odd * beside + even * across

    def slot(self, block, group):
        odd = lax.rem(block, 2)
        return odd * group + (1 - odd) * (group % 2 * 2 + group // 2)

    def first(self, block):
        side, _, partner, _ = self.order(block)
        return remote(
            self.parts.at[block, pl.ds(2 * (1 - side), 2)],
            self.come.at[block],
            self.sems.at[0, block],
            self.sems.at[1, block],
            {"width": partner},
        )

    def second(self, block):
        side, place, _, partner = self.order(block)
        return remote(
            self.parts.at[block, 2 * side + 1 - place],
            self.last.at[block],
            self.sems.at[2, block],
            self.sems.at[3, block],
            {"width": partner},
        )

    def middle(self, block):
        self.first(block).wait_recv()
        side = self.order(block)[0]
        for item in range(2):
            slot = 2 * side + item
            total = self.parts[block, slot].astype(F32) + self.come[block, item].astype(F32)
            self.parts[block, slot] = total.astype(BF16)
        self.second(block).start()

    def total(self, block):
        self.second(block).wait_recv()
        side, place = self.order(block)[:2]
        return self.parts[block, 2 * side + place].astype(F32) + self.last[block].astype(F32)

    def sent(self, block):
        self.first(block).wait_send()
        self.second(block).wait_send()


class Tiles:
    def __init__(self, source, blocks, sems, per_tile):
        self.source, self.blocks, self.sems, self.per_tile = source, blocks, sems, per_tile
        self.total = source.shape[2] // TILE
        self.chunk_rows = blocks.shape[1]
        self.pieces = source.shape[1] // self.chunk_rows
        self.chunks = source.shape[0] * self.pieces

    def turned(self, turn):
        return lax.rem(turn + lax.axis_index("seq") // self.per_tile, self.total)

    def fetch(self, turn, chunk):
        first = chunk % self.pieces * self.chunk_rows
        return pltpu.make_async_copy(
            self.source.at[
                chunk // self.pieces,
                pl.ds(first, self.chunk_rows),
                pl.ds(pl.multiple_of(self.turned(turn) * TILE, TILE), TILE),
            ],
            self.blocks.at[chunk % 2],
            self.sems.at[chunk % 2],
        )

    def begin(self):
        self.fetch(0, 0).start()
        self.fetch(0, 1).start()

    def block(self, turn, chunk):
        self.fetch(turn, chunk).wait()
        first = chunk % self.pieces * self.chunk_rows
        return chunk // self.pieces, slice(first, first + self.chunk_rows), self.blocks[chunk % 2]

    def used(self, turn, chunk):
        if chunk + 2 < self.chunks:
            self.fetch(turn, chunk + 2).start()
        else:

            @pl.when(turn + 1 < self.total)
            def _():
                self.fetch(turn + 1, chunk + 2 - self.chunks).start()

    def each(self, turn, act):
        for item in range(self.per_tile):
            act(self.turned(turn) * self.per_tile + item)


class OutGrad:
    def __init__(self, grad, gnorm, refs):
        (
            blocks,
            self.acc,
            self.stage,
            come,
            last,
            self.sums,
            self.landing,
            fetch,
            sems,
            self.send,
            self.receive,
        ) = refs
        self.gnorm = gnorm
        self.sub, self.cols = self.stage.shape[2:]
        self.meeting = Meeting(self.stage, come, last, sems)
        self.tiles = Tiles(grad, blocks, fetch, TILE // self.cols)
        self.width_total = lax.axis_size("width")
        self.seq_total = lax.axis_size("seq")
        self.owners = self.seq_total // self.width_total
        self.me, self.mine = lax.axis_index("seq"), lax.axis_index("width")

    def copy(self, target, action):
        owner = self.me // self.owners
        place = self.landing.at[lax.rem(self.me, self.owners), self.mine]
        receive = self.receive.at[lax.rem(self.me, self.owners), self.mine]
        both(
            (owner == self.mine) & (target == self.me),
            self.sums.at[target],
            place,
            self.send.at[target],
            receive,
            {"width": owner, "seq": target},
            action,
        )

    def combine(self, block):
        self.sums[block] = self.meeting.total(block).astype(BF16)
        self.copy(block, "start")

    def multiply(self, turn):
        for chunk in range(self.tiles.chunks):
            micro, rows, block = self.tiles.block(turn, chunk)
            part = mm_tn(self.gnorm[micro, rows, :], block)
            self.acc[...] = part if chunk == 0 else self.acc[...] + part
            self.tiles.used(turn, chunk)
        pl.when(turn == 0)(hear_all)
        for item in range(self.tiles.per_tile):
            block = self.tiles.turned(turn) * self.tiles.per_tile + item
            for group in range(self.width_total):
                self.stage[block, self.meeting.slot(block, group)] = self.acc[
                    group * self.sub : (group + 1) * self.sub,
                    item * self.cols : (item + 1) * self.cols,
                ].astype(BF16)
            self.meeting.first(block).start()

    def finish(self, out_ref):
        def sent(block, carry):
            self.meeting.sent(block)
            self.copy(block, "send")
            return carry

        lax.fori_loop(0, self.seq_total, sent, 0)
        for item in range(self.owners):
            for group in range(self.width_total):
                source = self.mine * self.owners + item
                both(
                    (source == self.me) & (self.mine == group),
                    self.sums.at[self.me],
                    self.landing.at[item, group],
                    self.send.at[self.me],
                    self.receive.at[item, group],
                    {"width": group, "seq": source},
                    "receive",
                )
                row = (item * self.width_total + group) * self.sub
                out_ref[row : row + self.sub, :] = self.landing[item, group].astype(F32)


def out_grad_scratch(heads, group_rows, model_width):
    seq_total, width_total = lax.axis_size("seq"), lax.axis_size("width")
    sub, cols = heads * HEAD_DIM // width_total, model_width // seq_total
    owners = seq_total // width_total
    dma = pltpu.SemaphoreType.DMA
    return [
        pltpu.VMEM((2, min(group_rows, 1024), TILE), BF16),
        pltpu.VMEM((heads * HEAD_DIM, TILE), F32),
        pltpu.VMEM((seq_total, width_total, sub, cols), BF16),
        pltpu.VMEM((seq_total, 2, sub, cols), BF16),
        pltpu.VMEM((seq_total, sub, cols), BF16),
        pltpu.VMEM((seq_total, sub, cols), BF16),
        pltpu.VMEM((owners, width_total, sub, cols), BF16),
        dma((2,)),
        dma((4, seq_total)),
        dma((seq_total,)),
        dma((owners, width_total)),
    ]


class PairSum:
    def __init__(self, out, come, refs):
        self.out, self.come = out, come
        self.hold, self.leave, self.load, self.send, self.receive, self.local = refs
        me = lax.axis_index("seq")
        self.core, self.sibling = lax.rem(me, 2), me + 1 - 2 * lax.rem(me, 2)
        self.pairs = out.shape[0]

    def copy(self, pair):
        return remote(
            self.leave.at[lax.rem(pair, 2)],
            self.come.at[pair],
            self.send.at[pair],
            self.receive.at[pair],
            {"seq": self.sibling},
        )

    def put(self, position, earlier, block):
        pair = position // 2
        here = lax.rem(position, 2) == self.core

        @pl.when(here)
        def _():
            self.hold[lax.rem(pair, 2)] = block

        @pl.when(jnp.logical_not(here))
        def _():
            @pl.when((earlier >= 0) & (earlier < self.pairs))
            def _():
                self.copy(earlier).wait_send()

            self.leave[lax.rem(pair, 2)] = block
            self.copy(pair).start()

    def fetch(self, pair):
        return pltpu.make_async_copy(self.come.at[pair], self.load, self.local.at[0])

    def store(self, pair):
        return pltpu.make_async_copy(self.load, self.out.at[pair], self.local.at[1])

    def begin(self, pair, earlier):
        self.copy(pair).wait_recv()

        @pl.when((earlier >= 0) & (earlier < self.pairs))
        def _():
            self.store(earlier).wait()

        self.fetch(pair).start()

    def settle(self, pair):
        self.fetch(pair).wait()
        total = self.hold[lax.rem(pair, 2)].astype(F32) + self.load[...].astype(F32)
        self.load[...] = total.astype(BF16)
        self.store(pair).start()

    def finish(self, last):
        for pair in last:
            self.copy(pair).wait_send()


def pair_scratch(pairs, block, columns):
    dma = pltpu.SemaphoreType.DMA
    return [
        pltpu.VMEM((2, block, columns), BF16),
        pltpu.VMEM((2, block, columns), BF16),
        pltpu.VMEM((block, columns), BF16),
        dma((pairs,)),
        dma((pairs,)),
        dma((2,)),
    ]


def chip_groups(seq_total):
    return [list(range(core, seq_total, 2)) for core in range(2)]


class Chunk:
    def __init__(self, starts_ref, micro, chunk, rows, raw_dt, head_ref, expand, tri):
        first = chunk * rows
        column = lax.broadcasted_iota(jnp.int32, (rows, 1), 0) + first
        line = lax.broadcasted_iota(jnp.int32, (1, rows), 1) + first
        doc_col = doc_number(starts_ref, micro, column)
        doc_row = doc_number(starts_ref, micro, line)
        self.same = [
            (doc_number(starts_ref, micro, column - offset) == doc_col).astype(F32)
            for offset in range(1, TAPS)
        ]
        before = jnp.int32(0)
        last = jnp.int32(0)
        for item in range(starts_ref.shape[1]):
            before = before + (starts_ref[micro, item] <= first - 1).astype(jnp.int32)
            last = last + (starts_ref[micro, item] <= first + rows - 1).astype(jnp.int32)
        carry = (doc_col == before).astype(F32)
        same_last = (doc_col == last).astype(F32)
        self.bias = jnp.where((column >= line) & (doc_col == doc_row), 0.0, NEG)
        self.shifted_dt = raw_dt + head_ref[0:1]
        self.step = jnp.maximum(self.shifted_dt, 0.0) + jnp.log1p(
            jnp.exp(-jnp.abs(self.shifted_dt))
        )
        self.log_keep = self.step * head_ref[1:2]
        self.cum = prefix_sum(tri, self.log_keep)
        self.cum_t = self.cum.T
        carried = jnp.exp(self.cum) * carry
        left = jnp.exp(self.cum[rows - 1 :] - self.cum) * same_last
        spread = mm(
            halves(jnp.concatenate([self.step, carried, left], axis=0), 1), expand
        )
        self.step_cols = spread[:rows]
        self.carry_cols = spread[rows : 2 * rows]
        self.left_cols = spread[2 * rows :]
        self.keep_all = self.carry_cols[rows - 1 :]

    def decay(self, head):
        return jnp.exp(self.cum[:, head : head + 1] - self.cum_t[head : head + 1] + self.bias)


def head_groups(heads):
    size = 2 if heads % 2 == 0 else 1
    return size, heads // size


def stacked(value, size):
    if size == 1:
        return value.astype(BF16)
    lane = lax.broadcasted_iota(jnp.int32, value.shape, 1)
    first = jnp.where(lane < HEAD_DIM, value, 0.0)
    second = jnp.where(lane < HEAD_DIM, 0.0, value)
    return jnp.concatenate([first, second], axis=0).astype(BF16)


def convolved(ext, micro, rows, taps_ref, same):
    current = ext[micro, 8 : 8 + rows, :]
    total = taps_ref[TAPS : TAPS + 1] + taps_ref[TAPS - 1 : TAPS] * current
    views = []
    for offset in range(1, TAPS):
        view = ext[micro, 8 - offset : 8 - offset + rows, :] * same[offset - 1]
        views.append(view)
        total = total + taps_ref[TAPS - 1 - offset : TAPS - offset] * view
    return current, views, total


def forward_kernel(
    micros,
    heads,
    starts_ref,
    x_ref,
    weight_ref,
    out_weight_ref,
    g_ref,
    conv_weight_ref,
    conv_bias_ref,
    gate_gain_ref,
    skip_ref,
    step_bias_ref,
    decay_ref,
    proj_ref,
    gg_ref,
    branch_ref,
    mixed_ref,
    states_ref,
    tails_ref,
    sums_ref,
    taps_ref,
    cols_ref,
    head_ref,
    expand_ref,
    gather_ref,
    tri_ref,
    g_out,
    come_ref,
    ext,
    state,
    table,
    *sems,
):
    chunk, chunks = pl.program_id(0), pl.num_programs(0)
    rows = x_ref.shape[1]
    width = heads * HEAD_DIM
    conv_width = 2 * STATE + width
    size, groups = head_groups(heads)
    line = Line(g_ref, g_out, sems[:6])
    pairs = PairSum(branch_ref, come_ref, sems[6:])
    early = min((g_out.shape[1] // g_ref.shape[1] - 1) // 2, line.events())

    @pl.when(chunk == 0)
    def _():
        greet(("seq",))
        line.start()

    @pl.when((lax.rem(chunk, 2) == 0) & (chunk >= 2) & (chunk // 2 - 1 < early))
    def _():
        line.hop(chunk // 2 - 1)

    @pl.when((lax.rem(chunk, 2) == 0) & (chunk >= 2))
    def _():
        pairs.begin(chunk // 2 - 1, chunk // 2 - 2)

    @pl.when(chunk == 0)
    def _():
        ext[:, :8, :] = jnp.zeros((micros, 8, conv_width), F32)
        state[...] = jnp.zeros_like(state)
        me = lax.axis_index("seq")
        lane_of = lax.broadcasted_iota(jnp.int32, (LANES, width), 0)
        head_of = lax.broadcasted_iota(jnp.int32, (LANES, width), 1) // HEAD_DIM
        spread = (lane_of == head_of).astype(F32).astype(BF16)
        expand_ref[:LANES] = spread
        expand_ref[LANES:] = spread
        lane_of = lax.broadcasted_iota(jnp.int32, (width, LANES), 1)
        head_of = lax.broadcasted_iota(jnp.int32, (width, LANES), 0) // HEAD_DIM
        folded = (lane_of == head_of).astype(F32).astype(BF16)
        gather_ref[:width] = folded
        gather_ref[width:] = folded
        later = lax.broadcasted_iota(jnp.int32, (rows, rows), 0)
        sooner = lax.broadcasted_iota(jnp.int32, (rows, rows), 1)
        tri_ref[...] = (later >= sooner).astype(F32).astype(BF16)

        table[...] = jnp.zeros_like(table)
        table[0:TAPS] = conv_weight_ref[:, :INNER]
        table[TAPS : TAPS + 1] = conv_bias_ref[:, :INNER]
        table[TAPS + 1 : TAPS + 2] = gate_gain_ref[...]
        local = pltpu.roll(table[...], lax.rem(INNER - me * width, jnp.int32(INNER)), 1)[
            :, :width
        ]
        taps_ref[...] = jnp.zeros_like(taps_ref)
        taps_ref[0:TAPS, : 2 * STATE] = conv_weight_ref[:, INNER:]
        taps_ref[TAPS : TAPS + 1, : 2 * STATE] = conv_bias_ref[:, INNER:]
        taps_ref[0 : TAPS + 1, 2 * STATE :] = local[: TAPS + 1]
        head_ref[...] = jnp.zeros_like(head_ref)
        head_ref[0:1, :HEADS] = step_bias_ref[...]
        head_ref[1:2, :HEADS] = -jnp.exp(decay_ref[...])
        head_ref[2:3, :HEADS] = skip_ref[...]
        own_heads = pltpu.roll(
            head_ref[...], lax.rem(LANES - me * heads, jnp.int32(LANES)), 1
        )
        head_ref[...] = own_heads
        head_row = me * heads + (
            lax.broadcasted_iota(jnp.int32, (1, width), 1) // HEAD_DIM
        )
        limit = HEADS // 8 * jnp.left_shift(jnp.int32(1), lax.axis_index("width"))
        cols_ref[0:1] = mm(halves(own_heads, 1), expand_ref[...])[2:3]
        cols_ref[1:2] = local[TAPS + 1 : TAPS + 2]
        cols_ref[2:3] = (head_row < limit).astype(F32)
        cols_ref[3:8] = jnp.zeros((5, width), F32)

    skip, gain, mask = cols_ref[0:1], cols_ref[1:2], cols_ref[2:3]
    rows_in = x_ref[...].reshape(micros * rows, x_ref.shape[2])
    proj_ref[...] = mm(rows_in, weight_ref[...]).astype(BF16).reshape(proj_ref.shape)
    sums, gated_gains = [], []
    for micro in range(micros):
        tails_ref[micro] = ext[micro, :8, :]
        ext[micro, 8 : 8 + rows, :] = proj_ref[micro, :, :conv_width].astype(F32)
        raw_dt = proj_ref[micro, :, conv_width + width :].astype(F32)
        at = Chunk(
            starts_ref, micro, chunk, rows, raw_dt, head_ref, expand_ref[...], tri_ref[...]
        )
        conv = convolved(ext, micro, rows, taps_ref, at.same)[2]
        act = conv * sigmoid(conv)
        write = act[:, :STATE].astype(BF16)
        read = act[:, STATE : 2 * STATE].astype(BF16)
        x_heads = act[:, 2 * STATE :]
        scores = mm_nt(read, write)
        inputs = x_heads * at.step_cols
        state_in = state[micro]
        state_low = state_in.astype(BF16)
        states_ref[micro] = state_low
        outs = []
        for group in range(groups):
            matrices = [
                (at.decay(group * size + item) * scores).astype(BF16) for item in range(size)
            ]
            span = slice(group * size * HEAD_DIM, (group + 1) * size * HEAD_DIM)
            outs.append(mm(jnp.concatenate(matrices, axis=1), stacked(inputs[:, span], size)))
        mixed = jnp.concatenate(outs, axis=1) + at.carry_cols * mm(read, state_low)
        state[micro] = at.keep_all * state_in + mm_tn(
            write, (inputs * at.left_cols).astype(BF16)
        )
        mixed = mixed + skip * x_heads
        mixed_ref[micro] = mixed
        gate = proj_ref[micro, :, conv_width : conv_width + width].astype(F32)
        gated = mask * mixed * (gate * sigmoid(gate))
        gated_gain = (gated * gain).astype(BF16)
        gg_ref[micro] = gated_gain
        gated_gains.append(gated_gain)
        square = jnp.sum(gated * gated, axis=1, keepdims=True)
        lane = lax.broadcasted_iota(jnp.int32, (rows, LANES), 1)
        sums.append(jnp.where(lane == 0, square, 0.0).T[:2])
        ext[micro, :8, :] = ext[micro, rows : rows + 8, :]
    pad = sums_ref.shape[0] - 2 * micros
    if pad:
        sums.append(jnp.zeros((pad, rows), F32))
    sums_ref[...] = jnp.concatenate(sums, axis=0)
    branch = mm(jnp.concatenate(gated_gains, axis=0), out_weight_ref[...]).astype(BF16)

    @pl.when((lax.rem(chunk, 2) == 0) & (chunk >= 2))
    def _():
        pairs.settle(chunk // 2 - 1)

    pairs.put(chunk, chunk // 2 - 2, branch)

    @pl.when(chunk == chunks - 1)
    def _():
        pair_count = branch_ref.shape[0]
        line.hops(early)
        pairs.begin(jnp.int32(pair_count - 1), jnp.int32(pair_count - 2))
        pairs.settle(jnp.int32(pair_count - 1))
        line.finish()
        pairs.store(pair_count - 1).wait()
        pairs.finish(range(max(0, pair_count - 2), pair_count))


def cross_kernel(
    g_ref, out_weight_ref, gg_ref, sums_ref, dnorm_ref, total_ref, mine, slots, send, receive
):
    chunk, chunks = pl.program_id(0), pl.num_programs(0)
    micros, rows, model_width = g_ref.shape
    me = lax.axis_index("seq")

    @pl.when(chunk == 0)
    def _():
        greet(("seq",), hear=False)

    grads = g_ref[...].reshape(micros * rows, model_width)
    dnorm = mm_nt(grads, out_weight_ref[...])
    gg = gg_ref[...].reshape(micros * rows, dnorm.shape[1])
    dnorm_ref[...] = dnorm.reshape(dnorm_ref.shape)
    cross = jnp.sum(dnorm * gg.astype(F32), axis=1, keepdims=True)
    lane = lax.broadcasted_iota(jnp.int32, (rows, LANES), 1)
    lines = []
    for micro in range(micros):
        part = cross[micro * rows : (micro + 1) * rows]
        lines.append(jnp.where(lane == 1, part, 0.0).T[:2])
    pad = sums_ref.shape[0] - 2 * micros
    if pad:
        lines.append(jnp.zeros((pad, rows), F32))
    mine[chunk] = sums_ref[...] + jnp.concatenate(lines, axis=0)

    @pl.when(chunk == chunks - 1)
    def _():
        hear(("seq",))

        def copy(turn, owner):
            peer = lax.rem(me + turn, chunks)
            return remote(
                mine, slots.at[owner], send.at[peer], receive.at[owner], {"seq": peer}
            )

        def start(turn, carry):
            copy(turn, me).start()
            return carry

        def finish(turn, carry):
            copy(turn, me).wait_send()
            copy(turn, lax.rem(me + turn, chunks)).wait_recv()
            return carry

        lax.fori_loop(1, chunks, start, 0)
        slots[me] = mine[...]
        lax.fori_loop(1, chunks, finish, 0)

        def add(owner, total):
            return total + slots[owner]

        total_ref[...] = lax.fori_loop(1, chunks, add, slots[0])


def backward_kernel(
    micros,
    heads,
    starts_ref,
    active_ref,
    proj_ref,
    dnorm_ref,
    mixed_ref,
    states_ref,
    tails_ref,
    sums_ref,
    weight_ref,
    taps_ref,
    head_ref,
    cols_ref,
    expand_ref,
    gather_ref,
    tri_ref,
    dproj_ref,
    partial_ref,
    gconv_ref,
    gcols_ref,
    ghead_ref,
    come_ref,
    ext,
    heads_ext,
    dstate,
    *pair_refs,
):
    chunks = pl.num_programs(0)
    step_index = pl.program_id(0)
    rows = proj_ref.shape[1]
    pairs = PairSum(partial_ref, come_ref, pair_refs)

    @pl.when(step_index == 0)
    def _():
        heads_ext[:, :, rows:, :] = jnp.zeros((micros, TAPS - 1, 8, ext.shape[2]), F32)
        dstate[...] = jnp.zeros_like(dstate)
        gconv_ref[...] = jnp.zeros_like(gconv_ref)
        gcols_ref[...] = jnp.zeros_like(gcols_ref)
        ghead_ref[...] = jnp.zeros_like(ghead_ref)
        barrier = pltpu.get_barrier_semaphore()
        pl.semaphore_signal(
            barrier, inc=1, device_id={"seq": pairs.sibling}, device_id_type=MESH
        )

    position = chunks - 1 - step_index

    @pl.when((lax.rem(position, 2) == 1) & (step_index >= 2))
    def _():
        pairs.begin((position + 1) // 2, (position + 1) // 2 + 1)

    for micro in range(micros):
        backward_rows(
            micro,
            heads,
            chunks - 1 - step_index,
            starts_ref,
            active_ref,
            proj_ref.at[micro],
            dnorm_ref.at[micro],
            mixed_ref.at[micro],
            states_ref.at[micro],
            tails_ref.at[micro],
            sums_ref,
            taps_ref,
            head_ref,
            cols_ref,
            expand_ref,
            gather_ref,
            tri_ref,
            dproj_ref.at[micro],
            gconv_ref,
            gcols_ref,
            ghead_ref,
            ext,
            heads_ext.at[micro],
            dstate.at[micro],
        )
    d_rows = dproj_ref[...].reshape(micros * rows, dproj_ref.shape[2])
    partial_rows = mm_nt(d_rows, weight_ref[...]).astype(BF16)

    @pl.when(step_index == 0)
    def _():
        pl.semaphore_wait(pltpu.get_barrier_semaphore(), 1)

    @pl.when((lax.rem(position, 2) == 1) & (step_index >= 2))
    def _():
        pairs.settle((position + 1) // 2)

    pairs.put(position, position // 2 + 2, partial_rows)

    @pl.when(step_index == chunks - 1)
    def _():
        ghead_ref[2:3] = mm(halves(gcols_ref[...], 1), gather_ref[...])[0:1]
        pairs.begin(jnp.int32(0), jnp.int32(1))
        pairs.settle(jnp.int32(0))
        pairs.store(0).wait()
        pairs.finish(range(min(2, partial_ref.shape[0])))


def backward_rows(
    micro,
    heads,
    chunk,
    starts_ref,
    active_ref,
    proj_ref,
    dnorm_ref,
    mixed_ref,
    states_ref,
    tails_ref,
    sums_ref,
    taps_ref,
    head_ref,
    cols_ref,
    expand_ref,
    gather_ref,
    tri_ref,
    dproj_ref,
    gconv_ref,
    gcols_ref,
    ghead_ref,
    ext,
    heads_ext,
    dstate,
):
    rows = proj_ref.shape[0]
    width = heads * HEAD_DIM
    conv_width = 2 * STATE + width
    size, groups = head_groups(heads)
    skip, gain, mask = cols_ref[0:1], cols_ref[1:2], cols_ref[2:3]
    tri = tri_ref[...]
    gather = gather_ref[...]
    inverse_active = 1.0 / active_ref[0]
    sums = jnp.concatenate(
        [sums_ref[...], jnp.zeros((LANES - sums_ref.shape[0], rows), F32)], axis=0
    ).T
    ext[micro, :8, :] = tails_ref[...]
    ext[micro, 8 : 8 + rows, :] = proj_ref[:, :conv_width].astype(F32)
    raw_dt = proj_ref[:, conv_width + width :].astype(F32)
    at = Chunk(starts_ref, micro, chunk, rows, raw_dt, head_ref, expand_ref[...], tri)
    current, views, conv = convolved(ext, micro, rows, taps_ref, at.same)
    conv_sig = sigmoid(conv)
    act = conv * conv_sig
    write = act[:, :STATE].astype(BF16)
    read = act[:, STATE : 2 * STATE].astype(BF16)
    x_heads = act[:, 2 * STATE :]
    scores = mm_nt(read, write)
    inputs = x_heads * at.step_cols

    gate = proj_ref[:, conv_width : conv_width + width].astype(F32)
    gate_sig = sigmoid(gate)
    gate_act = gate * gate_sig
    masked = mask * mixed_ref[...]
    gated = masked * gate_act
    root = lax.rsqrt(sums[:, 2 * micro : 2 * micro + 1] * inverse_active + EPSILON)
    pull = root * root * root * sums[:, 2 * micro + 1 : 2 * micro + 2] * inverse_active
    dnorm = dnorm_ref[...]
    scaled = gated * root
    d_gated = root * dnorm * gain - gated * pull
    d_gate = d_gated * masked * (gate_sig * (1.0 + gate * (1.0 - gate_sig)))
    d_mixed = mask * d_gated * gate_act
    gcols_ref[0:1] += jnp.sum(d_mixed * x_heads, axis=0, keepdims=True)
    gcols_ref[1:2] += jnp.sum(dnorm * scaled, axis=0, keepdims=True)

    state_low = states_ref[...]
    d_state = dstate[...]
    d_state_low = d_state.astype(BF16)
    from_state = (d_mixed * at.carry_cols).astype(BF16)
    left = inputs * at.left_cols
    left_low = left.astype(BF16)
    d_left = mm(write, d_state_low)
    state_out = mm(read, state_low)
    d_read = mm_nt(from_state, state_low)
    d_write = mm_nt(left_low, d_state_low)
    d_mixed_low = d_mixed.astype(BF16).astype(F32)
    inputs_low = inputs.astype(BF16).astype(F32)
    d_scores = jnp.zeros((rows, rows), F32)
    locals_out, d_locals = [], []
    for group in range(groups):
        span = slice(group * size * HEAD_DIM, (group + 1) * size * HEAD_DIM)
        decays = [at.decay(group * size + item) for item in range(size)]
        matrices = [(decay * scores).astype(BF16) for decay in decays]
        in_stack = stacked(inputs[:, span], size)
        out_stack = stacked(d_mixed[:, span], size)
        locals_out.append(mm(jnp.concatenate(matrices, axis=1), in_stack))
        d_locals.append(mm_tn(jnp.concatenate(matrices, axis=0), out_stack))
        d_matrices = mm_nt(out_stack, inputs[:, span].astype(BF16))
        for item in range(size):
            d_scores = (
                d_scores + d_matrices[item * rows : (item + 1) * rows] * decays[item]
            )
    local_out = jnp.concatenate(locals_out, axis=1)
    d_local = jnp.concatenate(d_locals, axis=1)
    d_scores_low = d_scores.astype(BF16)
    d_read = d_read + mm(d_scores_low, write)
    d_write = d_write + mm_tn(d_scores_low, read)
    d_inputs = d_local + at.left_cols * d_left
    d_x = skip * d_mixed + d_inputs * at.step_cols

    passed = left * d_left
    cum_terms = (
        d_mixed_low * local_out
        + d_mixed * at.carry_cols * state_out
        - inputs_low * d_local
        - passed
    )
    kept = jnp.sum(d_state * at.keep_all * state_low.astype(F32), axis=0, keepdims=True)
    final = jnp.sum(passed, axis=0, keepdims=True) + kept
    stack = jnp.concatenate(
        [cum_terms, d_inputs * x_heads, jnp.broadcast_to(final, (8, width))], axis=0
    )
    reduced = mm(halves(stack, 1), gather)
    d_cum = reduced[:rows]
    d_step = reduced[rows : 2 * rows]
    final_row = reduced[2 * rows : 2 * rows + 1]
    total = jnp.sum(d_cum, axis=0, keepdims=True) + final_row
    d_log = total - prefix_sum(tri, d_cum) + d_cum
    d_step = d_step + d_log * head_ref[1:2]
    d_dt = d_step * sigmoid(at.shifted_dt)
    ghead_ref[0:1] += jnp.sum(d_log * at.log_keep, axis=0, keepdims=True)
    ghead_ref[1:2] += jnp.sum(d_dt, axis=0, keepdims=True)
    dstate[...] = at.keep_all * d_state + mm_tn(read, from_state)

    d_conv = jnp.concatenate([d_write, d_read, d_x], axis=1) * (
        conv_sig * (1.0 + conv * (1.0 - conv_sig))
    )
    gconv_ref[TAPS : TAPS + 1] += jnp.sum(d_conv, axis=0, keepdims=True)
    gconv_ref[TAPS - 1 : TAPS] += jnp.sum(d_conv * current, axis=0, keepdims=True)
    d_raw = taps_ref[TAPS - 1 : TAPS] * d_conv
    for offset in range(1, TAPS):
        tap = TAPS - 1 - offset
        gconv_ref[tap : tap + 1] += jnp.sum(
            d_conv * views[offset - 1], axis=0, keepdims=True
        )
        heads_ext[offset - 1, :rows, :] = d_conv * at.same[offset - 1]
        d_raw = d_raw + taps_ref[tap : tap + 1] * (
            heads_ext[offset - 1, offset : offset + rows, :]
        )
        heads_ext[offset - 1, rows:, :] = heads_ext[offset - 1, :8, :]
    dproj_ref[:, :conv_width] = d_raw.astype(BF16)
    dproj_ref[:, conv_width : conv_width + width] = d_gate.astype(BF16)
    dproj_ref[:, conv_width + width :] = d_dt.astype(BF16)


def constant(shape):
    return pl.BlockSpec(shape, lambda index: (0,) * len(shape))


def run_forward(
    heads, starts, x, weight, out_weight, g, smalls, collective_id
):
    micros, rows, model_width = g.shape
    chunks = x.shape[1] // rows
    width = heads * HEAD_DIM
    conv_width = 2 * STATE + width
    block = micros * rows
    sum_rows = -(-2 * micros // 8) * 8
    columns = weight.shape[1]

    def whole(value):
        return pl.BlockSpec(
            value.shape, lambda index: (0,) * value.ndim, pipeline_mode=pl.Buffered(1)
        )

    def row_block(size):
        return pl.BlockSpec((micros, rows, size), lambda index: (0, index, 0))

    return pl.pallas_call(
        partial(forward_kernel, micros, heads),
        grid=(chunks,),
        in_specs=[
            pl.BlockSpec(memory_space=pltpu.SMEM),
            row_block(model_width),
            whole(weight),
            whole(out_weight),
            ANY,
        ]
        + [whole(item) for item in smalls],
        out_specs=[
            row_block(columns),
            row_block(width),
            ANY,
            row_block(width),
            pl.BlockSpec((None, micros, STATE, width), lambda index: (index, 0, 0, 0)),
            pl.BlockSpec((None, micros, 8, conv_width), lambda index: (index, 0, 0, 0)),
            pl.BlockSpec((None, sum_rows, rows), lambda index: (index, 0, 0)),
            constant((8, conv_width)),
            constant((8, width)),
            constant((8, LANES)),
            constant((2 * LANES, width)),
            constant((2 * width, LANES)),
            constant((rows, rows)),
            ANY,
            ANY,
        ],
        out_shape=[
            jax.ShapeDtypeStruct((micros, chunks * rows, columns), BF16),
            jax.ShapeDtypeStruct((micros, chunks * rows, width), BF16),
            jax.ShapeDtypeStruct((chunks // 2, block, model_width), BF16),
            jax.ShapeDtypeStruct((micros, chunks * rows, width), F32),
            jax.ShapeDtypeStruct((chunks, micros, STATE, width), BF16),
            jax.ShapeDtypeStruct((chunks, micros, 8, conv_width), F32),
            jax.ShapeDtypeStruct((chunks, sum_rows, rows), F32),
            jax.ShapeDtypeStruct((8, conv_width), F32),
            jax.ShapeDtypeStruct((8, width), F32),
            jax.ShapeDtypeStruct((8, LANES), F32),
            jax.ShapeDtypeStruct((2 * LANES, width), BF16),
            jax.ShapeDtypeStruct((2 * width, LANES), BF16),
            jax.ShapeDtypeStruct((rows, rows), BF16),
            jax.ShapeDtypeStruct((micros, chunks * rows, model_width), BF16),
            jax.ShapeDtypeStruct((chunks // 2, block, model_width), BF16),
        ],
        scratch_shapes=[
            pltpu.VMEM((micros, rows + 8, conv_width), F32),
            pltpu.VMEM((micros, STATE, width), F32),
            pltpu.VMEM((8, INNER), F32),
        ]
        + line_sems(chunks // 2, micros)
        + pair_scratch(chunks // 2, block, model_width),
        compiler_params=pltpu.CompilerParams(
            collective_id=collective_id, has_side_effects=True, vmem_limit_bytes=56 << 20
        ),
        cost_estimate=pl.CostEstimate(
            flops=60 * 10**9, bytes_accessed=150 * 10**6, transcendentals=0
        ),
        name="mixer_forward",
    )(starts, x, weight, out_weight, g, *smalls)


def run_cross(g, out_weight, gg, sums, collective_id):
    chunks = sums.shape[0]
    micros, all_rows, model_width = g.shape
    rows, width = all_rows // chunks, gg.shape[2]

    def row_block(size):
        return pl.BlockSpec((micros, rows, size), lambda index: (0, index, 0))

    return pl.pallas_call(
        cross_kernel,
        grid=(chunks,),
        in_specs=[
            row_block(model_width),
            pl.BlockSpec(out_weight.shape, lambda index: (0, 0), pipeline_mode=pl.Buffered(1)),
            row_block(width),
            pl.BlockSpec((None,) + sums.shape[1:], lambda index: (index, 0, 0)),
        ],
        out_specs=[row_block(width), constant(sums.shape)],
        out_shape=[
            jax.ShapeDtypeStruct((micros, all_rows, width), F32),
            jax.ShapeDtypeStruct(sums.shape, F32),
        ],
        scratch_shapes=[
            pltpu.VMEM(sums.shape, F32),
            pltpu.VMEM((chunks,) + sums.shape, F32),
            pltpu.SemaphoreType.DMA((chunks,)),
            pltpu.SemaphoreType.DMA((chunks,)),
        ],
        compiler_params=pltpu.CompilerParams(
            collective_id=collective_id, has_side_effects=True, vmem_limit_bytes=60 << 20
        ),
        cost_estimate=pl.CostEstimate(
            flops=12 * 10**9, bytes_accessed=16 * 10**6, transcendentals=0
        ),
        name="cross_sums",
    )(g, out_weight, gg, sums)


def run_backward(
    heads,
    starts,
    active,
    proj,
    dnorm,
    mixed,
    states,
    tails,
    sums,
    weight,
    shared,
    collective_id,
):
    micros, all_rows, columns = proj.shape
    chunks = sums.shape[0]
    rows = all_rows // chunks
    width = heads * HEAD_DIM
    conv_width = 2 * STATE + width
    model_width = weight.shape[0]

    def row_block(size):
        return pl.BlockSpec((micros, rows, size), lambda index: (0, chunks - 1 - index, 0))

    def chunk_block(shape):
        return pl.BlockSpec((None, micros) + shape, lambda index: (chunks - 1 - index, 0, 0, 0))

    return pl.pallas_call(
        partial(backward_kernel, micros, heads),
        grid=(chunks,),
        in_specs=[
            pl.BlockSpec(memory_space=pltpu.SMEM),
            pl.BlockSpec(memory_space=pltpu.SMEM),
            row_block(columns),
            row_block(width),
            row_block(width),
            chunk_block((STATE, width)),
            chunk_block((8, conv_width)),
            pl.BlockSpec((None, sums.shape[1], rows), lambda index: (chunks - 1 - index, 0, 0)),
            pl.BlockSpec(weight.shape, lambda index: (0, 0), pipeline_mode=pl.Buffered(1)),
        ]
        + [constant(item.shape) for item in shared],
        out_specs=[
            row_block(columns),
            ANY,
            constant((8, conv_width)),
            constant((8, width)),
            constant((8, LANES)),
            ANY,
        ],
        out_shape=[
            jax.ShapeDtypeStruct((micros, all_rows, columns), BF16),
            jax.ShapeDtypeStruct((chunks // 2, micros * rows, model_width), BF16),
            jax.ShapeDtypeStruct((8, conv_width), F32),
            jax.ShapeDtypeStruct((8, width), F32),
            jax.ShapeDtypeStruct((8, LANES), F32),
            jax.ShapeDtypeStruct((chunks // 2, micros * rows, model_width), BF16),
        ],
        scratch_shapes=[
            pltpu.VMEM((micros, rows + 8, conv_width), F32),
            pltpu.VMEM((micros, TAPS - 1, rows + 8, conv_width), F32),
            pltpu.VMEM((micros, STATE, width), F32),
        ]
        + pair_scratch(chunks // 2, micros * rows, model_width),
        compiler_params=pltpu.CompilerParams(
            collective_id=collective_id, has_side_effects=True, vmem_limit_bytes=60 << 20
        ),
        cost_estimate=pl.CostEstimate(
            flops=60 * 10**9, bytes_accessed=60 * 10**6, transcendentals=0
        ),
        name="mixer_backward",
    )(starts, active, proj, dnorm, mixed, states, tails, sums, weight, *shared)


def gather_kernel(
    x_ref,
    w_ref,
    x_out,
    w_out,
    w_send,
    w_receive,
    f_send,
    f_receive,
    keep,
    *sems,
):
    seq_total, width_total = lax.axis_size("seq"), lax.axis_size("width")
    me, mine = lax.axis_index("seq"), lax.axis_index("width")
    quarter = w_ref.shape[1]
    depth = quarter * width_total
    line = Line(x_ref, x_out, sems)
    greet(("seq", "width"))

    def rows(source, group):
        return pl.ds(pl.multiple_of(source * depth + group * quarter, 8), quarter)

    def deal(turn, from_peer):
        peer = lax.rem(me + turn, seq_total)
        owner = peer if from_peer else me
        return remote(
            w_ref.at[peer],
            w_out.at[rows(owner, mine)],
            w_send.at[peer],
            w_receive.at[owner],
            {"seq": peer},
        )

    def deal_start(turn, carry):
        deal(turn, False).start()
        return carry

    lax.fori_loop(1, seq_total, deal_start, 0)
    w_own = pltpu.make_async_copy(w_ref.at[me], w_out.at[rows(me, mine)], keep.at[0])
    w_own.start()
    line.start()

    def forward(source, turn, from_peer):
        peer = lax.rem(mine + turn, width_total)
        group = peer if from_peer else mine
        where = w_out.at[rows(source, group)]
        return remote(
            where, where, f_send.at[peer, source], f_receive.at[group, source], {"width": peer}
        )

    def forward_start(source):
        for turn in range(1, width_total):
            forward(source, turn, False).start()

    def deal_pass(turn, carry):
        deal(turn, True).wait_recv()
        forward_start(lax.rem(me + turn, seq_total))
        return carry

    w_own.wait()
    forward_start(me)
    lax.fori_loop(1, seq_total, deal_pass, 0)
    line.hops(0)

    def deal_end(turn, carry):
        deal(turn, False).wait_send()
        return carry

    lax.fori_loop(1, seq_total, deal_end, 0)

    def forward_end(source, carry):
        for turn in range(1, width_total):
            forward(source, turn, False).wait_send()
            forward(source, turn, True).wait_recv()
        return carry

    lax.fori_loop(0, seq_total, forward_end, 0)
    line.finish()


def gather_rows(x, pieces, collective_id):
    seq_total, width_total = lax.axis_size("seq"), lax.axis_size("width")
    parts, rows, model_width = x.shape
    whole = (parts, rows * seq_total, model_width)
    weight = (seq_total * width_total * pieces.shape[1], pieces.shape[2])
    dma = pltpu.SemaphoreType.DMA
    return pl.pallas_call(
        gather_kernel,
        in_specs=[ANY] * 2,
        out_specs=[ANY] * 2,
        out_shape=[
            jax.ShapeDtypeStruct(whole, x.dtype),
            jax.ShapeDtypeStruct(weight, pieces.dtype),
        ],
        scratch_shapes=[
            dma((seq_total,)),
            dma((seq_total,)),
            dma((width_total, seq_total)),
            dma((width_total, seq_total)),
            dma((1,)),
        ]
        + line_sems(seq_total // 2, parts),
        compiler_params=pltpu.CompilerParams(
            collective_id=collective_id, has_side_effects=True
        ),
        cost_estimate=pl.CostEstimate(
            flops=80 * 10**9, bytes_accessed=200 * 10**6, transcendentals=0
        ),
        name="gather_rows",
    )(x, pieces)


def home_kernel(
    layout,
    normed_ref,
    columns_far,
    gconv_ref,
    gcols_ref,
    ghead_ref,
    in_gain_ref,
    dproj_far,
    grad_ref,
    gnorm_ref,
    shard_in_ref,
    shard_out_ref,
    taps_out,
    bias_out,
    gain_out,
    head_out,
    in_gain_out,
    zx_ref,
    bc_ref,
    small_out,
    line_buffer,
    blocks_in,
    acc,
    stage,
    arrived,
    last_arrived,
    sum_x,
    sum_z,
    sum_b,
    small_stage,
    small_slots,
    fetch,
    in_sems,
    zx_send,
    zx_receive,
    bc_send,
    bc_receive,
    small_send,
    small_receive,
    last_send,
    last_receive,
    bc_total,
    bc_last,
    bc_last_send,
    bc_last_receive,
    columns_ref,
    dproj_ref,
    bring,
    *out_refs,
):
    seq_total, width_total, quarter, width, slots, shard, heads = layout
    micros = normed_ref.shape[0]
    me, mine = lax.axis_index("seq"), lax.axis_index("width")
    depth = quarter * width_total
    conv_width = 2 * STATE + width
    per_tile = TILE // depth
    tiles = seq_total // per_tile
    rows_in = Tiles(normed_ref, blocks_in, fetch, per_tile)
    meeting = Meeting(stage, arrived, last_arrived, in_sems)
    out_grad = OutGrad(grad_ref, gnorm_ref, out_refs)
    out_grad.tiles.begin()
    dproj_in = pltpu.make_async_copy(dproj_far, dproj_ref, bring.at[0])
    columns_in = pltpu.make_async_copy(columns_far, columns_ref, bring.at[1])
    dproj_in.start()
    columns_in.start()
    call_all()

    def out_multiply(turn, carry):
        out_grad.multiply(turn)

        @pl.when(turn >= MIDDLE)
        def _():
            out_grad.tiles.each(turn - MIDDLE, out_grad.meeting.middle)

        @pl.when(turn >= LAST)
        def _():
            out_grad.tiles.each(turn - LAST, out_grad.combine)

        return carry

    rows_in.begin()
    lax.fori_loop(0, tiles, out_multiply, 0)
    dproj_in.wait()
    columns_in.wait()

    conv_end = conv_width + width
    small_stage[:, :conv_width] = gconv_ref[...]
    small_stage[:, conv_width:conv_end] = gcols_ref[...]
    small_stage[:, conv_end : conv_end + LANES] = ghead_ref[...]

    def block_copy(sums, sem_row, number, block, second, action):
        low = (number * width) // shard
        high = ((number + 1) * width - 1) // shard
        owner = high if second else low
        slot = number - (owner * shard) // width

        def act():
            both(
                (owner == mine) & (block == me),
                sums.at[block],
                zx_ref.at[slot, mine],
                zx_send.at[sem_row, block],
                zx_receive.at[slot, mine],
                {"width": owner, "seq": block},
                action,
            )

        if second:
            pl.when(high != low)(act)
        else:
            act()

    def bc_copy(block, action):
        both(
            block == me,
            sum_b.at[block],
            bc_ref.at[me],
            bc_send.at[block],
            bc_receive.at[me],
            {"seq": block},
            action,
        )

    def bc_home(source, action):
        both(
            (mine == width_total - 1) & (source == mine),
            bc_total,
            bc_last.at[source],
            bc_last_send.at[0],
            bc_last_receive.at[source],
            {"width": width_total - 1},
            action,
        )

    def pieces_of(block, action):
        for second in (False, True):
            block_copy(sum_z, int(second), me, block, second, action)
            block_copy(sum_x, 2 + int(second), seq_total + me, block, second, action)
        bc_copy(block, action)

    def combine(block):
        low = meeting.total(block).astype(BF16)
        sum_b[block, :, : 2 * STATE] = low[:, : 2 * STATE]
        sum_x[block] = low[:, 2 * STATE : conv_width]
        sum_z[block] = low[:, conv_width : conv_width + width]
        sum_b[block, :, 2 * STATE :] = low[:, conv_width + width :]
        pieces_of(block, "start")

    def multiply(turn, carry):
        tile = rows_in.turned(turn)
        for chunk in range(rows_in.chunks):
            micro, rows, block = rows_in.block(turn, chunk)
            part = mm_tn(block, dproj_ref[micro, rows, :])
            acc[...] = part if chunk == 0 else acc[...] + part
            rows_in.used(turn, chunk)
        for item in range(per_tile):
            block = tile * per_tile + item
            for group in range(width_total):
                row = item * depth + group * quarter
                stage[block, meeting.slot(block, group)] = acc[row : row + quarter].astype(BF16)
            meeting.first(block).start()
        weights = columns_ref[pl.ds(pl.multiple_of(tile * TILE, TILE), TILE), :]
        product = (acc[...] * weights.astype(F32)).astype(BF16)
        line = mm_nt(jnp.ones((8, product.shape[1]), BF16), product)
        small_stage[pl.ds(tile, 1), conv_end + LANES :] = line[:1]

        @pl.when(turn < MIDDLE)
        def _():
            out_grad.tiles.each(tiles - MIDDLE + turn, out_grad.meeting.middle)

        @pl.when(turn >= MIDDLE)
        def _():
            rows_in.each(turn - MIDDLE, meeting.middle)

        @pl.when(turn < LAST)
        def _():
            out_grad.tiles.each(tiles - LAST + turn, out_grad.combine)

        @pl.when(turn >= LAST)
        def _():
            rows_in.each(turn - LAST, combine)

        return carry

    lax.fori_loop(0, tiles, multiply, 0)

    def small_hop(turn, from_peer):
        peer = lax.rem(mine + turn, width_total)
        group = peer if from_peer else mine
        return remote(
            small_stage,
            small_slots.at[group],
            small_send.at[peer],
            small_receive.at[group],
            {"width": peer},
        )

    for turn in range(1, width_total):
        small_hop(turn, False).start()
    small_slots[mine] = small_stage[...]

    for turn in range(tiles - MIDDLE, tiles):
        rows_in.each(turn, meeting.middle)
    for turn in range(tiles - LAST, tiles):
        rows_in.each(turn, combine)

    for turn in range(1, width_total):
        small_hop(turn, True).wait_recv()
        small_hop(turn, False).wait_send()
    total = small_slots[0]
    for group in range(1, width_total):
        total = total + small_slots[group]
    small_stage[...] = total

    def last_hop(turn, from_peer):
        peer = lax.rem(me + turn, seq_total)
        owner = peer if from_peer else me
        return remote(
            small_stage,
            small_out.at[owner],
            last_send.at[peer],
            last_receive.at[owner],
            {"seq": peer},
        )

    def last_start(turn, carry):
        last_hop(turn, False).start()
        return carry

    lax.fori_loop(1, seq_total, last_start, 0)
    small_out[me] = small_stage[...]

    out_grad.finish(shard_out_ref)

    def bc_arrive(turn, carry):
        source = lax.rem(me + turn, seq_total)
        both(
            source == me,
            sum_b.at[me],
            bc_ref.at[source],
            bc_send.at[me],
            bc_receive.at[source],
            {"seq": source},
            "receive",
        )
        return carry

    lax.fori_loop(0, seq_total, bc_arrive, 0)

    def bc_add(source, total):
        return total + bc_ref[source, :, : 2 * STATE].astype(F32)

    bc_sum = lax.fori_loop(1, seq_total, bc_add, bc_ref[0, :, : 2 * STATE].astype(F32))
    bc_total[:, : 2 * STATE] = bc_sum.astype(BF16)
    for source in range(seq_total):
        at = 2 * STATE + source * heads
        bc_total[:, at : at + heads] = bc_ref[source, :, 2 * STATE : 2 * STATE + heads]
    bc_home(mine, "start")

    def last_end(turn, carry):
        last_hop(turn, False).wait_send()
        last_hop(turn, True).wait_recv()
        return carry

    lax.fori_loop(1, seq_total, last_end, 0)

    def small_add(source, total):
        return total + small_out[source]

    total = lax.fori_loop(1, seq_total, small_add, small_out[0])
    taps_out[:, INNER:] = total[:TAPS, : 2 * STATE]
    bias_out[:, INNER:] = total[TAPS : TAPS + 1, : 2 * STATE]
    in_gain_out[...] = total[:, conv_end + LANES :] / in_gain_ref[...]
    for source in range(seq_total):
        first = source * width
        taps_out[:, first : first + width] = small_out[source, :TAPS, 2 * STATE : conv_width]
        bias_out[:, first : first + width] = small_out[
            source, TAPS : TAPS + 1, 2 * STATE : conv_width
        ]
        gain_out[:, first : first + width] = small_out[source, 1:2, conv_width:conv_end]
        head_out[:, source * heads : (source + 1) * heads] = small_out[
            source, :, conv_end : conv_end + heads
        ]

    first = (mine * shard) // width

    def landed(slot, carry):
        number = first + slot
        source = lax.rem(number, seq_total)

        @pl.when((number < 2 * seq_total) & (number * width < (mine + 1) * shard))
        def _():
            for group in range(width_total):
                both(
                    (source == me) & (mine == group),
                    sum_z.at[me],
                    zx_ref.at[slot, group],
                    zx_send.at[0, me],
                    zx_receive.at[slot, group],
                    {"width": group, "seq": source},
                    "receive",
                )

        return carry

    lax.fori_loop(0, slots, landed, 0)

    @pl.when(mine == width_total - 1)
    def _():
        for source in range(width_total):
            bc_home(source, "receive")

    edge = (slots - -(-(2 * STATE + HEADS) // width)) * width
    for group in range(width_total):
        for slot in range(slots):
            line_buffer[:, slot * width : (slot + 1) * width] = zx_ref[slot, group].astype(F32)

        @pl.when(mine == width_total - 1)
        def _():
            line_buffer[:, edge : edge + 2 * STATE + HEADS] = bc_last[
                group, :, : 2 * STATE + HEADS
            ].astype(F32)

        total_lanes = line_buffer.shape[1]
        start = lax.rem(mine * shard, jnp.int32(width))
        rolled = pltpu.roll(
            line_buffer[...], lax.rem(total_lanes - start, jnp.int32(total_lanes)), 1
        )
        shard_in_ref[group * quarter : (group + 1) * quarter, :] = rolled[:, :shard].astype(BF16)

    def sent(block, carry):
        meeting.sent(block)
        pieces_of(block, "send")
        return carry

    lax.fori_loop(0, seq_total, sent, 0)
    bc_home(mine, "send")


def bring_home(normed, dproj, columns, smalls, in_gain, grad, gnorm, heads, collective_id):
    seq_total, width_total = lax.axis_size("seq"), lax.axis_size("width")
    width = heads * HEAD_DIM
    micros, group_rows, model_width = normed.shape
    depth = model_width // seq_total
    quarter = depth // width_total
    shard = (INNER + CONV + HEADS) // width_total
    slots = max(
        ((group + 1) * shard - 1) // width - group * shard // width + 1
        for group in range(width_total)
    )
    all_columns = dproj.shape[2]
    layout = (seq_total, width_total, quarter, width, slots, shard, heads)
    rest = all_columns - 2 * width
    small = (8, 2 * STATE + 2 * width + LANES + TILE)
    lanes = -(-slots * width // LANES) * LANES
    dma = pltpu.SemaphoreType.DMA
    vmem = pl.BlockSpec(memory_space=pltpu.VMEM)
    return pl.pallas_call(
        partial(home_kernel, layout),
        in_specs=[ANY, ANY] + [vmem] * 4 + [ANY, ANY, vmem],
        out_specs=[vmem] * 7,
        out_shape=[
            jax.ShapeDtypeStruct((depth, shard), BF16),
            jax.ShapeDtypeStruct((seq_total // width_total * width, model_width // seq_total), F32),
            jax.ShapeDtypeStruct((TAPS, CONV), F32),
            jax.ShapeDtypeStruct((1, CONV), F32),
            jax.ShapeDtypeStruct((1, INNER), F32),
            jax.ShapeDtypeStruct((8, HEADS), F32),
            jax.ShapeDtypeStruct(in_gain.shape, F32),
        ],
        scratch_shapes=[
            pltpu.VMEM((slots, width_total, quarter, width), BF16),
            pltpu.VMEM((seq_total, quarter, rest), BF16),
            pltpu.VMEM((seq_total,) + small, F32),
            pltpu.VMEM((quarter, lanes), F32),
            pltpu.VMEM((2, min(group_rows, 1024), TILE), BF16),
            pltpu.VMEM((TILE, all_columns), F32),
            pltpu.VMEM((seq_total, width_total, quarter, all_columns), BF16),
            pltpu.VMEM((seq_total, 2, quarter, all_columns), BF16),
            pltpu.VMEM((seq_total, quarter, all_columns), BF16),
            pltpu.VMEM((seq_total, quarter, width), BF16),
            pltpu.VMEM((seq_total, quarter, width), BF16),
            pltpu.VMEM((seq_total, quarter, rest), BF16),
            pltpu.VMEM(small, F32),
            pltpu.VMEM((width_total,) + small, F32),
            dma((2,)),
            dma((4, seq_total)),
            dma((4, seq_total)),
            dma((slots, width_total)),
            dma((seq_total,)),
            dma((seq_total,)),
            dma((width_total,)),
            dma((width_total,)),
            dma((seq_total,)),
            dma((seq_total,)),
            pltpu.VMEM((quarter, rest), BF16),
            pltpu.VMEM((width_total, quarter, rest), BF16),
            dma((1,)),
            dma((width_total,)),
            pltpu.VMEM(columns.shape, BF16),
            pltpu.VMEM(dproj.shape, BF16),
            dma((2,)),
        ]
        + out_grad_scratch(heads, group_rows, model_width),
        compiler_params=pltpu.CompilerParams(
            collective_id=collective_id, has_side_effects=True, vmem_limit_bytes=62 << 20
        ),
        cost_estimate=pl.CostEstimate(
            flops=150 * 10**9, bytes_accessed=8 * normed.size, transcendentals=0
        ),
        name="bring_home",
    )(normed, columns, *smalls, in_gain, dproj, grad, gnorm)


def own(value, start, count, axis=0):
    return lax.dynamic_slice_in_dim(value, start, count, axis)


def per_device(
    hidden_in,
    starts,
    in_gain,
    in_weight,
    conv_weight,
    conv_bias,
    step_bias,
    decay_log,
    skip_gain,
    gate_gain,
    out_weight,
    cotangent,
):
    seq_total = lax.axis_size("seq")
    seq_index = lax.axis_index("seq")
    group_index = lax.axis_index("width")
    micros, rows, model_width = hidden_in.shape[1:]
    heads = HEADS // seq_total
    width = heads * HEAD_DIM
    depth = in_weight.shape[0]
    head_count = HEADS // 8 * jnp.left_shift(jnp.int32(1), group_index)
    active = head_count.astype(F32) * HEAD_DIM

    hidden = hidden_in[0].astype(F32)
    grads = cotangent[0]
    root_in = lax.rsqrt(jnp.mean(hidden * hidden, axis=2, keepdims=True) + EPSILON)
    normed = (hidden * root_in * in_gain).astype(BF16)

    dt_pad = LANES
    width_total = lax.axis_size("width")
    quarter = depth // width_total
    in_quarter = own(in_weight, group_index * quarter, quarter)
    gates = in_quarter[:, :INNER].reshape(quarter, seq_total, width)
    xs = in_quarter[:, INNER : 2 * INNER].reshape(quarter, seq_total, width)
    bc = jnp.broadcast_to(
        in_quarter[:, None, 2 * INNER : INNER + CONV], (quarter, seq_total, 2 * STATE)
    )
    dts = in_quarter[:, INNER + CONV :].reshape(quarter, seq_total, heads)
    dts = jnp.pad(dts, ((0, 0), (0, 0), (0, dt_pad - heads)))
    pieces = jnp.concatenate([bc, xs, gates, dts], axis=2).transpose(1, 0, 2)
    all_normed, columns = gather_rows(normed, pieces, 0)

    smalls = [
        conv_weight,
        conv_bias[None],
        gate_gain[None],
        skip_gain[None],
        step_bias[None],
        decay_log[None],
    ]
    forward = run_forward(
        heads, starts[0], all_normed, columns, out_weight, grads, smalls, 3
    )
    proj, gg, branch, mixed, states, tails, sums = forward[:7]
    taps, cols, head, expand, gather, tri, all_grad = forward[7:14]
    chip_wise = dict(axis_index_groups=chip_groups(seq_total), scatter_dimension=0, tiled=True)
    branch = lax.psum_scatter(branch, "seq", **chip_wise)
    dnorm, sums = run_cross(all_grad, out_weight, gg, sums, 1)
    roots = lax.rsqrt(sums[:, : 2 * micros : 2] / active + EPSILON)
    own_roots = own(roots, seq_index, 1).reshape(micros, rows, 1)
    all_roots = roots.transpose(1, 0, 2).reshape(micros, seq_total * rows, 1)
    gnorm = (gg.astype(F32) * all_roots).astype(BF16)

    dproj, partial_rows, *smalls = run_backward(
        heads,
        starts[0],
        active[None],
        proj,
        dnorm,
        mixed,
        states,
        tails,
        sums,
        columns,
        [taps, head, cols, expand, gather, tri],
        4,
    )
    smalls.pop()
    scattered = lax.psum_scatter(partial_rows, "seq", **chip_wise)
    head_sums, branch = lax.optimization_barrier((smalls[2], branch))
    home = bring_home(
        all_normed,
        dproj,
        columns,
        [smalls[0], smalls[1], head_sums],
        in_gain.reshape(-1, TILE),
        all_grad,
        gnorm,
        heads,
        2,
    )
    shard_in, shard_out, taps_sum, bias_sum, gain_sum, head_sums, in_gain_sum = home
    output = hidden + branch.reshape(hidden.shape).astype(F32) * own_roots
    scattered, in_gain_sum = lax.optimization_barrier((scattered, in_gain_sum))
    gained = scattered.reshape(hidden.shape).astype(F32) * in_gain
    pull = jnp.mean(gained * hidden, axis=2, keepdims=True) * (root_in * root_in * root_in)
    hidden_grads = grads.astype(F32) + root_in * gained - hidden * pull
    shape = hidden_in.shape
    return (
        output.astype(BF16).reshape(shape),
        hidden_grads.astype(BF16).reshape(shape),
        in_gain_sum.reshape(-1),
        shard_in.astype(F32),
        taps_sum,
        bias_sum[0],
        head_sums[1],
        head_sums[0],
        head_sums[2],
        gain_sum[0],
        shard_out,
    )


def solution(mesh):
    in_specs = (
        P("width", None, "seq", None),
        P("width", None, None),
        P(),
        P("seq", None),
        P(),
        P(),
        P(),
        P(),
        P(),
        P(),
        P("seq", None),
        P("width", None, "seq", None),
    )
    out_specs = (
        P("width", None, "seq", None),
        P("width", None, "seq", None),
        P(),
        P("seq", "width"),
        P(),
        P(),
        P(),
        P(),
        P(),
        P(),
        P("width", "seq"),
    )
    return jax.shard_map(
        per_device, mesh=mesh, in_specs=in_specs, out_specs=out_specs, check_vma=False
    )
```
